32 devices in a mesh: dp: 4 (over z), ctx: 2 (over y), tp: 4 (over x, core).
Axes of the slice: x: 2, y: 2, z: 4, core: 2. Of those that a mesh axis runs over, the one named last changes fastest.
Arguments:
- inputs: bfloat16 [8, 1024, 1024], P('dp', ('ctx', 'tp')), may hold values from -6 to 6
- segment_ids: int32 [8, 1024], P('dp'), may hold values from 0 to 5, as said below
- query_weight: bfloat16 [1024, 1024], P(('dp', 'ctx'), 'tp'), may hold values from -0.25 to 0.25
- key_weight: bfloat16 [1024, 1024], P(('dp', 'ctx'), 'tp'), may hold values from -0.1875 to 0.1875
- value_weight: bfloat16 [1024, 1024], P(('dp', 'ctx'), 'tp'), may hold values from -0.1875 to 0.1875
- output_weight: bfloat16 [1024, 1024], P('tp', ('dp', 'ctx')), may hold values from -0.75 to 0.75
- up_weight: bfloat16 [1024, 4096], P(('dp', 'ctx'), 'tp'), may hold values from -0.1875 to 0.1875
- down_weight: bfloat16 [4096, 1024], P('tp', ('dp', 'ctx')), may hold values from -0.09375 to 0.09375
- querybias: float32 [1024], replicated, may hold values from -4 to 4
- valuebias: float32 [1024], replicated, may hold values from -4 to 4
- outputbias: float32 [1024], replicated, may hold values from -3 to 3
- upbias: float32 [4096], replicated, may hold values from -4 to 4
- downbias: float32 [1024], replicated, may hold values from -3 to 3
- norm_gain: float32 [1024], replicated, may hold values from 0.5 to 1.5
- norm_shift: float32 [1024], replicated, may hold values from -3 to 3
- final_gain: float32 [1024], replicated, may hold values from 0.5 to 1.5
- final_shift: float32 [1024], replicated, may hold values from -3 to 3
- cotangent: bfloat16 [8, 1024, 1024], P('dp', ('ctx', 'tp')), may hold values from -6 to 6
Outputs:
- layer_out: bfloat16 [8, 1024, 1024], P('dp', ('ctx', 'tp'))
- input_grad: float32 [8, 1024, 1024], P('dp', ('ctx', 'tp'))
- query_grad: float32 [1024, 1024], P(('dp', 'ctx'), 'tp')
- key_grad: float32 [1024, 1024], P(('dp', 'ctx'), 'tp')
- value_grad: float32 [1024, 1024], P(('dp', 'ctx'), 'tp')
- output_grad: float32 [1024, 1024], P('tp', ('dp', 'ctx'))
- up_grad: float32 [1024, 4096], P(('dp', 'ctx'), 'tp')
- down_grad: float32 [4096, 1024], P('tp', ('dp', 'ctx'))
- querybias_grad: float32 [1024], replicated
- valuebias_grad: float32 [1024], replicated
- outputbias_grad: float32 [1024], replicated
- upbias_grad: float32 [4096], replicated
- downbias_grad: float32 [1024], replicated
- normgain_grad: float32 [1024], replicated
- normshift_grad: float32 [1024], replicated
- finalgain_grad: float32 [1024], replicated
- finalshift_grad: float32 [1024], replicated
The draws below stay inside these ranges and needn't reach their ends.
Inputs may be any that keep to these rules, and one draw needn't show every extreme that they name: `segment_ids`: within each sequence the ids start at 0 and rise by one at each new document; each document has 204 to 2049 tokens, except that the last one of a sequence may be cut short. In the first sequence the first document has 204 to 511 tokens and the second has 2049, cut short where the sequence ends. In the last sequence every document has 204 tokens, the last one cut short where the sequence ends.
All inputs are finite; a program needn't handle non-finite values.
Results may differ from the reference program's by a relative error of at most 0.015.
The reference program's roundings to bfloat16 on the way count: a program that leaves them out, or rounds other values in their place, can miss the bound.
Values may be sent and summed in bfloat16 or wider, within the bound.
A program may use at most 384 MiB of HBM per device.

```python
import jax
import jax.numpy as jnp
from jax import lax

D = 1024
H = 16
HEAD_DIM = 64
FF = 4096
CTX_TOKENS = 512
MAXDOC = 2049
MINDOC = 204
BATCH = 8
SEQ_LEN = 1024


def draw_segment_ids(key, part):
    length_key, first_key = jax.random.split(jax.random.fold_in(key, 7))
    count = SEQ_LEN // MINDOC + 2
    lengths = jax.random.randint(length_key, (BATCH, count), MINDOC, MAXDOC + 1, dtype=jnp.int32)
    first_len = jax.random.randint(first_key, (), MINDOC, CTX_TOKENS, dtype=jnp.int32)
    column = jnp.arange(count)[None, :]
    sequence = jnp.arange(BATCH)[:, None]
    lengths = jnp.where(jnp.logical_and(sequence == 0, column == 0), first_len, lengths)
    lengths = jnp.where(jnp.logical_and(sequence == 0, column == 1), MAXDOC, lengths)
    lengths = jnp.where(sequence == BATCH - 1, MINDOC, lengths)
    ends = jnp.cumsum(lengths, axis=1)
    position = jnp.arange(SEQ_LEN)
    passed = (ends[:, None, :] <= position[None, :, None]).astype(jnp.int32)
    return jnp.sum(passed, axis=2).astype(jnp.int32)


def spiked(drawn, own_key, source, target, shards_of, factor):
    owner, partner = [(jnp.arange(drawn.shape[dim]) // (drawn.shape[dim] // shards_of)).reshape([-1 if axis == dim else 1 for axis in range(drawn.ndim)]) for dim in (source, target)]
    chosen = jax.random.permutation(own_key, shards_of)[partner]
    strong = (owner == chosen) | (owner == (partner + shards_of // 2) % shards_of)
    return jnp.where(strong, factor * drawn, drawn)


def block_levels(rng, extent, pieces, smallest, high):
    loudness, own = 1.0, jax.random.fold_in(rng, 6)
    for dim, shards_of in pieces:
        steps = jnp.exp(jax.random.uniform(jax.random.fold_in(own, dim), (shards_of,), jnp.float32, smallest / len(pieces), high / len(pieces)))
        loudness = loudness * jnp.repeat(steps, extent[dim] // shards_of).reshape([-1 if axis == dim else 1 for axis in range(len(extent))])
    return loudness


def scatter_about(key, extent, deviation, most, shards=(), kind=jnp.bfloat16):
    drawn = jax.random.normal(key, extent, jnp.float32) * deviation
    if len(shards) > 0:
        drawn = block_levels(key, extent, shards, -0.22, 0.18) * drawn
    return jnp.clip(drawn, min=-most, max=most).astype(kind)


def bell_draw_with(rng, shape, deviation, most, cuts, heavy, kind=jnp.bfloat16):
    entries = deviation * jax.random.normal(rng, shape, jnp.float32)
    if cuts:
        entries = entries * block_levels(rng, shape, cuts, -0.22, 0.18)
    return jnp.clip(spiked(entries, jax.random.fold_in(rng, 3), *heavy), -most, most).astype(kind)


def setup_inputs(seed: int = 0) -> dict:
    key_list = jax.random.split(jax.random.key(seed), 19)
    return {
        "inputs": scatter_about(key_list[0], (BATCH, SEQ_LEN, D), 1.0, 6.0, ((0, 4), (1, 8))),
        "segment_ids": draw_segment_ids(jax.random.fold_in(key_list[18], 71), 0),
        "query_weight": scatter_about(key_list[2], (D, D), (D // 2) ** -0.5, 0.25, ((0, 8), (1, 4))),
        "key_weight": scatter_about(key_list[3], (D, D), D ** -0.5, 0.1875, ((0, 8), (1, 4))),
        "value_weight": scatter_about(key_list[4], (D, D), D ** -0.5, 0.1875, ((0, 8), (1, 4))),
        "output_weight": scatter_about(key_list[5], (D, D), (D // 16) ** -0.5, 0.75, ((0, 4), (1, 8))),
        "up_weight": scatter_about(key_list[6], (D, FF), D ** -0.5, 0.1875, ((0, 8), (1, 4))),
        "down_weight": scatter_about(key_list[7], (FF, D), FF ** -0.5, 0.09375, ((0, 4), (1, 8))),
        "querybias": scatter_about(key_list[8], (D,), 0.3, 4.0, (), jnp.float32),
        "valuebias": scatter_about(key_list[9], (D,), 0.3, 4.0, (), jnp.float32),
        "outputbias": scatter_about(key_list[10], (D,), 0.2, 3.0, (), jnp.float32),
        "upbias": scatter_about(key_list[11], (FF,), 0.3, 4.0, (), jnp.float32),
        "downbias": scatter_about(key_list[12], (D,), 0.2, 3.0, (), jnp.float32),
        "norm_gain": jnp.clip(1.0 + 0.1 * jax.random.normal(key_list[13], (D,), jnp.float32), 0.5, 1.5),
        "norm_shift": scatter_about(key_list[14], (D,), 0.2, 3.0, (), jnp.float32),
        "final_gain": jnp.clip(1.0 + 0.1 * jax.random.normal(key_list[15], (D,), jnp.float32), 0.5, 1.5),
        "final_shift": scatter_about(key_list[16], (D,), 0.2, 3.0, (), jnp.float32),
        "cotangent": bell_draw_with(key_list[17], (BATCH, SEQ_LEN, D), 1.0, 6.0, ((0, 4), (1, 8)), (1, 2, 8, 2.0)),
    }


@jax.custom_vjp
def low(v):
    return lax.optimization_barrier(v.astype(jnp.bfloat16)).astype(jnp.float32)

@jax.custom_vjp
def low_back(v):
    return v

def low_keep(v):
    return (low(v), None)

def low_pass(kept, grad):
    return (grad,)

def back_keep(v):
    return (v, None)

def back_low(kept, grad):
    return (low(grad),)
low.defvjp(low_keep, low_pass)
low_back.defvjp(back_keep, back_low)

def matmul(left_side, right_side):
    return jnp.einsum('btd,de->bte', left_side, right_side, precision=lax.Precision.HIGHEST)

def layer_norm(hidden, gain_vec, shift_vec):
    center = hidden - lax.optimization_barrier(jnp.mean(hidden, axis=-1, keepdims=True))
    variance = lax.optimization_barrier(jnp.mean(center * center, axis=-1, keepdims=True))
    return center * lax.rsqrt(variance + 1e-05) * gain_vec + shift_vec

def gelu_curve(pre_act):
    return 0.5 * pre_act * (1.0 + lax.erf(pre_act * 0.7071067811865476))

def attend_sequence(packed):
    queries, key_rows, value_rows, seq_ids = packed
    blocks_count = queries.shape[0] // CTX_TOKENS
    query_blocks = queries.reshape(blocks_count, CTX_TOKENS, H, HEAD_DIM)
    id_blocks = seq_ids.reshape(blocks_count, CTX_TOKENS)

    def one_block(block_in):
        query_rows, query_ids = block_in
        scores = low_back(jnp.einsum('qhd,khd->hqk', query_rows, key_rows, precision=lax.Precision.HIGHEST))
        same_doc = (query_ids[:, None] == seq_ids[None, :])[None]
        masked = jnp.where(same_doc, scores, -1e+30)
        highest = lax.optimization_barrier(jnp.max(masked, axis=-1, keepdims=True))
        exponent = jnp.where(same_doc, jnp.exp(masked - highest), 0.0)
        attn_probs = exponent / lax.optimization_barrier(jnp.sum(exponent, axis=-1, keepdims=True))
        return jnp.einsum('hqk,khd->qhd', low(attn_probs), value_rows, precision=lax.Precision.HIGHEST)
    mixture = lax.map(jax.checkpoint(one_block), (query_blocks, id_blocks))
    return mixture.reshape(queries.shape[0], H * HEAD_DIM)

def forward(inputs, query_weight, key_weight, value_weight, output_weight, up_weight, down_weight, querybias, valuebias, outputbias, upbias, downbias, norm_gain, norm_shift, final_gain, final_shift, segment_ids):
    batch_rows = inputs.shape[0]
    seq_len = inputs.shape[1]
    score_scale = HEAD_DIM ** (-0.5)
    queries = low_back(low((matmul(inputs, query_weight) + querybias) * score_scale))
    key_rows = low_back(low(matmul(inputs, key_weight)))
    value_rows = low_back(low(matmul(inputs, value_weight) + valuebias))

    def heads_of(tensor):
        return tensor.reshape(batch_rows, seq_len, H, HEAD_DIM)
    attended = lax.map(attend_sequence, (heads_of(queries), heads_of(key_rows), heads_of(value_rows), segment_ids))
    attended = low_back(low(attended))
    first_sum = inputs + low_back(matmul(attended, output_weight) + outputbias)
    normed_first = layer_norm(first_sum, norm_gain, norm_shift)
    hidden_pre = low_back(matmul(low(normed_first), up_weight) + upbias)
    second_sum = normed_first + low_back(matmul(low(gelu_curve(hidden_pre)), down_weight) + downbias)
    return layer_norm(second_sum, final_gain, final_shift)

def reference(inputs, segment_ids, query_weight, key_weight, value_weight, output_weight, up_weight, down_weight, querybias, valuebias, outputbias, upbias, downbias, norm_gain, norm_shift, final_gain, final_shift, cotangent):
    floats = [tensor.astype(jnp.float32) for tensor in (inputs, query_weight, key_weight, value_weight, output_weight, up_weight, down_weight, querybias, valuebias, outputbias, upbias, downbias, norm_gain, norm_shift, final_gain, final_shift)]

    def closed(*operands):
        return forward(*operands, segment_ids)
    result, pullback = jax.vjp(closed, *floats)
    gradients = pullback(cotangent.astype(jnp.float32))
    return (result.astype(jnp.bfloat16), gradients[0], gradients[1], gradients[2], gradients[3], gradients[4], gradients[5], gradients[6], gradients[7], gradients[8], gradients[9], gradients[10], gradients[11], gradients[12], gradients[13], gradients[14], gradients[15])
```

```python
import functools

import jax
import jax.numpy as jnp
from jax import lax
from jax.experimental import pallas as pl
from jax.experimental.pallas import tpu as pltpu
from jax.sharding import PartitionSpec as P

HEAD_DIM = 64
REACH = 4


def shifted(block, axis, distance):
    devices = range(lax.axis_size(axis))
    route = [(i - distance, i) for i in devices if i - distance in devices]
    return lax.ppermute(block, axis, route)


def for_sending(shard):

    def short(part):
        return part.astype(jnp.bfloat16) if part.dtype == jnp.float32 else part

    return jax.tree.map(short, shard)


def layer_norm(hidden, gain_vec, shift_vec):
    center = hidden - jnp.mean(hidden, axis=-1, keepdims=True)
    inverse = lax.rsqrt(jnp.mean(center * center, axis=-1, keepdims=True) + 1e-05)
    normed = center * inverse
    return (normed * gain_vec + shift_vec, normed, inverse)


def norm_back(upstream, normed, inverse, gain_vec):
    scaled = upstream * gain_vec
    return inverse * (
        scaled
        - jnp.mean(scaled, axis=-1, keepdims=True)
        - normed * jnp.mean(scaled * normed, axis=-1, keepdims=True)
    )


def gelu_curve(pre_act):
    return 0.5 * pre_act * (1.0 + lax.erf(pre_act * 0.7071067811865476))


def gelu_slope(pre_act):
    return (
        0.5 * (1.0 + lax.erf(pre_act * 0.7071067811865476))
        + pre_act * jnp.exp(-0.5 * pre_act * pre_act) * 0.3989422804014327
    )


def product(left_side, right_side):
    return jnp.einsum("btd,de->bte", left_side, right_side, preferred_element_type=jnp.float32)


def transposed(left_side, right_side):
    return jnp.einsum("btn,mn->btm", left_side, right_side, preferred_element_type=jnp.float32)


def weight_term(left_side, right_side):
    return jnp.einsum("btd,bte->de", left_side, right_side, preferred_element_type=jnp.float32)


def block_scores(query_rows, key_rows, block_mask):
    scores = jnp.einsum("bqhd,bkhd->bhqk", query_rows, key_rows, preferred_element_type=jnp.float32)
    return jnp.where(block_mask, scores, -1e30)


def probabilities(query_rows, key_rows, block_mask, log_total):
    scores = block_scores(query_rows, key_rows, block_mask)
    return jnp.where(block_mask, jnp.exp(scores - log_total[..., None]), 0.0)


def placed(local_part, full_len, place_at):
    empty = jnp.zeros((full_len,), jnp.float32)
    return lax.dynamic_update_slice_in_dim(empty, local_part, place_at * local_part.shape[0], 0)


def ring_plan(
    inputs,
    segment_ids,
    query_weight,
    key_weight,
    value_weight,
    output_weight,
    up_weight,
    down_weight,
    querybias,
    valuebias,
    outputbias,
    upbias,
    downbias,
    norm_gain,
    norm_shift,
    final_gain,
    final_shift,
    cotangent,
):
    tp_count = lax.axis_size("tp")
    tp_place = lax.axis_index("tp")
    ctx_count = lax.axis_size("ctx")
    ctx_place = lax.axis_index("ctx")
    batch_rows, part_rows, model_width = inputs.shape
    shard_rows = part_rows * tp_count
    full_query, full_key, full_value, full_output, full_up, full_down = (
        lax.all_gather(query_weight, ("dp", "ctx"), axis=0, tiled=True),
        lax.all_gather(key_weight, ("dp", "ctx"), axis=0, tiled=True),
        lax.all_gather(value_weight, ("dp", "ctx"), axis=0, tiled=True),
        lax.all_gather(output_weight, ("dp", "ctx"), axis=1, tiled=True),
        lax.all_gather(up_weight, ("dp", "ctx"), axis=0, tiled=True),
        lax.all_gather(down_weight, ("dp", "ctx"), axis=1, tiled=True),
    )
    local_width = full_query.shape[1]
    local_heads = local_width // HEAD_DIM
    hidden_width = full_up.shape[1]
    query_offset = lax.dynamic_slice_in_dim(querybias, tp_place * local_width, local_width)
    value_offset = lax.dynamic_slice_in_dim(valuebias, tp_place * local_width, local_width)
    up_offset = lax.dynamic_slice_in_dim(upbias, tp_place * hidden_width, hidden_width)
    score_scale = HEAD_DIM ** (-0.5)

    def split_heads(tensor):
        return tensor.reshape(batch_rows, shard_rows, local_heads, HEAD_DIM)

    def join_heads(tensor):
        return tensor.reshape(batch_rows, shard_rows, local_width)

    tokens = lax.all_gather(inputs, "tp", axis=1, tiled=True)
    queries = split_heads(
        ((product(tokens, full_query) + query_offset) * score_scale).astype(jnp.bfloat16)
    )
    key_rows = split_heads(product(tokens, full_key).astype(jnp.bfloat16))
    value_rows = split_heads((product(tokens, full_value) + value_offset).astype(jnp.bfloat16))
    own_ids = lax.dynamic_slice_in_dim(segment_ids, ctx_place * shard_rows, shard_rows, 1)
    offsets = [0] + [
        offset for offset in range(-REACH, REACH + 1) if offset != 0 and abs(offset) < ctx_count
    ]
    mask_of = {}
    block_of = {}
    for offset in offsets:
        source = ctx_place + offset
        begin_at = jnp.clip(source, 0, ctx_count - 1) * shard_rows
        other_ids = lax.dynamic_slice_in_dim(segment_ids, begin_at, shard_rows, 1)
        inside = jnp.logical_and(source >= 0, source < ctx_count)
        mask_of[offset] = jnp.logical_and(own_ids[:, :, None] == other_ids[:, None, :], inside)[
            :, None
        ]
        if offset == 0:
            block_of[offset] = (key_rows, value_rows)
        else:
            block_of[offset] = shifted((key_rows, value_rows), "ctx", -offset)
    running = jnp.full((batch_rows, local_heads, shard_rows), -1e30, jnp.float32)
    totals = jnp.zeros((batch_rows, local_heads, shard_rows), jnp.float32)
    for offset in offsets:
        scores = block_scores(queries, block_of[offset][0], mask_of[offset])
        highest = jnp.maximum(running, jnp.max(scores, axis=-1))
        weights = jnp.where(mask_of[offset], jnp.exp(scores - highest[..., None]), 0.0)
        totals = totals * jnp.exp(running - highest) + jnp.sum(weights, axis=-1)
        running = highest
    log_total = running + jnp.log(totals)
    mixture = jnp.zeros((batch_rows, shard_rows, local_heads, HEAD_DIM), jnp.float32)
    for offset in offsets:
        attn_probs = probabilities(queries, block_of[offset][0], mask_of[offset], log_total)
        mixture = mixture + jnp.einsum(
            "bhqk,bkhd->bqhd",
            attn_probs.astype(jnp.bfloat16),
            block_of[offset][1],
            preferred_element_type=jnp.float32,
        )
    attended = join_heads(mixture).astype(jnp.bfloat16)
    output_part = lax.psum_scatter(
        product(attended, full_output), "tp", scatter_dimension=1, tiled=True
    )
    first_sum = inputs.astype(jnp.float32) + output_part + outputbias
    normed_first, first_normed, first_inverse = layer_norm(first_sum, norm_gain, norm_shift)
    normed_rows = lax.all_gather(normed_first.astype(jnp.bfloat16), "tp", axis=1, tiled=True)
    hidden_pre = product(normed_rows, full_up) + up_offset
    hidden_low = gelu_curve(hidden_pre).astype(jnp.bfloat16)
    down_part = lax.psum_scatter(
        product(hidden_low, full_down), "tp", scatter_dimension=1, tiled=True
    )
    second_sum = normed_first + down_part + downbias
    result, second_normed, second_inverse = layer_norm(second_sum, final_gain, final_shift)
    upstream = cotangent.astype(jnp.float32)
    finalgain_grad = jnp.sum(upstream * second_normed, axis=(0, 1))
    finalshift_grad = jnp.sum(upstream, axis=(0, 1))
    second_grad = norm_back(upstream, second_normed, second_inverse, final_gain)
    down_low = second_grad.astype(jnp.bfloat16)
    downbias_grad = jnp.sum(down_low, axis=(0, 1), dtype=jnp.float32)
    down_rows = lax.all_gather(down_low, "tp", axis=1, tiled=True)
    down_grad = weight_term(hidden_low, down_rows)
    hidden_grad = (transposed(down_rows, full_down) * gelu_slope(hidden_pre)).astype(jnp.bfloat16)
    upbias_part = jnp.sum(hidden_grad, axis=(0, 1), dtype=jnp.float32)
    up_grad = weight_term(normed_rows, hidden_grad)
    normed_grad = (
        lax.psum_scatter(transposed(hidden_grad, full_up), "tp", scatter_dimension=1, tiled=True)
        + second_grad
    )
    normgain_grad = jnp.sum(normed_grad * first_normed, axis=(0, 1))
    normshift_grad = jnp.sum(normed_grad, axis=(0, 1))
    first_grad = norm_back(normed_grad, first_normed, first_inverse, norm_gain)
    output_low = first_grad.astype(jnp.bfloat16)
    outputbias_grad = jnp.sum(output_low, axis=(0, 1), dtype=jnp.float32)
    output_rows = lax.all_gather(output_low, "tp", axis=1, tiled=True)
    output_grad = weight_term(attended, output_rows)
    mixed_grad = split_heads(transposed(output_rows, full_output).astype(jnp.bfloat16))
    row_dot = jnp.zeros((batch_rows, local_heads, shard_rows), jnp.float32)
    for offset in offsets:
        attn_probs = probabilities(queries, block_of[offset][0], mask_of[offset], log_total)
        prob_grad = jnp.einsum(
            "bqhd,bkhd->bhqk", mixed_grad, block_of[offset][1], preferred_element_type=jnp.float32
        )
        row_dot = row_dot + jnp.sum(attn_probs * prob_grad, axis=-1)
    query_acc = jnp.zeros((batch_rows, shard_rows, local_heads, HEAD_DIM), jnp.float32)
    key_parts = {}
    for offset in offsets:
        attn_probs = probabilities(queries, block_of[offset][0], mask_of[offset], log_total)
        prob_grad = jnp.einsum(
            "bqhd,bkhd->bhqk", mixed_grad, block_of[offset][1], preferred_element_type=jnp.float32
        )
        score_grad = (attn_probs * (prob_grad - row_dot[..., None])).astype(jnp.bfloat16)
        query_acc = query_acc + jnp.einsum(
            "bhqk,bkhd->bqhd", score_grad, block_of[offset][0], preferred_element_type=jnp.float32
        )
        key_term = jnp.einsum(
            "bhqk,bqhd->bkhd", score_grad, queries, preferred_element_type=jnp.float32
        )
        value_term = jnp.einsum(
            "bhqk,bqhd->bkhd",
            attn_probs.astype(jnp.bfloat16),
            mixed_grad,
            preferred_element_type=jnp.float32,
        )
        key_parts[offset] = (key_term, value_term)
    own_key, own_value = key_parts[0]
    for offset in offsets[1:]:
        back_key, back_value = shifted(for_sending(key_parts[offset]), "ctx", offset)
        own_key = own_key + back_key
        own_value = own_value + back_value
    query_pre = (
        join_heads(query_acc.astype(jnp.bfloat16)).astype(jnp.float32) * score_scale
    ).astype(jnp.bfloat16)
    key_low = join_heads(own_key.astype(jnp.bfloat16))
    value_low = join_heads(own_value.astype(jnp.bfloat16))
    querybias_part = jnp.sum(query_pre, axis=(0, 1), dtype=jnp.float32)
    valuebias_part = jnp.sum(value_low, axis=(0, 1), dtype=jnp.float32)
    query_grad = weight_term(tokens, query_pre)
    key_grad = weight_term(tokens, key_low)
    value_grad = weight_term(tokens, value_low)
    input_part = (
        transposed(query_pre, full_query)
        + transposed(key_low, full_key)
        + transposed(value_low, full_value)
    )
    input_grad = (
        lax.psum_scatter(
            input_part.astype(jnp.bfloat16), "tp", scatter_dimension=1, tiled=True
        ).astype(jnp.float32)
        + first_grad
    )
    query_grad, key_grad, value_grad, output_grad, up_grad, down_grad = (
        lax.psum_scatter(query_grad, ("dp", "ctx"), scatter_dimension=0, tiled=True),
        lax.psum_scatter(key_grad, ("dp", "ctx"), scatter_dimension=0, tiled=True),
        lax.psum_scatter(value_grad, ("dp", "ctx"), scatter_dimension=0, tiled=True),
        lax.psum_scatter(output_grad, ("dp", "ctx"), scatter_dimension=1, tiled=True),
        lax.psum_scatter(up_grad, ("dp", "ctx"), scatter_dimension=0, tiled=True),
        lax.psum_scatter(down_grad, ("dp", "ctx"), scatter_dimension=1, tiled=True),
    )
    summed = lax.psum(
        (
            placed(querybias_part, model_width, tp_place),
            placed(valuebias_part, model_width, tp_place),
            outputbias_grad,
            placed(upbias_part, hidden_width * tp_count, tp_place),
            downbias_grad,
            normgain_grad,
            normshift_grad,
            finalgain_grad,
            finalshift_grad,
        ),
        ("dp", "ctx", "tp"),
    )
    return (
        result.astype(jnp.bfloat16),
        input_grad,
        query_grad,
        key_grad,
        value_grad,
        output_grad,
        up_grad,
        down_grad,
        summed[0],
        summed[1],
        summed[2],
        summed[3],
        summed[4],
        summed[5],
        summed[6],
        summed[7],
        summed[8],
    )


MESH = pl.DeviceIdType.MESH
LOWEST = -1e30
VMEM = pl.BlockSpec(memory_space=pltpu.VMEM)
LEFT = pl.BlockSpec(memory_space=pl.ANY)


class Seat:
    def __init__(self):
        self.dp_count = lax.axis_size("dp")
        self.dp = lax.axis_index("dp")
        self.ctx = lax.axis_index("ctx")
        self.tp = lax.axis_index("tp")
        self.tp_pair = self.tp + 1 - 2 * (self.tp % 2)
        self.tp_side = (self.tp + 2) % 4
        self.tp_far = (self.tp_pair + 2) % 4
        self.pair = (self.dp, self.ctx, self.tp_pair)
        self.side = (self.dp, self.ctx, self.tp_side)
        self.twin = (self.dp, 1 - self.ctx, self.tp)
        self.above = ((self.dp + 1) % self.dp_count, self.ctx, self.tp)
        self.below = ((self.dp + self.dp_count - 1) % self.dp_count, self.ctx, self.tp)

    def meet(self, names):
        barrier = pltpu.get_barrier_semaphore()
        for name in names:
            pl.semaphore_signal(
                barrier, inc=1, device_id=getattr(self, name), device_id_type=MESH
            )
        pl.semaphore_wait(barrier, len(names))


def remote(source, target, send_sem, recv_sem, to):
    return pltpu.make_async_remote_copy(
        src_ref=source,
        dst_ref=target,
        send_sem=send_sem,
        recv_sem=recv_sem,
        device_id=to,
        device_id_type=MESH,
    )


class RingGather:
    def __init__(self, seat, shard, block, sems, at):
        self.seat, self.shard, self.block, self.at = seat, shard, block, at
        self.own_sem, self.z_send, self.z_recv, self.y_send, self.y_recv = sems
        self.count = seat.dp_count

    def index(self, step, ctx):
        origin = (self.seat.dp + self.count - step) % self.count
        return origin * 2 + ctx

    def held(self, step):
        return self.block(self.index(step, self.seat.ctx))

    def own(self):
        return pltpu.make_async_copy(self.shard, self.held(0), self.own_sem.at[self.at])

    def z(self, step):
        source = self.shard if step == 0 else self.held(step)
        return remote(
            source,
            self.held(step),
            self.z_send.at[self.at, step],
            self.z_recv.at[self.at, step],
            self.seat.above,
        )

    def z_in(self, step):
        view = self.held(step + 1)
        return remote(
            view,
            view,
            self.z_send.at[self.at, step],
            self.z_recv.at[self.at, step],
            self.seat.above,
        )

    def y(self, step):
        source = self.shard if step == 0 else self.held(step)
        return remote(
            source,
            self.held(step),
            self.y_send.at[self.at, step],
            self.y_recv.at[self.at, step],
            self.seat.twin,
        )

    def y_in(self, step):
        view = self.block(self.index(step, 1 - self.seat.ctx))
        return remote(
            view,
            view,
            self.y_send.at[self.at, step],
            self.y_recv.at[self.at, step],
            self.seat.twin,
        )

    def begin(self):
        self.own().start()
        self.z(0).start()
        self.y(0).start()

    def pass_on(self, step):
        self.z_in(step).wait_recv()
        if step + 1 < self.count - 1:
            self.z(step + 1).start()
        self.y(step + 1).start()

    def land(self):
        self.own().wait()
        for step in range(self.count):
            self.y_in(step).wait_recv()

    def close(self):
        for step in range(self.count - 1):
            self.z(step).wait_send()
        for step in range(self.count):
            self.y(step).wait_send()


def gather_sems(pieces, count):
    dma = pltpu.SemaphoreType.DMA
    return [
        dma((pieces,)),
        dma((pieces, count - 1)),
        dma((pieces, count - 1)),
        dma((pieces, count)),
        dma((pieces, count)),
    ]


def dot(left_side, right_side):
    return jnp.dot(left_side, right_side, preferred_element_type=jnp.float32)


def dot_nt(left_side, right_side):
    return lax.dot_general(
        left_side, right_side, (((1,), (1,)), ((), ())), preferred_element_type=jnp.float32
    )


def dot_tn(left_side, right_side):
    return lax.dot_general(
        left_side, right_side, (((0,), (0,)), ((), ())), preferred_element_type=jnp.float32
    )


def aligned(start, size):
    return pl.ds(pl.multiple_of(start, size), size)


def attend_kernel(
    inputs_ref,
    ids_ref,
    query_shard,
    key_shard,
    value_shard,
    output_shard,
    up_shard,
    down_shard,
    query_bias,
    value_bias,
    tokens_ref,
    query_full,
    key_full,
    value_full,
    output_full,
    up_full,
    down_full,
    query_ref,
    key_ref,
    value_ref,
    mixed_ref,
    log_ref,
    attended_ref,
    other_ref,
    flipped_ref,
    ids_down,
    token_send,
    token_recv,
    token_own,
    *sems,
):
    seat = Seat()
    batch, part, width = inputs_ref.shape
    rows = tokens_ref.shape[1]
    local = query_full.shape[1]
    heads = local // HEAD_DIM
    depth = query_shard.shape[0]
    seat.meet(("pair", "side", "twin", "above", "below"))

    def cut(half, place):
        return half.at[:, aligned(place * part, part), :]

    def token_copy(relation, source, target, to):
        return remote(source, target, token_send.at[relation], token_recv.at[relation], to)

    here = cut(tokens_ref, seat.tp)
    there = cut(other_ref, seat.tp)
    here_side = cut(tokens_ref, seat.tp_side)
    there_side = cut(other_ref, seat.tp_side)
    sends = [
        token_copy(0, inputs_ref, here, seat.pair),
        token_copy(1, inputs_ref, here, seat.side),
        token_copy(2, inputs_ref, there, seat.twin),
        token_copy(3, there, there, seat.side),
        token_copy(4, here_side, here_side, seat.pair),
        token_copy(5, there, there, seat.pair),
        token_copy(6, there_side, there_side, seat.pair),
    ]
    landed = [
        cut(tokens_ref, seat.tp_pair),
        here_side,
        there,
        there_side,
        cut(tokens_ref, seat.tp_far),
        cut(other_ref, seat.tp_pair),
        cut(other_ref, seat.tp_far),
    ]

    def token_in(relation):
        token_copy(relation, landed[relation], landed[relation], seat.pair).wait_recv()

    own_tokens = pltpu.make_async_copy(inputs_ref, here, token_own)
    own_tokens.start()
    for relation in range(3):
        sends[relation].start()

    def by_rows(full):
        return lambda r: full.at[aligned(r * depth, depth), :]

    def by_columns(full):
        return lambda r: full.at[:, aligned(r * depth, depth)]

    weights = [
        RingGather(seat, query_shard, by_rows(query_full), sems, 0),
        RingGather(seat, key_shard, by_rows(key_full), sems, 1),
        RingGather(seat, value_shard, by_rows(value_full), sems, 2),
    ]
    later = [
        RingGather(seat, output_shard, by_columns(output_full), sems, 3),
        RingGather(seat, up_shard, by_rows(up_full), sems, 4),
        RingGather(seat, down_shard, by_columns(down_full), sems, 5),
    ]
    hops = seat.dp_count - 1
    for weight in weights:
        weight.begin()
    for step in range(hops):
        for weight in weights:
            weight.pass_on(step)
    for weight in later:
        weight.begin()
    token_in(1)
    sends[4].start()
    token_in(2)
    sends[3].start()
    sends[5].start()

    for b in range(batch):
        for half in range(2):
            row_ids = ids_ref[b : b + 1, aligned((seat.ctx if half == 0 else 1 - seat.ctx) * rows, rows)]
            spread = jnp.broadcast_to(row_ids.astype(jnp.float32), (128, rows))
            ids_down[b, half * rows : (half + 1) * rows, :] = spread.T

    bias_at = aligned(seat.tp * local, local)
    query_offset = query_bias[:, bias_at]
    value_offset = value_bias[:, bias_at]
    tile = rows // 2
    for weight in weights:
        weight.land()
    own_tokens.wait()
    token_in(0)
    token_in(4)

    def project(half_ref, half):
        def one(index, carry):
            b, piece = index // 2, index % 2
            block = half_ref[b, aligned(piece * tile, tile), :]
            spot = aligned(half * rows + piece * tile, tile)
            if half == 0:
                scaled = (dot(block, query_full[...]) + query_offset) * HEAD_DIM ** (-0.5)
                query_ref[b, aligned(piece * tile, tile), :] = scaled.astype(jnp.bfloat16)
            key_ref[b, spot, :] = dot(block, key_full[...]).astype(jnp.bfloat16)
            value_rows = dot(block, value_full[...]) + value_offset
            value_ref[b, spot, :] = value_rows.astype(jnp.bfloat16)
            flipped_ref[b, :, spot] = value_rows.T.astype(jnp.bfloat16)
            return carry

        lax.fori_loop(0, batch * 2, one, 0)

    project(tokens_ref, 0)
    token_in(3)
    sends[6].start()
    token_in(5)
    token_in(6)
    project(other_ref, 1)

    lane_head = lax.broadcasted_iota(jnp.int32, (1, local), 1) // HEAD_DIM

    def attend(index, carry):
        for step in range(hops):
            @pl.when(index == 2 * step + 1)
            def _():
                for weight in later:
                    weight.pass_on(step)

        b, h = index // heads, index % heads
        own_rows = aligned(h * HEAD_DIM, HEAD_DIM)
        chosen = jnp.where(lane_head == h, query_ref[b], jnp.zeros((), jnp.bfloat16))
        scores = dot_nt(key_ref[b], chosen)
        own_ids = ids_ref[b, aligned(seat.ctx * rows, rows)].astype(jnp.float32)
        same = jnp.tile(ids_down[b], (1, rows // 128)) == own_ids[None, :]
        scores = jnp.where(same, scores, LOWEST)
        highest = jnp.max(scores, axis=0, keepdims=True)
        raised = jnp.exp(scores - highest)
        total = jnp.sum(raised, axis=0, keepdims=True)
        shares = (raised * (1.0 / total)).astype(jnp.bfloat16)
        mixed_ref[b, own_rows, :] = dot(flipped_ref[b, own_rows, :], shares)
        log_ref[index] = highest + jnp.log(total)
        return carry

    lax.fori_loop(0, batch * heads, attend, 0)
    for b in range(batch):
        attended_ref[b] = mixed_ref[b].T.astype(jnp.bfloat16)
    for weight in later:
        weight.land()
    for copy in sends:
        copy.wait_send()
    for weight in weights + later:
        weight.close()


def attend_forward(
    inputs, segment_ids, shards, querybias, valuebias
):
    count = lax.axis_size("dp")
    batch, part, width = inputs.shape
    rows = part * lax.axis_size("tp")
    local = shards[0].shape[1]
    hidden = shards[4].shape[1]
    heads = local // HEAD_DIM
    bf16, f32 = jnp.bfloat16, jnp.float32
    outs = [
        ((batch, rows, width), bf16, VMEM),
        ((width, local), bf16, VMEM),
        ((width, local), bf16, VMEM),
        ((width, local), bf16, VMEM),
        ((local, width), bf16, LEFT),
        ((width, hidden), bf16, LEFT),
        ((hidden, width), bf16, LEFT),
        ((batch, rows, local), bf16, VMEM),
        ((batch, 2 * rows, local), bf16, VMEM),
        ((batch, 2 * rows, local), bf16, VMEM),
        ((batch, local, rows), f32, VMEM),
        ((batch * heads, 1, rows), f32, VMEM),
        ((batch, rows, local), bf16, VMEM),
    ]
    dma = pltpu.SemaphoreType.DMA
    return pl.pallas_call(
        attend_kernel,
        name="attend_forward",
        out_shape=[jax.ShapeDtypeStruct(shape, kind) for shape, kind, _ in outs],
        in_specs=[VMEM] * 10,
        out_specs=[space for _, _, space in outs],
        scratch_shapes=[
            pltpu.VMEM((batch, rows, width), bf16),
            pltpu.VMEM((batch, local, 2 * rows), bf16),
            pltpu.VMEM((batch, 2 * rows, 128), f32),
            dma((7,)),
            dma((7,)),
            dma(()),
            *gather_sems(6, count),
        ],
        compiler_params=pltpu.CompilerParams(
            collective_id=1, has_side_effects=True, vmem_limit_bytes=56 * 2**20
        ),
    )(
        inputs,
        segment_ids,
        *shards,
        querybias.reshape(1, -1),
        valuebias.reshape(1, -1),
    )


def fused_plan(
    inputs,
    segment_ids,
    query_weight,
    key_weight,
    value_weight,
    output_weight,
    up_weight,
    down_weight,
    querybias,
    valuebias,
    outputbias,
    upbias,
    downbias,
    norm_gain,
    norm_shift,
    final_gain,
    final_shift,
    cotangent,
):
    tp_count = lax.axis_size("tp")
    tp_place = lax.axis_index("tp")
    ctx_count = lax.axis_size("ctx")
    ctx_place = lax.axis_index("ctx")
    batch_rows, part_rows, model_width = inputs.shape
    shard_rows = part_rows * tp_count
    (
        tokens,
        full_query,
        full_key,
        full_value,
        full_output,
        full_up,
        full_down,
        queries,
        both_keys,
        both_values,
        mixture,
        log_rows,
        attended,
    ) = attend_forward(
        inputs,
        segment_ids,
        (query_weight, key_weight, value_weight, output_weight, up_weight, down_weight),
        querybias,
        valuebias,
    )
    local_width = full_query.shape[1]
    local_heads = local_width // HEAD_DIM
    hidden_width = full_up.shape[1]
    up_offset = lax.dynamic_slice_in_dim(upbias, tp_place * hidden_width, hidden_width)
    score_scale = HEAD_DIM ** (-0.5)

    def split_heads(tensor):
        return tensor.reshape(batch_rows, shard_rows, local_heads, HEAD_DIM)

    def join_heads(tensor):
        return tensor.reshape(batch_rows, shard_rows, local_width)

    queries = split_heads(queries)
    log_total = log_rows.reshape(batch_rows, local_heads, shard_rows)
    own_ids = lax.dynamic_slice_in_dim(segment_ids, ctx_place * shard_rows, shard_rows, 1)
    other_ids = lax.dynamic_slice_in_dim(segment_ids, (1 - ctx_place) * shard_rows, shard_rows, 1)
    offsets = [0, 1]
    mask_of = {
        0: (own_ids[:, :, None] == own_ids[:, None, :])[:, None],
        1: (own_ids[:, :, None] == other_ids[:, None, :])[:, None],
    }
    block_of = {
        half: tuple(
            split_heads(both[:, half * shard_rows : (half + 1) * shard_rows])
            for both in (both_keys, both_values)
        )
        for half in (0, 1)
    }
    output_part = lax.psum_scatter(
        product(attended, full_output), "tp", scatter_dimension=1, tiled=True
    )
    first_sum = inputs.astype(jnp.float32) + output_part + outputbias
    normed_first, first_normed, first_inverse = layer_norm(first_sum, norm_gain, norm_shift)
    normed_rows = lax.all_gather(normed_first.astype(jnp.bfloat16), "tp", axis=1, tiled=True)
    hidden_pre = product(normed_rows, full_up) + up_offset
    hidden_low = gelu_curve(hidden_pre).astype(jnp.bfloat16)
    down_part = lax.psum_scatter(
        product(hidden_low, full_down), "tp", scatter_dimension=1, tiled=True
    )
    second_sum = normed_first + down_part + downbias
    result, second_normed, second_inverse = layer_norm(second_sum, final_gain, final_shift)
    upstream = cotangent.astype(jnp.float32)
    finalgain_grad = jnp.sum(upstream * second_normed, axis=(0, 1))
    finalshift_grad = jnp.sum(upstream, axis=(0, 1))
    second_grad = norm_back(upstream, second_normed, second_inverse, final_gain)
    down_low = second_grad.astype(jnp.bfloat16)
    downbias_grad = jnp.sum(down_low, axis=(0, 1), dtype=jnp.float32)
    down_rows = lax.all_gather(down_low, "tp", axis=1, tiled=True)
    down_grad = weight_term(hidden_low, down_rows)
    hidden_grad = (transposed(down_rows, full_down) * gelu_slope(hidden_pre)).astype(jnp.bfloat16)
    upbias_part = jnp.sum(hidden_grad, axis=(0, 1), dtype=jnp.float32)
    up_grad = weight_term(normed_rows, hidden_grad)
    normed_grad = (
        lax.psum_scatter(transposed(hidden_grad, full_up), "tp", scatter_dimension=1, tiled=True)
        + second_grad
    )
    normgain_grad = jnp.sum(normed_grad * first_normed, axis=(0, 1))
    normshift_grad = jnp.sum(normed_grad, axis=(0, 1))
    first_grad = norm_back(normed_grad, first_normed, first_inverse, norm_gain)
    output_low = first_grad.astype(jnp.bfloat16)
    outputbias_grad = jnp.sum(output_low, axis=(0, 1), dtype=jnp.float32)
    output_rows = lax.all_gather(output_low, "tp", axis=1, tiled=True)
    output_grad = weight_term(attended, output_rows)
    mixed_grad = split_heads(transposed(output_rows, full_output).astype(jnp.bfloat16))
    row_dot = jnp.zeros((batch_rows, local_heads, shard_rows), jnp.float32)
    for offset in offsets:
        attn_probs = probabilities(queries, block_of[offset][0], mask_of[offset], log_total)
        prob_grad = jnp.einsum(
            "bqhd,bkhd->bhqk", mixed_grad, block_of[offset][1], preferred_element_type=jnp.float32
        )
        row_dot = row_dot + jnp.sum(attn_probs * prob_grad, axis=-1)
    query_acc = jnp.zeros((batch_rows, shard_rows, local_heads, HEAD_DIM), jnp.float32)
    key_parts = {}
    for offset in offsets:
        attn_probs = probabilities(queries, block_of[offset][0], mask_of[offset], log_total)
        prob_grad = jnp.einsum(
            "bqhd,bkhd->bhqk", mixed_grad, block_of[offset][1], preferred_element_type=jnp.float32
        )
        score_grad = (attn_probs * (prob_grad - row_dot[..., None])).astype(jnp.bfloat16)
        query_acc = query_acc + jnp.einsum(
            "bhqk,bkhd->bqhd", score_grad, block_of[offset][0], preferred_element_type=jnp.float32
        )
        key_term = jnp.einsum(
            "bhqk,bqhd->bkhd", score_grad, queries, preferred_element_type=jnp.float32
        )
        value_term = jnp.einsum(
            "bhqk,bqhd->bkhd",
            attn_probs.astype(jnp.bfloat16),
            mixed_grad,
            preferred_element_type=jnp.float32,
        )
        key_parts[offset] = (key_term, value_term)
    own_key, own_value = key_parts[0]
    for offset in offsets[1:]:
        back_key, back_value = lax.ppermute(
            for_sending(key_parts[offset]), "ctx", [(0, 1), (1, 0)]
        )
        own_key = own_key + back_key
        own_value = own_value + back_value
    query_pre = (
        join_heads(query_acc.astype(jnp.bfloat16)).astype(jnp.float32) * score_scale
    ).astype(jnp.bfloat16)
    key_low = join_heads(own_key.astype(jnp.bfloat16))
    value_low = join_heads(own_value.astype(jnp.bfloat16))
    querybias_part = jnp.sum(query_pre, axis=(0, 1), dtype=jnp.float32)
    valuebias_part = jnp.sum(value_low, axis=(0, 1), dtype=jnp.float32)
    query_grad = weight_term(tokens, query_pre)
    key_grad = weight_term(tokens, key_low)
    value_grad = weight_term(tokens, value_low)
    input_part = (
        transposed(query_pre, full_query)
        + transposed(key_low, full_key)
        + transposed(value_low, full_value)
    )
    input_grad = (
        lax.psum_scatter(
            input_part.astype(jnp.bfloat16), "tp", scatter_dimension=1, tiled=True
        ).astype(jnp.float32)
        + first_grad
    )
    query_grad, key_grad, value_grad, output_grad, up_grad, down_grad = (
        lax.psum_scatter(query_grad, ("dp", "ctx"), scatter_dimension=0, tiled=True),
        lax.psum_scatter(key_grad, ("dp", "ctx"), scatter_dimension=0, tiled=True),
        lax.psum_scatter(value_grad, ("dp", "ctx"), scatter_dimension=0, tiled=True),
        lax.psum_scatter(output_grad, ("dp", "ctx"), scatter_dimension=1, tiled=True),
        lax.psum_scatter(up_grad, ("dp", "ctx"), scatter_dimension=0, tiled=True),
        lax.psum_scatter(down_grad, ("dp", "ctx"), scatter_dimension=1, tiled=True),
    )
    summed = lax.psum(
        (
            placed(querybias_part, model_width, tp_place),
            placed(valuebias_part, model_width, tp_place),
            outputbias_grad,
            placed(upbias_part, hidden_width * tp_count, tp_place),
            downbias_grad,
            normgain_grad,
            normshift_grad,
            finalgain_grad,
            finalshift_grad,
        ),
        ("dp", "ctx", "tp"),
    )
    return (
        result.astype(jnp.bfloat16),
        input_grad,
        query_grad,
        key_grad,
        value_grad,
        output_grad,
        up_grad,
        down_grad,
        summed[0],
        summed[1],
        summed[2],
        summed[3],
        summed[4],
        summed[5],
        summed[6],
        summed[7],
        summed[8],
    )


def solution(mesh):
    fits = mesh.shape["ctx"] == 2 and mesh.shape["tp"] == 4 and mesh.shape["dp"] > 2
    placed = (
        P("dp", ("ctx", "tp"), None),
        P("dp", None),
        P(("dp", "ctx"), "tp"),
        P(("dp", "ctx"), "tp"),
        P(("dp", "ctx"), "tp"),
        P("tp", ("dp", "ctx")),
        P(("dp", "ctx"), "tp"),
        P("tp", ("dp", "ctx")),
        P(),
        P(),
        P(),
        P(),
        P(),
        P(),
        P(),
        P(),
        P(),
        P("dp", ("ctx", "tp"), None),
    )
    return jax.shard_map(
        fused_plan if fits else ring_plan,
        mesh=mesh,
        in_specs=placed,
        out_specs=(
            P("dp", ("ctx", "tp"), None),
            P("dp", ("ctx", "tp"), None),
            P(("dp", "ctx"), "tp"),
            P(("dp", "ctx"), "tp"),
            P(("dp", "ctx"), "tp"),
            P("tp", ("dp", "ctx")),
            P(("dp", "ctx"), "tp"),
            P("tp", ("dp", "ctx")),
            P(),
            P(),
            P(),
            P(),
            P(),
            P(),
            P(),
            P(),
            P(),
        ),
        check_vma=False,
    )
```

```python
import functools

import jax
import jax.numpy as jnp
from jax import lax
from jax.experimental import pallas as pl
from jax.experimental.pallas import tpu as pltpu
from jax.sharding import PartitionSpec as P

HEAD_DIM = 64
REACH = 4


def shifted(block, axis, distance):
    devices = range(lax.axis_size(axis))
    route = [(i - distance, i) for i in devices if i - distance in devices]
    return lax.ppermute(block, axis, route)


def for_sending(shard):

    def short(part):
        return part.astype(jnp.bfloat16) if part.dtype == jnp.float32 else part

    return jax.tree.map(short, shard)


def layer_norm(hidden, gain_vec, shift_vec):
    center = hidden - jnp.mean(hidden, axis=-1, keepdims=True)
    inverse = lax.rsqrt(jnp.mean(center * center, axis=-1, keepdims=True) + 1e-05)
    normed = center * inverse
    return (normed * gain_vec + shift_vec, normed, inverse)


def norm_back(upstream, normed, inverse, gain_vec):
    scaled = upstream * gain_vec
    return inverse * (
        scaled
        - jnp.mean(scaled, axis=-1, keepdims=True)
        - normed * jnp.mean(scaled * normed, axis=-1, keepdims=True)
    )


def gelu_curve(pre_act):
    return 0.5 * pre_act * (1.0 + lax.erf(pre_act * 0.7071067811865476))


def gelu_slope(pre_act):
    return (
        0.5 * (1.0 + lax.erf(pre_act * 0.7071067811865476))
        + pre_act * jnp.exp(-0.5 * pre_act * pre_act) * 0.3989422804014327
    )


def product(left_side, right_side):
    return jnp.einsum("btd,de->bte", left_side, right_side, preferred_element_type=jnp.float32)


def transposed(left_side, right_side):
    return jnp.einsum("btn,mn->btm", left_side, right_side, preferred_element_type=jnp.float32)


def weight_term(left_side, right_side):
    return jnp.einsum("btd,bte->de", left_side, right_side, preferred_element_type=jnp.float32)


def block_scores(query_rows, key_rows, block_mask):
    scores = jnp.einsum("bqhd,bkhd->bhqk", query_rows, key_rows, preferred_element_type=jnp.float32)
    return jnp.where(block_mask, scores, -1e30)


def probabilities(query_rows, key_rows, block_mask, log_total):
    scores = block_scores(query_rows, key_rows, block_mask)
    return jnp.where(block_mask, jnp.exp(scores - log_total[..., None]), 0.0)


def placed(local_part, full_len, place_at):
    empty = jnp.zeros((full_len,), jnp.float32)
    return lax.dynamic_update_slice_in_dim(empty, local_part, place_at * local_part.shape[0], 0)


def ring_plan(
    inputs,
    segment_ids,
    query_weight,
    key_weight,
    value_weight,
    output_weight,
    up_weight,
    down_weight,
    querybias,
    valuebias,
    outputbias,
    upbias,
    downbias,
    norm_gain,
    norm_shift,
    final_gain,
    final_shift,
    cotangent,
):
    tp_count = lax.axis_size("tp")
    tp_place = lax.axis_index("tp")
    ctx_count = lax.axis_size("ctx")
    ctx_place = lax.axis_index("ctx")
    batch_rows, part_rows, model_width = inputs.shape
    shard_rows = part_rows * tp_count
    full_query, full_key, full_value, full_output, full_up, full_down = (
        lax.all_gather(query_weight, ("dp", "ctx"), axis=0, tiled=True),
        lax.all_gather(key_weight, ("dp", "ctx"), axis=0, tiled=True),
        lax.all_gather(value_weight, ("dp", "ctx"), axis=0, tiled=True),
        lax.all_gather(output_weight, ("dp", "ctx"), axis=1, tiled=True),
        lax.all_gather(up_weight, ("dp", "ctx"), axis=0, tiled=True),
        lax.all_gather(down_weight, ("dp", "ctx"), axis=1, tiled=True),
    )
    local_width = full_query.shape[1]
    local_heads = local_width // HEAD_DIM
    hidden_width = full_up.shape[1]
    query_offset = lax.dynamic_slice_in_dim(querybias, tp_place * local_width, local_width)
    value_offset = lax.dynamic_slice_in_dim(valuebias, tp_place * local_width, local_width)
    up_offset = lax.dynamic_slice_in_dim(upbias, tp_place * hidden_width, hidden_width)
    score_scale = HEAD_DIM ** (-0.5)

    def split_heads(tensor):
        return tensor.reshape(batch_rows, shard_rows, local_heads, HEAD_DIM)

    def join_heads(tensor):
        return tensor.reshape(batch_rows, shard_rows, local_width)

    tokens = lax.all_gather(inputs, "tp", axis=1, tiled=True)
    queries = split_heads(
        ((product(tokens, full_query) + query_offset) * score_scale).astype(jnp.bfloat16)
    )
    key_rows = split_heads(product(tokens, full_key).astype(jnp.bfloat16))
    value_rows = split_heads((product(tokens, full_value) + value_offset).astype(jnp.bfloat16))
    own_ids = lax.dynamic_slice_in_dim(segment_ids, ctx_place * shard_rows, shard_rows, 1)
    offsets = [0] + [
        offset for offset in range(-REACH, REACH + 1) if offset != 0 and abs(offset) < ctx_count
    ]
    mask_of = {}
    block_of = {}
    for offset in offsets:
        source = ctx_place + offset
        begin_at = jnp.clip(source, 0, ctx_count - 1) * shard_rows
        other_ids = lax.dynamic_slice_in_dim(segment_ids, begin_at, shard_rows, 1)
        inside = jnp.logical_and(source >= 0, source < ctx_count)
        mask_of[offset] = jnp.logical_and(own_ids[:, :, None] == other_ids[:, None, :], inside)[
            :, None
        ]
        if offset == 0:
            block_of[offset] = (key_rows, value_rows)
        else:
            block_of[offset] = shifted((key_rows, value_rows), "ctx", -offset)
    running = jnp.full((batch_rows, local_heads, shard_rows), -1e30, jnp.float32)
    totals = jnp.zeros((batch_rows, local_heads, shard_rows), jnp.float32)
    for offset in offsets:
        scores = block_scores(queries, block_of[offset][0], mask_of[offset])
        highest = jnp.maximum(running, jnp.max(scores, axis=-1))
        weights = jnp.where(mask_of[offset], jnp.exp(scores - highest[..., None]), 0.0)
        totals = totals * jnp.exp(running - highest) + jnp.sum(weights, axis=-1)
        running = highest
    log_total = running + jnp.log(totals)
    mixture = jnp.zeros((batch_rows, shard_rows, local_heads, HEAD_DIM), jnp.float32)
    for offset in offsets:
        attn_probs = probabilities(queries, block_of[offset][0], mask_of[offset], log_total)
        mixture = mixture + jnp.einsum(
            "bhqk,bkhd->bqhd",
            attn_probs.astype(jnp.bfloat16),
            block_of[offset][1],
            preferred_element_type=jnp.float32,
        )
    attended = join_heads(mixture).astype(jnp.bfloat16)
    output_part = lax.psum_scatter(
        product(attended, full_output), "tp", scatter_dimension=1, tiled=True
    )
    first_sum = inputs.astype(jnp.float32) + output_part + outputbias
    normed_first, first_normed, first_inverse = layer_norm(first_sum, norm_gain, norm_shift)
    normed_rows = lax.all_gather(normed_first.astype(jnp.bfloat16), "tp", axis=1, tiled=True)
    hidden_pre = product(normed_rows, full_up) + up_offset
    hidden_low = gelu_curve(hidden_pre).astype(jnp.bfloat16)
    down_part = lax.psum_scatter(
        product(hidden_low, full_down), "tp", scatter_dimension=1, tiled=True
    )
    second_sum = normed_first + down_part + downbias
    result, second_normed, second_inverse = layer_norm(second_sum, final_gain, final_shift)
    upstream = cotangent.astype(jnp.float32)
    finalgain_grad = jnp.sum(upstream * second_normed, axis=(0, 1))
    finalshift_grad = jnp.sum(upstream, axis=(0, 1))
    second_grad = norm_back(upstream, second_normed, second_inverse, final_gain)
    down_low = second_grad.astype(jnp.bfloat16)
    downbias_grad = jnp.sum(down_low, axis=(0, 1), dtype=jnp.float32)
    down_rows = lax.all_gather(down_low, "tp", axis=1, tiled=True)
    down_grad = weight_term(hidden_low, down_rows)
    hidden_grad = (transposed(down_rows, full_down) * gelu_slope(hidden_pre)).astype(jnp.bfloat16)
    upbias_part = jnp.sum(hidden_grad, axis=(0, 1), dtype=jnp.float32)
    up_grad = weight_term(normed_rows, hidden_grad)
    normed_grad = (
        lax.psum_scatter(transposed(hidden_grad, full_up), "tp", scatter_dimension=1, tiled=True)
        + second_grad
    )
    normgain_grad = jnp.sum(normed_grad * first_normed, axis=(0, 1))
    normshift_grad = jnp.sum(normed_grad, axis=(0, 1))
    first_grad = norm_back(normed_grad, first_normed, first_inverse, norm_gain)
    output_low = first_grad.astype(jnp.bfloat16)
    outputbias_grad = jnp.sum(output_low, axis=(0, 1), dtype=jnp.float32)
    output_rows = lax.all_gather(output_low, "tp", axis=1, tiled=True)
    output_grad = weight_term(attended, output_rows)
    mixed_grad = split_heads(transposed(output_rows, full_output).astype(jnp.bfloat16))
    row_dot = jnp.zeros((batch_rows, local_heads, shard_rows), jnp.float32)
    for offset in offsets:
        attn_probs = probabilities(queries, block_of[offset][0], mask_of[offset], log_total)
        prob_grad = jnp.einsum(
            "bqhd,bkhd->bhqk", mixed_grad, block_of[offset][1], preferred_element_type=jnp.float32
        )
        row_dot = row_dot + jnp.sum(attn_probs * prob_grad, axis=-1)
    query_acc = jnp.zeros((batch_rows, shard_rows, local_heads, HEAD_DIM), jnp.float32)
    key_parts = {}
    for offset in offsets:
        attn_probs = probabilities(queries, block_of[offset][0], mask_of[offset], log_total)
        prob_grad = jnp.einsum(
            "bqhd,bkhd->bhqk", mixed_grad, block_of[offset][1], preferred_element_type=jnp.float32
        )
        score_grad = (attn_probs * (prob_grad - row_dot[..., None])).astype(jnp.bfloat16)
        query_acc = query_acc + jnp.einsum(
            "bhqk,bkhd->bqhd", score_grad, block_of[offset][0], preferred_element_type=jnp.float32
        )
        key_term = jnp.einsum(
            "bhqk,bqhd->bkhd", score_grad, queries, preferred_element_type=jnp.float32
        )
        value_term = jnp.einsum(
            "bhqk,bqhd->bkhd",
            attn_probs.astype(jnp.bfloat16),
            mixed_grad,
            preferred_element_type=jnp.float32,
        )
        key_parts[offset] = (key_term, value_term)
    own_key, own_value = key_parts[0]
    for offset in offsets[1:]:
        back_key, back_value = shifted(for_sending(key_parts[offset]), "ctx", offset)
        own_key = own_key + back_key
        own_value = own_value + back_value
    query_pre = (
        join_heads(query_acc.astype(jnp.bfloat16)).astype(jnp.float32) * score_scale
    ).astype(jnp.bfloat16)
    key_low = join_heads(own_key.astype(jnp.bfloat16))
    value_low = join_heads(own_value.astype(jnp.bfloat16))
    querybias_part = jnp.sum(query_pre, axis=(0, 1), dtype=jnp.float32)
    valuebias_part = jnp.sum(value_low, axis=(0, 1), dtype=jnp.float32)
    query_grad = weight_term(tokens, query_pre)
    key_grad = weight_term(tokens, key_low)
    value_grad = weight_term(tokens, value_low)
    input_part = (
        transposed(query_pre, full_query)
        + transposed(key_low, full_key)
        + transposed(value_low, full_value)
    )
    input_grad = (
        lax.psum_scatter(
            input_part.astype(jnp.bfloat16), "tp", scatter_dimension=1, tiled=True
        ).astype(jnp.float32)
        + first_grad
    )
    query_grad, key_grad, value_grad, output_grad, up_grad, down_grad = (
        lax.psum_scatter(query_grad, ("dp", "ctx"), scatter_dimension=0, tiled=True),
        lax.psum_scatter(key_grad, ("dp", "ctx"), scatter_dimension=0, tiled=True),
        lax.psum_scatter(value_grad, ("dp", "ctx"), scatter_dimension=0, tiled=True),
        lax.psum_scatter(output_grad, ("dp", "ctx"), scatter_dimension=1, tiled=True),
        lax.psum_scatter(up_grad, ("dp", "ctx"), scatter_dimension=0, tiled=True),
        lax.psum_scatter(down_grad, ("dp", "ctx"), scatter_dimension=1, tiled=True),
    )
    summed = lax.psum(
        (
            placed(querybias_part, model_width, tp_place),
            placed(valuebias_part, model_width, tp_place),
            outputbias_grad,
            placed(upbias_part, hidden_width * tp_count, tp_place),
            downbias_grad,
            normgain_grad,
            normshift_grad,
            finalgain_grad,
            finalshift_grad,
        ),
        ("dp", "ctx", "tp"),
    )
    return (
        result.astype(jnp.bfloat16),
        input_grad,
        query_grad,
        key_grad,
        value_grad,
        output_grad,
        up_grad,
        down_grad,
        summed[0],
        summed[1],
        summed[2],
        summed[3],
        summed[4],
        summed[5],
        summed[6],
        summed[7],
        summed[8],
    )


MESH = pl.DeviceIdType.MESH
LOWEST = -1e30
VMEM = pl.BlockSpec(memory_space=pltpu.VMEM)
LEFT = pl.BlockSpec(memory_space=pl.ANY)


class Seat:
    def __init__(self):
        self.dp_count = lax.axis_size("dp")
        self.dp = lax.axis_index("dp")
        self.ctx = lax.axis_index("ctx")
        self.tp = lax.axis_index("tp")
        self.tp_pair = self.tp + 1 - 2 * (self.tp % 2)
        self.tp_side = (self.tp + 2) % 4
        self.tp_far = (self.tp_pair + 2) % 4
        self.pair = (self.dp, self.ctx, self.tp_pair)
        self.side = (self.dp, self.ctx, self.tp_side)
        self.twin = (self.dp, 1 - self.ctx, self.tp)
        self.above = ((self.dp + 1) % self.dp_count, self.ctx, self.tp)
        self.below = ((self.dp + self.dp_count - 1) % self.dp_count, self.ctx, self.tp)

    def meet(self, names):
        barrier = pltpu.get_barrier_semaphore()
        for name in names:
            pl.semaphore_signal(
                barrier, inc=1, device_id=getattr(self, name), device_id_type=MESH
            )
        pl.semaphore_wait(barrier, len(names))


def remote(source, target, send_sem, recv_sem, to):
    return pltpu.make_async_remote_copy(
        src_ref=source,
        dst_ref=target,
        send_sem=send_sem,
        recv_sem=recv_sem,
        device_id=to,
        device_id_type=MESH,
    )


class RingGather:
    def __init__(self, seat, shard, block, sems, at):
        self.seat, self.shard, self.block, self.at = seat, shard, block, at
        self.own_sem, self.z_send, self.z_recv, self.y_send, self.y_recv = sems
        self.count = seat.dp_count

    def index(self, step, ctx):
        origin = (self.seat.dp + self.count - step) % self.count
        return origin * 2 + ctx

    def held(self, step):
        return self.block(self.index(step, self.seat.ctx))

    def own(self):
        return pltpu.make_async_copy(self.shard, self.held(0), self.own_sem.at[self.at])

    def z(self, step):
        source = self.shard if step == 0 else self.held(step)
        return remote(
            source,
            self.held(step),
            self.z_send.at[self.at, step],
            self.z_recv.at[self.at, step],
            self.seat.above,
        )

    def z_in(self, step):
        view = self.held(step + 1)
        return remote(
            view,
            view,
            self.z_send.at[self.at, step],
            self.z_recv.at[self.at, step],
            self.seat.above,
        )

    def y(self, step):
        source = self.shard if step == 0 else self.held(step)
        return remote(
            source,
            self.held(step),
            self.y_send.at[self.at, step],
            self.y_recv.at[self.at, step],
            self.seat.twin,
        )

    def y_in(self, step):
        view = self.block(self.index(step, 1 - self.seat.ctx))
        return remote(
            view,
            view,
            self.y_send.at[self.at, step],
            self.y_recv.at[self.at, step],
            self.seat.twin,
        )

    def begin(self):
        self.own().start()
        self.z(0).start()
        self.y(0).start()

    def pass_on(self, step):
        self.z_in(step).wait_recv()
        if step + 1 < self.count - 1:
            self.z(step + 1).start()
        self.y(step + 1).start()

    def land(self):
        self.own().wait()
        for step in range(self.count):
            self.y_in(step).wait_recv()

    def close(self):
        for step in range(self.count - 1):
            self.z(step).wait_send()
        for step in range(self.count):
            self.y(step).wait_send()


def gather_sems(pieces, count):
    dma = pltpu.SemaphoreType.DMA
    return [
        dma((pieces,)),
        dma((pieces, count - 1)),
        dma((pieces, count - 1)),
        dma((pieces, count)),
        dma((pieces, count)),
    ]


def dot(left_side, right_side):
    return jnp.dot(left_side, right_side, preferred_element_type=jnp.float32)


def dot_nt(left_side, right_side):
    return lax.dot_general(
        left_side, right_side, (((1,), (1,)), ((), ())), preferred_element_type=jnp.float32
    )


def dot_tn(left_side, right_side):
    return lax.dot_general(
        left_side, right_side, (((0,), (0,)), ((), ())), preferred_element_type=jnp.float32
    )


def aligned(start, size):
    return pl.ds(pl.multiple_of(start, size), size)


def attend_kernel(
    inputs_ref,
    ids_ref,
    query_shard,
    key_shard,
    value_shard,
    output_shard,
    up_shard,
    down_shard,
    query_bias,
    value_bias,
    tokens_ref,
    query_full,
    key_full,
    value_full,
    output_full,
    up_full,
    down_full,
    query_ref,
    key_ref,
    value_ref,
    mixed_ref,
    log_ref,
    attended_ref,
    other_ref,
    flipped_ref,
    ids_down,
    token_send,
    token_recv,
    token_own,
    *sems,
):
    seat = Seat()
    batch, part, width = inputs_ref.shape
    rows = tokens_ref.shape[1]
    local = query_full.shape[1]
    heads = local // HEAD_DIM
    depth = query_shard.shape[0]
    seat.meet(("pair", "side", "twin", "above", "below"))

    def cut(half, place):
        return half.at[:, aligned(place * part, part), :]

    def token_copy(relation, source, target, to):
        return remote(source, target, token_send.at[relation], token_recv.at[relation], to)

    here = cut(tokens_ref, seat.tp)
    there = cut(other_ref, seat.tp)
    here_side = cut(tokens_ref, seat.tp_side)
    there_side = cut(other_ref, seat.tp_side)
    sends = [
        token_copy(0, inputs_ref, here, seat.pair),
        token_copy(1, inputs_ref, here, seat.side),
        token_copy(2, inputs_ref, there, seat.twin),
        token_copy(3, there, there, seat.side),
        token_copy(4, here_side, here_side, seat.pair),
        token_copy(5, there, there, seat.pair),
        token_copy(6, there_side, there_side, seat.pair),
    ]
    landed = [
        cut(tokens_ref, seat.tp_pair),
        here_side,
        there,
        there_side,
        cut(tokens_ref, seat.tp_far),
        cut(other_ref, seat.tp_pair),
        cut(other_ref, seat.tp_far),
    ]

    def token_in(relation):
        token_copy(relation, landed[relation], landed[relation], seat.pair).wait_recv()

    own_tokens = pltpu.make_async_copy(inputs_ref, here, token_own)
    own_tokens.start()
    for relation in range(3):
        sends[relation].start()

    def by_rows(full):
        return lambda r: full.at[aligned(r * depth, depth), :]

    def by_columns(full):
        return lambda r: full.at[:, aligned(r * depth, depth)]

    weights = [
        RingGather(seat, query_shard, by_rows(query_full), sems, 0),
        RingGather(seat, key_shard, by_rows(key_full), sems, 1),
        RingGather(seat, value_shard, by_rows(value_full), sems, 2),
    ]
    later = [
        RingGather(seat, output_shard, by_columns(output_full), sems, 3),
        RingGather(seat, up_shard, by_rows(up_full), sems, 4),
        RingGather(seat, down_shard, by_columns(down_full), sems, 5),
    ]
    hops = seat.dp_count - 1
    for weight in weights:
        weight.begin()
    for step in range(hops):
        for weight in weights:
            weight.pass_on(step)
    for weight in later:
        weight.begin()
    token_in(1)
    sends[4].start()
    token_in(2)
    sends[3].start()
    sends[5].start()

    for b in range(batch):
        for half in range(2):
            row_ids = ids_ref[b : b + 1, aligned((seat.ctx if half == 0 else 1 - seat.ctx) * rows, rows)]
            spread = jnp.broadcast_to(row_ids.astype(jnp.float32), (128, rows))
            ids_down[b, half * rows : (half + 1) * rows, :] = spread.T

    bias_at = aligned(seat.tp * local, local)
    query_offset = query_bias[:, bias_at]
    value_offset = value_bias[:, bias_at]
    tile = rows // 2
    for weight in weights:
        weight.land()
    own_tokens.wait()
    token_in(0)
    token_in(4)

    def project(half_ref, half):
        def one(index, carry):
            b, piece = index // 2, index % 2
            block = half_ref[b, aligned(piece * tile, tile), :]
            spot = aligned(half * rows + piece * tile, tile)
            if half == 0:
                scaled = (dot(block, query_full[...]) + query_offset) * HEAD_DIM ** (-0.5)
                query_ref[b, aligned(piece * tile, tile), :] = scaled.astype(jnp.bfloat16)
            key_ref[b, spot, :] = dot(block, key_full[...]).astype(jnp.bfloat16)
            value_rows = dot(block, value_full[...]) + value_offset
            value_ref[b, spot, :] = value_rows.astype(jnp.bfloat16)
            flipped_ref[b, :, spot] = value_rows.T.astype(jnp.bfloat16)
            return carry

        lax.fori_loop(0, batch * 2, one, 0)

    project(tokens_ref, 0)
    token_in(3)
    sends[6].start()
    token_in(5)
    token_in(6)
    project(other_ref, 1)

    lane_head = lax.broadcasted_iota(jnp.int32, (1, local), 1) // HEAD_DIM

    def attend(index, carry):
        for step in range(hops):
            @pl.when(index == 2 * step + 1)
            def _():
                for weight in later:
                    weight.pass_on(step)

        b, h = index // heads, index % heads
        own_rows = aligned(h * HEAD_DIM, HEAD_DIM)
        chosen = jnp.where(lane_head == h, query_ref[b], jnp.zeros((), jnp.bfloat16))
        scores = dot_nt(key_ref[b], chosen)
        own_ids = ids_ref[b, aligned(seat.ctx * rows, rows)].astype(jnp.float32)
        same = jnp.tile(ids_down[b], (1, rows // 128)) == own_ids[None, :]
        scores = jnp.where(same, scores, LOWEST)
        highest = jnp.max(scores, axis=0, keepdims=True)
        raised = jnp.exp(scores - highest)
        total = jnp.sum(raised, axis=0, keepdims=True)
        shares = (raised * (1.0 / total)).astype(jnp.bfloat16)
        mixed_ref[b, own_rows, :] = dot(flipped_ref[b, own_rows, :], shares)
        log_ref[index] = highest + jnp.log(total)
        return carry

    lax.fori_loop(0, batch * heads, attend, 0)
    for b in range(batch):
        attended_ref[b] = mixed_ref[b].T.astype(jnp.bfloat16)
    for weight in later:
        weight.land()
    for copy in sends:
        copy.wait_send()
    for weight in weights + later:
        weight.close()


def attend_forward(
    inputs, segment_ids, shards, querybias, valuebias
):
    count = lax.axis_size("dp")
    batch, part, width = inputs.shape
    rows = part * lax.axis_size("tp")
    local = shards[0].shape[1]
    hidden = shards[4].shape[1]
    heads = local // HEAD_DIM
    bf16, f32 = jnp.bfloat16, jnp.float32
    outs = [
        ((batch, rows, width), bf16, VMEM),
        ((width, local), bf16, VMEM),
        ((width, local), bf16, VMEM),
        ((width, local), bf16, VMEM),
        ((local, width), bf16, LEFT),
        ((width, hidden), bf16, LEFT),
        ((hidden, width), bf16, LEFT),
        ((batch, rows, local), bf16, VMEM),
        ((batch, 2 * rows, local), bf16, VMEM),
        ((batch, 2 * rows, local), bf16, VMEM),
        ((batch, local, rows), f32, VMEM),
        ((batch * heads, 1, rows), f32, VMEM),
        ((batch, rows, local), bf16, VMEM),
    ]
    dma = pltpu.SemaphoreType.DMA
    return pl.pallas_call(
        attend_kernel,
        name="attend_forward",
        out_shape=[jax.ShapeDtypeStruct(shape, kind) for shape, kind, _ in outs],
        in_specs=[VMEM] * 10,
        out_specs=[space for _, _, space in outs],
        scratch_shapes=[
            pltpu.VMEM((batch, rows, width), bf16),
            pltpu.VMEM((batch, local, 2 * rows), bf16),
            pltpu.VMEM((batch, 2 * rows, 128), f32),
            dma((7,)),
            dma((7,)),
            dma(()),
            *gather_sems(6, count),
        ],
        compiler_params=pltpu.CompilerParams(
            collective_id=1, has_side_effects=True, vmem_limit_bytes=56 * 2**20
        ),
    )(
        inputs,
        segment_ids,
        *shards,
        querybias.reshape(1, -1),
        valuebias.reshape(1, -1),
    )


VECTOR_ROWS = 16
ROW_QUERY, ROW_VALUE, ROW_OUTPUT, ROW_DOWN = 0, 1, 2, 3
ROW_GAIN, ROW_SHIFT, ROW_FINAL_GAIN, ROW_FINAL_SHIFT, ROW_UP = 4, 5, 6, 7, 8


class TokenScatter:
    def __init__(self, seat, buffers, sems, at):
        self.seat, self.at = seat, at
        self.pair_out, self.pair_in, self.side_out, self.side_in = buffers
        self.send, self.recv = sems

    def copy(self, k):
        at, seat = self.at, self.seat
        if k < 2:
            source, target, to = self.pair_out.at[at, k], self.pair_in.at[at, k], seat.pair
        else:
            source, target, to = self.side_out.at[at], self.side_in.at[at], seat.side
        return remote(source, target, self.send.at[at, k], self.recv.at[at, k], to)

    def give(self, compute, total):
        seat, at = self.seat, self.at
        part = self.side_out.shape[1]
        group = seat.tp // 2
        mine = aligned((seat.tp % 2) * part, part)
        others = aligned((1 - seat.tp % 2) * part, part)
        compute(1 - group)
        self.pair_out[at, 0] = total[others, :].astype(jnp.bfloat16)
        self.copy(0).start()
        self.side_out[at] = total[mine, :].astype(jnp.bfloat16)
        compute(group)
        self.pair_out[at, 1] = total[others, :].astype(jnp.bfloat16)
        self.copy(1).start()
        self.copy(0).wait_recv()
        self.side_out[at] = (
            self.side_out[at].astype(jnp.float32) + self.pair_in[at, 0].astype(jnp.float32)
        ).astype(jnp.bfloat16)
        self.copy(2).start()
        return mine

    def take(self):
        self.copy(1).wait_recv()
        self.copy(2).wait_recv()
        return self.pair_in[self.at, 1].astype(jnp.float32) + self.side_in[self.at].astype(
            jnp.float32
        )

    def close(self):
        for k in range(3):
            self.copy(k).wait_send()


class TokenGather:
    def __init__(self, seat, full, b, part, sems, at):
        self.seat = seat
        self.send, self.recv = sems
        self.at = at
        self.view = lambda place: full.at[b, aligned(place * part, part), :]

    def copy(self, k, place, to):
        view = self.view(place)
        return remote(view, view, self.send.at[self.at, k], self.recv.at[self.at, k], to)

    def give(self):
        seat = self.seat
        self.copy(0, seat.tp, seat.side).start()
        self.copy(1, seat.tp, seat.pair).start()

    def relay(self):
        seat = self.seat
        self.copy(0, seat.tp_side, seat.side).wait_recv()
        self.copy(2, seat.tp_side, seat.pair).start()

    def land(self):
        seat = self.seat
        self.copy(1, seat.tp_pair, seat.pair).wait_recv()
        self.copy(2, seat.tp_far, seat.pair).wait_recv()

    def close(self):
        seat = self.seat
        for k, place in ((0, seat.tp), (1, seat.tp), (2, seat.tp_side)):
            self.copy(k, place, seat.pair).wait_send()


def row_mean(rows):
    return jnp.mean(rows, axis=-1, keepdims=True)


def feed_kernel(
    inputs_ref,
    attended_ref,
    cotangent_ref,
    output_full,
    up_full,
    down_full,
    output_bias,
    up_bias,
    down_bias,
    norm_gain,
    norm_shift,
    final_gain,
    final_shift,
    result_ref,
    first_ref,
    mixed_ref,
    output_part,
    up_part,
    down_part,
    vectors_ref,
    normed_rows,
    hidden_rows,
    slope_rows,
    down_rows,
    back_rows,
    output_rows,
    normed_keep,
    scaled_keep,
    inverse_keep,
    second_keep,
    total_own,
    total,
    pair_out,
    pair_in,
    side_out,
    side_in,
    scatter_send,
    scatter_recv,
    gather_send,
    gather_recv,
):
    seat = Seat()
    batch, part, width = inputs_ref.shape
    rows = attended_ref.shape[1]
    hidden = up_full.shape[1]
    f32, bf16 = jnp.float32, jnp.bfloat16
    seat.meet(("pair", "side"))
    buffers = (pair_out, pair_in, side_out, side_in)
    scatters = [
        TokenScatter(seat, buffers, (scatter_send, scatter_recv), k) for k in range(3 * batch)
    ]
    gathers = [
        TokenGather(seat, full, b, part, (gather_send, gather_recv), k * batch + b)
        for k, full in enumerate((normed_rows, down_rows, output_rows))
        for b in range(batch)
    ]
    wide = 256
    up_offset = lambda at: up_bias[:, pl.ds(pl.multiple_of(seat.tp * hidden + at * wide, wide), wide)]

    def over(tiles, body):
        def one(index, carry):
            body(index)
            return carry

        lax.fori_loop(0, tiles, one, 0)

    def spread(lhs_ref, b, weight, flipped):
        def compute(group):
            lhs = lhs_ref[b, aligned(group * 2 * part, 2 * part), :]

            def tile(index):
                columns = aligned(index * wide, wide)
                if flipped:
                    total[:, columns] = dot_nt(lhs, weight[columns, :])
                else:
                    total[:, columns] = dot(lhs, weight[:, columns])

            over(width // wide, tile)

        return compute

    def scatter(k, b, lhs_ref, weight, flipped):
        mine = scatters[k * batch + b].give(spread(lhs_ref, b, weight, flipped), total)
        total_own[b] = total[mine, :]

    def collected(k, b):
        return total_own[b] + scatters[k * batch + b].take()

    own_rows = aligned(seat.tp * part, part)
    vectors_ref[...] = jnp.zeros_like(vectors_ref)

    def add_vector(row, values):
        vectors_ref[row : row + 1, :] += jnp.sum(values, axis=0, keepdims=True)

    def first_norm(b):
        first_sum = inputs_ref[b].astype(f32) + (collected(0, b) + output_bias[...])
        center = first_sum - row_mean(first_sum)
        inverse = lax.rsqrt(row_mean(center * center) + 1e-05)
        normed = center * inverse
        scaled = normed * norm_gain[...] + norm_shift[...]
        normed_keep[b] = normed
        inverse_keep[b] = inverse
        scaled_keep[b] = scaled
        normed_rows[b, own_rows, :] = scaled.astype(bf16)
        gathers[b].give()

    def raise_up(b):
        gathers[b].land()
        lhs = normed_rows[b]

        def tile(index):
            columns = aligned(index * wide, wide)
            pre = dot(lhs, up_full[:, columns]) + up_offset(index)
            half = 0.5 * (1.0 + lax.erf(pre * 0.7071067811865476))
            hidden_rows[b, :, columns] = (pre * half).astype(bf16)
            slope_rows[b, :, columns] = half + pre * jnp.exp(-0.5 * pre * pre) * 0.3989422804014327

        over(hidden // wide, tile)

    def second_norm(b):
        second_sum = scaled_keep[b] + (collected(1, b) + down_bias[...])
        center = second_sum - row_mean(second_sum)
        inverse = lax.rsqrt(row_mean(center * center) + 1e-05)
        normed = center * inverse
        result_ref[b] = (normed * final_gain[...] + final_shift[...]).astype(bf16)
        upstream = cotangent_ref[b].astype(f32)
        add_vector(ROW_FINAL_GAIN, upstream * normed)
        add_vector(ROW_FINAL_SHIFT, upstream)
        scaled = upstream * final_gain[...]
        second = inverse * (scaled - row_mean(scaled) - normed * row_mean(scaled * normed))
        second_keep[b] = second
        low = second.astype(bf16)
        down_rows[b, own_rows, :] = low
        gathers[batch + b].give()
        add_vector(ROW_DOWN, low.astype(f32))

    def lower(b):
        gathers[batch + b].land()
        lhs = down_rows[b]

        def tile(index):
            columns = aligned(index * wide, wide)
            back = (dot_nt(lhs, down_full[columns, :]) * slope_rows[b, :, columns]).astype(bf16)
            back_rows[b, :, columns] = back
            place = pl.ds(pl.multiple_of(index * wide, wide), wide)
            up_sum[:, place] += jnp.sum(back.astype(f32), axis=0, keepdims=True)

        over(hidden // wide, tile)

    up_sum = vectors_ref.at[ROW_UP : ROW_UP + 1, :]

    def first_back(b):
        grad = collected(2, b) + second_keep[b]
        normed = normed_keep[b]
        add_vector(ROW_GAIN, grad * normed)
        add_vector(ROW_SHIFT, grad)
        scaled = grad * norm_gain[...]
        first = inverse_keep[b] * (
            scaled - row_mean(scaled) - normed * row_mean(scaled * normed)
        )
        first_ref[b] = first
        low = first.astype(bf16)
        output_rows[b, own_rows, :] = low
        gathers[2 * batch + b].give()
        add_vector(ROW_OUTPUT, low.astype(f32))

    def mix_back(b):
        gathers[2 * batch + b].land()
        mixed_ref[b] = dot_nt(output_rows[b], output_full[...]).astype(bf16)

    def weight_tiles(left_ref, right_ref, target, first, last):
        left = left_ref[...].reshape(batch * rows, left_ref.shape[2])
        right_width = right_ref.shape[2]

        def tile(index):
            columns = aligned((first + index) * wide, wide)
            right = right_ref[:, :, columns].reshape(batch * rows, wide)
            target[:, columns] = dot_tn(left, right).astype(bf16)

        over(last - first, tile)

    for b in range(batch):
        scatter(0, b, attended_ref, output_full, False)
    for b in range(batch):
        first_norm(b)
    gathers[0].relay()
    raise_up(0)
    gathers[1].relay()
    scatter(1, 0, hidden_rows, down_full, False)
    raise_up(1)
    scatter(1, 1, hidden_rows, down_full, False)
    second_norm(0)
    second_norm(1)
    gathers[batch].relay()
    lower(0)
    gathers[batch + 1].relay()
    scatter(2, 0, back_rows, up_full, True)
    lower(1)
    scatter(2, 1, back_rows, up_full, True)
    weight_tiles(hidden_rows, down_rows, down_part, 0, 2)
    first_back(0)
    weight_tiles(hidden_rows, down_rows, down_part, 2, 4)
    first_back(1)
    weight_tiles(normed_rows, back_rows, up_part, 0, 2)
    gathers[2 * batch].relay()
    mix_back(0)
    gathers[2 * batch + 1].relay()
    weight_tiles(normed_rows, back_rows, up_part, 2, 4)
    mix_back(1)
    weight_tiles(attended_ref, output_rows, output_part, 0, 4)
    for k in scatters + gathers:
        k.close()


def feed_both_ways(
    inputs, attended, cotangent, output_full, up_full, down_full, vectors
):
    batch, part, width = inputs.shape
    rows, local = attended.shape[1:]
    hidden = up_full.shape[1]
    bf16, f32 = jnp.bfloat16, jnp.float32
    outs = [
        ((batch, part, width), bf16),
        ((batch, part, width), f32),
        ((batch, rows, local), bf16),
        ((local, width), bf16),
        ((width, hidden), bf16),
        ((hidden, width), bf16),
        ((VECTOR_ROWS, width), f32),
    ]
    dma = pltpu.SemaphoreType.DMA
    return pl.pallas_call(
        feed_kernel,
        name="feed_both_ways",
        out_shape=[jax.ShapeDtypeStruct(shape, kind) for shape, kind in outs],
        in_specs=[VMEM] * 13,
        out_specs=[VMEM] * len(outs),
        scratch_shapes=[
            pltpu.VMEM((batch, rows, width), bf16),
            pltpu.VMEM((batch, rows, hidden), bf16),
            pltpu.VMEM((batch, rows, hidden), f32),
            pltpu.VMEM((batch, rows, width), bf16),
            pltpu.VMEM((batch, rows, hidden), bf16),
            pltpu.VMEM((batch, rows, width), bf16),
            pltpu.VMEM((batch, part, width), f32),
            pltpu.VMEM((batch, part, width), f32),
            pltpu.VMEM((batch, part, 1), f32),
            pltpu.VMEM((batch, part, width), f32),
            pltpu.VMEM((batch, part, width), f32),
            pltpu.VMEM((2 * part, width), f32),
            pltpu.VMEM((3 * batch, 2, part, width), bf16),
            pltpu.VMEM((3 * batch, 2, part, width), bf16),
            pltpu.VMEM((3 * batch, part, width), bf16),
            pltpu.VMEM((3 * batch, part, width), bf16),
            dma((3 * batch, 3)),
            dma((3 * batch, 3)),
            dma((3 * batch, 3)),
            dma((3 * batch, 3)),
        ],
        compiler_params=pltpu.CompilerParams(
            collective_id=2, has_side_effects=True, vmem_limit_bytes=63 * 2**20
        ),
    )(
        inputs,
        attended,
        cotangent,
        output_full,
        up_full,
        down_full,
        *[vector.reshape(1, -1) for vector in vectors],
    )


def fused_plan(
    inputs,
    segment_ids,
    query_weight,
    key_weight,
    value_weight,
    output_weight,
    up_weight,
    down_weight,
    querybias,
    valuebias,
    outputbias,
    upbias,
    downbias,
    norm_gain,
    norm_shift,
    final_gain,
    final_shift,
    cotangent,
):
    tp_count = lax.axis_size("tp")
    tp_place = lax.axis_index("tp")
    ctx_count = lax.axis_size("ctx")
    ctx_place = lax.axis_index("ctx")
    batch_rows, part_rows, model_width = inputs.shape
    shard_rows = part_rows * tp_count
    (
        tokens,
        full_query,
        full_key,
        full_value,
        full_output,
        full_up,
        full_down,
        queries,
        both_keys,
        both_values,
        mixture,
        log_rows,
        attended,
    ) = attend_forward(
        inputs,
        segment_ids,
        (query_weight, key_weight, value_weight, output_weight, up_weight, down_weight),
        querybias,
        valuebias,
    )
    local_width = full_query.shape[1]
    local_heads = local_width // HEAD_DIM
    hidden_width = full_up.shape[1]
    score_scale = HEAD_DIM ** (-0.5)

    def split_heads(tensor):
        return tensor.reshape(batch_rows, shard_rows, local_heads, HEAD_DIM)

    def join_heads(tensor):
        return tensor.reshape(batch_rows, shard_rows, local_width)

    queries = split_heads(queries)
    log_total = log_rows.reshape(batch_rows, local_heads, shard_rows)
    own_ids = lax.dynamic_slice_in_dim(segment_ids, ctx_place * shard_rows, shard_rows, 1)
    other_ids = lax.dynamic_slice_in_dim(segment_ids, (1 - ctx_place) * shard_rows, shard_rows, 1)
    offsets = [0, 1]
    mask_of = {
        0: (own_ids[:, :, None] == own_ids[:, None, :])[:, None],
        1: (own_ids[:, :, None] == other_ids[:, None, :])[:, None],
    }
    block_of = {
        half: tuple(
            split_heads(both[:, half * shard_rows : (half + 1) * shard_rows])
            for both in (both_keys, both_values)
        )
        for half in (0, 1)
    }
    (
        result,
        first_grad,
        mixed_grad,
        output_grad,
        up_grad,
        down_grad,
        vectors,
    ) = feed_both_ways(
        inputs,
        attended,
        cotangent,
        full_output,
        full_up,
        full_down,
        (outputbias, upbias, downbias, norm_gain, norm_shift, final_gain, final_shift),
    )
    mixed_grad = split_heads(mixed_grad)
    outputbias_grad = vectors[ROW_OUTPUT]
    upbias_part = vectors[ROW_UP]
    downbias_grad = vectors[ROW_DOWN]
    normgain_grad = vectors[ROW_GAIN]
    normshift_grad = vectors[ROW_SHIFT]
    finalgain_grad = vectors[ROW_FINAL_GAIN]
    finalshift_grad = vectors[ROW_FINAL_SHIFT]
    row_dot = jnp.zeros((batch_rows, local_heads, shard_rows), jnp.float32)
    for offset in offsets:
        attn_probs = probabilities(queries, block_of[offset][0], mask_of[offset], log_total)
        prob_grad = jnp.einsum(
            "bqhd,bkhd->bhqk", mixed_grad, block_of[offset][1], preferred_element_type=jnp.float32
        )
        row_dot = row_dot + jnp.sum(attn_probs * prob_grad, axis=-1)
    query_acc = jnp.zeros((batch_rows, shard_rows, local_heads, HEAD_DIM), jnp.float32)
    key_parts = {}
    for offset in offsets:
        attn_probs = probabilities(queries, block_of[offset][0], mask_of[offset], log_total)
        prob_grad = jnp.einsum(
            "bqhd,bkhd->bhqk", mixed_grad, block_of[offset][1], preferred_element_type=jnp.float32
        )
        score_grad = (attn_probs * (prob_grad - row_dot[..., None])).astype(jnp.bfloat16)
        query_acc = query_acc + jnp.einsum(
            "bhqk,bkhd->bqhd", score_grad, block_of[offset][0], preferred_element_type=jnp.float32
        )
        key_term = jnp.einsum(
            "bhqk,bqhd->bkhd", score_grad, queries, preferred_element_type=jnp.float32
        )
        value_term = jnp.einsum(
            "bhqk,bqhd->bkhd",
            attn_probs.astype(jnp.bfloat16),
            mixed_grad,
            preferred_element_type=jnp.float32,
        )
        key_parts[offset] = (key_term, value_term)
    own_key, own_value = key_parts[0]
    for offset in offsets[1:]:
        back_key, back_value = lax.ppermute(
            for_sending(key_parts[offset]), "ctx", [(0, 1), (1, 0)]
        )
        own_key = own_key + back_key
        own_value = own_value + back_value
    query_pre = (
        join_heads(query_acc.astype(jnp.bfloat16)).astype(jnp.float32) * score_scale
    ).astype(jnp.bfloat16)
    key_low = join_heads(own_key.astype(jnp.bfloat16))
    value_low = join_heads(own_value.astype(jnp.bfloat16))
    querybias_part = jnp.sum(query_pre, axis=(0, 1), dtype=jnp.float32)
    valuebias_part = jnp.sum(value_low, axis=(0, 1), dtype=jnp.float32)
    query_grad = weight_term(tokens, query_pre)
    key_grad = weight_term(tokens, key_low)
    value_grad = weight_term(tokens, value_low)
    input_part = (
        transposed(query_pre, full_query)
        + transposed(key_low, full_key)
        + transposed(value_low, full_value)
    )
    input_grad = (
        lax.psum_scatter(
            input_part.astype(jnp.bfloat16), "tp", scatter_dimension=1, tiled=True
        ).astype(jnp.float32)
        + first_grad
    )
    query_grad, key_grad, value_grad, output_grad, up_grad, down_grad = (
        lax.psum_scatter(
            query_grad.astype(jnp.bfloat16), ("dp", "ctx"), scatter_dimension=0, tiled=True
        ).astype(jnp.float32),
        lax.psum_scatter(
            key_grad.astype(jnp.bfloat16), ("dp", "ctx"), scatter_dimension=0, tiled=True
        ).astype(jnp.float32),
        lax.psum_scatter(
            value_grad.astype(jnp.bfloat16), ("dp", "ctx"), scatter_dimension=0, tiled=True
        ).astype(jnp.float32),
        lax.psum_scatter(
            output_grad.astype(jnp.bfloat16), ("dp", "ctx"), scatter_dimension=1, tiled=True
        ).astype(jnp.float32),
        lax.psum_scatter(
            up_grad.astype(jnp.bfloat16), ("dp", "ctx"), scatter_dimension=0, tiled=True
        ).astype(jnp.float32),
        lax.psum_scatter(
            down_grad.astype(jnp.bfloat16), ("dp", "ctx"), scatter_dimension=1, tiled=True
        ).astype(jnp.float32),
    )
    summed = lax.psum(
        (
            placed(querybias_part, model_width, tp_place),
            placed(valuebias_part, model_width, tp_place),
            outputbias_grad,
            placed(upbias_part, hidden_width * tp_count, tp_place),
            downbias_grad,
            normgain_grad,
            normshift_grad,
            finalgain_grad,
            finalshift_grad,
        ),
        ("dp", "ctx", "tp"),
    )
    return (
        result,
        input_grad,
        query_grad,
        key_grad,
        value_grad,
        output_grad,
        up_grad,
        down_grad,
        summed[0],
        summed[1],
        summed[2],
        summed[3],
        summed[4],
        summed[5],
        summed[6],
        summed[7],
        summed[8],
    )


def solution(mesh):
    fits = mesh.shape["ctx"] == 2 and mesh.shape["tp"] == 4 and mesh.shape["dp"] > 2
    placed = (
        P("dp", ("ctx", "tp"), None),
        P("dp", None),
        P(("dp", "ctx"), "tp"),
        P(("dp", "ctx"), "tp"),
        P(("dp", "ctx"), "tp"),
        P("tp", ("dp", "ctx")),
        P(("dp", "ctx"), "tp"),
        P("tp", ("dp", "ctx")),
        P(),
        P(),
        P(),
        P(),
        P(),
        P(),
        P(),
        P(),
        P(),
        P("dp", ("ctx", "tp"), None),
    )
    return jax.shard_map(
        fused_plan if fits else ring_plan,
        mesh=mesh,
        in_specs=placed,
        out_specs=(
            P("dp", ("ctx", "tp"), None),
            P("dp", ("ctx", "tp"), None),
            P(("dp", "ctx"), "tp"),
            P(("dp", "ctx"), "tp"),
            P(("dp", "ctx"), "tp"),
            P("tp", ("dp", "ctx")),
            P(("dp", "ctx"), "tp"),
            P("tp", ("dp", "ctx")),
            P(),
            P(),
            P(),
            P(),
            P(),
            P(),
            P(),
            P(),
            P(),
        ),
        check_vma=False,
    )
```

```python
import functools

import jax
import jax.numpy as jnp
from jax import lax
from jax.experimental import pallas as pl
from jax.experimental.pallas import tpu as pltpu
from jax.sharding import PartitionSpec as P

HEAD_DIM = 64
REACH = 4


def shifted(block, axis, distance):
    devices = range(lax.axis_size(axis))
    route = [(i - distance, i) for i in devices if i - distance in devices]
    return lax.ppermute(block, axis, route)


def for_sending(shard):

    def short(part):
        return part.astype(jnp.bfloat16) if part.dtype == jnp.float32 else part

    return jax.tree.map(short, shard)


def layer_norm(hidden, gain_vec, shift_vec):
    center = hidden - jnp.mean(hidden, axis=-1, keepdims=True)
    inverse = lax.rsqrt(jnp.mean(center * center, axis=-1, keepdims=True) + 1e-05)
    normed = center * inverse
    return (normed * gain_vec + shift_vec, normed, inverse)


def norm_back(upstream, normed, inverse, gain_vec):
    scaled = upstream * gain_vec
    return inverse * (
        scaled
        - jnp.mean(scaled, axis=-1, keepdims=True)
        - normed * jnp.mean(scaled * normed, axis=-1, keepdims=True)
    )


def gelu_curve(pre_act):
    return 0.5 * pre_act * (1.0 + lax.erf(pre_act * 0.7071067811865476))


def gelu_slope(pre_act):
    return (
        0.5 * (1.0 + lax.erf(pre_act * 0.7071067811865476))
        + pre_act * jnp.exp(-0.5 * pre_act * pre_act) * 0.3989422804014327
    )


def product(left_side, right_side):
    return jnp.einsum("btd,de->bte", left_side, right_side, preferred_element_type=jnp.float32)


def transposed(left_side, right_side):
    return jnp.einsum("btn,mn->btm", left_side, right_side, preferred_element_type=jnp.float32)


def weight_term(left_side, right_side):
    return jnp.einsum("btd,bte->de", left_side, right_side, preferred_element_type=jnp.float32)


def block_scores(query_rows, key_rows, block_mask):
    scores = jnp.einsum("bqhd,bkhd->bhqk", query_rows, key_rows, preferred_element_type=jnp.float32)
    return jnp.where(block_mask, scores, -1e30)


def probabilities(query_rows, key_rows, block_mask, log_total):
    scores = block_scores(query_rows, key_rows, block_mask)
    return jnp.where(block_mask, jnp.exp(scores - log_total[..., None]), 0.0)


def placed(local_part, full_len, place_at):
    empty = jnp.zeros((full_len,), jnp.float32)
    return lax.dynamic_update_slice_in_dim(empty, local_part, place_at * local_part.shape[0], 0)


def ring_plan(
    inputs,
    segment_ids,
    query_weight,
    key_weight,
    value_weight,
    output_weight,
    up_weight,
    down_weight,
    querybias,
    valuebias,
    outputbias,
    upbias,
    downbias,
    norm_gain,
    norm_shift,
    final_gain,
    final_shift,
    cotangent,
):
    tp_count = lax.axis_size("tp")
    tp_place = lax.axis_index("tp")
    ctx_count = lax.axis_size("ctx")
    ctx_place = lax.axis_index("ctx")
    batch_rows, part_rows, model_width = inputs.shape
    shard_rows = part_rows * tp_count
    full_query, full_key, full_value, full_output, full_up, full_down = (
        lax.all_gather(query_weight, ("dp", "ctx"), axis=0, tiled=True),
        lax.all_gather(key_weight, ("dp", "ctx"), axis=0, tiled=True),
        lax.all_gather(value_weight, ("dp", "ctx"), axis=0, tiled=True),
        lax.all_gather(output_weight, ("dp", "ctx"), axis=1, tiled=True),
        lax.all_gather(up_weight, ("dp", "ctx"), axis=0, tiled=True),
        lax.all_gather(down_weight, ("dp", "ctx"), axis=1, tiled=True),
    )
    local_width = full_query.shape[1]
    local_heads = local_width // HEAD_DIM
    hidden_width = full_up.shape[1]
    query_offset = lax.dynamic_slice_in_dim(querybias, tp_place * local_width, local_width)
    value_offset = lax.dynamic_slice_in_dim(valuebias, tp_place * local_width, local_width)
    up_offset = lax.dynamic_slice_in_dim(upbias, tp_place * hidden_width, hidden_width)
    score_scale = HEAD_DIM ** (-0.5)

    def split_heads(tensor):
        return tensor.reshape(batch_rows, shard_rows, local_heads, HEAD_DIM)

    def join_heads(tensor):
        return tensor.reshape(batch_rows, shard_rows, local_width)

    tokens = lax.all_gather(inputs, "tp", axis=1, tiled=True)
    queries = split_heads(
        ((product(tokens, full_query) + query_offset) * score_scale).astype(jnp.bfloat16)
    )
    key_rows = split_heads(product(tokens, full_key).astype(jnp.bfloat16))
    value_rows = split_heads((product(tokens, full_value) + value_offset).astype(jnp.bfloat16))
    own_ids = lax.dynamic_slice_in_dim(segment_ids, ctx_place * shard_rows, shard_rows, 1)
    offsets = [0] + [
        offset for offset in range(-REACH, REACH + 1) if offset != 0 and abs(offset) < ctx_count
    ]
    mask_of = {}
    block_of = {}
    for offset in offsets:
        source = ctx_place + offset
        begin_at = jnp.clip(source, 0, ctx_count - 1) * shard_rows
        other_ids = lax.dynamic_slice_in_dim(segment_ids, begin_at, shard_rows, 1)
        inside = jnp.logical_and(source >= 0, source < ctx_count)
        mask_of[offset] = jnp.logical_and(own_ids[:, :, None] == other_ids[:, None, :], inside)[
            :, None
        ]
        if offset == 0:
            block_of[offset] = (key_rows, value_rows)
        else:
            block_of[offset] = shifted((key_rows, value_rows), "ctx", -offset)
    running = jnp.full((batch_rows, local_heads, shard_rows), -1e30, jnp.float32)
    totals = jnp.zeros((batch_rows, local_heads, shard_rows), jnp.float32)
    for offset in offsets:
        scores = block_scores(queries, block_of[offset][0], mask_of[offset])
        highest = jnp.maximum(running, jnp.max(scores, axis=-1))
        weights = jnp.where(mask_of[offset], jnp.exp(scores - highest[..., None]), 0.0)
        totals = totals * jnp.exp(running - highest) + jnp.sum(weights, axis=-1)
        running = highest
    log_total = running + jnp.log(totals)
    mixture = jnp.zeros((batch_rows, shard_rows, local_heads, HEAD_DIM), jnp.float32)
    for offset in offsets:
        attn_probs = probabilities(queries, block_of[offset][0], mask_of[offset], log_total)
        mixture = mixture + jnp.einsum(
            "bhqk,bkhd->bqhd",
            attn_probs.astype(jnp.bfloat16),
            block_of[offset][1],
            preferred_element_type=jnp.float32,
        )
    attended = join_heads(mixture).astype(jnp.bfloat16)
    output_part = lax.psum_scatter(
        product(attended, full_output), "tp", scatter_dimension=1, tiled=True
    )
    first_sum = inputs.astype(jnp.float32) + output_part + outputbias
    normed_first, first_normed, first_inverse = layer_norm(first_sum, norm_gain, norm_shift)
    normed_rows = lax.all_gather(normed_first.astype(jnp.bfloat16), "tp", axis=1, tiled=True)
    hidden_pre = product(normed_rows, full_up) + up_offset
    hidden_low = gelu_curve(hidden_pre).astype(jnp.bfloat16)
    down_part = lax.psum_scatter(
        product(hidden_low, full_down), "tp", scatter_dimension=1, tiled=True
    )
    second_sum = normed_first + down_part + downbias
    result, second_normed, second_inverse = layer_norm(second_sum, final_gain, final_shift)
    upstream = cotangent.astype(jnp.float32)
    finalgain_grad = jnp.sum(upstream * second_normed, axis=(0, 1))
    finalshift_grad = jnp.sum(upstream, axis=(0, 1))
    second_grad = norm_back(upstream, second_normed, second_inverse, final_gain)
    down_low = second_grad.astype(jnp.bfloat16)
    downbias_grad = jnp.sum(down_low, axis=(0, 1), dtype=jnp.float32)
    down_rows = lax.all_gather(down_low, "tp", axis=1, tiled=True)
    down_grad = weight_term(hidden_low, down_rows)
    hidden_grad = (transposed(down_rows, full_down) * gelu_slope(hidden_pre)).astype(jnp.bfloat16)
    upbias_part = jnp.sum(hidden_grad, axis=(0, 1), dtype=jnp.float32)
    up_grad = weight_term(normed_rows, hidden_grad)
    normed_grad = (
        lax.psum_scatter(transposed(hidden_grad, full_up), "tp", scatter_dimension=1, tiled=True)
        + second_grad
    )
    normgain_grad = jnp.sum(normed_grad * first_normed, axis=(0, 1))
    normshift_grad = jnp.sum(normed_grad, axis=(0, 1))
    first_grad = norm_back(normed_grad, first_normed, first_inverse, norm_gain)
    output_low = first_grad.astype(jnp.bfloat16)
    outputbias_grad = jnp.sum(output_low, axis=(0, 1), dtype=jnp.float32)
    output_rows = lax.all_gather(output_low, "tp", axis=1, tiled=True)
    output_grad = weight_term(attended, output_rows)
    mixed_grad = split_heads(transposed(output_rows, full_output).astype(jnp.bfloat16))
    row_dot = jnp.zeros((batch_rows, local_heads, shard_rows), jnp.float32)
    for offset in offsets:
        attn_probs = probabilities(queries, block_of[offset][0], mask_of[offset], log_total)
        prob_grad = jnp.einsum(
            "bqhd,bkhd->bhqk", mixed_grad, block_of[offset][1], preferred_element_type=jnp.float32
        )
        row_dot = row_dot + jnp.sum(attn_probs * prob_grad, axis=-1)
    query_acc = jnp.zeros((batch_rows, shard_rows, local_heads, HEAD_DIM), jnp.float32)
    key_parts = {}
    for offset in offsets:
        attn_probs = probabilities(queries, block_of[offset][0], mask_of[offset], log_total)
        prob_grad = jnp.einsum(
            "bqhd,bkhd->bhqk", mixed_grad, block_of[offset][1], preferred_element_type=jnp.float32
        )
        score_grad = (attn_probs * (prob_grad - row_dot[..., None])).astype(jnp.bfloat16)
        query_acc = query_acc + jnp.einsum(
            "bhqk,bkhd->bqhd", score_grad, block_of[offset][0], preferred_element_type=jnp.float32
        )
        key_term = jnp.einsum(
            "bhqk,bqhd->bkhd", score_grad, queries, preferred_element_type=jnp.float32
        )
        value_term = jnp.einsum(
            "bhqk,bqhd->bkhd",
            attn_probs.astype(jnp.bfloat16),
            mixed_grad,
            preferred_element_type=jnp.float32,
        )
        key_parts[offset] = (key_term, value_term)
    own_key, own_value = key_parts[0]
    for offset in offsets[1:]:
        back_key, back_value = shifted(for_sending(key_parts[offset]), "ctx", offset)
        own_key = own_key + back_key
        own_value = own_value + back_value
    query_pre = (
        join_heads(query_acc.astype(jnp.bfloat16)).astype(jnp.float32) * score_scale
    ).astype(jnp.bfloat16)
    key_low = join_heads(own_key.astype(jnp.bfloat16))
    value_low = join_heads(own_value.astype(jnp.bfloat16))
    querybias_part = jnp.sum(query_pre, axis=(0, 1), dtype=jnp.float32)
    valuebias_part = jnp.sum(value_low, axis=(0, 1), dtype=jnp.float32)
    query_grad = weight_term(tokens, query_pre)
    key_grad = weight_term(tokens, key_low)
    value_grad = weight_term(tokens, value_low)
    input_part = (
        transposed(query_pre, full_query)
        + transposed(key_low, full_key)
        + transposed(value_low, full_value)
    )
    input_grad = (
        lax.psum_scatter(
            input_part.astype(jnp.bfloat16), "tp", scatter_dimension=1, tiled=True
        ).astype(jnp.float32)
        + first_grad
    )
    query_grad, key_grad, value_grad, output_grad, up_grad, down_grad = (
        lax.psum_scatter(query_grad, ("dp", "ctx"), scatter_dimension=0, tiled=True),
        lax.psum_scatter(key_grad, ("dp", "ctx"), scatter_dimension=0, tiled=True),
        lax.psum_scatter(value_grad, ("dp", "ctx"), scatter_dimension=0, tiled=True),
        lax.psum_scatter(output_grad, ("dp", "ctx"), scatter_dimension=1, tiled=True),
        lax.psum_scatter(up_grad, ("dp", "ctx"), scatter_dimension=0, tiled=True),
        lax.psum_scatter(down_grad, ("dp", "ctx"), scatter_dimension=1, tiled=True),
    )
    summed = lax.psum(
        (
            placed(querybias_part, model_width, tp_place),
            placed(valuebias_part, model_width, tp_place),
            outputbias_grad,
            placed(upbias_part, hidden_width * tp_count, tp_place),
            downbias_grad,
            normgain_grad,
            normshift_grad,
            finalgain_grad,
            finalshift_grad,
        ),
        ("dp", "ctx", "tp"),
    )
    return (
        result.astype(jnp.bfloat16),
        input_grad,
        query_grad,
        key_grad,
        value_grad,
        output_grad,
        up_grad,
        down_grad,
        summed[0],
        summed[1],
        summed[2],
        summed[3],
        summed[4],
        summed[5],
        summed[6],
        summed[7],
        summed[8],
    )


MESH = pl.DeviceIdType.MESH
LOWEST = -1e30
VMEM = pl.BlockSpec(memory_space=pltpu.VMEM)
LEFT = pl.BlockSpec(memory_space=pl.ANY)


class Seat:
    def __init__(self):
        self.dp_count = lax.axis_size("dp")
        self.dp = lax.axis_index("dp")
        self.ctx = lax.axis_index("ctx")
        self.tp = lax.axis_index("tp")
        self.tp_pair = self.tp + 1 - 2 * (self.tp % 2)
        self.tp_side = (self.tp + 2) % 4
        self.tp_far = (self.tp_pair + 2) % 4
        self.pair = (self.dp, self.ctx, self.tp_pair)
        self.side = (self.dp, self.ctx, self.tp_side)
        self.twin = (self.dp, 1 - self.ctx, self.tp)
        self.above = ((self.dp + 1) % self.dp_count, self.ctx, self.tp)
        self.below = ((self.dp + self.dp_count - 1) % self.dp_count, self.ctx, self.tp)

    def meet(self, names):
        barrier = pltpu.get_barrier_semaphore()
        for name in names:
            pl.semaphore_signal(
                barrier, inc=1, device_id=getattr(self, name), device_id_type=MESH
            )
        pl.semaphore_wait(barrier, len(names))


def remote(source, target, send_sem, recv_sem, to):
    return pltpu.make_async_remote_copy(
        src_ref=source,
        dst_ref=target,
        send_sem=send_sem,
        recv_sem=recv_sem,
        device_id=to,
        device_id_type=MESH,
    )


class RingGather:
    def __init__(self, seat, shard, block, sems, at):
        self.seat, self.shard, self.block, self.at = seat, shard, block, at
        self.own_sem, self.z_send, self.z_recv, self.y_send, self.y_recv = sems
        self.count = seat.dp_count

    def index(self, step, ctx):
        origin = (self.seat.dp + self.count - step) % self.count
        return origin * 2 + ctx

    def held(self, step):
        return self.block(self.index(step, self.seat.ctx))

    def own(self):
        return pltpu.make_async_copy(self.shard, self.held(0), self.own_sem.at[self.at])

    def z(self, step):
        source = self.shard if step == 0 else self.held(step)
        return remote(
            source,
            self.held(step),
            self.z_send.at[self.at, step],
            self.z_recv.at[self.at, step],
            self.seat.above,
        )

    def z_in(self, step):
        view = self.held(step + 1)
        return remote(
            view,
            view,
            self.z_send.at[self.at, step],
            self.z_recv.at[self.at, step],
            self.seat.above,
        )

    def y(self, step):
        source = self.shard if step == 0 else self.held(step)
        return remote(
            source,
            self.held(step),
            self.y_send.at[self.at, step],
            self.y_recv.at[self.at, step],
            self.seat.twin,
        )

    def y_in(self, step):
        view = self.block(self.index(step, 1 - self.seat.ctx))
        return remote(
            view,
            view,
            self.y_send.at[self.at, step],
            self.y_recv.at[self.at, step],
            self.seat.twin,
        )

    def begin(self):
        self.own().start()
        self.z(0).start()
        self.y(0).start()

    def pass_on(self, step):
        self.z_in(step).wait_recv()
        if step + 1 < self.count - 1:
            self.z(step + 1).start()
        self.y(step + 1).start()

    def land(self):
        self.own().wait()
        for step in range(self.count):
            self.y_in(step).wait_recv()

    def close(self):
        for step in range(self.count - 1):
            self.z(step).wait_send()
        for step in range(self.count):
            self.y(step).wait_send()


def gather_sems(pieces, count):
    dma = pltpu.SemaphoreType.DMA
    return [
        dma((pieces,)),
        dma((pieces, count - 1)),
        dma((pieces, count - 1)),
        dma((pieces, count)),
        dma((pieces, count)),
    ]


def dot(left_side, right_side):
    return jnp.dot(left_side, right_side, preferred_element_type=jnp.float32)


def dot_nt(left_side, right_side):
    return lax.dot_general(
        left_side, right_side, (((1,), (1,)), ((), ())), preferred_element_type=jnp.float32
    )


def dot_tn(left_side, right_side):
    return lax.dot_general(
        left_side, right_side, (((0,), (0,)), ((), ())), preferred_element_type=jnp.float32
    )


def aligned(start, size):
    return pl.ds(pl.multiple_of(start, size), size)


def attend_kernel(
    inputs_ref,
    ids_ref,
    query_shard,
    key_shard,
    value_shard,
    output_shard,
    up_shard,
    down_shard,
    query_bias,
    value_bias,
    tokens_ref,
    other_ref,
    query_full,
    key_full,
    value_full,
    output_full,
    up_full,
    down_full,
    query_ref,
    key_ref,
    value_ref,
    mixed_ref,
    log_ref,
    attended_ref,
    flipped_ref,
    ids_down,
    token_send,
    token_recv,
    token_own,
    *sems,
):
    seat = Seat()
    batch, part, width = inputs_ref.shape
    rows = tokens_ref.shape[1]
    local = query_full.shape[1]
    heads = local // HEAD_DIM
    depth = query_shard.shape[0]
    seat.meet(("pair", "side", "twin", "above", "below"))

    def cut(half, place):
        return half.at[:, aligned(place * part, part), :]

    def token_copy(relation, source, target, to):
        return remote(source, target, token_send.at[relation], token_recv.at[relation], to)

    here = cut(tokens_ref, seat.tp)
    there = cut(other_ref, seat.tp)
    here_side = cut(tokens_ref, seat.tp_side)
    there_side = cut(other_ref, seat.tp_side)
    sends = [
        token_copy(0, inputs_ref, here, seat.pair),
        token_copy(1, inputs_ref, here, seat.side),
        token_copy(2, inputs_ref, there, seat.twin),
        token_copy(3, there, there, seat.side),
        token_copy(4, here_side, here_side, seat.pair),
        token_copy(5, there, there, seat.pair),
        token_copy(6, there_side, there_side, seat.pair),
    ]
    landed = [
        cut(tokens_ref, seat.tp_pair),
        here_side,
        there,
        there_side,
        cut(tokens_ref, seat.tp_far),
        cut(other_ref, seat.tp_pair),
        cut(other_ref, seat.tp_far),
    ]

    def token_in(relation):
        token_copy(relation, landed[relation], landed[relation], seat.pair).wait_recv()

    own_tokens = pltpu.make_async_copy(inputs_ref, here, token_own)
    own_tokens.start()
    for relation in range(3):
        sends[relation].start()

    def by_rows(full):
        return lambda r: full.at[aligned(r * depth, depth), :]

    def by_columns(full):
        return lambda r: full.at[:, aligned(r * depth, depth)]

    weights = [
        RingGather(seat, query_shard, by_rows(query_full), sems, 0),
        RingGather(seat, key_shard, by_rows(key_full), sems, 1),
        RingGather(seat, value_shard, by_rows(value_full), sems, 2),
    ]
    later = [
        RingGather(seat, output_shard, by_columns(output_full), sems, 3),
        RingGather(seat, up_shard, by_rows(up_full), sems, 4),
        RingGather(seat, down_shard, by_columns(down_full), sems, 5),
    ]
    hops = seat.dp_count - 1
    for weight in weights:
        weight.begin()
    for step in range(hops):
        for weight in weights:
            weight.pass_on(step)
    for weight in later:
        weight.begin()
    token_in(1)
    sends[4].start()
    token_in(2)
    sends[3].start()
    sends[5].start()

    for b in range(batch):
        for half in range(2):
            row_ids = ids_ref[b : b + 1, aligned((seat.ctx if half == 0 else 1 - seat.ctx) * rows, rows)]
            spread = jnp.broadcast_to(row_ids.astype(jnp.float32), (128, rows))
            ids_down[b, half * rows : (half + 1) * rows, :] = spread.T

    bias_at = aligned(seat.tp * local, local)
    query_offset = query_bias[:, bias_at]
    value_offset = value_bias[:, bias_at]
    tile = rows // 2
    for weight in weights:
        weight.land()
    own_tokens.wait()
    token_in(0)
    token_in(4)

    def project(half_ref, half):
        def one(index, carry):
            b, piece = index // 2, index % 2
            block = half_ref[b, aligned(piece * tile, tile), :]
            spot = aligned(half * rows + piece * tile, tile)
            if half == 0:
                scaled = (dot(block, query_full[...]) + query_offset) * HEAD_DIM ** (-0.5)
                query_ref[b, aligned(piece * tile, tile), :] = scaled.astype(jnp.bfloat16)
            key_ref[b, spot, :] = dot(block, key_full[...]).astype(jnp.bfloat16)
            value_rows = dot(block, value_full[...]) + value_offset
            value_ref[b, spot, :] = value_rows.astype(jnp.bfloat16)
            flipped_ref[b, :, spot] = value_rows.T.astype(jnp.bfloat16)
            return carry

        lax.fori_loop(0, batch * 2, one, 0)

    project(tokens_ref, 0)
    token_in(3)
    sends[6].start()
    token_in(5)
    token_in(6)
    project(other_ref, 1)

    lane_head = lax.broadcasted_iota(jnp.int32, (1, local), 1) // HEAD_DIM

    def attend(index, carry):
        for step in range(hops):
            @pl.when(index == 2 * step + 1)
            def _():
                for weight in later:
                    weight.pass_on(step)

        b, h = index // heads, index % heads
        own_rows = aligned(h * HEAD_DIM, HEAD_DIM)
        chosen = jnp.where(lane_head == h, query_ref[b], jnp.zeros((), jnp.bfloat16))
        scores = dot_nt(key_ref[b], chosen)
        own_ids = ids_ref[b, aligned(seat.ctx * rows, rows)].astype(jnp.float32)
        same = jnp.tile(ids_down[b], (1, rows // 128)) == own_ids[None, :]
        scores = jnp.where(same, scores, LOWEST)
        highest = jnp.max(scores, axis=0, keepdims=True)
        raised = jnp.exp(scores - highest)
        total = jnp.sum(raised, axis=0, keepdims=True)
        shares = (raised * (1.0 / total)).astype(jnp.bfloat16)
        mixed_ref[b, own_rows, :] = dot(flipped_ref[b, own_rows, :], shares)
        log_ref[index] = highest + jnp.log(total)
        return carry

    lax.fori_loop(0, batch * heads, attend, 0)
    for b in range(batch):
        attended_ref[b] = mixed_ref[b].T.astype(jnp.bfloat16)
    for weight in later:
        weight.land()
    for copy in sends:
        copy.wait_send()
    for weight in weights + later:
        weight.close()


def attend_forward(
    inputs, segment_ids, shards, querybias, valuebias
):
    count = lax.axis_size("dp")
    batch, part, width = inputs.shape
    rows = part * lax.axis_size("tp")
    local = shards[0].shape[1]
    hidden = shards[4].shape[1]
    heads = local // HEAD_DIM
    bf16, f32 = jnp.bfloat16, jnp.float32
    outs = [
        ((batch, rows, width), bf16, VMEM),
        ((batch, rows, width), bf16, VMEM),
        ((width, local), bf16, VMEM),
        ((width, local), bf16, VMEM),
        ((width, local), bf16, VMEM),
        ((local, width), bf16, LEFT),
        ((width, hidden), bf16, LEFT),
        ((hidden, width), bf16, LEFT),
        ((batch, rows, local), bf16, VMEM),
        ((batch, 2 * rows, local), bf16, VMEM),
        ((batch, 2 * rows, local), bf16, VMEM),
        ((batch, local, rows), f32, VMEM),
        ((batch * heads, 1, rows), f32, VMEM),
        ((batch, rows, local), bf16, VMEM),
    ]
    dma = pltpu.SemaphoreType.DMA
    return pl.pallas_call(
        attend_kernel,
        name="attend_forward",
        out_shape=[jax.ShapeDtypeStruct(shape, kind) for shape, kind, _ in outs],
        in_specs=[VMEM] * 10,
        out_specs=[space for _, _, space in outs],
        scratch_shapes=[
            pltpu.VMEM((batch, local, 2 * rows), bf16),
            pltpu.VMEM((batch, 2 * rows, 128), f32),
            dma((7,)),
            dma((7,)),
            dma(()),
            *gather_sems(6, count),
        ],
        compiler_params=pltpu.CompilerParams(
            collective_id=1, has_side_effects=True, vmem_limit_bytes=56 * 2**20
        ),
    )(
        inputs,
        segment_ids,
        *shards,
        querybias.reshape(1, -1),
        valuebias.reshape(1, -1),
    )


VECTOR_ROWS = 16
ROW_QUERY, ROW_VALUE, ROW_OUTPUT, ROW_DOWN = 0, 1, 2, 3
ROW_GAIN, ROW_SHIFT, ROW_FINAL_GAIN, ROW_FINAL_SHIFT, ROW_UP = 4, 5, 6, 7, 8


class TokenScatter:
    def __init__(self, seat, buffers, sems, at):
        self.seat, self.at = seat, at
        self.pair_out, self.pair_in, self.side_out, self.side_in = buffers
        self.send, self.recv = sems

    def copy(self, k):
        at, seat = self.at, self.seat
        if k < 2:
            source, target, to = self.pair_out.at[at, k], self.pair_in.at[at, k], seat.pair
        else:
            source, target, to = self.side_out.at[at], self.side_in.at[at], seat.side
        return remote(source, target, self.send.at[at, k], self.recv.at[at, k], to)

    def give(self, compute, total):
        seat, at = self.seat, self.at
        part = self.side_out.shape[1]
        group = seat.tp // 2
        mine = aligned((seat.tp % 2) * part, part)
        others = aligned((1 - seat.tp % 2) * part, part)
        compute(1 - group)
        self.pair_out[at, 0] = total[others, :].astype(jnp.bfloat16)
        self.copy(0).start()
        self.side_out[at] = total[mine, :].astype(jnp.bfloat16)
        compute(group)
        self.pair_out[at, 1] = total[others, :].astype(jnp.bfloat16)
        self.copy(1).start()
        self.copy(0).wait_recv()
        self.side_out[at] = (
            self.side_out[at].astype(jnp.float32) + self.pair_in[at, 0].astype(jnp.float32)
        ).astype(jnp.bfloat16)
        self.copy(2).start()
        return mine

    def take(self):
        self.copy(1).wait_recv()
        self.copy(2).wait_recv()
        return self.pair_in[self.at, 1].astype(jnp.float32) + self.side_in[self.at].astype(
            jnp.float32
        )

    def close(self):
        for k in range(3):
            self.copy(k).wait_send()


class TokenGather:
    def __init__(self, seat, full, b, part, sems, at):
        self.seat = seat
        self.send, self.recv = sems
        self.at = at
        self.view = lambda place: full.at[b, aligned(place * part, part), :]

    def copy(self, k, place, to):
        view = self.view(place)
        return remote(view, view, self.send.at[self.at, k], self.recv.at[self.at, k], to)

    def give(self):
        seat = self.seat
        self.copy(0, seat.tp, seat.side).start()
        self.copy(1, seat.tp, seat.pair).start()

    def relay(self):
        seat = self.seat
        self.copy(0, seat.tp_side, seat.side).wait_recv()
        self.copy(2, seat.tp_side, seat.pair).start()

    def land(self):
        seat = self.seat
        self.copy(1, seat.tp_pair, seat.pair).wait_recv()
        self.copy(2, seat.tp_far, seat.pair).wait_recv()

    def close(self):
        seat = self.seat
        for k, place in ((0, seat.tp), (1, seat.tp), (2, seat.tp_side)):
            self.copy(k, place, seat.pair).wait_send()


def row_mean(rows):
    return jnp.mean(rows, axis=-1, keepdims=True)


def feed_kernel(
    inputs_ref,
    attended_ref,
    cotangent_ref,
    output_full,
    up_full,
    down_full,
    output_bias,
    up_bias,
    down_bias,
    norm_gain,
    norm_shift,
    final_gain,
    final_shift,
    result_ref,
    first_ref,
    mixed_ref,
    output_part,
    up_part,
    down_part,
    vectors_ref,
    normed_rows,
    hidden_rows,
    slope_rows,
    down_rows,
    back_rows,
    output_rows,
    normed_keep,
    scaled_keep,
    inverse_keep,
    second_keep,
    total_own,
    total,
    pair_out,
    pair_in,
    side_out,
    side_in,
    scatter_send,
    scatter_recv,
    gather_send,
    gather_recv,
):
    seat = Seat()
    batch, part, width = inputs_ref.shape
    rows = attended_ref.shape[1]
    hidden = up_full.shape[1]
    f32, bf16 = jnp.float32, jnp.bfloat16
    seat.meet(("pair", "side"))
    buffers = (pair_out, pair_in, side_out, side_in)
    scatters = [
        TokenScatter(seat, buffers, (scatter_send, scatter_recv), k) for k in range(3 * batch)
    ]
    gathers = [
        TokenGather(seat, full, b, part, (gather_send, gather_recv), k * batch + b)
        for k, full in enumerate((normed_rows, down_rows, output_rows))
        for b in range(batch)
    ]
    wide = 256
    up_offset = lambda at: up_bias[:, pl.ds(pl.multiple_of(seat.tp * hidden + at * wide, wide), wide)]

    def over(tiles, body):
        def one(index, carry):
            body(index)
            return carry

        lax.fori_loop(0, tiles, one, 0)

    def spread(lhs_ref, b, weight, flipped):
        def compute(group):
            lhs = lhs_ref[b, aligned(group * 2 * part, 2 * part), :]

            def tile(index):
                columns = aligned(index * wide, wide)
                if flipped:
                    total[:, columns] = dot_nt(lhs, weight[columns, :])
                else:
                    total[:, columns] = dot(lhs, weight[:, columns])

            over(width // wide, tile)

        return compute

    def scatter(k, b, lhs_ref, weight, flipped):
        mine = scatters[k * batch + b].give(spread(lhs_ref, b, weight, flipped), total)
        total_own[b] = total[mine, :]

    def collected(k, b):
        return total_own[b] + scatters[k * batch + b].take()

    own_rows = aligned(seat.tp * part, part)
    vectors_ref[...] = jnp.zeros_like(vectors_ref)

    def add_vector(row, values):
        vectors_ref[row : row + 1, :] += jnp.sum(values, axis=0, keepdims=True)

    def first_norm(b):
        first_sum = inputs_ref[b].astype(f32) + (collected(0, b) + output_bias[...])
        center = first_sum - row_mean(first_sum)
        inverse = lax.rsqrt(row_mean(center * center) + 1e-05)
        normed = center * inverse
        scaled = normed * norm_gain[...] + norm_shift[...]
        normed_keep[b] = normed
        inverse_keep[b] = inverse
        scaled_keep[b] = scaled
        normed_rows[b, own_rows, :] = scaled.astype(bf16)
        gathers[b].give()

    def raise_up(b):
        gathers[b].land()
        lhs = normed_rows[b]

        def tile(index):
            columns = aligned(index * wide, wide)
            pre = dot(lhs, up_full[:, columns]) + up_offset(index)
            half = 0.5 * (1.0 + lax.erf(pre * 0.7071067811865476))
            hidden_rows[b, :, columns] = (pre * half).astype(bf16)
            slope_rows[b, :, columns] = half + pre * jnp.exp(-0.5 * pre * pre) * 0.3989422804014327

        over(hidden // wide, tile)

    def second_norm(b):
        second_sum = scaled_keep[b] + (collected(1, b) + down_bias[...])
        center = second_sum - row_mean(second_sum)
        inverse = lax.rsqrt(row_mean(center * center) + 1e-05)
        normed = center * inverse
        result_ref[b] = (normed * final_gain[...] + final_shift[...]).astype(bf16)
        upstream = cotangent_ref[b].astype(f32)
        add_vector(ROW_FINAL_GAIN, upstream * normed)
        add_vector(ROW_FINAL_SHIFT, upstream)
        scaled = upstream * final_gain[...]
        second = inverse * (scaled - row_mean(scaled) - normed * row_mean(scaled * normed))
        second_keep[b] = second
        low = second.astype(bf16)
        down_rows[b, own_rows, :] = low
        gathers[batch + b].give()
        add_vector(ROW_DOWN, low.astype(f32))

    def lower(b):
        gathers[batch + b].land()
        lhs = down_rows[b]

        def tile(index):
            columns = aligned(index * wide, wide)
            back = (dot_nt(lhs, down_full[columns, :]) * slope_rows[b, :, columns]).astype(bf16)
            back_rows[b, :, columns] = back
            place = pl.ds(pl.multiple_of(index * wide, wide), wide)
            up_sum[:, place] += jnp.sum(back.astype(f32), axis=0, keepdims=True)

        over(hidden // wide, tile)

    up_sum = vectors_ref.at[ROW_UP : ROW_UP + 1, :]

    def first_back(b):
        grad = collected(2, b) + second_keep[b]
        normed = normed_keep[b]
        add_vector(ROW_GAIN, grad * normed)
        add_vector(ROW_SHIFT, grad)
        scaled = grad * norm_gain[...]
        first = inverse_keep[b] * (
            scaled - row_mean(scaled) - normed * row_mean(scaled * normed)
        )
        first_ref[b] = first
        low = first.astype(bf16)
        output_rows[b, own_rows, :] = low
        gathers[2 * batch + b].give()
        add_vector(ROW_OUTPUT, low.astype(f32))

    def mix_back(b):
        gathers[2 * batch + b].land()
        mixed_ref[b] = dot_nt(output_rows[b], output_full[...]).astype(bf16)

    def weight_tiles(left_ref, right_ref, target, first, last):
        left = left_ref[...].reshape(batch * rows, left_ref.shape[2])
        right_width = right_ref.shape[2]

        def tile(index):
            columns = aligned((first + index) * wide, wide)
            right = right_ref[:, :, columns].reshape(batch * rows, wide)
            target[:, columns] = dot_tn(left, right).astype(bf16)

        over(last - first, tile)

    for b in range(batch):
        scatter(0, b, attended_ref, output_full, False)
    for b in range(batch):
        first_norm(b)
    gathers[0].relay()
    raise_up(0)
    gathers[1].relay()
    scatter(1, 0, hidden_rows, down_full, False)
    raise_up(1)
    scatter(1, 1, hidden_rows, down_full, False)
    second_norm(0)
    second_norm(1)
    gathers[batch].relay()
    lower(0)
    gathers[batch + 1].relay()
    scatter(2, 0, back_rows, up_full, True)
    lower(1)
    scatter(2, 1, back_rows, up_full, True)
    weight_tiles(hidden_rows, down_rows, down_part, 0, 2)
    first_back(0)
    weight_tiles(hidden_rows, down_rows, down_part, 2, 4)
    first_back(1)
    weight_tiles(normed_rows, back_rows, up_part, 0, 2)
    gathers[2 * batch].relay()
    mix_back(0)
    gathers[2 * batch + 1].relay()
    weight_tiles(normed_rows, back_rows, up_part, 2, 4)
    mix_back(1)
    weight_tiles(attended_ref, output_rows, output_part, 0, 4)
    for k in scatters + gathers:
        k.close()


def feed_both_ways(
    inputs, attended, cotangent, output_full, up_full, down_full, vectors
):
    batch, part, width = inputs.shape
    rows, local = attended.shape[1:]
    hidden = up_full.shape[1]
    bf16, f32 = jnp.bfloat16, jnp.float32
    outs = [
        ((batch, part, width), bf16),
        ((batch, part, width), f32),
        ((batch, rows, local), bf16),
        ((local, width), bf16),
        ((width, hidden), bf16),
        ((hidden, width), bf16),
        ((VECTOR_ROWS, width), f32),
    ]
    dma = pltpu.SemaphoreType.DMA
    return pl.pallas_call(
        feed_kernel,
        name="feed_both_ways",
        out_shape=[jax.ShapeDtypeStruct(shape, kind) for shape, kind in outs],
        in_specs=[VMEM] * 13,
        out_specs=[VMEM] * len(outs),
        scratch_shapes=[
            pltpu.VMEM((batch, rows, width), bf16),
            pltpu.VMEM((batch, rows, hidden), bf16),
            pltpu.VMEM((batch, rows, hidden), f32),
            pltpu.VMEM((batch, rows, width), bf16),
            pltpu.VMEM((batch, rows, hidden), bf16),
            pltpu.VMEM((batch, rows, width), bf16),
            pltpu.VMEM((batch, part, width), f32),
            pltpu.VMEM((batch, part, width), f32),
            pltpu.VMEM((batch, part, 1), f32),
            pltpu.VMEM((batch, part, width), f32),
            pltpu.VMEM((batch, part, width), f32),
            pltpu.VMEM((2 * part, width), f32),
            pltpu.VMEM((3 * batch, 2, part, width), bf16),
            pltpu.VMEM((3 * batch, 2, part, width), bf16),
            pltpu.VMEM((3 * batch, part, width), bf16),
            pltpu.VMEM((3 * batch, part, width), bf16),
            dma((3 * batch, 3)),
            dma((3 * batch, 3)),
            dma((3 * batch, 3)),
            dma((3 * batch, 3)),
        ],
        compiler_params=pltpu.CompilerParams(
            collective_id=2, has_side_effects=True, vmem_limit_bytes=63 * 2**20
        ),
    )(
        inputs,
        attended,
        cotangent,
        output_full,
        up_full,
        down_full,
        *[vector.reshape(1, -1) for vector in vectors],
    )


class PairedReduce:
    def __init__(self, seat, partial, block, twin_in, ring_out, ring_in, sems, at):
        self.seat, self.partial, self.block, self.at = seat, partial, block, at
        self.twin_in, self.ring_out, self.ring_in = twin_in, ring_out, ring_in
        self.y_send, self.y_recv, self.z_send, self.z_recv = sems
        self.count = seat.dp_count

    def mine(self, step, ctx):
        owner = (self.seat.dp + 2 * self.count - 1 - step) % self.count
        return self.block(self.partial, owner * 2 + ctx)

    def y(self, step):
        return remote(
            self.mine(step, 1 - self.seat.ctx),
            self.twin_in.at[step],
            self.y_send.at[self.at, step],
            self.y_recv.at[self.at, step],
            self.seat.twin,
        )

    def z(self, step):
        return remote(
            self.ring_out.at[step],
            self.ring_in.at[step],
            self.z_send.at[self.at, step],
            self.z_recv.at[self.at, step],
            self.seat.above,
        )

    def begin(self):
        for step in range(self.count):
            self.y(step).start()

    def advance(self, step):
        self.y(step).wait_recv()
        total = self.mine(step, self.seat.ctx)[...].astype(jnp.float32) + self.twin_in[
            step
        ].astype(jnp.float32)
        if step > 0:
            self.z(step - 1).wait_recv()
            total = total + self.ring_in[step - 1].astype(jnp.float32)
        if step == self.count - 1:
            return total
        self.ring_out[step] = total.astype(jnp.bfloat16)
        self.z(step).start()

    def close(self):
        for step in range(self.count):
            self.y(step).wait_send()
        for step in range(self.count - 1):
            self.z(step).wait_send()


class RingReduce:
    def __init__(self, seat, partial, pair, ring_out, ring_in, half_out, half_in, sems, at):
        self.seat, self.partial, self.pair, self.at = seat, partial, pair, at
        self.ring_out, self.ring_in, self.half_out, self.half_in = ring_out, ring_in, half_out, half_in
        self.y_send, self.y_recv, self.z_send, self.z_recv = sems
        self.count = seat.dp_count

    def mine(self, step):
        owner = (self.seat.dp + 2 * self.count - 1 - step) % self.count
        return self.pair(self.partial, owner)

    def z(self, step):
        return remote(
            self.mine(0) if step == 0 else self.ring_out.at[step - 1],
            self.ring_in.at[step],
            self.z_send.at[self.at, step],
            self.z_recv.at[self.at, step],
            self.seat.above,
        )

    def y(self):
        return remote(
            self.half_out,
            self.half_in,
            self.y_send.at[self.at, 0],
            self.y_recv.at[self.at, 0],
            self.seat.twin,
        )

    def begin(self):
        self.z(0).start()

    def advance(self, step):
        self.z(step - 1).wait_recv()
        total = self.mine(step)[...].astype(jnp.float32) + self.ring_in[step - 1].astype(
            jnp.float32
        )
        if step == self.count - 1:
            return total
        self.ring_out[step - 1] = total.astype(jnp.bfloat16)
        self.z(step).start()

    def close(self):
        self.y().wait_send()
        for step in range(self.count - 1):
            self.z(step).wait_send()


def back_kernel(
    tokens_ref,
    other_ref,
    ids_ref,
    query_ref,
    key_ref,
    value_ref,
    mixed_ref,
    log_ref,
    grad_ref,
    query_full,
    key_full,
    value_full,
    first_ref,
    output_part,
    up_part,
    down_part,
    vectors_ref,
    input_grad,
    query_grad,
    key_grad,
    value_grad,
    output_grad,
    up_grad,
    down_grad,
    sums_ref,
    ids_down,
    key_flip,
    row_dots,
    query_flip,
    key_sum,
    value_sum,
    lows,
    weight_sum,
    weight_low,
    total,
    total_own,
    pair_out,
    pair_in,
    side_out,
    side_in,
    scatter_send,
    scatter_recv,
    other_out,
    other_in,
    other_send,
    other_recv,
    thin_twin,
    thin_out,
    thin_in,
    output_twin,
    output_out,
    output_in,
    down_twin,
    down_out,
    down_in,
    up_out,
    up_in,
    up_half_out,
    up_half_in,
    sum_in,
    sum_all,
    sum_send,
    sum_recv,
    *sems,
):
    seat = Seat()
    count = seat.dp_count
    batch, part, width = first_ref.shape
    rows = tokens_ref.shape[1]
    local = query_full.shape[1]
    heads = local // HEAD_DIM
    depth = width // (2 * count)
    f32, bf16 = jnp.float32, jnp.bfloat16

    barrier = pltpu.get_barrier_semaphore()
    around = [((seat.dp + away) % count, seat.ctx, seat.tp) for away in range(1, count)]
    for to in [seat.pair, seat.side, seat.twin] + around:
        pl.semaphore_signal(barrier, inc=1, device_id=to, device_id_type=MESH)
    pl.semaphore_wait(barrier, 2 + count)

    columns = lambda ref, r: ref.at[:, aligned(r * depth, depth)]
    thin = [
        PairedReduce(
            seat, weight_low.at[k], columns,
            thin_twin.at[k], thin_out.at[k], thin_in.at[k], sems, k,
        )
        for k in range(3)
    ]
    from_output = PairedReduce(
        seat, output_part, columns, output_twin, output_out, output_in, sems, 3
    )
    from_down = PairedReduce(seat, down_part, columns, down_twin, down_out, down_in, sems, 4)
    from_up = RingReduce(
        seat, up_part, lambda ref, owner: ref.at[aligned(owner * 2 * depth, 2 * depth), :],
        up_out, up_in, up_half_out, up_half_in, sems, 5,
    )
    from_up.begin()
    from_output.begin()
    from_down.begin()
    scatters = [
        TokenScatter(
            seat, (pair_out, pair_in, side_out, side_in), (scatter_send, scatter_recv), k
        )
        for k in range(2 * batch)
    ]
    wide = 256

    for b in range(batch):
        for half in range(2):
            row_ids = ids_ref[b : b + 1, aligned((seat.ctx if half == 0 else 1 - seat.ctx) * rows, rows)]
            spread = jnp.broadcast_to(row_ids.astype(f32), (128, rows))
            ids_down[b, half * rows : (half + 1) * rows, :] = spread.T
    lane_head = lax.broadcasted_iota(jnp.int32, (1, local), 1) // HEAD_DIM
    nothing = jnp.zeros((), bf16)
    bias_at = aligned(seat.tp * local, local)
    up_row = 8
    sums_ref[...] = jnp.zeros_like(sums_ref)
    sums_ref[2:8, :] = vectors_ref[2:8, :]
    sums_ref[pl.ds(up_row + seat.tp, 1), :] = vectors_ref[ROW_UP : ROW_UP + 1, :]

    def heads_back(b, services):
        key_flip[...] = key_ref[b].astype(f32).T.astype(bf16)
        product_rows = grad_ref[b].astype(f32).T * mixed_ref[b]
        for h in range(heads):
            row_dots[h] = jnp.sum(
                product_rows[h * HEAD_DIM : (h + 1) * HEAD_DIM], axis=0, keepdims=True
            )
        key_sum[...] = jnp.zeros_like(key_sum)
        value_sum[...] = jnp.zeros_like(value_sum)
        own_ids = ids_ref[b : b + 1, aligned(seat.ctx * rows, rows)].astype(f32)

        def one(h, carry):
            for when, service in services:
                pl.when(h == when)(service)
            own = aligned(h * HEAD_DIM, HEAD_DIM)
            query_rows = jnp.where(lane_head == h, query_ref[b], nothing)
            grad_rows = jnp.where(lane_head == h, grad_ref[b], nothing)
            same = jnp.tile(ids_down[b], (1, rows // 128)) == own_ids
            scores = jnp.where(same, dot_nt(key_ref[b], query_rows), LOWEST)
            probs = jnp.exp(scores - log_ref[b * heads + h])
            value_sum[...] += dot(probs.astype(bf16), grad_rows)
            prob_grad = dot_nt(value_ref[b], grad_rows)
            score_grad = (probs * (prob_grad - row_dots[h])).astype(bf16)
            key_sum[...] += dot(score_grad, query_rows)
            query_flip[own, :] = dot(key_flip[own, :], score_grad)
            return carry

        lax.fori_loop(0, heads, one, 0)

    def sequence_back(b):
        flipped = (query_flip[...].astype(bf16).astype(f32) * HEAD_DIM ** (-0.5)).astype(bf16)
        upright = flipped.astype(f32).T
        lows[0, :rows, :] = upright.astype(bf16)
        key_low = key_sum[...].astype(bf16)
        value_low = value_sum[...].astype(bf16)
        lows[1] = key_low
        lows[2] = value_low
        sums_ref[0:1, bias_at] += jnp.sum(upright, axis=0, keepdims=True)
        sums_ref[1:2, bias_at] += jnp.sum(value_low.astype(f32), axis=0, keepdims=True)
        flips = [flipped, key_low.astype(f32).T.astype(bf16), value_low.astype(f32).T.astype(bf16)]

        for k in range(3):
            def tile(index, carry, k=k):
                at = aligned(index * wide, wide)
                term = dot(flips[k][:, :rows], tokens_ref[b, :, at])
                if k > 0:
                    term = term + dot(flips[k][:, rows:], other_ref[b, :, at])
                if b > 0:
                    term = term + weight_sum[k, :, at]
                if b == batch - 1:
                    weight_low[k, :, at] = term.astype(bf16)
                else:
                    weight_sum[k, :, at] = term
                return carry

            lax.fori_loop(0, width // wide, tile, 0)

    def input_back(b, half):
        def compute(group):
            at = aligned(half * rows + group * 2 * part, 2 * part)

            def tile(index, carry):
                row_at = aligned(index * wide, wide)
                term = dot_nt(lows[1, at, :], key_full[row_at, :]) + dot_nt(
                    lows[2, at, :], value_full[row_at, :]
                )
                if half == 0:
                    term = term + dot_nt(lows[0, at, :], query_full[row_at, :])
                total[:, row_at] = term
                return carry

            lax.fori_loop(0, width // wide, tile, 0)

        mine = scatters[2 * b + half].give(compute, total)
        total_own[2 * b + half] = total[mine, :]

    def other_copy(b):
        return remote(
            other_out.at[b], other_in.at[b], other_send.at[b], other_recv.at[b], seat.twin
        )

    def other_give(b):
        other_out[b] = (total_own[2 * b + 1] + scatters[2 * b + 1].take()).astype(bf16)
        other_copy(b).start()

    def input_take(b):
        own = total_own[2 * b] + scatters[2 * b].take()
        other_copy(b).wait_recv()
        input_grad[b] = (own + other_in[b].astype(f32)) + first_ref[b]

    def both(step):
        def service():
            from_output.advance(step)
            from_down.advance(step)

        return service

    def lift(step):
        def service():
            from_up.advance(step)

        return service

    heads_back(0, [(2, both(0)), (heads - 1, lift(1))])
    sequence_back(0)
    input_back(0, 1)
    input_back(0, 0)
    heads_back(1, [(0, both(1)), (1, lambda: other_give(0)), (heads - 1, lift(2))])
    sequence_back(1)
    for k in thin:
        k.begin()
    input_back(1, 1)
    input_back(1, 0)

    def sum_copy(stage, to):
        return remote(sum_all.at[stage], sum_in.at[stage], sum_send.at[stage], sum_recv.at[stage], to)

    def sum_stage(stage, to):
        sum_all[stage] = sums_ref[...]
        sum_copy(stage, to).start()

    def sum_add(stage, to):
        sum_copy(stage, to).wait_recv()
        sums_ref[...] = sums_ref[...] + sum_in[stage]

    sum_stage(0, seat.pair)
    both(2)()
    for k in thin:
        k.advance(0)
    sum_add(0, seat.pair)
    sum_stage(1, seat.side)
    input_take(0)
    other_give(1)
    for k in thin:
        k.advance(1)
    sum_add(1, seat.side)
    sum_stage(2, seat.twin)
    half_rows = aligned(seat.ctx * depth, depth)
    other_half = aligned((1 - seat.ctx) * depth, depth)
    up_total = total
    up_total[...] = from_up.advance(count - 1)
    up_half_out[...] = up_total[other_half, :].astype(bf16)
    from_up.y().start()
    output_grad[...] = from_output.advance(count - 1)
    down_grad[...] = from_down.advance(count - 1)
    sum_add(2, seat.twin)

    def around_copy(away):
        stage = 4 + away
        return remote(
            sum_all.at[3], sum_in.at[stage], sum_send.at[stage], sum_recv.at[stage], around[away]
        )

    sum_all[3] = sums_ref[...]
    for away in range(count - 1):
        around_copy(away).start()
    for k in thin:
        k.advance(2)
    from_up.y().wait_recv()
    up_grad[...] = up_total[half_rows, :] + up_half_in[...].astype(f32)
    input_take(1)
    sum_in[3] = sums_ref[...]
    for away in range(count - 1):
        around_copy(away).wait_recv()
    gathered = jnp.zeros_like(sums_ref[...])
    for origin in range(count):
        gathered = gathered + sum_in[3 + (seat.dp + count - origin) % count]
    sums_ref[...] = gathered
    for k, target in zip(thin, (query_grad, key_grad, value_grad)):
        target[...] = k.advance(count - 1).T

    for stage, to in enumerate((seat.pair, seat.side, seat.twin)):
        sum_copy(stage, to).wait_send()
    for away in range(count - 1):
        around_copy(away).wait_send()
    for b in range(batch):
        other_copy(b).wait_send()
    for k in scatters + thin + [from_output, from_down, from_up]:
        k.close()


def attend_backward(first_grad, *operands):
    tokens, query_full, output_part, up_part, down_part = (
        operands[0],
        operands[9],
        operands[12],
        operands[13],
        operands[14],
    )
    count = lax.axis_size("dp")
    batch, part, width = first_grad.shape
    rows = tokens.shape[1]
    local = query_full.shape[1]
    hidden = up_part.shape[1]
    heads = local // HEAD_DIM
    depth = width // (2 * count)
    bf16, f32 = jnp.bfloat16, jnp.float32
    outs = [
        (batch, part, width),
        (depth, local),
        (depth, local),
        (depth, local),
        (local, depth),
        (depth, hidden),
        (hidden, depth),
        (VECTOR_ROWS, width),
    ]
    dma = pltpu.SemaphoreType.DMA
    scratch = [
        ((batch, 2 * rows, 128), f32),
        ((local, 2 * rows), bf16),
        ((heads, 1, rows), f32),
        ((local, rows), f32),
        ((2 * rows, local), f32),
        ((2 * rows, local), f32),
        ((3, 2 * rows, local), bf16),
        ((3, local, width), f32),
        ((3, local, width), bf16),
        ((2 * part, width), f32),
        ((2 * batch, part, width), f32),
        ((2 * batch, 2, part, width), bf16),
        ((2 * batch, 2, part, width), bf16),
        ((2 * batch, part, width), bf16),
        ((2 * batch, part, width), bf16),
        dma((2 * batch, 3)),
        dma((2 * batch, 3)),
        ((batch, part, width), bf16),
        ((batch, part, width), bf16),
        dma((batch,)),
        dma((batch,)),
        ((3, count, local, depth), bf16),
        ((3, count - 1, local, depth), bf16),
        ((3, count - 1, local, depth), bf16),
        ((count, local, depth), bf16),
        ((count - 1, local, depth), bf16),
        ((count - 1, local, depth), bf16),
        ((count, hidden, depth), bf16),
        ((count - 1, hidden, depth), bf16),
        ((count - 1, hidden, depth), bf16),
        ((count - 2, 2 * depth, hidden), bf16),
        ((count - 1, 2 * depth, hidden), bf16),
        ((depth, hidden), bf16),
        ((depth, hidden), bf16),
        ((3 + count, VECTOR_ROWS, width), f32),
        ((4, VECTOR_ROWS, width), f32),
        dma((3 + count,)),
        dma((3 + count,)),
        dma((6, count)),
        dma((6, count)),
        dma((6, count - 1)),
        dma((6, count - 1)),
    ]
    return pl.pallas_call(
        back_kernel,
        name="attend_backward",
        out_shape=[jax.ShapeDtypeStruct(shape, f32) for shape in outs],
        in_specs=[VMEM] * (len(operands) + 1),
        out_specs=[VMEM] * len(outs),
        scratch_shapes=[
            pltpu.VMEM(*item) if isinstance(item, tuple) else item for item in scratch
        ],
        compiler_params=pltpu.CompilerParams(
            collective_id=3, has_side_effects=True, vmem_limit_bytes=63 * 2**20
        ),
    )(*operands[:12], first_grad, *operands[12:])


def fused_plan(
    inputs,
    segment_ids,
    query_weight,
    key_weight,
    value_weight,
    output_weight,
    up_weight,
    down_weight,
    querybias,
    valuebias,
    outputbias,
    upbias,
    downbias,
    norm_gain,
    norm_shift,
    final_gain,
    final_shift,
    cotangent,
):
    (
        tokens,
        other_tokens,
        full_query,
        full_key,
        full_value,
        full_output,
        full_up,
        full_down,
        queries,
        both_keys,
        both_values,
        mixture,
        log_rows,
        attended,
    ) = attend_forward(
        inputs,
        segment_ids,
        (query_weight, key_weight, value_weight, output_weight, up_weight, down_weight),
        querybias,
        valuebias,
    )
    result, first_grad, mixed_grad, output_part, up_part, down_part, vectors = feed_both_ways(
        inputs,
        attended,
        cotangent,
        full_output,
        full_up,
        full_down,
        (outputbias, upbias, downbias, norm_gain, norm_shift, final_gain, final_shift),
    )
    (
        input_grad,
        query_grad,
        key_grad,
        value_grad,
        output_grad,
        up_grad,
        down_grad,
        sums,
    ) = attend_backward(
        first_grad,
        tokens,
        other_tokens,
        segment_ids,
        queries,
        both_keys,
        both_values,
        mixture,
        log_rows,
        mixed_grad,
        full_query,
        full_key,
        full_value,
        output_part,
        up_part,
        down_part,
        vectors,
    )
    return (
        result,
        input_grad,
        query_grad,
        key_grad,
        value_grad,
        output_grad,
        up_grad,
        down_grad,
        sums[ROW_QUERY],
        sums[ROW_VALUE],
        sums[ROW_OUTPUT],
        sums[8:12].reshape(-1),
        sums[ROW_DOWN],
        sums[ROW_GAIN],
        sums[ROW_SHIFT],
        sums[ROW_FINAL_GAIN],
        sums[ROW_FINAL_SHIFT],
    )


def solution(mesh):
    fits = mesh.shape["ctx"] == 2 and mesh.shape["tp"] == 4 and mesh.shape["dp"] > 2
    placed = (
        P("dp", ("ctx", "tp"), None),
        P("dp", None),
        P(("dp", "ctx"), "tp"),
        P(("dp", "ctx"), "tp"),
        P(("dp", "ctx"), "tp"),
        P("tp", ("dp", "ctx")),
        P(("dp", "ctx"), "tp"),
        P("tp", ("dp", "ctx")),
        P(),
        P(),
        P(),
        P(),
        P(),
        P(),
        P(),
        P(),
        P(),
        P("dp", ("ctx", "tp"), None),
    )
    return jax.shard_map(
        fused_plan if fits else ring_plan,
        mesh=mesh,
        in_specs=placed,
        out_specs=(
            P("dp", ("ctx", "tp"), None),
            P("dp", ("ctx", "tp"), None),
            P(("dp", "ctx"), "tp"),
            P(("dp", "ctx"), "tp"),
            P(("dp", "ctx"), "tp"),
            P("tp", ("dp", "ctx")),
            P(("dp", "ctx"), "tp"),
            P("tp", ("dp", "ctx")),
            P(),
            P(),
            P(),
            P(),
            P(),
            P(),
            P(),
            P(),
            P(),
        ),
        check_vma=False,
    )
```

```python
import functools

import jax
import jax.numpy as jnp
from jax import lax
from jax.experimental import pallas as pl
from jax.experimental.pallas import tpu as pltpu
from jax.sharding import PartitionSpec as P

HEAD_DIM = 64
REACH = 4


def shifted(block, axis, distance):
    devices = range(lax.axis_size(axis))
    route = [(i - distance, i) for i in devices if i - distance in devices]
    return lax.ppermute(block, axis, route)


def for_sending(shard):

    def short(part):
        return part.astype(jnp.bfloat16) if part.dtype == jnp.float32 else part

    return jax.tree.map(short, shard)


def layer_norm(hidden, gain_vec, shift_vec):
    center = hidden - jnp.mean(hidden, axis=-1, keepdims=True)
    inverse = lax.rsqrt(jnp.mean(center * center, axis=-1, keepdims=True) + 1e-05)
    normed = center * inverse
    return (normed * gain_vec + shift_vec, normed, inverse)


def norm_back(upstream, normed, inverse, gain_vec):
    scaled = upstream * gain_vec
    return inverse * (
        scaled
        - jnp.mean(scaled, axis=-1, keepdims=True)
        - normed * jnp.mean(scaled * normed, axis=-1, keepdims=True)
    )


def gelu_curve(pre_act):
    return 0.5 * pre_act * (1.0 + lax.erf(pre_act * 0.7071067811865476))


def gelu_slope(pre_act):
    return (
        0.5 * (1.0 + lax.erf(pre_act * 0.7071067811865476))
        + pre_act * jnp.exp(-0.5 * pre_act * pre_act) * 0.3989422804014327
    )


def product(left_side, right_side):
    return jnp.einsum("btd,de->bte", left_side, right_side, preferred_element_type=jnp.float32)


def transposed(left_side, right_side):
    return jnp.einsum("btn,mn->btm", left_side, right_side, preferred_element_type=jnp.float32)


def weight_term(left_side, right_side):
    return jnp.einsum("btd,bte->de", left_side, right_side, preferred_element_type=jnp.float32)


def block_scores(query_rows, key_rows, block_mask):
    scores = jnp.einsum("bqhd,bkhd->bhqk", query_rows, key_rows, preferred_element_type=jnp.float32)
    return jnp.where(block_mask, scores, -1e30)


def probabilities(query_rows, key_rows, block_mask, log_total):
    scores = block_scores(query_rows, key_rows, block_mask)
    return jnp.where(block_mask, jnp.exp(scores - log_total[..., None]), 0.0)


def placed(local_part, full_len, place_at):
    empty = jnp.zeros((full_len,), jnp.float32)
    return lax.dynamic_update_slice_in_dim(empty, local_part, place_at * local_part.shape[0], 0)


def ring_plan(
    inputs,
    segment_ids,
    query_weight,
    key_weight,
    value_weight,
    output_weight,
    up_weight,
    down_weight,
    querybias,
    valuebias,
    outputbias,
    upbias,
    downbias,
    norm_gain,
    norm_shift,
    final_gain,
    final_shift,
    cotangent,
):
    tp_count = lax.axis_size("tp")
    tp_place = lax.axis_index("tp")
    ctx_count = lax.axis_size("ctx")
    ctx_place = lax.axis_index("ctx")
    batch_rows, part_rows, model_width = inputs.shape
    shard_rows = part_rows * tp_count
    full_query, full_key, full_value, full_output, full_up, full_down = (
        lax.all_gather(query_weight, ("dp", "ctx"), axis=0, tiled=True),
        lax.all_gather(key_weight, ("dp", "ctx"), axis=0, tiled=True),
        lax.all_gather(value_weight, ("dp", "ctx"), axis=0, tiled=True),
        lax.all_gather(output_weight, ("dp", "ctx"), axis=1, tiled=True),
        lax.all_gather(up_weight, ("dp", "ctx"), axis=0, tiled=True),
        lax.all_gather(down_weight, ("dp", "ctx"), axis=1, tiled=True),
    )
    local_width = full_query.shape[1]
    local_heads = local_width // HEAD_DIM
    hidden_width = full_up.shape[1]
    query_offset = lax.dynamic_slice_in_dim(querybias, tp_place * local_width, local_width)
    value_offset = lax.dynamic_slice_in_dim(valuebias, tp_place * local_width, local_width)
    up_offset = lax.dynamic_slice_in_dim(upbias, tp_place * hidden_width, hidden_width)
    score_scale = HEAD_DIM ** (-0.5)

    def split_heads(tensor):
        return tensor.reshape(batch_rows, shard_rows, local_heads, HEAD_DIM)

    def join_heads(tensor):
        return tensor.reshape(batch_rows, shard_rows, local_width)

    tokens = lax.all_gather(inputs, "tp", axis=1, tiled=True)
    queries = split_heads(
        ((product(tokens, full_query) + query_offset) * score_scale).astype(jnp.bfloat16)
    )
    key_rows = split_heads(product(tokens, full_key).astype(jnp.bfloat16))
    value_rows = split_heads((product(tokens, full_value) + value_offset).astype(jnp.bfloat16))
    own_ids = lax.dynamic_slice_in_dim(segment_ids, ctx_place * shard_rows, shard_rows, 1)
    offsets = [0] + [
        offset for offset in range(-REACH, REACH + 1) if offset != 0 and abs(offset) < ctx_count
    ]
    mask_of = {}
    block_of = {}
    for offset in offsets:
        source = ctx_place + offset
        begin_at = jnp.clip(source, 0, ctx_count - 1) * shard_rows
        other_ids = lax.dynamic_slice_in_dim(segment_ids, begin_at, shard_rows, 1)
        inside = jnp.logical_and(source >= 0, source < ctx_count)
        mask_of[offset] = jnp.logical_and(own_ids[:, :, None] == other_ids[:, None, :], inside)[
            :, None
        ]
        if offset == 0:
            block_of[offset] = (key_rows, value_rows)
        else:
            block_of[offset] = shifted((key_rows, value_rows), "ctx", -offset)
    running = jnp.full((batch_rows, local_heads, shard_rows), -1e30, jnp.float32)
    totals = jnp.zeros((batch_rows, local_heads, shard_rows), jnp.float32)
    for offset in offsets:
        scores = block_scores(queries, block_of[offset][0], mask_of[offset])
        highest = jnp.maximum(running, jnp.max(scores, axis=-1))
        weights = jnp.where(mask_of[offset], jnp.exp(scores - highest[..., None]), 0.0)
        totals = totals * jnp.exp(running - highest) + jnp.sum(weights, axis=-1)
        running = highest
    log_total = running + jnp.log(totals)
    mixture = jnp.zeros((batch_rows, shard_rows, local_heads, HEAD_DIM), jnp.float32)
    for offset in offsets:
        attn_probs = probabilities(queries, block_of[offset][0], mask_of[offset], log_total)
        mixture = mixture + jnp.einsum(
            "bhqk,bkhd->bqhd",
            attn_probs.astype(jnp.bfloat16),
            block_of[offset][1],
            preferred_element_type=jnp.float32,
        )
    attended = join_heads(mixture).astype(jnp.bfloat16)
    output_part = lax.psum_scatter(
        product(attended, full_output), "tp", scatter_dimension=1, tiled=True
    )
    first_sum = inputs.astype(jnp.float32) + output_part + outputbias
    normed_first, first_normed, first_inverse = layer_norm(first_sum, norm_gain, norm_shift)
    normed_rows = lax.all_gather(normed_first.astype(jnp.bfloat16), "tp", axis=1, tiled=True)
    hidden_pre = product(normed_rows, full_up) + up_offset
    hidden_low = gelu_curve(hidden_pre).astype(jnp.bfloat16)
    down_part = lax.psum_scatter(
        product(hidden_low, full_down), "tp", scatter_dimension=1, tiled=True
    )
    second_sum = normed_first + down_part + downbias
    result, second_normed, second_inverse = layer_norm(second_sum, final_gain, final_shift)
    upstream = cotangent.astype(jnp.float32)
    finalgain_grad = jnp.sum(upstream * second_normed, axis=(0, 1))
    finalshift_grad = jnp.sum(upstream, axis=(0, 1))
    second_grad = norm_back(upstream, second_normed, second_inverse, final_gain)
    down_low = second_grad.astype(jnp.bfloat16)
    downbias_grad = jnp.sum(down_low, axis=(0, 1), dtype=jnp.float32)
    down_rows = lax.all_gather(down_low, "tp", axis=1, tiled=True)
    down_grad = weight_term(hidden_low, down_rows)
    hidden_grad = (transposed(down_rows, full_down) * gelu_slope(hidden_pre)).astype(jnp.bfloat16)
    upbias_part = jnp.sum(hidden_grad, axis=(0, 1), dtype=jnp.float32)
    up_grad = weight_term(normed_rows, hidden_grad)
    normed_grad = (
        lax.psum_scatter(transposed(hidden_grad, full_up), "tp", scatter_dimension=1, tiled=True)
        + second_grad
    )
    normgain_grad = jnp.sum(normed_grad * first_normed, axis=(0, 1))
    normshift_grad = jnp.sum(normed_grad, axis=(0, 1))
    first_grad = norm_back(normed_grad, first_normed, first_inverse, norm_gain)
    output_low = first_grad.astype(jnp.bfloat16)
    outputbias_grad = jnp.sum(output_low, axis=(0, 1), dtype=jnp.float32)
    output_rows = lax.all_gather(output_low, "tp", axis=1, tiled=True)
    output_grad = weight_term(attended, output_rows)
    mixed_grad = split_heads(transposed(output_rows, full_output).astype(jnp.bfloat16))
    row_dot = jnp.zeros((batch_rows, local_heads, shard_rows), jnp.float32)
    for offset in offsets:
        attn_probs = probabilities(queries, block_of[offset][0], mask_of[offset], log_total)
        prob_grad = jnp.einsum(
            "bqhd,bkhd->bhqk", mixed_grad, block_of[offset][1], preferred_element_type=jnp.float32
        )
        row_dot = row_dot + jnp.sum(attn_probs * prob_grad, axis=-1)
    query_acc = jnp.zeros((batch_rows, shard_rows, local_heads, HEAD_DIM), jnp.float32)
    key_parts = {}
    for offset in offsets:
        attn_probs = probabilities(queries, block_of[offset][0], mask_of[offset], log_total)
        prob_grad = jnp.einsum(
            "bqhd,bkhd->bhqk", mixed_grad, block_of[offset][1], preferred_element_type=jnp.float32
        )
        score_grad = (attn_probs * (prob_grad - row_dot[..., None])).astype(jnp.bfloat16)
        query_acc = query_acc + jnp.einsum(
            "bhqk,bkhd->bqhd", score_grad, block_of[offset][0], preferred_element_type=jnp.float32
        )
        key_term = jnp.einsum(
            "bhqk,bqhd->bkhd", score_grad, queries, preferred_element_type=jnp.float32
        )
        value_term = jnp.einsum(
            "bhqk,bqhd->bkhd",
            attn_probs.astype(jnp.bfloat16),
            mixed_grad,
            preferred_element_type=jnp.float32,
        )
        key_parts[offset] = (key_term, value_term)
    own_key, own_value = key_parts[0]
    for offset in offsets[1:]:
        back_key, back_value = shifted(for_sending(key_parts[offset]), "ctx", offset)
        own_key = own_key + back_key
        own_value = own_value + back_value
    query_pre = (
        join_heads(query_acc.astype(jnp.bfloat16)).astype(jnp.float32) * score_scale
    ).astype(jnp.bfloat16)
    key_low = join_heads(own_key.astype(jnp.bfloat16))
    value_low = join_heads(own_value.astype(jnp.bfloat16))
    querybias_part = jnp.sum(query_pre, axis=(0, 1), dtype=jnp.float32)
    valuebias_part = jnp.sum(value_low, axis=(0, 1), dtype=jnp.float32)
    query_grad = weight_term(tokens, query_pre)
    key_grad = weight_term(tokens, key_low)
    value_grad = weight_term(tokens, value_low)
    input_part = (
        transposed(query_pre, full_query)
        + transposed(key_low, full_key)
        + transposed(value_low, full_value)
    )
    input_grad = (
        lax.psum_scatter(
            input_part.astype(jnp.bfloat16), "tp", scatter_dimension=1, tiled=True
        ).astype(jnp.float32)
        + first_grad
    )
    query_grad, key_grad, value_grad, output_grad, up_grad, down_grad = (
        lax.psum_scatter(query_grad, ("dp", "ctx"), scatter_dimension=0, tiled=True),
        lax.psum_scatter(key_grad, ("dp", "ctx"), scatter_dimension=0, tiled=True),
        lax.psum_scatter(value_grad, ("dp", "ctx"), scatter_dimension=0, tiled=True),
        lax.psum_scatter(output_grad, ("dp", "ctx"), scatter_dimension=1, tiled=True),
        lax.psum_scatter(up_grad, ("dp", "ctx"), scatter_dimension=0, tiled=True),
        lax.psum_scatter(down_grad, ("dp", "ctx"), scatter_dimension=1, tiled=True),
    )
    summed = lax.psum(
        (
            placed(querybias_part, model_width, tp_place),
            placed(valuebias_part, model_width, tp_place),
            outputbias_grad,
            placed(upbias_part, hidden_width * tp_count, tp_place),
            downbias_grad,
            normgain_grad,
            normshift_grad,
            finalgain_grad,
            finalshift_grad,
        ),
        ("dp", "ctx", "tp"),
    )
    return (
        result.astype(jnp.bfloat16),
        input_grad,
        query_grad,
        key_grad,
        value_grad,
        output_grad,
        up_grad,
        down_grad,
        summed[0],
        summed[1],
        summed[2],
        summed[3],
        summed[4],
        summed[5],
        summed[6],
        summed[7],
        summed[8],
    )


MESH = pl.DeviceIdType.MESH
LOWEST = -1e30
VMEM = pl.BlockSpec(memory_space=pltpu.VMEM)
LEFT = pl.BlockSpec(memory_space=pl.ANY)


class Seat:
    def __init__(self):
        self.dp_count = lax.axis_size("dp")
        self.dp = lax.axis_index("dp")
        self.ctx = lax.axis_index("ctx")
        self.tp = lax.axis_index("tp")
        self.tp_pair = self.tp + 1 - 2 * (self.tp % 2)
        self.tp_side = (self.tp + 2) % 4
        self.tp_far = (self.tp_pair + 2) % 4
        self.pair = (self.dp, self.ctx, self.tp_pair)
        self.side = (self.dp, self.ctx, self.tp_side)
        self.twin = (self.dp, 1 - self.ctx, self.tp)
        self.above = ((self.dp + 1) % self.dp_count, self.ctx, self.tp)
        self.below = ((self.dp + self.dp_count - 1) % self.dp_count, self.ctx, self.tp)

    def meet(self, names):
        barrier = pltpu.get_barrier_semaphore()
        for name in names:
            pl.semaphore_signal(
                barrier, inc=1, device_id=getattr(self, name), device_id_type=MESH
            )
        pl.semaphore_wait(barrier, len(names))


def remote(source, target, send_sem, recv_sem, to):
    return pltpu.make_async_remote_copy(
        src_ref=source,
        dst_ref=target,
        send_sem=send_sem,
        recv_sem=recv_sem,
        device_id=to,
        device_id_type=MESH,
    )


class RingGather:
    def __init__(self, seat, shard, block, sems, at):
        self.seat, self.shard, self.block, self.at = seat, shard, block, at
        self.own_sem, self.z_send, self.z_recv, self.y_send, self.y_recv = sems
        self.count = seat.dp_count

    def index(self, step, ctx):
        origin = (self.seat.dp + self.count - step) % self.count
        return origin * 2 + ctx

    def held(self, step):
        return self.block(self.index(step, self.seat.ctx))

    def own(self):
        return pltpu.make_async_copy(self.shard, self.held(0), self.own_sem.at[self.at])

    def z(self, step):
        source = self.shard if step == 0 else self.held(step)
        return remote(
            source,
            self.held(step),
            self.z_send.at[self.at, step],
            self.z_recv.at[self.at, step],
            self.seat.above,
        )

    def z_in(self, step):
        view = self.held(step + 1)
        return remote(
            view,
            view,
            self.z_send.at[self.at, step],
            self.z_recv.at[self.at, step],
            self.seat.above,
        )

    def y(self, step):
        source = self.shard if step == 0 else self.held(step)
        return remote(
            source,
            self.held(step),
            self.y_send.at[self.at, step],
            self.y_recv.at[self.at, step],
            self.seat.twin,
        )

    def y_in(self, step):
        view = self.block(self.index(step, 1 - self.seat.ctx))
        return remote(
            view,
            view,
            self.y_send.at[self.at, step],
            self.y_recv.at[self.at, step],
            self.seat.twin,
        )

    def begin(self):
        self.own().start()
        self.z(0).start()
        self.y(0).start()

    def pass_on(self, step):
        self.z_in(step).wait_recv()
        if step + 1 < self.count - 1:
            self.z(step + 1).start()
        self.y(step + 1).start()

    def land(self):
        self.own().wait()
        for step in range(self.count):
            self.y_in(step).wait_recv()

    def close(self):
        for step in range(self.count - 1):
            self.z(step).wait_send()
        for step in range(self.count):
            self.y(step).wait_send()


def dot(left_side, right_side):
    return jnp.dot(left_side, right_side, preferred_element_type=jnp.float32)


def dot_nt(left_side, right_side):
    return lax.dot_general(
        left_side, right_side, (((1,), (1,)), ((), ())), preferred_element_type=jnp.float32
    )


def dot_tn(left_side, right_side):
    return lax.dot_general(
        left_side, right_side, (((0,), (0,)), ((), ())), preferred_element_type=jnp.float32
    )


def aligned(start, size):
    return pl.ds(pl.multiple_of(start, size), size)


VECTOR_ROWS = 16
ROW_QUERY, ROW_VALUE, ROW_OUTPUT, ROW_DOWN = 0, 1, 2, 3
ROW_GAIN, ROW_SHIFT, ROW_FINAL_GAIN, ROW_FINAL_SHIFT, ROW_UP = 4, 5, 6, 7, 8


class TokenScatter:
    def __init__(self, seat, buffers, sems, at, slot):
        self.seat, self.at, self.slot = seat, at, slot
        self.pair_out, self.pair_in, self.side_out, self.side_in = buffers
        self.send, self.recv = sems

    def copy(self, k):
        at, seat, slot = self.at, self.seat, self.slot
        if k < 2:
            source, target, to = self.pair_out.at[slot, k], self.pair_in.at[slot, k], seat.pair
        else:
            source, target, to = self.side_out.at[slot], self.side_in.at[slot], seat.side
        return remote(source, target, self.send.at[at, k], self.recv.at[at, k], to)

    def give(self, compute, total):
        seat, at = self.seat, self.slot
        part = self.side_out.shape[1]
        group = seat.tp // 2
        mine = aligned((seat.tp % 2) * part, part)
        others = aligned((1 - seat.tp % 2) * part, part)
        compute(1 - group)
        self.pair_out[at, 0] = total[others, :].astype(jnp.bfloat16)
        self.copy(0).start()
        self.side_out[at] = total[mine, :].astype(jnp.bfloat16)
        compute(group)
        self.pair_out[at, 1] = total[others, :].astype(jnp.bfloat16)
        self.copy(1).start()
        self.copy(0).wait_recv()
        self.side_out[at] = (
            self.side_out[at].astype(jnp.float32) + self.pair_in[at, 0].astype(jnp.float32)
        ).astype(jnp.bfloat16)
        self.copy(2).start()
        return mine

    def take(self):
        self.copy(1).wait_recv()
        self.copy(2).wait_recv()
        return self.pair_in[self.slot, 1].astype(jnp.float32) + self.side_in[self.slot].astype(
            jnp.float32
        )

    def close(self):
        for k in range(3):
            self.copy(k).wait_send()


class TokenGather:
    def __init__(self, seat, full, b, part, sems, at):
        self.seat = seat
        self.send, self.recv = sems
        self.at = at
        self.view = lambda place: full.at[b, aligned(place * part, part), :]

    def copy(self, k, place, to):
        view = self.view(place)
        return remote(view, view, self.send.at[self.at, k], self.recv.at[self.at, k], to)

    def give(self):
        seat = self.seat
        self.copy(0, seat.tp, seat.side).start()
        self.copy(1, seat.tp, seat.pair).start()

    def relay(self):
        seat = self.seat
        self.copy(0, seat.tp_side, seat.side).wait_recv()
        self.copy(2, seat.tp_side, seat.pair).start()

    def land(self):
        seat = self.seat
        self.copy(1, seat.tp_pair, seat.pair).wait_recv()
        self.copy(2, seat.tp_far, seat.pair).wait_recv()

    def close(self):
        seat = self.seat
        for k, place in ((0, seat.tp), (1, seat.tp), (2, seat.tp_side)):
            self.copy(k, place, seat.pair).wait_send()


def row_mean(rows):
    return jnp.mean(rows, axis=-1, keepdims=True)


class PairedReduce:
    def __init__(self, seat, partial, block, twin_in, ring_out, ring_in, sems, at):
        self.seat, self.partial, self.block, self.at = seat, partial, block, at
        self.twin_in, self.ring_out, self.ring_in = twin_in, ring_out, ring_in
        self.y_send, self.y_recv, self.z_send, self.z_recv = sems
        self.count = seat.dp_count

    def mine(self, step, ctx):
        owner = (self.seat.dp + 2 * self.count - 1 - step) % self.count
        return self.block(self.partial, owner * 2 + ctx)

    def y(self, step):
        return remote(
            self.mine(step, 1 - self.seat.ctx),
            self.twin_in.at[step],
            self.y_send.at[self.at, step],
            self.y_recv.at[self.at, step],
            self.seat.twin,
        )

    def z(self, step):
        return remote(
            self.ring_out(step),
            self.ring_in.at[step],
            self.z_send.at[self.at, step],
            self.z_recv.at[self.at, step],
            self.seat.above,
        )

    def begin(self):
        for step in range(self.count):
            self.y(step).start()

    def advance(self, step):
        self.y(step).wait_recv()
        total = self.mine(step, self.seat.ctx)[...].astype(jnp.float32) + self.twin_in[
            step
        ].astype(jnp.float32)
        if step > 0:
            self.z(step - 1).wait_recv()
            total = total + self.ring_in[step - 1].astype(jnp.float32)
        if step == self.count - 1:
            return total
        self.ring_out(step)[...] = total.astype(jnp.bfloat16)
        self.z(step).start()

    def close(self):
        for step in range(self.count):
            self.y(step).wait_send()
        for step in range(self.count - 1):
            self.z(step).wait_send()


class RingReduce:
    def __init__(self, seat, partial, pair, ring_out, ring_in, half_out, half_in, sems, at):
        self.seat, self.partial, self.pair, self.at = seat, partial, pair, at
        self.ring_out, self.ring_in, self.half_out, self.half_in = ring_out, ring_in, half_out, half_in
        self.y_send, self.y_recv, self.z_send, self.z_recv = sems
        self.count = seat.dp_count

    def mine(self, step):
        owner = (self.seat.dp + 2 * self.count - 1 - step) % self.count
        return self.pair(self.partial, owner)

    def z(self, step):
        return remote(
            self.mine(0) if step == 0 else self.ring_out(step - 1),
            self.ring_in.at[step],
            self.z_send.at[self.at, step],
            self.z_recv.at[self.at, step],
            self.seat.above,
        )

    def y(self):
        return remote(
            self.half_out,
            self.half_in,
            self.y_send.at[self.at, 0],
            self.y_recv.at[self.at, 0],
            self.seat.twin,
        )

    def begin(self):
        self.z(0).start()

    def advance(self, step):
        self.z(step - 1).wait_recv()
        total = self.mine(step)[...].astype(jnp.float32) + self.ring_in[step - 1].astype(
            jnp.float32
        )
        if step == self.count - 1:
            return total
        self.ring_out(step - 1)[...] = total.astype(jnp.bfloat16)
        self.z(step).start()

    def close(self):
        self.y().wait_send()
        for step in range(self.count - 1):
            self.z(step).wait_send()


class Parts:
    def __init__(self, names, refs):
        self.__dict__.update(zip(names, refs))


def layer_kernel(names, *refs):
    r = Parts(names, refs)
    seat = Seat()
    count = seat.dp_count
    hops = count - 1
    batch, part, width = r.result.shape
    rows = r.tokens.shape[1]
    local = r.query_full.shape[1]
    hidden = r.up_full.shape[1]
    heads = local // HEAD_DIM
    depth = width // (2 * count)
    wide = 256
    f32, bf16 = jnp.float32, jnp.bfloat16

    barrier = pltpu.get_barrier_semaphore()
    around = [((seat.dp + away) % count, seat.ctx, seat.tp) for away in range(1, count)]
    for to in [seat.pair, seat.side, seat.twin] + around:
        pl.semaphore_signal(barrier, inc=1, device_id=to, device_id_type=MESH)
    pl.semaphore_wait(barrier, 2 + count)

    def over(tiles, body):
        def one(index, carry):
            body(index)
            return carry

        lax.fori_loop(0, tiles, one, 0)

    def over_heads(body, services):
        def one(h):
            for when, service in services:
                pl.when(h == when)(service)
            body(h)

        over(heads, one)

    def cut(half, place):
        return half.at[:, aligned(place * part, part), :]

    def token_copy(relation, source, target, to):
        return remote(source, target, r.token_send.at[relation], r.token_recv.at[relation], to)

    here, there = cut(r.tokens, seat.tp), cut(r.other, seat.tp)
    here_side, there_side = cut(r.tokens, seat.tp_side), cut(r.other, seat.tp_side)
    sends = [
        lambda: token_copy(0, r.inputs, here, seat.pair),
        lambda: token_copy(1, r.inputs, here, seat.side),
        lambda: token_copy(2, r.inputs, there, seat.twin),
        lambda: token_copy(3, there, there, seat.side),
        lambda: token_copy(4, here_side, here_side, seat.pair),
        lambda: token_copy(5, there, there, seat.pair),
        lambda: token_copy(6, there_side, there_side, seat.pair),
    ]
    landed = [
        cut(r.tokens, seat.tp_pair),
        here_side,
        there,
        there_side,
        cut(r.tokens, seat.tp_far),
        cut(r.other, seat.tp_pair),
        cut(r.other, seat.tp_far),
    ]

    def token_in(relation):
        token_copy(relation, landed[relation], landed[relation], seat.pair).wait_recv()

    own_tokens = pltpu.make_async_copy(r.inputs, here, r.local_sem.at[0])
    own_tokens.start()
    upstream = lambda b: r.weight_low.at[0, b * part : (b + 1) * part, :]
    own_cotangent = [
        pltpu.make_async_copy(r.cotangent.at[b], upstream(b), r.local_sem.at[1 + b])
        for b in range(batch)
    ]
    for copy in own_cotangent:
        copy.start()
    for relation in (1, 2, 0):
        sends[relation]().start()

    def by_rows(full):
        return lambda at: full.at[aligned(at * depth, depth), :]

    def by_columns(full):
        return lambda at: full.at[:, aligned(at * depth, depth)]

    gather_sems = (r.own_sem, r.gz_send, r.gz_recv, r.gy_send, r.gy_recv)
    weights = [
        RingGather(seat, shard, view(full), gather_sems, at)
        for at, (shard, full, view) in enumerate(
            (
                (r.query_weight, r.query_full, by_rows),
                (r.key_weight, r.key_full, by_rows),
                (r.value_weight, r.value_full, by_rows),
                (r.output_weight, r.output_full, by_columns),
                (r.up_weight, r.up_full, by_rows),
                (r.down_weight, r.down_full, by_columns),
            )
        )
    ]
    to_output, to_up, to_down = weights[3:]
    for weight in weights[:3]:
        weight.begin()
    for step in range(hops):
        for weight in weights[:3]:
            weight.pass_on(step)
    to_output.begin()
    to_up.begin()
    token_in(1)
    sends[4]().start()
    token_in(2)
    sends[3]().start()
    sends[5]().start()

    for b in range(batch):
        for half in range(2):
            row_ids = r.ids[b : b + 1, aligned((seat.ctx if half == 0 else 1 - seat.ctx) * rows, rows)]
            spread = jnp.broadcast_to(row_ids.astype(f32), (128, rows))
            r.ids_down[b, half * rows : (half + 1) * rows, :] = spread.T
    bias_at = aligned(seat.tp * local, local)
    query_offset = r.query_bias[:, bias_at]
    value_offset = r.value_bias[:, bias_at]
    tile_rows = rows // 2
    for weight in weights[:3]:
        weight.land()
    own_tokens.wait()
    token_in(0)
    token_in(4)

    def project(half_ref, half):
        def one(index):
            b, piece = index // 2, index % 2
            block = half_ref[b, aligned(piece * tile_rows, tile_rows), :]
            spot = aligned(half * rows + piece * tile_rows, tile_rows)
            if half == 0:
                scaled = (dot(block, r.query_full[...]) + query_offset) * HEAD_DIM ** (-0.5)
                r.queries[b, aligned(piece * tile_rows, tile_rows), :] = scaled.astype(bf16)
            r.keys[b, spot, :] = dot(block, r.key_full[...]).astype(bf16)
            value_rows = dot(block, r.value_full[...]) + value_offset
            r.values[b, spot, :] = value_rows.astype(bf16)
            r.flipped[b, :, spot] = value_rows.T.astype(bf16)

        over(batch * 2, one)

    project(r.tokens, 0)
    token_in(3)
    sends[6]().start()
    token_in(5)
    token_in(6)
    project(r.other, 1)

    lane_head = lax.broadcasted_iota(jnp.int32, (1, local), 1) // HEAD_DIM
    nothing = jnp.zeros((), bf16)

    def own_ids(b):
        return r.ids[b : b + 1, aligned(seat.ctx * rows, rows)].astype(f32)

    def attend(b, services):
        row_ids = own_ids(b)

        def one(h):
            own = aligned(h * HEAD_DIM, HEAD_DIM)
            chosen = jnp.where(lane_head == h, r.queries[b], nothing)
            same = jnp.tile(r.ids_down[b], (1, rows // 128)) == row_ids
            scores = jnp.where(same, dot_nt(r.keys[b], chosen), LOWEST)
            highest = jnp.max(scores, axis=0, keepdims=True)
            raised = jnp.exp(scores - highest)
            total = jnp.sum(raised, axis=0, keepdims=True)
            shares = (raised * (1.0 / total)).astype(bf16)
            r.mixture[b, own, :] = dot(r.flipped[b, own, :], shares)
            r.logs[b * heads + h] = highest + jnp.log(total)

        over_heads(one, services)
        r.attended[b] = r.mixture[b].T.astype(bf16)

    def passing(step, *which):
        def service():
            for weight in which:
                weight.pass_on(step)

        return service

    attend(0, [(1, passing(0, to_output, to_up)), (3, passing(1, to_output, to_up))])
    attend(1, [(1, passing(2, to_output, to_up)), (2, to_down.begin)])
    to_output.land()

    scatter_parts = (r.pair_out, r.pair_in, r.side_out, r.side_in)
    scatters = [
        TokenScatter(seat, scatter_parts, (r.scatter_send, r.scatter_recv), at, slot)
        for at, slot in list(enumerate(range(3 * batch)))
        + [(3 * batch + at, at) for at in range(2 * batch)]
    ]
    gathers = [
        TokenGather(seat, full, b, part, (r.gather_send, r.gather_recv), k * batch + b)
        for k, full in enumerate((r.normed_rows, r.down_rows, r.output_rows))
        for b in range(batch)
    ]

    def spread_rows(lhs_ref, b, weight, flipped):
        def compute(group):
            lhs = lhs_ref[b, aligned(group * 2 * part, 2 * part), :]

            def tile(index):
                at = aligned(index * wide, wide)
                if flipped:
                    r.total[:, at] = dot_nt(lhs, weight[at, :])
                else:
                    r.total[:, at] = dot(lhs, weight[:, at])

            over(width // wide, tile)

        return compute

    def scatter(k, b, lhs_ref, weight, flipped):
        mine = scatters[k * batch + b].give(spread_rows(lhs_ref, b, weight, flipped), r.total)
        r.total_own[b] = r.total[mine, :]

    def collected(k, b):
        return r.total_own[b] + scatters[k * batch + b].take()

    own_rows = aligned(seat.tp * part, part)
    r.sums[...] = jnp.zeros_like(r.sums)
    up_sum = r.sums.at[pl.ds(ROW_UP + seat.tp, 1), :]

    def add_vector(row, values):
        r.sums[row : row + 1, :] += jnp.sum(values, axis=0, keepdims=True)

    def first_norm(b):
        first_sum = r.tokens[b, own_rows, :].astype(f32) + (collected(0, b) + r.output_bias[...])
        center = first_sum - row_mean(first_sum)
        inverse = lax.rsqrt(row_mean(center * center) + 1e-05)
        normed = center * inverse
        scaled = normed * r.norm_gain[...] + r.norm_shift[...]
        r.keep[0, b] = normed
        r.keep[1, b] = scaled
        r.inverse_keep[b] = inverse
        r.normed_rows[b, own_rows, :] = scaled.astype(bf16)
        gathers[b].give()

    def raise_up(b):
        gathers[b].land()
        lhs = r.normed_rows[b]

        def tile(index):
            at = aligned(index * wide, wide)
            offset = r.up_bias[:, pl.ds(pl.multiple_of(seat.tp * hidden + index * wide, wide), wide)]
            pre = dot(lhs, r.up_full[:, at]) + offset
            half = 0.5 * (1.0 + lax.erf(pre * 0.7071067811865476))
            r.hidden_rows[b, :, at] = (pre * half).astype(bf16)
            slope = half + pre * jnp.exp(-0.5 * pre * pre) * 0.3989422804014327
            r.slope_rows[b, :, at] = slope.astype(bf16)

        over(hidden // wide, tile)

    def second_norm(b):
        second_sum = r.keep[1, b] + (collected(1, b) + r.down_bias[...])
        center = second_sum - row_mean(second_sum)
        inverse = lax.rsqrt(row_mean(center * center) + 1e-05)
        normed = center * inverse
        r.result[b] = (normed * r.final_gain[...] + r.final_shift[...]).astype(bf16)
        gradient = upstream(b)[...].astype(f32)
        add_vector(ROW_FINAL_GAIN, gradient * normed)
        add_vector(ROW_FINAL_SHIFT, gradient)
        scaled = gradient * r.final_gain[...]
        second = inverse * (scaled - row_mean(scaled) - normed * row_mean(scaled * normed))
        r.keep[2, b] = second
        low = second.astype(bf16)
        r.down_rows[b, own_rows, :] = low
        gathers[batch + b].give()
        add_vector(ROW_DOWN, low.astype(f32))

    def lower(b):
        gathers[batch + b].land()
        lhs = r.down_rows[b]

        def tile(index):
            at = aligned(index * wide, wide)
            back = dot_nt(lhs, r.down_full[at, :]) * r.slope_rows[b, :, at].astype(f32)
            back = back.astype(bf16)
            r.back_rows[b, :, at] = back
            up_sum[:, at] += jnp.sum(back.astype(f32), axis=0, keepdims=True)

        over(hidden // wide, tile)

    def first_back(b):
        grad = collected(2, b) + r.keep[2, b]
        normed = r.keep[0, b]
        add_vector(ROW_GAIN, grad * normed)
        add_vector(ROW_SHIFT, grad)
        scaled = grad * r.norm_gain[...]
        first = r.inverse_keep[b] * (
            scaled - row_mean(scaled) - normed * row_mean(scaled * normed)
        )
        r.input_grad[b] = first
        low = first.astype(bf16)
        r.output_rows[b, own_rows, :] = low
        gathers[2 * batch + b].give()
        add_vector(ROW_OUTPUT, low.astype(f32))

    def mix_back(b):
        gathers[2 * batch + b].land()
        r.mixed[b] = dot_nt(r.output_rows[b], r.output_full[...]).astype(bf16)

    def weight_tiles(left_ref, right_ref, store, first, last):
        left = left_ref[...].reshape(batch * rows, left_ref.shape[2])

        def tile(index):
            at = aligned((first + index) * wide, wide)
            right = right_ref[:, :, at].reshape(batch * rows, wide)
            store(at, dot_tn(left, right).astype(bf16))

        over(last - first, tile)

    def store_down(at, value):
        r.slope_rows[:, :, at] = value.reshape(batch, rows, wide)

    def store_up(at, value):
        r.hidden_rows[:, :, at] = value.reshape(batch, rows, wide)

    def store_output(at, value):
        r.output_part[:, at] = value

    reduce_sems = (r.ry_send, r.ry_recv, r.rz_send, r.rz_recv)
    columns = lambda ref, at: ref.at[:, aligned(at * depth, depth)]
    thin = [
        PairedReduce(
            seat, r.weight_low.at[k], columns,
            r.thin_twin.at[k], (lambda step, k=k: r.thin_out.at[k, step]), r.thin_in.at[k], reduce_sems, k,
        )
        for k in range(3)
    ]
    from_output = PairedReduce(
        seat, r.output_part, columns, r.output_twin, (lambda step: r.output_out.at[step]), r.output_in, reduce_sems, 3
    )
    from_down = PairedReduce(
        seat, r.slope_rows, lambda ref, at: ref.at[:, :, aligned(at * depth, depth)],
        r.down_twin, (lambda step: r.back_rows.at[:, :, aligned(step * depth, depth)]), r.down_in, reduce_sems, 4,
    )
    pairs_held = rows // (2 * depth)

    def up_pair(ref, owner):
        return ref.at[owner // pairs_held, aligned((owner % pairs_held) * 2 * depth, 2 * depth), :]

    from_up = RingReduce(
        seat, r.hidden_rows, up_pair, (lambda step: r.down_rows.at[step, : 2 * depth, :]), r.up_in, r.up_half_out, r.up_half_in, reduce_sems, 5
    )

    scatter(0, 0, r.attended, r.output_full, False)
    scatter(0, 1, r.attended, r.output_full, False)
    first_norm(0)
    to_down.pass_on(0)
    first_norm(1)
    to_down.pass_on(1)
    gathers[0].relay()
    to_up.land()
    raise_up(0)
    gathers[1].relay()
    to_down.pass_on(2)
    to_down.land()
    scatter(1, 0, r.hidden_rows, r.down_full, False)
    raise_up(1)
    scatter(1, 1, r.hidden_rows, r.down_full, False)
    for copy in own_cotangent:
        copy.wait()
    second_norm(0)
    second_norm(1)
    gathers[batch].relay()
    lower(0)
    gathers[batch + 1].relay()
    scatter(2, 0, r.back_rows, r.up_full, True)
    lower(1)
    scatter(2, 1, r.back_rows, r.up_full, True)
    weight_tiles(r.hidden_rows, r.down_rows, store_down, 0, 2)
    first_back(0)
    weight_tiles(r.hidden_rows, r.down_rows, store_down, 2, 4)
    from_down.begin()
    first_back(1)
    weight_tiles(r.normed_rows, r.back_rows, store_up, 0, 2)
    gathers[2 * batch].relay()
    mix_back(0)
    gathers[2 * batch + 1].relay()
    weight_tiles(r.normed_rows, r.back_rows, store_up, 2, 4)
    from_up.begin()
    mix_back(1)
    weight_tiles(r.attended, r.output_rows, store_output, 0, 4)
    from_output.begin()
    for k in scatters[: 3 * batch] + gathers:
        k.close()

    key_flip = r.flipped.at[0]

    def heads_back(b, services):
        key_flip[...] = r.keys[b].astype(f32).T.astype(bf16)
        product_rows = r.mixed[b].astype(f32).T * r.mixture[b]
        for h in range(heads):
            r.row_dots[h] = jnp.sum(
                product_rows[h * HEAD_DIM : (h + 1) * HEAD_DIM], axis=0, keepdims=True
            )
        r.key_sum[...] = jnp.zeros_like(r.key_sum)
        r.value_sum[...] = jnp.zeros_like(r.value_sum)
        row_ids = own_ids(b)

        def one(h):
            own = aligned(h * HEAD_DIM, HEAD_DIM)
            query_rows = jnp.where(lane_head == h, r.queries[b], nothing)
            grad_rows = jnp.where(lane_head == h, r.mixed[b], nothing)
            same = jnp.tile(r.ids_down[b], (1, rows // 128)) == row_ids
            scores = jnp.where(same, dot_nt(r.keys[b], query_rows), LOWEST)
            probs = jnp.exp(scores - r.logs[b * heads + h])
            r.value_sum[...] += dot(probs.astype(bf16), grad_rows)
            prob_grad = dot_nt(r.values[b], grad_rows)
            score_grad = (probs * (prob_grad - r.row_dots[h])).astype(bf16)
            r.key_sum[...] += dot(score_grad, query_rows)
            r.query_flip[own, :] = dot(key_flip[own, :], score_grad)

        over_heads(one, services)

    lows = lambda k: slice(k * local, (k + 1) * local)

    def sequence_back(b):
        flipped = (r.query_flip[...].astype(bf16).astype(f32) * HEAD_DIM ** (-0.5)).astype(bf16)
        upright = flipped.astype(f32).T
        key_low = r.key_sum[...].astype(bf16)
        value_low = r.value_sum[...].astype(bf16)
        r.normed_rows[0, :, lows(0)] = upright.astype(bf16)
        for half in range(2):
            r.normed_rows[half, :, lows(1)] = key_low[half * rows : (half + 1) * rows]
            r.normed_rows[half, :, lows(2)] = value_low[half * rows : (half + 1) * rows]
        r.sums[ROW_QUERY : ROW_QUERY + 1, bias_at] += jnp.sum(upright, axis=0, keepdims=True)
        r.sums[ROW_VALUE : ROW_VALUE + 1, bias_at] += jnp.sum(
            value_low.astype(f32), axis=0, keepdims=True
        )
        flips = [flipped, key_low.astype(f32).T.astype(bf16), value_low.astype(f32).T.astype(bf16)]

        for k in range(3):
            def tile(index, k=k):
                at = aligned(index * wide, wide)
                term = dot(flips[k][:, :rows], r.tokens[b, :, at])
                if k > 0:
                    term = term + dot(flips[k][:, rows:], r.other[b, :, at])
                if b > 0:
                    term = term + r.keep[k, :, :, at].reshape(local, wide)
                if b == batch - 1:
                    r.weight_low[k, :, at] = term.astype(bf16)
                else:
                    r.keep[k, :, :, at] = term.reshape(2, local // 2, wide)

            over(width // wide, tile)

    def input_back(b, half):
        def compute(group):
            at = aligned(group * 2 * part, 2 * part)

            def tile(index):
                row_at = aligned(index * wide, wide)
                term = dot_nt(r.normed_rows[half, at, lows(1)], r.key_full[row_at, :]) + dot_nt(
                    r.normed_rows[half, at, lows(2)], r.value_full[row_at, :]
                )
                if half == 0:
                    term = term + dot_nt(
                        r.normed_rows[half, at, lows(0)], r.query_full[row_at, :]
                    )
                r.total[:, row_at] = term

            over(width // wide, tile)

        mine = scatters[3 * batch + 2 * b + half].give(compute, r.total)
        r.total_own[2 * b + half] = r.total[mine, :]

    def other_copy(b):
        return remote(
            r.side_out.at[2 * batch + b],
            r.side_in.at[2 * batch + b],
            r.other_send.at[b],
            r.other_recv.at[b],
            seat.twin,
        )

    def other_give(b):
        r.side_out[2 * batch + b] = (
            r.total_own[2 * b + 1] + scatters[3 * batch + 2 * b + 1].take()
        ).astype(bf16)
        other_copy(b).start()

    def input_take(b):
        own = r.total_own[2 * b] + scatters[3 * batch + 2 * b].take()
        other_copy(b).wait_recv()
        r.input_grad[b] = (own + r.side_in[2 * batch + b].astype(f32)) + r.input_grad[b]

    def stepping(step, *which):
        def service():
            for piece in which:
                piece.advance(step)

        return service

    def down_done():
        r.down_grad[...] = from_down.advance(hops).reshape(hidden, depth)

    heads_back(0, [(0, stepping(0, from_down)), (2, stepping(1, from_down)), (3, stepping(0, from_output))])
    sequence_back(0)
    stepping(2, from_down)()
    stepping(1, from_up, from_output)()
    input_back(0, 1)
    input_back(0, 0)
    heads_back(1, [(0, down_done), (1, lambda: other_give(0)), (3, stepping(2, from_up, from_output))])
    sequence_back(1)
    for k in thin:
        k.begin()
    input_back(1, 1)
    input_back(1, 0)

    def sum_copy(stage, to):
        return remote(
            r.sum_all.at[stage], r.sum_in.at[stage], r.sum_send.at[stage], r.sum_recv.at[stage], to
        )

    def sum_stage(stage, to):
        r.sum_all[stage] = r.sums[...]
        sum_copy(stage, to).start()

    def sum_add(stage, to):
        sum_copy(stage, to).wait_recv()
        r.sums[...] = r.sums[...] + r.sum_in[stage]

    def around_copy(away):
        stage = 4 + away
        return remote(
            r.sum_all.at[3], r.sum_in.at[stage], r.sum_send.at[stage], r.sum_recv.at[stage], around[away]
        )

    sum_stage(0, seat.pair)
    for k in thin:
        k.advance(0)
    sum_add(0, seat.pair)
    sum_stage(1, seat.side)
    input_take(0)
    other_give(1)
    for k in thin:
        k.advance(1)
    sum_add(1, seat.side)
    sum_stage(2, seat.twin)
    r.total[...] = from_up.advance(hops)
    r.up_half_out[...] = r.total[aligned((1 - seat.ctx) * depth, depth), :].astype(bf16)
    from_up.y().start()
    r.output_grad[...] = from_output.advance(hops)
    sum_add(2, seat.twin)
    r.sum_all[3] = r.sums[...]
    for away in range(hops):
        around_copy(away).start()
    for k in thin:
        k.advance(2)
    from_up.y().wait_recv()
    r.up_grad[...] = r.total[aligned(seat.ctx * depth, depth), :] + r.up_half_in[...].astype(f32)
    input_take(1)
    r.sum_in[3] = r.sums[...]
    for away in range(hops):
        around_copy(away).wait_recv()
    gathered = jnp.zeros_like(r.sums[...])
    for origin in range(count):
        gathered = gathered + r.sum_in[3 + (seat.dp + count - origin) % count]
    r.sums[...] = gathered
    for k, target in zip(thin, (r.query_grad, r.key_grad, r.value_grad)):
        target[...] = k.advance(hops).T

    for stage, to in enumerate((seat.pair, seat.side, seat.twin)):
        sum_copy(stage, to).wait_send()
    for away in range(hops):
        around_copy(away).wait_send()
    for b in range(batch):
        other_copy(b).wait_send()
    for copy in sends:
        copy().wait_send()
    for piece in weights + scatters[3 * batch :] + thin + [from_output, from_down, from_up]:
        piece.close()


def layer_call(inputs, segment_ids, cotangent, shards, vectors):
    count = lax.axis_size("dp")
    batch, part, width = inputs.shape
    rows = part * lax.axis_size("tp")
    local = shards[0].shape[1]
    hidden = shards[4].shape[1]
    heads = local // HEAD_DIM
    depth = width // (2 * count)
    bf16, f32 = jnp.bfloat16, jnp.float32
    ins = [
        ("inputs", LEFT),
        ("cotangent", LEFT),
        ("query_weight", LEFT),
        ("key_weight", LEFT),
        ("value_weight", LEFT),
        ("output_weight", LEFT),
        ("up_weight", LEFT),
        ("down_weight", LEFT),
        ("ids", VMEM),
        ("query_bias", VMEM),
        ("value_bias", VMEM),
        ("output_bias", VMEM),
        ("up_bias", VMEM),
        ("down_bias", VMEM),
        ("norm_gain", VMEM),
        ("norm_shift", VMEM),
        ("final_gain", VMEM),
        ("final_shift", VMEM),
    ]
    outs = [
        ("result", (batch, part, width), bf16),
        ("input_grad", (batch, part, width), f32),
        ("query_grad", (depth, local), f32),
        ("key_grad", (depth, local), f32),
        ("value_grad", (depth, local), f32),
        ("output_grad", (local, depth), f32),
        ("up_grad", (depth, hidden), f32),
        ("down_grad", (hidden, depth), f32),
        ("sums", (VECTOR_ROWS, width), f32),
    ]
    scratch = [
        ("tokens", (batch, rows, width), bf16),
        ("other", (batch, rows, width), bf16),
        ("query_full", (width, local), bf16),
        ("key_full", (width, local), bf16),
        ("value_full", (width, local), bf16),
        ("output_full", (local, width), bf16),
        ("up_full", (width, hidden), bf16),
        ("down_full", (hidden, width), bf16),
        ("queries", (batch, rows, local), bf16),
        ("keys", (batch, 2 * rows, local), bf16),
        ("values", (batch, 2 * rows, local), bf16),
        ("flipped", (batch, local, 2 * rows), bf16),
        ("mixture", (batch, local, rows), f32),
        ("logs", (batch * heads, 1, rows), f32),
        ("attended", (batch, rows, local), bf16),
        ("ids_down", (batch, 2 * rows, 128), f32),
        ("normed_rows", (batch, rows, width), bf16),
        ("hidden_rows", (batch, rows, hidden), bf16),
        ("slope_rows", (batch, rows, hidden), bf16),
        ("down_rows", (batch, rows, width), bf16),
        ("back_rows", (batch, rows, hidden), bf16),
        ("output_rows", (batch, rows, width), bf16),
        ("keep", (3, batch, part, width), f32),
        ("inverse_keep", (batch, part, 1), f32),
        ("total_own", (2 * batch, part, width), f32),
        ("total", (2 * part, width), f32),
        ("pair_out", (3 * batch, 2, part, width), bf16),
        ("pair_in", (3 * batch, 2, part, width), bf16),
        ("side_out", (3 * batch, part, width), bf16),
        ("side_in", (3 * batch, part, width), bf16),
        ("mixed", (batch, rows, local), bf16),
        ("output_part", (local, width), bf16),
        ("row_dots", (heads, 1, rows), f32),
        ("query_flip", (local, rows), f32),
        ("key_sum", (2 * rows, local), f32),
        ("value_sum", (2 * rows, local), f32),
        ("weight_low", (3, local, width), bf16),
        ("thin_twin", (3, count, local, depth), bf16),
        ("thin_out", (3, count - 1, local, depth), bf16),
        ("thin_in", (3, count - 1, local, depth), bf16),
        ("output_twin", (count, local, depth), bf16),
        ("output_out", (count - 1, local, depth), bf16),
        ("output_in", (count - 1, local, depth), bf16),
        ("down_twin", (count, batch, rows, depth), bf16),
        ("down_in", (count - 1, batch, rows, depth), bf16),
        ("up_in", (count - 1, 2 * depth, hidden), bf16),
        ("up_half_out", (depth, hidden), bf16),
        ("up_half_in", (depth, hidden), bf16),
        ("sum_in", (3 + count, VECTOR_ROWS, width), f32),
        ("sum_all", (4, VECTOR_ROWS, width), f32),
    ]
    sems = [
        ("local_sem", (1 + batch,)),
        ("token_send", (7,)),
        ("token_recv", (7,)),
        ("own_sem", (6,)),
        ("gz_send", (6, count - 1)),
        ("gz_recv", (6, count - 1)),
        ("gy_send", (6, count)),
        ("gy_recv", (6, count)),
        ("scatter_send", (5 * batch, 3)),
        ("scatter_recv", (5 * batch, 3)),
        ("gather_send", (3 * batch, 3)),
        ("gather_recv", (3 * batch, 3)),
        ("other_send", (batch,)),
        ("other_recv", (batch,)),
        ("sum_send", (3 + count,)),
        ("sum_recv", (3 + count,)),
        ("ry_send", (6, count)),
        ("ry_recv", (6, count)),
        ("rz_send", (6, count - 1)),
        ("rz_recv", (6, count - 1)),
    ]
    names = [item[0] for group in (ins, outs, scratch, sems) for item in group]
    return pl.pallas_call(
        functools.partial(layer_kernel, names),
        name="layer",
        out_shape=[jax.ShapeDtypeStruct(shape, kind) for _, shape, kind in outs],
        in_specs=[space for _, space in ins],
        out_specs=[VMEM] * len(outs),
        scratch_shapes=[pltpu.VMEM(shape, kind) for _, shape, kind in scratch]
        + [pltpu.SemaphoreType.DMA(shape) for _, shape in sems],
        compiler_params=pltpu.CompilerParams(
            collective_id=1, has_side_effects=True, vmem_limit_bytes=67043328
        ),
    )(
        inputs,
        cotangent,
        *shards,
        segment_ids,
        *[vector.reshape(1, -1) for vector in vectors],
    )


def fused_plan(
    inputs,
    segment_ids,
    query_weight,
    key_weight,
    value_weight,
    output_weight,
    up_weight,
    down_weight,
    querybias,
    valuebias,
    outputbias,
    upbias,
    downbias,
    norm_gain,
    norm_shift,
    final_gain,
    final_shift,
    cotangent,
):
    *grads, sums = layer_call(
        inputs,
        segment_ids,
        cotangent,
        (query_weight, key_weight, value_weight, output_weight, up_weight, down_weight),
        (
            querybias,
            valuebias,
            outputbias,
            upbias,
            downbias,
            norm_gain,
            norm_shift,
            final_gain,
            final_shift,
        ),
    )
    return (
        *grads,
        sums[ROW_QUERY],
        sums[ROW_VALUE],
        sums[ROW_OUTPUT],
        sums[ROW_UP : ROW_UP + 4].reshape(-1),
        sums[ROW_DOWN],
        sums[ROW_GAIN],
        sums[ROW_SHIFT],
        sums[ROW_FINAL_GAIN],
        sums[ROW_FINAL_SHIFT],
    )


def solution(mesh):
    fits = mesh.shape["ctx"] == 2 and mesh.shape["tp"] == 4 and mesh.shape["dp"] > 2
    placed = (
        P("dp", ("ctx", "tp"), None),
        P("dp", None),
        P(("dp", "ctx"), "tp"),
        P(("dp", "ctx"), "tp"),
        P(("dp", "ctx"), "tp"),
        P("tp", ("dp", "ctx")),
        P(("dp", "ctx"), "tp"),
        P("tp", ("dp", "ctx")),
        P(),
        P(),
        P(),
        P(),
        P(),
        P(),
        P(),
        P(),
        P(),
        P("dp", ("ctx", "tp"), None),
    )
    return jax.shard_map(
        fused_plan if fits else ring_plan,
        mesh=mesh,
        in_specs=placed,
        out_specs=(
            P("dp", ("ctx", "tp"), None),
            P("dp", ("ctx", "tp"), None),
            P(("dp", "ctx"), "tp"),
            P(("dp", "ctx"), "tp"),
            P(("dp", "ctx"), "tp"),
            P("tp", ("dp", "ctx")),
            P(("dp", "ctx"), "tp"),
            P("tp", ("dp", "ctx")),
            P(),
            P(),
            P(),
            P(),
            P(),
            P(),
            P(),
            P(),
            P(),
        ),
        check_vma=False,
    )
```

```python
import functools

import jax
import jax.numpy as jnp
from jax import lax
from jax.experimental import pallas as pl
from jax.experimental.pallas import tpu as pltpu
from jax.sharding import PartitionSpec as P

HEAD_DIM = 64
REACH = 4


def shifted(block, axis, distance):
    devices = range(lax.axis_size(axis))
    route = [(i - distance, i) for i in devices if i - distance in devices]
    return lax.ppermute(block, axis, route)


def for_sending(shard):

    def short(part):
        return part.astype(jnp.bfloat16) if part.dtype == jnp.float32 else part

    return jax.tree.map(short, shard)


def layer_norm(hidden, gain_vec, shift_vec):
    center = hidden - jnp.mean(hidden, axis=-1, keepdims=True)
    inverse = lax.rsqrt(jnp.mean(center * center, axis=-1, keepdims=True) + 1e-05)
    normed = center * inverse
    return (normed * gain_vec + shift_vec, normed, inverse)


def norm_back(upstream, normed, inverse, gain_vec):
    scaled = upstream * gain_vec
    return inverse * (
        scaled
        - jnp.mean(scaled, axis=-1, keepdims=True)
        - normed * jnp.mean(scaled * normed, axis=-1, keepdims=True)
    )


def gelu_curve(pre_act):
    return 0.5 * pre_act * (1.0 + lax.erf(pre_act * 0.7071067811865476))


def gelu_slope(pre_act):
    return (
        0.5 * (1.0 + lax.erf(pre_act * 0.7071067811865476))
        + pre_act * jnp.exp(-0.5 * pre_act * pre_act) * 0.3989422804014327
    )


def product(left_side, right_side):
    return jnp.einsum("btd,de->bte", left_side, right_side, preferred_element_type=jnp.float32)


def transposed(left_side, right_side):
    return jnp.einsum("btn,mn->btm", left_side, right_side, preferred_element_type=jnp.float32)


def weight_term(left_side, right_side):
    return jnp.einsum("btd,bte->de", left_side, right_side, preferred_element_type=jnp.float32)


def block_scores(query_rows, key_rows, block_mask):
    scores = jnp.einsum("bqhd,bkhd->bhqk", query_rows, key_rows, preferred_element_type=jnp.float32)
    return jnp.where(block_mask, scores, -1e30)


def probabilities(query_rows, key_rows, block_mask, log_total):
    scores = block_scores(query_rows, key_rows, block_mask)
    return jnp.where(block_mask, jnp.exp(scores - log_total[..., None]), 0.0)


def placed(local_part, full_len, place_at):
    empty = jnp.zeros((full_len,), jnp.float32)
    return lax.dynamic_update_slice_in_dim(empty, local_part, place_at * local_part.shape[0], 0)


def ring_plan(
    inputs,
    segment_ids,
    query_weight,
    key_weight,
    value_weight,
    output_weight,
    up_weight,
    down_weight,
    querybias,
    valuebias,
    outputbias,
    upbias,
    downbias,
    norm_gain,
    norm_shift,
    final_gain,
    final_shift,
    cotangent,
):
    tp_count = lax.axis_size("tp")
    tp_place = lax.axis_index("tp")
    ctx_count = lax.axis_size("ctx")
    ctx_place = lax.axis_index("ctx")
    batch_rows, part_rows, model_width = inputs.shape
    shard_rows = part_rows * tp_count
    full_query, full_key, full_value, full_output, full_up, full_down = (
        lax.all_gather(query_weight, ("dp", "ctx"), axis=0, tiled=True),
        lax.all_gather(key_weight, ("dp", "ctx"), axis=0, tiled=True),
        lax.all_gather(value_weight, ("dp", "ctx"), axis=0, tiled=True),
        lax.all_gather(output_weight, ("dp", "ctx"), axis=1, tiled=True),
        lax.all_gather(up_weight, ("dp", "ctx"), axis=0, tiled=True),
        lax.all_gather(down_weight, ("dp", "ctx"), axis=1, tiled=True),
    )
    local_width = full_query.shape[1]
    local_heads = local_width // HEAD_DIM
    hidden_width = full_up.shape[1]
    query_offset = lax.dynamic_slice_in_dim(querybias, tp_place * local_width, local_width)
    value_offset = lax.dynamic_slice_in_dim(valuebias, tp_place * local_width, local_width)
    up_offset = lax.dynamic_slice_in_dim(upbias, tp_place * hidden_width, hidden_width)
    score_scale = HEAD_DIM ** (-0.5)

    def split_heads(tensor):
        return tensor.reshape(batch_rows, shard_rows, local_heads, HEAD_DIM)

    def join_heads(tensor):
        return tensor.reshape(batch_rows, shard_rows, local_width)

    tokens = lax.all_gather(inputs, "tp", axis=1, tiled=True)
    queries = split_heads(
        ((product(tokens, full_query) + query_offset) * score_scale).astype(jnp.bfloat16)
    )
    key_rows = split_heads(product(tokens, full_key).astype(jnp.bfloat16))
    value_rows = split_heads((product(tokens, full_value) + value_offset).astype(jnp.bfloat16))
    own_ids = lax.dynamic_slice_in_dim(segment_ids, ctx_place * shard_rows, shard_rows, 1)
    offsets = [0] + [
        offset for offset in range(-REACH, REACH + 1) if offset != 0 and abs(offset) < ctx_count
    ]
    mask_of = {}
    block_of = {}
    for offset in offsets:
        source = ctx_place + offset
        begin_at = jnp.clip(source, 0, ctx_count - 1) * shard_rows
        other_ids = lax.dynamic_slice_in_dim(segment_ids, begin_at, shard_rows, 1)
        inside = jnp.logical_and(source >= 0, source < ctx_count)
        mask_of[offset] = jnp.logical_and(own_ids[:, :, None] == other_ids[:, None, :], inside)[
            :, None
        ]
        if offset == 0:
            block_of[offset] = (key_rows, value_rows)
        else:
            block_of[offset] = shifted((key_rows, value_rows), "ctx", -offset)
    running = jnp.full((batch_rows, local_heads, shard_rows), -1e30, jnp.float32)
    totals = jnp.zeros((batch_rows, local_heads, shard_rows), jnp.float32)
    for offset in offsets:
        scores = block_scores(queries, block_of[offset][0], mask_of[offset])
        highest = jnp.maximum(running, jnp.max(scores, axis=-1))
        weights = jnp.where(mask_of[offset], jnp.exp(scores - highest[..., None]), 0.0)
        totals = totals * jnp.exp(running - highest) + jnp.sum(weights, axis=-1)
        running = highest
    log_total = running + jnp.log(totals)
    mixture = jnp.zeros((batch_rows, shard_rows, local_heads, HEAD_DIM), jnp.float32)
    for offset in offsets:
        attn_probs = probabilities(queries, block_of[offset][0], mask_of[offset], log_total)
        mixture = mixture + jnp.einsum(
            "bhqk,bkhd->bqhd",
            attn_probs.astype(jnp.bfloat16),
            block_of[offset][1],
            preferred_element_type=jnp.float32,
        )
    attended = join_heads(mixture).astype(jnp.bfloat16)
    output_part = lax.psum_scatter(
        product(attended, full_output), "tp", scatter_dimension=1, tiled=True
    )
    first_sum = inputs.astype(jnp.float32) + output_part + outputbias
    normed_first, first_normed, first_inverse = layer_norm(first_sum, norm_gain, norm_shift)
    normed_rows = lax.all_gather(normed_first.astype(jnp.bfloat16), "tp", axis=1, tiled=True)
    hidden_pre = product(normed_rows, full_up) + up_offset
    hidden_low = gelu_curve(hidden_pre).astype(jnp.bfloat16)
    down_part = lax.psum_scatter(
        product(hidden_low, full_down), "tp", scatter_dimension=1, tiled=True
    )
    second_sum = normed_first + down_part + downbias
    result, second_normed, second_inverse = layer_norm(second_sum, final_gain, final_shift)
    upstream = cotangent.astype(jnp.float32)
    finalgain_grad = jnp.sum(upstream * second_normed, axis=(0, 1))
    finalshift_grad = jnp.sum(upstream, axis=(0, 1))
    second_grad = norm_back(upstream, second_normed, second_inverse, final_gain)
    down_low = second_grad.astype(jnp.bfloat16)
    downbias_grad = jnp.sum(down_low, axis=(0, 1), dtype=jnp.float32)
    down_rows = lax.all_gather(down_low, "tp", axis=1, tiled=True)
    down_grad = weight_term(hidden_low, down_rows)
    hidden_grad = (transposed(down_rows, full_down) * gelu_slope(hidden_pre)).astype(jnp.bfloat16)
    upbias_part = jnp.sum(hidden_grad, axis=(0, 1), dtype=jnp.float32)
    up_grad = weight_term(normed_rows, hidden_grad)
    normed_grad = (
        lax.psum_scatter(transposed(hidden_grad, full_up), "tp", scatter_dimension=1, tiled=True)
        + second_grad
    )
    normgain_grad = jnp.sum(normed_grad * first_normed, axis=(0, 1))
    normshift_grad = jnp.sum(normed_grad, axis=(0, 1))
    first_grad = norm_back(normed_grad, first_normed, first_inverse, norm_gain)
    output_low = first_grad.astype(jnp.bfloat16)
    outputbias_grad = jnp.sum(output_low, axis=(0, 1), dtype=jnp.float32)
    output_rows = lax.all_gather(output_low, "tp", axis=1, tiled=True)
    output_grad = weight_term(attended, output_rows)
    mixed_grad = split_heads(transposed(output_rows, full_output).astype(jnp.bfloat16))
    row_dot = jnp.zeros((batch_rows, local_heads, shard_rows), jnp.float32)
    for offset in offsets:
        attn_probs = probabilities(queries, block_of[offset][0], mask_of[offset], log_total)
        prob_grad = jnp.einsum(
            "bqhd,bkhd->bhqk", mixed_grad, block_of[offset][1], preferred_element_type=jnp.float32
        )
        row_dot = row_dot + jnp.sum(attn_probs * prob_grad, axis=-1)
    query_acc = jnp.zeros((batch_rows, shard_rows, local_heads, HEAD_DIM), jnp.float32)
    key_parts = {}
    for offset in offsets:
        attn_probs = probabilities(queries, block_of[offset][0], mask_of[offset], log_total)
        prob_grad = jnp.einsum(
            "bqhd,bkhd->bhqk", mixed_grad, block_of[offset][1], preferred_element_type=jnp.float32
        )
        score_grad = (attn_probs * (prob_grad - row_dot[..., None])).astype(jnp.bfloat16)
        query_acc = query_acc + jnp.einsum(
            "bhqk,bkhd->bqhd", score_grad, block_of[offset][0], preferred_element_type=jnp.float32
        )
        key_term = jnp.einsum(
            "bhqk,bqhd->bkhd", score_grad, queries, preferred_element_type=jnp.float32
        )
        value_term = jnp.einsum(
            "bhqk,bqhd->bkhd",
            attn_probs.astype(jnp.bfloat16),
            mixed_grad,
            preferred_element_type=jnp.float32,
        )
        key_parts[offset] = (key_term, value_term)
    own_key, own_value = key_parts[0]
    for offset in offsets[1:]:
        back_key, back_value = shifted(for_sending(key_parts[offset]), "ctx", offset)
        own_key = own_key + back_key
        own_value = own_value + back_value
    query_pre = (
        join_heads(query_acc.astype(jnp.bfloat16)).astype(jnp.float32) * score_scale
    ).astype(jnp.bfloat16)
    key_low = join_heads(own_key.astype(jnp.bfloat16))
    value_low = join_heads(own_value.astype(jnp.bfloat16))
    querybias_part = jnp.sum(query_pre, axis=(0, 1), dtype=jnp.float32)
    valuebias_part = jnp.sum(value_low, axis=(0, 1), dtype=jnp.float32)
    query_grad = weight_term(tokens, query_pre)
    key_grad = weight_term(tokens, key_low)
    value_grad = weight_term(tokens, value_low)
    input_part = (
        transposed(query_pre, full_query)
        + transposed(key_low, full_key)
        + transposed(value_low, full_value)
    )
    input_grad = (
        lax.psum_scatter(
            input_part.astype(jnp.bfloat16), "tp", scatter_dimension=1, tiled=True
        ).astype(jnp.float32)
        + first_grad
    )
    query_grad, key_grad, value_grad, output_grad, up_grad, down_grad = (
        lax.psum_scatter(query_grad, ("dp", "ctx"), scatter_dimension=0, tiled=True),
        lax.psum_scatter(key_grad, ("dp", "ctx"), scatter_dimension=0, tiled=True),
        lax.psum_scatter(value_grad, ("dp", "ctx"), scatter_dimension=0, tiled=True),
        lax.psum_scatter(output_grad, ("dp", "ctx"), scatter_dimension=1, tiled=True),
        lax.psum_scatter(up_grad, ("dp", "ctx"), scatter_dimension=0, tiled=True),
        lax.psum_scatter(down_grad, ("dp", "ctx"), scatter_dimension=1, tiled=True),
    )
    summed = lax.psum(
        (
            placed(querybias_part, model_width, tp_place),
            placed(valuebias_part, model_width, tp_place),
            outputbias_grad,
            placed(upbias_part, hidden_width * tp_count, tp_place),
            downbias_grad,
            normgain_grad,
            normshift_grad,
            finalgain_grad,
            finalshift_grad,
        ),
        ("dp", "ctx", "tp"),
    )
    return (
        result.astype(jnp.bfloat16),
        input_grad,
        query_grad,
        key_grad,
        value_grad,
        output_grad,
        up_grad,
        down_grad,
        summed[0],
        summed[1],
        summed[2],
        summed[3],
        summed[4],
        summed[5],
        summed[6],
        summed[7],
        summed[8],
    )


MESH = pl.DeviceIdType.MESH
LOWEST = -1e30
VMEM = pl.BlockSpec(memory_space=pltpu.VMEM)
LEFT = pl.BlockSpec(memory_space=pl.ANY)


class Seat:
    def __init__(self):
        self.dp_count = lax.axis_size("dp")
        self.dp = lax.axis_index("dp")
        self.ctx = lax.axis_index("ctx")
        self.tp = lax.axis_index("tp")
        self.tp_pair = self.tp + 1 - 2 * (self.tp % 2)
        self.tp_side = (self.tp + 2) % 4
        self.tp_far = (self.tp_pair + 2) % 4
        self.pair = (self.dp, self.ctx, self.tp_pair)
        self.side = (self.dp, self.ctx, self.tp_side)
        self.twin = (self.dp, 1 - self.ctx, self.tp)
        self.above = ((self.dp + 1) % self.dp_count, self.ctx, self.tp)
        self.below = ((self.dp + self.dp_count - 1) % self.dp_count, self.ctx, self.tp)

    def meet(self, names):
        barrier = pltpu.get_barrier_semaphore()
        for name in names:
            pl.semaphore_signal(
                barrier, inc=1, device_id=getattr(self, name), device_id_type=MESH
            )
        pl.semaphore_wait(barrier, len(names))


def remote(source, target, send_sem, recv_sem, to):
    return pltpu.make_async_remote_copy(
        src_ref=source,
        dst_ref=target,
        send_sem=send_sem,
        recv_sem=recv_sem,
        device_id=to,
        device_id_type=MESH,
    )


class RingGather:
    def __init__(self, seat, shard, block, sems, at, twice=False):
        self.seat, self.shard, self.block, self.at = seat, shard, block, at
        self.own_sem, self.z_send, self.z_recv, self.y_send, self.y_recv = sems
        self.count = seat.dp_count
        self.twice = twice

    def held(self, step, other=0):
        origin = (self.seat.dp + self.count - step) % self.count
        place = self.seat.ctx if other == 0 else 1 - self.seat.ctx
        return self.block(origin * 2 + place)

    def own(self):
        return pltpu.make_async_copy(self.shard, self.held(0), self.own_sem.at[self.at])

    def z(self, step, other=0):
        source = self.shard if step == 0 and other == 0 else self.held(step, other)
        return remote(
            source,
            self.held(step, other),
            self.z_send.at[self.at, 2 * step + other],
            self.z_recv.at[self.at, 2 * step + other],
            self.seat.above,
        )

    def z_in(self, step, other=0):
        view = self.held(step + 1, other)
        return remote(
            view,
            view,
            self.z_send.at[self.at, 2 * step + other],
            self.z_recv.at[self.at, 2 * step + other],
            self.seat.above,
        )

    def y(self, step):
        source = self.shard if step == 0 else self.held(step)
        return remote(
            source,
            self.held(step),
            self.y_send.at[self.at, step],
            self.y_recv.at[self.at, step],
            self.seat.twin,
        )

    def y_in(self, step):
        view = self.held(step, 1)
        return remote(
            view,
            view,
            self.y_send.at[self.at, step],
            self.y_recv.at[self.at, step],
            self.seat.twin,
        )

    def begin(self):
        self.own().start()
        self.y(0).start()
        self.z(0).start()

    def join(self):
        self.y_in(0).wait_recv()
        self.z(0, 1).start()

    def pass_on(self, step):
        for other in range(2 if self.twice else 1):
            self.z_in(step, other).wait_recv()
            if step + 1 < self.count - 1:
                self.z(step + 1, other).start()
        if not self.twice:
            self.y(step + 1).start()

    def land(self):
        self.own().wait()
        if not self.twice:
            for step in range(self.count):
                self.y_in(step).wait_recv()

    def close(self):
        for step in range(self.count - 1):
            for other in range(2 if self.twice else 1):
                self.z(step, other).wait_send()
        for step in range(1 if self.twice else self.count):
            self.y(step).wait_send()


def dot(left_side, right_side):
    return jnp.dot(left_side, right_side, preferred_element_type=jnp.float32)


def dot_nt(left_side, right_side):
    return lax.dot_general(
        left_side, right_side, (((1,), (1,)), ((), ())), preferred_element_type=jnp.float32
    )


def dot_tn(left_side, right_side):
    return lax.dot_general(
        left_side, right_side, (((0,), (0,)), ((), ())), preferred_element_type=jnp.float32
    )


def aligned(start, size):
    return pl.ds(pl.multiple_of(start, size), size)


VECTOR_ROWS = 16
ROW_QUERY, ROW_VALUE, ROW_OUTPUT, ROW_DOWN = 0, 1, 2, 3
ROW_GAIN, ROW_SHIFT, ROW_FINAL_GAIN, ROW_FINAL_SHIFT, ROW_UP = 4, 5, 6, 7, 8


class TokenScatter:
    def __init__(self, seat, buffers, sems, at, slot):
        self.seat, self.at, self.slot = seat, at, slot
        self.pair_out, self.pair_in, self.side_out, self.side_in = buffers
        self.send, self.recv = sems

    def copy(self, k):
        at, seat, slot = self.at, self.seat, self.slot
        if k < 2:
            source, target, to = self.pair_out.at[slot, k], self.pair_in.at[slot, k], seat.pair
        else:
            source, target, to = self.side_out.at[slot], self.side_in.at[slot], seat.side
        return remote(source, target, self.send.at[at, k], self.recv.at[at, k], to)

    def give(self, compute, total):
        seat, at = self.seat, self.slot
        part = self.side_out.shape[1]
        group = seat.tp // 2
        mine = aligned((seat.tp % 2) * part, part)
        others = aligned((1 - seat.tp % 2) * part, part)
        compute(1 - group)
        self.pair_out[at, 0] = total[others, :].astype(jnp.bfloat16)
        self.copy(0).start()
        self.side_out[at] = total[mine, :].astype(jnp.bfloat16)
        compute(group)
        self.pair_out[at, 1] = total[others, :].astype(jnp.bfloat16)
        self.copy(1).start()
        self.copy(0).wait_recv()
        self.side_out[at] = (
            self.side_out[at].astype(jnp.float32) + self.pair_in[at, 0].astype(jnp.float32)
        ).astype(jnp.bfloat16)
        self.copy(2).start()
        return mine

    def take(self):
        self.copy(1).wait_recv()
        self.copy(2).wait_recv()
        return self.pair_in[self.slot, 1].astype(jnp.float32) + self.side_in[self.slot].astype(
            jnp.float32
        )

    def close(self):
        for k in range(3):
            self.copy(k).wait_send()


class TokenGather:
    def __init__(self, seat, full, b, part, sems, at):
        self.seat = seat
        self.send, self.recv = sems
        self.at = at
        self.view = lambda place: full.at[b, aligned(place * part, part), :]

    def copy(self, k, place, to):
        view = self.view(place)
        return remote(view, view, self.send.at[self.at, k], self.recv.at[self.at, k], to)

    def give(self):
        seat = self.seat
        self.copy(0, seat.tp, seat.side).start()
        self.copy(1, seat.tp, seat.pair).start()

    def relay(self):
        seat = self.seat
        self.copy(0, seat.tp_side, seat.side).wait_recv()
        self.copy(2, seat.tp_side, seat.pair).start()

    def land(self):
        seat = self.seat
        self.copy(1, seat.tp_pair, seat.pair).wait_recv()
        self.copy(2, seat.tp_far, seat.pair).wait_recv()

    def close(self):
        seat = self.seat
        for k, place in ((0, seat.tp), (1, seat.tp), (2, seat.tp_side)):
            self.copy(k, place, seat.pair).wait_send()


def row_mean(rows):
    return jnp.mean(rows, axis=-1, keepdims=True)


class PairedReduce:
    def __init__(self, seat, partial, block, twin_in, ring_out, ring_in, sems, at):
        self.seat, self.partial, self.block, self.at = seat, partial, block, at
        self.twin_in, self.ring_out, self.ring_in = twin_in, ring_out, ring_in
        self.y_send, self.y_recv, self.z_send, self.z_recv = sems
        self.count = seat.dp_count

    def mine(self, step, ctx):
        owner = (self.seat.dp + 2 * self.count - 1 - step) % self.count
        return self.block(self.partial, owner * 2 + ctx)

    def y(self, step):
        return remote(
            self.mine(step, 1 - self.seat.ctx),
            self.twin_in.at[step],
            self.y_send.at[self.at, step],
            self.y_recv.at[self.at, step],
            self.seat.twin,
        )

    def z(self, step):
        return remote(
            self.ring_out(step),
            self.ring_in.at[step],
            self.z_send.at[self.at, step],
            self.z_recv.at[self.at, step],
            self.seat.above,
        )

    def begin(self):
        for step in range(self.count):
            self.y(step).start()

    def advance(self, step):
        self.y(step).wait_recv()
        total = self.mine(step, self.seat.ctx)[...].astype(jnp.float32) + self.twin_in[
            step
        ].astype(jnp.float32)
        if step > 0:
            self.z(step - 1).wait_recv()
            total = total + self.ring_in[step - 1].astype(jnp.float32)
        if step == self.count - 1:
            return total
        self.ring_out(step)[...] = total.astype(jnp.bfloat16)
        self.z(step).start()

    def close(self):
        for step in range(self.count):
            self.y(step).wait_send()
        for step in range(self.count - 1):
            self.z(step).wait_send()


class Parts:
    def __init__(self, names, refs):
        self.__dict__.update(zip(names, refs))


def layer_kernel(names, *refs):
    r = Parts(names, refs)
    seat = Seat()
    count = seat.dp_count
    hops = count - 1
    batch, part, width = r.result.shape
    rows = r.tokens.shape[1]
    local = r.query_full.shape[1]
    hidden = r.up_full.shape[1]
    heads = local // HEAD_DIM
    depth = width // (2 * count)
    wide = 256
    f32, bf16 = jnp.float32, jnp.bfloat16

    barrier = pltpu.get_barrier_semaphore()
    around = [((seat.dp + away) % count, seat.ctx, seat.tp) for away in range(1, count)]
    for to in [seat.pair, seat.side, seat.twin] + around:
        pl.semaphore_signal(barrier, inc=1, device_id=to, device_id_type=MESH)
    pl.semaphore_wait(barrier, 2 + count)

    def over(tiles, body):
        def one(index, carry):
            body(index)
            return carry

        lax.fori_loop(0, tiles, one, 0)

    def over_heads(body, services):
        def one(h):
            for when, service in services:
                pl.when(h == when)(service)
            body(h)

        over(heads, one)

    def cut(half, place):
        return half.at[:, aligned(place * part, part), :]

    def token_copy(relation, source, target, to):
        return remote(source, target, r.token_send.at[relation], r.token_recv.at[relation], to)

    here, there = cut(r.tokens, seat.tp), cut(r.other, seat.tp)
    here_side, there_side = cut(r.tokens, seat.tp_side), cut(r.other, seat.tp_side)
    sends = [
        lambda: token_copy(0, r.inputs, here, seat.pair),
        lambda: token_copy(1, r.inputs, here, seat.side),
        lambda: token_copy(2, r.inputs, there, seat.twin),
        lambda: token_copy(3, there, there, seat.side),
        lambda: token_copy(4, here_side, here_side, seat.pair),
        lambda: token_copy(5, there, there, seat.pair),
        lambda: token_copy(6, there_side, there_side, seat.pair),
    ]
    landed = [
        cut(r.tokens, seat.tp_pair),
        here_side,
        there,
        there_side,
        cut(r.tokens, seat.tp_far),
        cut(r.other, seat.tp_pair),
        cut(r.other, seat.tp_far),
    ]

    def token_in(relation):
        token_copy(relation, landed[relation], landed[relation], seat.pair).wait_recv()

    own_tokens = pltpu.make_async_copy(r.inputs, here, r.local_sem.at[0])
    own_tokens.start()
    upstream = lambda b: r.weight_low.at[0, b * part : (b + 1) * part, :]
    own_cotangent = [
        pltpu.make_async_copy(r.cotangent.at[b], upstream(b), r.local_sem.at[1 + b])
        for b in range(batch)
    ]
    for copy in own_cotangent:
        copy.start()
    sends[1]().start()

    def by_rows(full):
        return lambda at: full.at[aligned(at * depth, depth), :]

    def by_columns(full):
        return lambda at: full.at[:, aligned(at * depth, depth)]

    def by_half_rows(half):
        def view(full):
            return lambda at: full.at[aligned(at * depth + half * (depth // 2), depth // 2), :]

        return view

    gather_sems = (r.own_sem, r.gz_send, r.gz_recv, r.gy_send, r.gy_recv)
    weights = [
        RingGather(seat, shard, view(full), gather_sems, at, twice)
        for at, (shard, full, view, twice) in enumerate(
            (
                (r.query_weight, r.query_full, by_rows, False),
                (r.key_weight, r.key_full, by_rows, False),
                (r.value_weight, r.value_full, by_rows, True),
                (r.output_weight, r.output_full, by_columns, False),
                (r.up_weight.at[: depth // 2, :], r.up_full, by_half_rows(0), False),
                (r.up_weight.at[depth // 2 :, :], r.up_full, by_half_rows(1), True),
                (r.down_weight, r.down_full, by_columns, False),
            )
        )
    ]
    to_output, to_up, to_up_too, to_down = weights[3:]
    for weight in weights[:3]:
        weight.begin()
    sends[2]().start()
    sends[0]().start()
    weights[2].join()
    to_output.begin()
    for weight in weights[:3]:
        weight.pass_on(0)
    to_up.begin()
    token_in(1)
    sends[4]().start()
    for weight in weights[:3]:
        weight.pass_on(1)
    to_output.pass_on(0)
    to_up_too.begin()
    token_in(2)
    sends[3]().start()
    sends[5]().start()
    for weight in weights[:3]:
        weight.pass_on(2)
    to_output.pass_on(1)
    to_up.pass_on(0)
    to_up_too.join()

    for b in range(batch):
        for half in range(2):
            row_ids = r.ids[b : b + 1, aligned((seat.ctx if half == 0 else 1 - seat.ctx) * rows, rows)]
            spread = jnp.broadcast_to(row_ids.astype(f32), (128, rows))
            r.ids_down[b, half * rows : (half + 1) * rows, :] = spread.T
    bias_at = aligned(seat.tp * local, local)
    query_offset = r.query_bias[:, bias_at]
    value_offset = r.value_bias[:, bias_at]
    tile_rows = rows // 2
    for weight in weights[:3]:
        weight.land()
    own_tokens.wait()
    token_in(0)
    token_in(4)

    def project(half_ref, half):
        def one(index):
            b, piece = index // 2, index % 2
            block = half_ref[b, aligned(piece * tile_rows, tile_rows), :]
            spot = aligned(half * rows + piece * tile_rows, tile_rows)
            if half == 0:
                scaled = (dot(block, r.query_full[...]) + query_offset) * HEAD_DIM ** (-0.5)
                r.queries[b, aligned(piece * tile_rows, tile_rows), :] = scaled.astype(bf16)
            r.keys[b, spot, :] = dot(block, r.key_full[...]).astype(bf16)
            value_rows = dot(block, r.value_full[...]) + value_offset
            r.values[b, spot, :] = value_rows.astype(bf16)
            r.flipped[b, :, spot] = value_rows.T.astype(bf16)

        over(batch * 2, one)

    project(r.tokens, 0)
    token_in(3)
    sends[6]().start()
    token_in(5)
    to_down.begin()
    to_output.pass_on(2)
    token_in(6)
    project(r.other, 1)
    to_up.pass_on(1)
    to_up_too.pass_on(0)

    lane_head = lax.broadcasted_iota(jnp.int32, (1, local), 1) // HEAD_DIM
    nothing = jnp.zeros((), bf16)

    def own_ids(b):
        return r.ids[b : b + 1, aligned(seat.ctx * rows, rows)].astype(f32)

    def attend(b, services):
        row_ids = own_ids(b)

        def one(h):
            own = aligned(h * HEAD_DIM, HEAD_DIM)
            chosen = jnp.where(lane_head == h, r.queries[b], nothing)
            same = jnp.tile(r.ids_down[b], (1, rows // 128)) == row_ids
            scores = jnp.where(same, dot_nt(r.keys[b], chosen), LOWEST)
            highest = jnp.max(scores, axis=0, keepdims=True)
            raised = jnp.exp(scores - highest)
            total = jnp.sum(raised, axis=0, keepdims=True)
            shares = (raised * (1.0 / total)).astype(bf16)
            r.mixture[b, own, :] = dot(r.flipped[b, own, :], shares)
            r.logs[b * heads + h] = highest + jnp.log(total)

        over_heads(one, services)
        r.attended[b] = r.mixture[b].T.astype(bf16)

    def passing(step, *which):
        def service():
            for weight in which:
                weight.pass_on(step)

        return service

    to_output.land()

    scatter_parts = (r.pair_out, r.pair_in, r.side_out, r.side_in)
    scatters = [
        TokenScatter(seat, scatter_parts, (r.scatter_send, r.scatter_recv), at, slot)
        for at, slot in list(enumerate(range(3 * batch)))
        + [(3 * batch + at, at) for at in range(2 * batch)]
    ]
    gathers = [
        TokenGather(seat, full, b, part, (r.gather_send, r.gather_recv), k * batch + b)
        for k, full in enumerate((r.normed_rows, r.down_rows, r.output_rows))
        for b in range(batch)
    ]

    def spread_rows(lhs_ref, b, weight, flipped):
        def compute(group):
            lhs = lhs_ref[b, aligned(group * 2 * part, 2 * part), :]

            def tile(index):
                at = aligned(index * wide, wide)
                if flipped:
                    r.total[:, at] = dot_nt(lhs, weight[at, :])
                else:
                    r.total[:, at] = dot(lhs, weight[:, at])

            over(width // wide, tile)

        return compute

    def scatter(k, b, lhs_ref, weight, flipped):
        mine = scatters[k * batch + b].give(spread_rows(lhs_ref, b, weight, flipped), r.total)
        r.total_own[b] = r.total[mine, :]

    def collected(k, b):
        return r.total_own[b] + scatters[k * batch + b].take()

    own_rows = aligned(seat.tp * part, part)
    r.sums[...] = jnp.zeros_like(r.sums)
    up_sum = r.sums.at[pl.ds(ROW_UP + seat.tp, 1), :]

    def add_vector(row, values):
        r.sums[row : row + 1, :] += jnp.sum(values, axis=0, keepdims=True)

    def first_norm(b):
        first_sum = r.tokens[b, own_rows, :].astype(f32) + (collected(0, b) + r.output_bias[...])
        center = first_sum - row_mean(first_sum)
        inverse = lax.rsqrt(row_mean(center * center) + 1e-05)
        normed = center * inverse
        scaled = normed * r.norm_gain[...] + r.norm_shift[...]
        r.keep[0, b] = normed
        r.keep[1, b] = scaled
        r.inverse_keep[b] = inverse
        r.normed_rows[b, own_rows, :] = scaled.astype(bf16)
        gathers[b].give()

    def raise_up(b):
        gathers[b].land()
        lhs = r.normed_rows[b]

        def tile(index):
            at = aligned(index * wide, wide)
            offset = r.up_bias[:, pl.ds(pl.multiple_of(seat.tp * hidden + index * wide, wide), wide)]
            pre = dot(lhs, r.up_full[:, at]) + offset
            half = 0.5 * (1.0 + lax.erf(pre * 0.7071067811865476))
            r.hidden_rows[b, :, at] = (pre * half).astype(bf16)
            slope = half + pre * jnp.exp(-0.5 * pre * pre) * 0.3989422804014327
            r.slope_rows[b, :, at] = slope.astype(bf16)

        over(hidden // wide, tile)

    def second_norm(b):
        second_sum = r.keep[1, b] + (collected(1, b) + r.down_bias[...])
        center = second_sum - row_mean(second_sum)
        inverse = lax.rsqrt(row_mean(center * center) + 1e-05)
        normed = center * inverse
        r.result[b] = (normed * r.final_gain[...] + r.final_shift[...]).astype(bf16)
        gradient = upstream(b)[...].astype(f32)
        add_vector(ROW_FINAL_GAIN, gradient * normed)
        add_vector(ROW_FINAL_SHIFT, gradient)
        scaled = gradient * r.final_gain[...]
        second = inverse * (scaled - row_mean(scaled) - normed * row_mean(scaled * normed))
        r.keep[2, b] = second
        low = second.astype(bf16)
        r.down_rows[b, own_rows, :] = low
        gathers[batch + b].give()
        add_vector(ROW_DOWN, low.astype(f32))

    def lower(b):
        gathers[batch + b].land()
        lhs = r.down_rows[b]

        def tile(index):
            at = aligned(index * wide, wide)
            back = dot_nt(lhs, r.down_full[at, :]) * r.slope_rows[b, :, at].astype(f32)
            back = back.astype(bf16)
            r.back_rows[b, :, at] = back
            up_sum[:, at] += jnp.sum(back.astype(f32), axis=0, keepdims=True)

        over(hidden // wide, tile)

    def first_back(b):
        grad = collected(2, b) + r.keep[2, b]
        normed = r.keep[0, b]
        add_vector(ROW_GAIN, grad * normed)
        add_vector(ROW_SHIFT, grad)
        scaled = grad * r.norm_gain[...]
        first = r.inverse_keep[b] * (
            scaled - row_mean(scaled) - normed * row_mean(scaled * normed)
        )
        r.input_grad[b] = first
        low = first.astype(bf16)
        r.output_rows[b, own_rows, :] = low
        gathers[2 * batch + b].give()
        add_vector(ROW_OUTPUT, low.astype(f32))

    def mix_back(b):
        gathers[2 * batch + b].land()
        r.mixed[b] = dot_nt(r.output_rows[b], r.output_full[...]).astype(bf16)

    def weight_tiles(left_ref, right_ref, store, first, last):
        left = left_ref[...].reshape(batch * rows, left_ref.shape[2])

        def tile(index):
            at = aligned((first + index) * wide, wide)
            right = right_ref[:, :, at].reshape(batch * rows, wide)
            store(at, dot_tn(left, right).astype(bf16))

        over(last - first, tile)

    def store_down(at, value):
        r.slope_rows[:, :, at] = value.reshape(batch, rows, wide)

    def store_up(at, value):
        r.hidden_rows[:, :, at] = value.reshape(batch, rows, wide)

    def store_output(at, value):
        r.output_part[:, at] = value

    reduce_sems = (r.ry_send, r.ry_recv, r.rz_send, r.rz_recv)
    columns = lambda ref, at: ref.at[:, aligned(at * depth, depth)]
    thin = [
        PairedReduce(
            seat, r.weight_low.at[k], columns,
            r.thin_twin.at[k], (lambda step, k=k: r.thin_out.at[k, step]), r.thin_in.at[k], reduce_sems, k,
        )
        for k in range(3)
    ]
    from_output = PairedReduce(
        seat, r.output_part, columns, r.output_twin, (lambda step: r.output_out.at[step]), r.output_in, reduce_sems, 3
    )
    from_down = PairedReduce(
        seat, r.slope_rows, lambda ref, at: ref.at[:, :, aligned(at * depth, depth)],
        r.down_twin, (lambda step: r.down_rows.at[:, :, step * depth : (step + 1) * depth]), r.down_in, reduce_sems, 4,
    )
    held = rows // depth

    def up_block(ref, at):
        return ref.at[at // held, aligned((at % held) * depth, depth), :]

    from_up = PairedReduce(
        seat, r.hidden_rows, up_block,
        r.up_twin, (lambda step: r.back_rows.at[0, step * depth : (step + 1) * depth, :]), r.up_in, reduce_sems, 5,
    )

    attend(0, [(3, passing(2, to_up))])
    scatter(0, 0, r.attended, r.output_full, False)
    attend(1, [(0, passing(0, to_down)), (2, passing(1, to_up_too))])
    scatter(0, 1, r.attended, r.output_full, False)
    to_down.pass_on(1)
    first_norm(0)
    first_norm(1)
    to_up_too.pass_on(2)
    gathers[0].relay()
    to_up.land()
    to_up_too.land()
    raise_up(0)
    gathers[1].relay()
    to_down.pass_on(2)
    to_down.land()
    scatter(1, 0, r.hidden_rows, r.down_full, False)
    raise_up(1)
    scatter(1, 1, r.hidden_rows, r.down_full, False)
    for copy in own_cotangent:
        copy.wait()
    second_norm(0)
    second_norm(1)
    gathers[batch].relay()
    lower(0)
    gathers[batch + 1].relay()
    scatter(2, 0, r.back_rows, r.up_full, True)
    lower(1)
    scatter(2, 1, r.back_rows, r.up_full, True)
    first_back(0)
    weight_tiles(r.hidden_rows, r.down_rows, store_down, 0, 2)
    first_back(1)
    weight_tiles(r.hidden_rows, r.down_rows, store_down, 2, 4)
    from_down.begin()
    for piece in gathers[batch : 2 * batch]:
        piece.close()
    gathers[2 * batch].relay()
    mix_back(0)

    key_flip = r.flipped.at[0]

    def heads_back(b, services):
        key_flip[...] = r.keys[b].astype(f32).T.astype(bf16)
        product_rows = r.mixed[b].astype(f32).T * r.mixture[b]
        for h in range(heads):
            r.row_dots[h] = jnp.sum(
                product_rows[h * HEAD_DIM : (h + 1) * HEAD_DIM], axis=0, keepdims=True
            )
        r.key_sum[...] = jnp.zeros_like(r.key_sum)
        r.value_sum[...] = jnp.zeros_like(r.value_sum)
        row_ids = own_ids(b)

        def one(h):
            own = aligned(h * HEAD_DIM, HEAD_DIM)
            query_rows = jnp.where(lane_head == h, r.queries[b], nothing)
            grad_rows = jnp.where(lane_head == h, r.mixed[b], nothing)
            same = jnp.tile(r.ids_down[b], (1, rows // 128)) == row_ids
            scores = jnp.where(same, dot_nt(r.keys[b], query_rows), LOWEST)
            probs = jnp.exp(scores - r.logs[b * heads + h])
            r.value_sum[...] += dot(probs.astype(bf16), grad_rows)
            prob_grad = dot_nt(r.values[b], grad_rows)
            score_grad = (probs * (prob_grad - r.row_dots[h])).astype(bf16)
            r.key_sum[...] += dot(score_grad, query_rows)
            r.query_flip[own, :] = dot(key_flip[own, :], score_grad)

        over_heads(one, services)

    lows = lambda k: slice(k * local, (k + 1) * local)

    def sequence_back(b):
        flipped = (r.query_flip[...].astype(bf16).astype(f32) * HEAD_DIM ** (-0.5)).astype(bf16)
        upright = flipped.astype(f32).T
        key_low = r.key_sum[...].astype(bf16)
        value_low = r.value_sum[...].astype(bf16)
        r.normed_rows[0, :, lows(0)] = upright.astype(bf16)
        for half in range(2):
            r.normed_rows[half, :, lows(1)] = key_low[half * rows : (half + 1) * rows]
            r.normed_rows[half, :, lows(2)] = value_low[half * rows : (half + 1) * rows]
        r.sums[ROW_QUERY : ROW_QUERY + 1, bias_at] += jnp.sum(upright, axis=0, keepdims=True)
        r.sums[ROW_VALUE : ROW_VALUE + 1, bias_at] += jnp.sum(
            value_low.astype(f32), axis=0, keepdims=True
        )
        flips = [flipped, key_low.astype(f32).T.astype(bf16), value_low.astype(f32).T.astype(bf16)]

        for k in range(3):
            def tile(index, k=k):
                at = aligned(index * wide, wide)
                term = dot(flips[k][:, :rows], r.tokens[b, :, at])
                if k > 0:
                    term = term + dot(flips[k][:, rows:], r.other[b, :, at])
                if b > 0:
                    term = term + r.keep[k, :, :, at].reshape(local, wide)
                if b == batch - 1:
                    r.weight_low[k, :, at] = term.astype(bf16)
                else:
                    r.keep[k, :, :, at] = term.reshape(2, local // 2, wide)

            over(width // wide, tile)

    def input_back(b, half):
        def compute(group):
            at = aligned(group * 2 * part, 2 * part)

            def tile(index):
                row_at = aligned(index * wide, wide)
                term = dot_nt(r.normed_rows[half, at, lows(1)], r.key_full[row_at, :]) + dot_nt(
                    r.normed_rows[half, at, lows(2)], r.value_full[row_at, :]
                )
                if half == 0:
                    term = term + dot_nt(
                        r.normed_rows[half, at, lows(0)], r.query_full[row_at, :]
                    )
                r.total[:, row_at] = term

            over(width // wide, tile)

        mine = scatters[3 * batch + 2 * b + half].give(compute, r.total)
        r.total_own[2 * b + half] = r.total[mine, :]

    def other_copy(b):
        return remote(
            r.side_out.at[2 * batch + b],
            r.side_in.at[2 * batch + b],
            r.other_send.at[b],
            r.other_recv.at[b],
            seat.twin,
        )

    def other_give(b):
        r.side_out[2 * batch + b] = (
            r.total_own[2 * b + 1] + scatters[3 * batch + 2 * b + 1].take()
        ).astype(bf16)
        other_copy(b).start()

    def input_take(b):
        own = r.total_own[2 * b] + scatters[3 * batch + 2 * b].take()
        other_copy(b).wait_recv()
        r.input_grad[b] = (own + r.side_in[2 * batch + b].astype(f32)) + r.input_grad[b]

    def stepping(step, *which):
        def service():
            for piece in which:
                piece.advance(step)

        return service

    def down_done():
        r.down_grad[...] = from_down.advance(hops).reshape(hidden, depth)

    heads_back(0, [(1, gathers[2 * batch + 1].relay), (3, stepping(0, from_down))])
    mix_back(1)
    weight_tiles(r.attended, r.output_rows, store_output, 0, 4)
    from_output.begin()
    weight_tiles(r.normed_rows, r.back_rows, store_up, 0, 4)
    from_up.begin()
    stepping(1, from_down)()
    for piece in scatters[: 3 * batch] + gathers[:batch] + gathers[2 * batch :]:
        piece.close()
    sequence_back(0)
    stepping(2, from_down)()
    input_back(0, 1)
    stepping(0, from_output)()
    input_back(0, 0)
    heads_back(1, [(0, down_done), (1, lambda: other_give(0)), (2, stepping(0, from_up)), (3, stepping(1, from_output))])
    stepping(1, from_up)()
    sequence_back(1)
    for step in range(count):
        for k in thin:
            k.y(step).start()
    stepping(2, from_up, from_output)()
    input_back(1, 1)
    input_back(1, 0)

    def sum_copy(stage, to):
        return remote(
            r.sum_all.at[stage], r.sum_in.at[stage], r.sum_send.at[stage], r.sum_recv.at[stage], to
        )

    def sum_stage(stage, to):
        r.sum_all[stage] = r.sums[...]
        sum_copy(stage, to).start()

    def sum_add(stage, to):
        sum_copy(stage, to).wait_recv()
        r.sums[...] = r.sums[...] + r.sum_in[stage]

    def around_copy(away):
        stage = 4 + away
        return remote(
            r.sum_all.at[3], r.sum_in.at[stage], r.sum_send.at[stage], r.sum_recv.at[stage], around[away]
        )

    sum_stage(0, seat.pair)
    for k in thin:
        k.advance(0)
    sum_add(0, seat.pair)
    sum_stage(1, seat.side)
    input_take(0)
    other_give(1)
    for k in thin:
        k.advance(1)
    sum_add(1, seat.side)
    sum_stage(2, seat.twin)
    r.up_grad[...] = from_up.advance(hops)
    r.output_grad[...] = from_output.advance(hops)
    sum_add(2, seat.twin)
    r.sum_all[3] = r.sums[...]
    for away in range(hops):
        around_copy(away).start()
    for k in thin:
        k.advance(2)
    input_take(1)
    r.sum_in[3] = r.sums[...]
    for away in range(hops):
        around_copy(away).wait_recv()
    gathered = jnp.zeros_like(r.sums[...])
    for origin in range(count):
        gathered = gathered + r.sum_in[3 + (seat.dp + count - origin) % count]
    r.sums[...] = gathered
    for k, target in zip(thin, (r.query_grad, r.key_grad, r.value_grad)):
        target[...] = k.advance(hops).T

    for stage, to in enumerate((seat.pair, seat.side, seat.twin)):
        sum_copy(stage, to).wait_send()
    for away in range(hops):
        around_copy(away).wait_send()
    for b in range(batch):
        other_copy(b).wait_send()
    for copy in sends:
        copy().wait_send()
    for piece in weights + scatters[3 * batch :] + thin + [from_output, from_down, from_up]:
        piece.close()


def layer_call(inputs, segment_ids, cotangent, shards, vectors):
    count = lax.axis_size("dp")
    batch, part, width = inputs.shape
    rows = part * lax.axis_size("tp")
    local = shards[0].shape[1]
    hidden = shards[4].shape[1]
    heads = local // HEAD_DIM
    depth = width // (2 * count)
    bf16, f32 = jnp.bfloat16, jnp.float32
    ins = [
        ("inputs", LEFT),
        ("cotangent", LEFT),
        ("query_weight", LEFT),
        ("key_weight", LEFT),
        ("value_weight", LEFT),
        ("output_weight", LEFT),
        ("up_weight", LEFT),
        ("down_weight", LEFT),
        ("ids", VMEM),
        ("query_bias", VMEM),
        ("value_bias", VMEM),
        ("output_bias", VMEM),
        ("up_bias", VMEM),
        ("down_bias", VMEM),
        ("norm_gain", VMEM),
        ("norm_shift", VMEM),
        ("final_gain", VMEM),
        ("final_shift", VMEM),
    ]
    outs = [
        ("result", (batch, part, width), bf16),
        ("input_grad", (batch, part, width), f32),
        ("query_grad", (depth, local), f32),
        ("key_grad", (depth, local), f32),
        ("value_grad", (depth, local), f32),
        ("output_grad", (local, depth), f32),
        ("up_grad", (depth, hidden), f32),
        ("down_grad", (hidden, depth), f32),
        ("sums", (VECTOR_ROWS, width), f32),
    ]
    scratch = [
        ("tokens", (batch, rows, width), bf16),
        ("other", (batch, rows, width), bf16),
        ("query_full", (width, local), bf16),
        ("key_full", (width, local), bf16),
        ("value_full", (width, local), bf16),
        ("output_full", (local, width), bf16),
        ("up_full", (width, hidden), bf16),
        ("down_full", (hidden, width), bf16),
        ("queries", (batch, rows, local), bf16),
        ("keys", (batch, 2 * rows, local), bf16),
        ("values", (batch, 2 * rows, local), bf16),
        ("flipped", (batch, local, 2 * rows), bf16),
        ("mixture", (batch, local, rows), f32),
        ("logs", (batch * heads, 1, rows), f32),
        ("attended", (batch, rows, local), bf16),
        ("ids_down", (batch, 2 * rows, 128), f32),
        ("normed_rows", (batch, rows, width), bf16),
        ("hidden_rows", (batch, rows, hidden), bf16),
        ("slope_rows", (batch, rows, hidden), bf16),
        ("down_rows", (batch, rows, width), bf16),
        ("back_rows", (batch, rows, hidden), bf16),
        ("output_rows", (batch, rows, width), bf16),
        ("keep", (3, batch, part, width), f32),
        ("inverse_keep", (batch, part, 1), f32),
        ("total_own", (2 * batch, part, width), f32),
        ("total", (2 * part, width), f32),
        ("pair_out", (3 * batch, 2, part, width), bf16),
        ("pair_in", (3 * batch, 2, part, width), bf16),
        ("side_out", (3 * batch, part, width), bf16),
        ("side_in", (3 * batch, part, width), bf16),
        ("mixed", (batch, rows, local), bf16),
        ("output_part", (local, width), bf16),
        ("row_dots", (heads, 1, rows), f32),
        ("query_flip", (local, rows), f32),
        ("key_sum", (2 * rows, local), f32),
        ("value_sum", (2 * rows, local), f32),
        ("weight_low", (3, local, width), bf16),
        ("thin_twin", (3, count, local, depth), bf16),
        ("thin_out", (3, count - 1, local, depth), bf16),
        ("thin_in", (3, count - 1, local, depth), bf16),
        ("output_twin", (count, local, depth), bf16),
        ("output_out", (count - 1, local, depth), bf16),
        ("output_in", (count - 1, local, depth), bf16),
        ("down_twin", (count, batch, rows, depth), bf16),
        ("down_in", (count - 1, batch, rows, depth), bf16),
        ("up_twin", (count, depth, hidden), bf16),
        ("up_in", (count - 1, depth, hidden), bf16),
        ("sum_in", (3 + count, VECTOR_ROWS, width), f32),
        ("sum_all", (4, VECTOR_ROWS, width), f32),
    ]
    sems = [
        ("local_sem", (1 + batch,)),
        ("token_send", (7,)),
        ("token_recv", (7,)),
        ("own_sem", (7,)),
        ("gz_send", (7, 2 * (count - 1))),
        ("gz_recv", (7, 2 * (count - 1))),
        ("gy_send", (7, count)),
        ("gy_recv", (7, count)),
        ("scatter_send", (5 * batch, 3)),
        ("scatter_recv", (5 * batch, 3)),
        ("gather_send", (3 * batch, 3)),
        ("gather_recv", (3 * batch, 3)),
        ("other_send", (batch,)),
        ("other_recv", (batch,)),
        ("sum_send", (3 + count,)),
        ("sum_recv", (3 + count,)),
        ("ry_send", (6, count)),
        ("ry_recv", (6, count)),
        ("rz_send", (6, count - 1)),
        ("rz_recv", (6, count - 1)),
    ]
    names = [item[0] for group in (ins, outs, scratch, sems) for item in group]
    return pl.pallas_call(
        functools.partial(layer_kernel, names),
        name="layer",
        out_shape=[jax.ShapeDtypeStruct(shape, kind) for _, shape, kind in outs],
        in_specs=[space for _, space in ins],
        out_specs=[VMEM] * len(outs),
        scratch_shapes=[pltpu.VMEM(shape, kind) for _, shape, kind in scratch]
        + [pltpu.SemaphoreType.DMA(shape) for _, shape in sems],
        compiler_params=pltpu.CompilerParams(
            collective_id=1, has_side_effects=True, vmem_limit_bytes=67043328
        ),
    )(
        inputs,
        cotangent,
        *shards,
        segment_ids,
        *[vector.reshape(1, -1) for vector in vectors],
    )


def settle_kernel(moved, *refs):
    total = moved + 1
    sources, vectors, targets = refs[:moved], refs[moved], refs[total : total + moved]
    rows_out = refs[total + moved : total + moved + 9]
    held = refs[total + moved + 9 : total + 2 * moved + 9]
    in_sem, out_sem = refs[-2:]
    width = vectors.shape[1]
    into = [
        pltpu.make_async_copy(source, place, in_sem.at[k])
        for k, (source, place) in enumerate(zip(sources, held))
    ]
    out = [
        pltpu.make_async_copy(place, target, out_sem.at[k])
        for k, (place, target) in enumerate(zip(held, targets))
    ]
    for copy in into:
        copy.start()
    for row in range(8):
        rows_out[row][...] = vectors[row : row + 1, :]
    for k in range(4):
        rows_out[8][:, k * width : (k + 1) * width] = vectors[ROW_UP + k : ROW_UP + k + 1, :]
    for first, second in zip(into, out):
        first.wait()
        second.start()
    for copy in out:
        copy.wait()


def settle(arrays, sums):
    moved = len(arrays)
    width = sums.shape[1]
    same = [jax.ShapeDtypeStruct(array.shape, array.dtype) for array in arrays]
    rows_out = [jax.ShapeDtypeStruct((1, width), jnp.float32)] * 8
    rows_out.append(jax.ShapeDtypeStruct((1, 4 * width), jnp.float32))
    return pl.pallas_call(
        functools.partial(settle_kernel, moved),
        name="settle",
        out_shape=same + rows_out,
        in_specs=[LEFT] * moved + [VMEM],
        out_specs=[LEFT] * moved + [VMEM] * 9,
        scratch_shapes=[pltpu.VMEM(array.shape, array.dtype) for array in arrays]
        + [pltpu.SemaphoreType.DMA((moved,)), pltpu.SemaphoreType.DMA((moved,))],
        compiler_params=pltpu.CompilerParams(vmem_limit_bytes=56 * 2**20),
    )(*arrays, sums)


def fused_plan(
    inputs,
    segment_ids,
    query_weight,
    key_weight,
    value_weight,
    output_weight,
    up_weight,
    down_weight,
    querybias,
    valuebias,
    outputbias,
    upbias,
    downbias,
    norm_gain,
    norm_shift,
    final_gain,
    final_shift,
    cotangent,
):
    *grads, sums = layer_call(
        inputs,
        segment_ids,
        cotangent,
        (query_weight, key_weight, value_weight, output_weight, up_weight, down_weight),
        (
            querybias,
            valuebias,
            outputbias,
            upbias,
            downbias,
            norm_gain,
            norm_shift,
            final_gain,
            final_shift,
        ),
    )
    *outs, query, value, output, down, gain, shift, last_gain, last_shift, up = settle(grads, sums)
    rows = (query, value, output, up, down, gain, shift, last_gain, last_shift)
    return (*outs, *[row.reshape(-1) for row in rows])


def solution(mesh):
    fits = mesh.shape["ctx"] == 2 and mesh.shape["tp"] == 4 and mesh.shape["dp"] > 2
    placed = (
        P("dp", ("ctx", "tp"), None),
        P("dp", None),
        P(("dp", "ctx"), "tp"),
        P(("dp", "ctx"), "tp"),
        P(("dp", "ctx"), "tp"),
        P("tp", ("dp", "ctx")),
        P(("dp", "ctx"), "tp"),
        P("tp", ("dp", "ctx")),
        P(),
        P(),
        P(),
        P(),
        P(),
        P(),
        P(),
        P(),
        P(),
        P("dp", ("ctx", "tp"), None),
    )
    return jax.shard_map(
        fused_plan if fits else ring_plan,
        mesh=mesh,
        in_specs=placed,
        out_specs=(
            P("dp", ("ctx", "tp"), None),
            P("dp", ("ctx", "tp"), None),
            P(("dp", "ctx"), "tp"),
            P(("dp", "ctx"), "tp"),
            P(("dp", "ctx"), "tp"),
            P("tp", ("dp", "ctx")),
            P(("dp", "ctx"), "tp"),
            P("tp", ("dp", "ctx")),
            P(),
            P(),
            P(),
            P(),
            P(),
            P(),
            P(),
            P(),
            P(),
        ),
        check_vma=False,
    )
```

```python
import functools

import jax
import jax.numpy as jnp
from jax import lax
from jax.experimental import pallas as pl
from jax.experimental.pallas import tpu as pltpu
from jax.sharding import PartitionSpec as P

HEAD_DIM = 64
REACH = 4


def shifted(block, axis, distance):
    devices = range(lax.axis_size(axis))
    route = [(i - distance, i) for i in devices if i - distance in devices]
    return lax.ppermute(block, axis, route)


def for_sending(shard):

    def short(part):
        return part.astype(jnp.bfloat16) if part.dtype == jnp.float32 else part

    return jax.tree.map(short, shard)


def layer_norm(hidden, gain_vec, shift_vec):
    center = hidden - jnp.mean(hidden, axis=-1, keepdims=True)
    inverse = lax.rsqrt(jnp.mean(center * center, axis=-1, keepdims=True) + 1e-05)
    normed = center * inverse
    return (normed * gain_vec + shift_vec, normed, inverse)


def norm_back(upstream, normed, inverse, gain_vec):
    scaled = upstream * gain_vec
    return inverse * (
        scaled
        - jnp.mean(scaled, axis=-1, keepdims=True)
        - normed * jnp.mean(scaled * normed, axis=-1, keepdims=True)
    )


def gelu_curve(pre_act):
    return 0.5 * pre_act * (1.0 + lax.erf(pre_act * 0.7071067811865476))


def gelu_slope(pre_act):
    return (
        0.5 * (1.0 + lax.erf(pre_act * 0.7071067811865476))
        + pre_act * jnp.exp(-0.5 * pre_act * pre_act) * 0.3989422804014327
    )


def product(left_side, right_side):
    return jnp.einsum("btd,de->bte", left_side, right_side, preferred_element_type=jnp.float32)


def transposed(left_side, right_side):
    return jnp.einsum("btn,mn->btm", left_side, right_side, preferred_element_type=jnp.float32)


def weight_term(left_side, right_side):
    return jnp.einsum("btd,bte->de", left_side, right_side, preferred_element_type=jnp.float32)


def block_scores(query_rows, key_rows, block_mask):
    scores = jnp.einsum("bqhd,bkhd->bhqk", query_rows, key_rows, preferred_element_type=jnp.float32)
    return jnp.where(block_mask, scores, -1e30)


def probabilities(query_rows, key_rows, block_mask, log_total):
    scores = block_scores(query_rows, key_rows, block_mask)
    return jnp.where(block_mask, jnp.exp(scores - log_total[..., None]), 0.0)


def placed(local_part, full_len, place_at):
    empty = jnp.zeros((full_len,), jnp.float32)
    return lax.dynamic_update_slice_in_dim(empty, local_part, place_at * local_part.shape[0], 0)


def ring_plan(
    inputs,
    segment_ids,
    query_weight,
    key_weight,
    value_weight,
    output_weight,
    up_weight,
    down_weight,
    querybias,
    valuebias,
    outputbias,
    upbias,
    downbias,
    norm_gain,
    norm_shift,
    final_gain,
    final_shift,
    cotangent,
):
    tp_count = lax.axis_size("tp")
    tp_place = lax.axis_index("tp")
    ctx_count = lax.axis_size("ctx")
    ctx_place = lax.axis_index("ctx")
    batch_rows, part_rows, model_width = inputs.shape
    shard_rows = part_rows * tp_count
    full_query, full_key, full_value, full_output, full_up, full_down = (
        lax.all_gather(query_weight, ("dp", "ctx"), axis=0, tiled=True),
        lax.all_gather(key_weight, ("dp", "ctx"), axis=0, tiled=True),
        lax.all_gather(value_weight, ("dp", "ctx"), axis=0, tiled=True),
        lax.all_gather(output_weight, ("dp", "ctx"), axis=1, tiled=True),
        lax.all_gather(up_weight, ("dp", "ctx"), axis=0, tiled=True),
        lax.all_gather(down_weight, ("dp", "ctx"), axis=1, tiled=True),
    )
    local_width = full_query.shape[1]
    local_heads = local_width // HEAD_DIM
    hidden_width = full_up.shape[1]
    query_offset = lax.dynamic_slice_in_dim(querybias, tp_place * local_width, local_width)
    value_offset = lax.dynamic_slice_in_dim(valuebias, tp_place * local_width, local_width)
    up_offset = lax.dynamic_slice_in_dim(upbias, tp_place * hidden_width, hidden_width)
    score_scale = HEAD_DIM ** (-0.5)

    def split_heads(tensor):
        return tensor.reshape(batch_rows, shard_rows, local_heads, HEAD_DIM)

    def join_heads(tensor):
        return tensor.reshape(batch_rows, shard_rows, local_width)

    tokens = lax.all_gather(inputs, "tp", axis=1, tiled=True)
    queries = split_heads(
        ((product(tokens, full_query) + query_offset) * score_scale).astype(jnp.bfloat16)
    )
    key_rows = split_heads(product(tokens, full_key).astype(jnp.bfloat16))
    value_rows = split_heads((product(tokens, full_value) + value_offset).astype(jnp.bfloat16))
    own_ids = lax.dynamic_slice_in_dim(segment_ids, ctx_place * shard_rows, shard_rows, 1)
    offsets = [0] + [
        offset for offset in range(-REACH, REACH + 1) if offset != 0 and abs(offset) < ctx_count
    ]
    mask_of = {}
    block_of = {}
    for offset in offsets:
        source = ctx_place + offset
        begin_at = jnp.clip(source, 0, ctx_count - 1) * shard_rows
        other_ids = lax.dynamic_slice_in_dim(segment_ids, begin_at, shard_rows, 1)
        inside = jnp.logical_and(source >= 0, source < ctx_count)
        mask_of[offset] = jnp.logical_and(own_ids[:, :, None] == other_ids[:, None, :], inside)[
            :, None
        ]
        if offset == 0:
            block_of[offset] = (key_rows, value_rows)
        else:
            block_of[offset] = shifted((key_rows, value_rows), "ctx", -offset)
    running = jnp.full((batch_rows, local_heads, shard_rows), -1e30, jnp.float32)
    totals = jnp.zeros((batch_rows, local_heads, shard_rows), jnp.float32)
    for offset in offsets:
        scores = block_scores(queries, block_of[offset][0], mask_of[offset])
        highest = jnp.maximum(running, jnp.max(scores, axis=-1))
        weights = jnp.where(mask_of[offset], jnp.exp(scores - highest[..., None]), 0.0)
        totals = totals * jnp.exp(running - highest) + jnp.sum(weights, axis=-1)
        running = highest
    log_total = running + jnp.log(totals)
    mixture = jnp.zeros((batch_rows, shard_rows, local_heads, HEAD_DIM), jnp.float32)
    for offset in offsets:
        attn_probs = probabilities(queries, block_of[offset][0], mask_of[offset], log_total)
        mixture = mixture + jnp.einsum(
            "bhqk,bkhd->bqhd",
            attn_probs.astype(jnp.bfloat16),
            block_of[offset][1],
            preferred_element_type=jnp.float32,
        )
    attended = join_heads(mixture).astype(jnp.bfloat16)
    output_part = lax.psum_scatter(
        product(attended, full_output), "tp", scatter_dimension=1, tiled=True
    )
    first_sum = inputs.astype(jnp.float32) + output_part + outputbias
    normed_first, first_normed, first_inverse = layer_norm(first_sum, norm_gain, norm_shift)
    normed_rows = lax.all_gather(normed_first.astype(jnp.bfloat16), "tp", axis=1, tiled=True)
    hidden_pre = product(normed_rows, full_up) + up_offset
    hidden_low = gelu_curve(hidden_pre).astype(jnp.bfloat16)
    down_part = lax.psum_scatter(
        product(hidden_low, full_down), "tp", scatter_dimension=1, tiled=True
    )
    second_sum = normed_first + down_part + downbias
    result, second_normed, second_inverse = layer_norm(second_sum, final_gain, final_shift)
    upstream = cotangent.astype(jnp.float32)
    finalgain_grad = jnp.sum(upstream * second_normed, axis=(0, 1))
    finalshift_grad = jnp.sum(upstream, axis=(0, 1))
    second_grad = norm_back(upstream, second_normed, second_inverse, final_gain)
    down_low = second_grad.astype(jnp.bfloat16)
    downbias_grad = jnp.sum(down_low, axis=(0, 1), dtype=jnp.float32)
    down_rows = lax.all_gather(down_low, "tp", axis=1, tiled=True)
    down_grad = weight_term(hidden_low, down_rows)
    hidden_grad = (transposed(down_rows, full_down) * gelu_slope(hidden_pre)).astype(jnp.bfloat16)
    upbias_part = jnp.sum(hidden_grad, axis=(0, 1), dtype=jnp.float32)
    up_grad = weight_term(normed_rows, hidden_grad)
    normed_grad = (
        lax.psum_scatter(transposed(hidden_grad, full_up), "tp", scatter_dimension=1, tiled=True)
        + second_grad
    )
    normgain_grad = jnp.sum(normed_grad * first_normed, axis=(0, 1))
    normshift_grad = jnp.sum(normed_grad, axis=(0, 1))
    first_grad = norm_back(normed_grad, first_normed, first_inverse, norm_gain)
    output_low = first_grad.astype(jnp.bfloat16)
    outputbias_grad = jnp.sum(output_low, axis=(0, 1), dtype=jnp.float32)
    output_rows = lax.all_gather(output_low, "tp", axis=1, tiled=True)
    output_grad = weight_term(attended, output_rows)
    mixed_grad = split_heads(transposed(output_rows, full_output).astype(jnp.bfloat16))
    row_dot = jnp.zeros((batch_rows, local_heads, shard_rows), jnp.float32)
    for offset in offsets:
        attn_probs = probabilities(queries, block_of[offset][0], mask_of[offset], log_total)
        prob_grad = jnp.einsum(
            "bqhd,bkhd->bhqk", mixed_grad, block_of[offset][1], preferred_element_type=jnp.float32
        )
        row_dot = row_dot + jnp.sum(attn_probs * prob_grad, axis=-1)
    query_acc = jnp.zeros((batch_rows, shard_rows, local_heads, HEAD_DIM), jnp.float32)
    key_parts = {}
    for offset in offsets:
        attn_probs = probabilities(queries, block_of[offset][0], mask_of[offset], log_total)
        prob_grad = jnp.einsum(
            "bqhd,bkhd->bhqk", mixed_grad, block_of[offset][1], preferred_element_type=jnp.float32
        )
        score_grad = (attn_probs * (prob_grad - row_dot[..., None])).astype(jnp.bfloat16)
        query_acc = query_acc + jnp.einsum(
            "bhqk,bkhd->bqhd", score_grad, block_of[offset][0], preferred_element_type=jnp.float32
        )
        key_term = jnp.einsum(
            "bhqk,bqhd->bkhd", score_grad, queries, preferred_element_type=jnp.float32
        )
        value_term = jnp.einsum(
            "bhqk,bqhd->bkhd",
            attn_probs.astype(jnp.bfloat16),
            mixed_grad,
            preferred_element_type=jnp.float32,
        )
        key_parts[offset] = (key_term, value_term)
    own_key, own_value = key_parts[0]
    for offset in offsets[1:]:
        back_key, back_value = shifted(for_sending(key_parts[offset]), "ctx", offset)
        own_key = own_key + back_key
        own_value = own_value + back_value
    query_pre = (
        join_heads(query_acc.astype(jnp.bfloat16)).astype(jnp.float32) * score_scale
    ).astype(jnp.bfloat16)
    key_low = join_heads(own_key.astype(jnp.bfloat16))
    value_low = join_heads(own_value.astype(jnp.bfloat16))
    querybias_part = jnp.sum(query_pre, axis=(0, 1), dtype=jnp.float32)
    valuebias_part = jnp.sum(value_low, axis=(0, 1), dtype=jnp.float32)
    query_grad = weight_term(tokens, query_pre)
    key_grad = weight_term(tokens, key_low)
    value_grad = weight_term(tokens, value_low)
    input_part = (
        transposed(query_pre, full_query)
        + transposed(key_low, full_key)
        + transposed(value_low, full_value)
    )
    input_grad = (
        lax.psum_scatter(
            input_part.astype(jnp.bfloat16), "tp", scatter_dimension=1, tiled=True
        ).astype(jnp.float32)
        + first_grad
    )
    query_grad, key_grad, value_grad, output_grad, up_grad, down_grad = (
        lax.psum_scatter(query_grad, ("dp", "ctx"), scatter_dimension=0, tiled=True),
        lax.psum_scatter(key_grad, ("dp", "ctx"), scatter_dimension=0, tiled=True),
        lax.psum_scatter(value_grad, ("dp", "ctx"), scatter_dimension=0, tiled=True),
        lax.psum_scatter(output_grad, ("dp", "ctx"), scatter_dimension=1, tiled=True),
        lax.psum_scatter(up_grad, ("dp", "ctx"), scatter_dimension=0, tiled=True),
        lax.psum_scatter(down_grad, ("dp", "ctx"), scatter_dimension=1, tiled=True),
    )
    summed = lax.psum(
        (
            placed(querybias_part, model_width, tp_place),
            placed(valuebias_part, model_width, tp_place),
            outputbias_grad,
            placed(upbias_part, hidden_width * tp_count, tp_place),
            downbias_grad,
            normgain_grad,
            normshift_grad,
            finalgain_grad,
            finalshift_grad,
        ),
        ("dp", "ctx", "tp"),
    )
    return (
        result.astype(jnp.bfloat16),
        input_grad,
        query_grad,
        key_grad,
        value_grad,
        output_grad,
        up_grad,
        down_grad,
        summed[0],
        summed[1],
        summed[2],
        summed[3],
        summed[4],
        summed[5],
        summed[6],
        summed[7],
        summed[8],
    )


MESH = pl.DeviceIdType.MESH
LOWEST = -1e30
VMEM = pl.BlockSpec(memory_space=pltpu.VMEM)
LEFT = pl.BlockSpec(memory_space=pl.ANY)


class Seat:
    def __init__(self):
        self.dp_count = lax.axis_size("dp")
        self.dp = lax.axis_index("dp")
        self.ctx = lax.axis_index("ctx")
        self.tp = lax.axis_index("tp")
        self.tp_pair = self.tp + 1 - 2 * (self.tp % 2)
        self.tp_side = (self.tp + 2) % 4
        self.tp_far = (self.tp_pair + 2) % 4
        self.pair = (self.dp, self.ctx, self.tp_pair)
        self.side = (self.dp, self.ctx, self.tp_side)
        self.twin = (self.dp, 1 - self.ctx, self.tp)
        self.above = ((self.dp + 1) % self.dp_count, self.ctx, self.tp)
        self.below = ((self.dp + self.dp_count - 1) % self.dp_count, self.ctx, self.tp)

    def meet(self, names):
        barrier = pltpu.get_barrier_semaphore()
        for name in names:
            pl.semaphore_signal(
                barrier, inc=1, device_id=getattr(self, name), device_id_type=MESH
            )
        pl.semaphore_wait(barrier, len(names))


def remote(source, target, send_sem, recv_sem, to):
    return pltpu.make_async_remote_copy(
        src_ref=source,
        dst_ref=target,
        send_sem=send_sem,
        recv_sem=recv_sem,
        device_id=to,
        device_id_type=MESH,
    )


class RingGather:
    def __init__(self, seat, shard, block, sems, at, twice=False):
        self.seat, self.shard, self.block, self.at = seat, shard, block, at
        self.own_sem, self.z_send, self.z_recv, self.y_send, self.y_recv = sems
        self.count = seat.dp_count
        self.twice = twice

    def held(self, step, other=0):
        origin = (self.seat.dp + self.count - step) % self.count
        place = self.seat.ctx if other == 0 else 1 - self.seat.ctx
        return self.block(origin * 2 + place)

    def own(self):
        return pltpu.make_async_copy(self.shard, self.held(0), self.own_sem.at[self.at])

    def z(self, step, other=0):
        source = self.shard if step == 0 and other == 0 else self.held(step, other)
        return remote(
            source,
            self.held(step, other),
            self.z_send.at[self.at, 2 * step + other],
            self.z_recv.at[self.at, 2 * step + other],
            self.seat.above,
        )

    def z_in(self, step, other=0):
        view = self.held(step + 1, other)
        return remote(
            view,
            view,
            self.z_send.at[self.at, 2 * step + other],
            self.z_recv.at[self.at, 2 * step + other],
            self.seat.above,
        )

    def y(self, step):
        source = self.shard if step == 0 else self.held(step)
        return remote(
            source,
            self.held(step),
            self.y_send.at[self.at, step],
            self.y_recv.at[self.at, step],
            self.seat.twin,
        )

    def y_in(self, step):
        view = self.held(step, 1)
        return remote(
            view,
            view,
            self.y_send.at[self.at, step],
            self.y_recv.at[self.at, step],
            self.seat.twin,
        )

    def begin(self):
        self.own().start()
        self.y(0).start()
        self.z(0).start()

    def join(self):
        self.y_in(0).wait_recv()
        self.z(0, 1).start()

    def pass_on(self, step):
        for other in range(2 if self.twice else 1):
            self.z_in(step, other).wait_recv()
            if step + 1 < self.count - 1:
                self.z(step + 1, other).start()
        if not self.twice:
            self.y(step + 1).start()

    def land(self):
        self.own().wait()
        if not self.twice:
            for step in range(self.count):
                self.y_in(step).wait_recv()

    def close(self):
        for step in range(self.count - 1):
            for other in range(2 if self.twice else 1):
                self.z(step, other).wait_send()
        for step in range(1 if self.twice else self.count):
            self.y(step).wait_send()


def dot(left_side, right_side):
    return jnp.dot(left_side, right_side, preferred_element_type=jnp.float32)


def dot_nt(left_side, right_side):
    return lax.dot_general(
        left_side, right_side, (((1,), (1,)), ((), ())), preferred_element_type=jnp.float32
    )


def dot_tn(left_side, right_side):
    return lax.dot_general(
        left_side, right_side, (((0,), (0,)), ((), ())), preferred_element_type=jnp.float32
    )


def aligned(start, size):
    return pl.ds(pl.multiple_of(start, size), size)


VECTOR_ROWS = 16
ROW_QUERY, ROW_VALUE, ROW_OUTPUT, ROW_DOWN = 0, 1, 2, 3
ROW_GAIN, ROW_SHIFT, ROW_FINAL_GAIN, ROW_FINAL_SHIFT, ROW_UP = 4, 5, 6, 7, 8


class TokenScatter:
    def __init__(self, seat, buffers, sems, at, slot):
        self.seat, self.at, self.slot = seat, at, slot
        self.pair_out, self.pair_in, self.side_out, self.side_in = buffers
        self.send, self.recv = sems

    def copy(self, k):
        at, seat, slot = self.at, self.seat, self.slot
        if k < 2:
            source, target, to = self.pair_out.at[slot, k], self.pair_in.at[slot, k], seat.pair
        else:
            source, target, to = self.side_out.at[slot], self.side_in.at[slot], seat.side
        return remote(source, target, self.send.at[at, k], self.recv.at[at, k], to)

    def give(self, compute, total):
        seat, at = self.seat, self.slot
        part = self.side_out.shape[1]
        group = seat.tp // 2
        mine = aligned((seat.tp % 2) * part, part)
        others = aligned((1 - seat.tp % 2) * part, part)
        compute(1 - group)
        self.pair_out[at, 0] = total[others, :].astype(jnp.bfloat16)
        self.copy(0).start()
        self.side_out[at] = total[mine, :].astype(jnp.bfloat16)
        compute(group)
        self.pair_out[at, 1] = total[others, :].astype(jnp.bfloat16)
        self.copy(1).start()
        self.copy(0).wait_recv()
        self.side_out[at] = (
            self.side_out[at].astype(jnp.float32) + self.pair_in[at, 0].astype(jnp.float32)
        ).astype(jnp.bfloat16)
        self.copy(2).start()
        return mine

    def take(self):
        self.copy(1).wait_recv()
        self.copy(2).wait_recv()
        return self.pair_in[self.slot, 1].astype(jnp.float32) + self.side_in[self.slot].astype(
            jnp.float32
        )

    def close(self):
        for k in range(3):
            self.copy(k).wait_send()


class TokenGather:
    def __init__(self, seat, full, b, part, sems, at):
        self.seat = seat
        self.send, self.recv = sems
        self.at = at
        self.view = lambda place: full.at[b, aligned(place * part, part), :]

    def copy(self, k, place, to):
        view = self.view(place)
        return remote(view, view, self.send.at[self.at, k], self.recv.at[self.at, k], to)

    def give(self):
        seat = self.seat
        self.copy(0, seat.tp, seat.side).start()
        self.copy(1, seat.tp, seat.pair).start()

    def relay(self):
        seat = self.seat
        self.copy(0, seat.tp_side, seat.side).wait_recv()
        self.copy(2, seat.tp_side, seat.pair).start()

    def land(self):
        seat = self.seat
        self.copy(1, seat.tp_pair, seat.pair).wait_recv()
        self.copy(2, seat.tp_far, seat.pair).wait_recv()

    def close(self):
        seat = self.seat
        for k, place in ((0, seat.tp), (1, seat.tp), (2, seat.tp_side)):
            self.copy(k, place, seat.pair).wait_send()


def row_mean(rows):
    return jnp.mean(rows, axis=-1, keepdims=True)


class PairedReduce:
    def __init__(self, seat, partial, block, twin_in, ring_out, ring_in, sems, at):
        self.seat, self.partial, self.block, self.at = seat, partial, block, at
        self.twin_in, self.ring_out, self.ring_in = twin_in, ring_out, ring_in
        self.y_send, self.y_recv, self.z_send, self.z_recv = sems
        self.count = seat.dp_count

    def mine(self, step, ctx):
        owner = (self.seat.dp + 2 * self.count - 1 - step) % self.count
        return self.block(self.partial, owner * 2 + ctx)

    def y(self, step):
        return remote(
            self.mine(step, 1 - self.seat.ctx),
            self.twin_in.at[step],
            self.y_send.at[self.at, step],
            self.y_recv.at[self.at, step],
            self.seat.twin,
        )

    def z(self, step):
        return remote(
            self.ring_out(step),
            self.ring_in.at[step],
            self.z_send.at[self.at, step],
            self.z_recv.at[self.at, step],
            self.seat.above,
        )

    def begin(self):
        for step in range(self.count):
            self.y(step).start()

    def advance(self, step):
        self.y(step).wait_recv()
        total = self.mine(step, self.seat.ctx)[...].astype(jnp.float32) + self.twin_in[
            step
        ].astype(jnp.float32)
        if step > 0:
            self.z(step - 1).wait_recv()
            total = total + self.ring_in[step - 1].astype(jnp.float32)
        if step == self.count - 1:
            return total
        self.ring_out(step)[...] = total.astype(jnp.bfloat16)
        self.z(step).start()

    def close(self):
        for step in range(self.count):
            self.y(step).wait_send()
        for step in range(self.count - 1):
            self.z(step).wait_send()


class RingReduce:
    def __init__(self, seat, partial, pair, ring_out, ring_in, half_out, half_in, sems, at):
        self.seat, self.partial, self.pair, self.at = seat, partial, pair, at
        self.ring_out, self.ring_in, self.half_out, self.half_in = ring_out, ring_in, half_out, half_in
        self.y_send, self.y_recv, self.z_send, self.z_recv = sems
        self.count = seat.dp_count

    def mine(self, step):
        owner = (self.seat.dp + 2 * self.count - 1 - step) % self.count
        return self.pair(self.partial, owner)

    def z(self, step):
        return remote(
            self.mine(0) if step == 0 else self.ring_out(step - 1),
            self.ring_in.at[step],
            self.z_send.at[self.at, step],
            self.z_recv.at[self.at, step],
            self.seat.above,
        )

    def y(self):
        return remote(
            self.half_out,
            self.half_in,
            self.y_send.at[self.at, 0],
            self.y_recv.at[self.at, 0],
            self.seat.twin,
        )

    def begin(self):
        self.z(0).start()

    def advance(self, step):
        self.z(step - 1).wait_recv()
        total = self.mine(step)[...].astype(jnp.float32) + self.ring_in[step - 1].astype(
            jnp.float32
        )
        if step == self.count - 1:
            return total
        self.ring_out(step - 1)[...] = total.astype(jnp.bfloat16)
        self.z(step).start()

    def close(self):
        self.y().wait_send()
        for step in range(self.count - 1):
            self.z(step).wait_send()


class Parts:
    def __init__(self, names, refs):
        self.__dict__.update(zip(names, refs))


def layer_kernel(names, *refs):
    r = Parts(names, refs)
    seat = Seat()
    count = seat.dp_count
    hops = count - 1
    batch, part, width = r.result.shape
    rows = r.tokens.shape[1]
    local = r.query_full.shape[1]
    hidden = r.up_full.shape[1]
    heads = local // HEAD_DIM
    depth = width // (2 * count)
    wide = 256
    f32, bf16 = jnp.float32, jnp.bfloat16

    barrier = pltpu.get_barrier_semaphore()
    around = [((seat.dp + away) % count, seat.ctx, seat.tp) for away in range(1, count)]
    for to in [seat.pair, seat.side, seat.twin] + around:
        pl.semaphore_signal(barrier, inc=1, device_id=to, device_id_type=MESH)
    pl.semaphore_wait(barrier, 2 + count)

    def over(tiles, body):
        def one(index, carry):
            body(index)
            return carry

        lax.fori_loop(0, tiles, one, 0)

    def over_heads(body, services):
        def one(h):
            for when, service in services:
                pl.when(h == when)(service)
            body(h)

        over(heads, one)

    def cut(half, place):
        return lambda b: half.at[b, aligned(place * part, part), :]

    def token_copy(relation, b, source, target, to):
        at = 2 * relation + b
        return remote(source(b), target(b), r.token_send.at[at], r.token_recv.at[at], to)

    here, there = cut(r.tokens, seat.tp), cut(r.other, seat.tp)
    here_side, there_side = cut(r.tokens, seat.tp_side), cut(r.other, seat.tp_side)
    given = lambda b: r.inputs.at[b]
    landed = [
        cut(r.tokens, seat.tp_pair),
        here_side,
        there,
        there_side,
        cut(r.tokens, seat.tp_far),
        cut(r.other, seat.tp_pair),
        cut(r.other, seat.tp_far),
    ]

    def token_out(relation, b):
        return token_copy(
            relation,
            b,
            *(
                (given, here, seat.pair),
                (given, here, seat.side),
                (given, there, seat.twin),
                (there, there, seat.side),
                (here_side, here_side, seat.pair),
                (there, there, seat.pair),
                (there_side, there_side, seat.pair),
            )[relation],
        )

    def token_in(relation, b):
        token_copy(relation, b, landed[relation], landed[relation], seat.pair).wait_recv()

    own_tokens = [
        pltpu.make_async_copy(r.inputs.at[b], here(b), r.local_sem.at[b]) for b in range(batch)
    ]
    upstream = lambda b: r.weight_low.at[0, b * part : (b + 1) * part, :]
    own_cotangent = [
        pltpu.make_async_copy(r.cotangent.at[b], upstream(b), r.local_sem.at[batch + b])
        for b in range(batch)
    ]
    for copy in own_tokens + own_cotangent:
        copy.start()

    def by_rows(full):
        return lambda at: full.at[aligned(at * depth, depth), :]

    def by_columns(full):
        return lambda at: full.at[:, aligned(at * depth, depth)]

    def by_half_rows(half):
        def view(full):
            return lambda at: full.at[aligned(at * depth + half * (depth // 2), depth // 2), :]

        return view

    gather_sems = (r.own_sem, r.gz_send, r.gz_recv, r.gy_send, r.gy_recv)
    weights = [
        RingGather(seat, shard, view(full), gather_sems, at, twice)
        for at, (shard, full, view, twice) in enumerate(
            (
                (r.query_weight, r.query_full, by_rows, False),
                (r.key_weight, r.key_full, by_rows, True),
                (r.value_weight, r.value_full, by_rows, True),
                (r.output_weight, r.output_full, by_columns, False),
                (r.up_weight.at[: depth // 2, :], r.up_full, by_half_rows(0), False),
                (r.up_weight.at[depth // 2 :, :], r.up_full, by_half_rows(1), True),
                (r.down_weight, r.down_full, by_columns, False),
            )
        )
    ]
    to_output, to_up, to_up_too, to_down = weights[3:]
    to_query, to_key, to_value = weights[:3]
    to_value.begin()
    to_key.begin()
    for b in range(batch):
        token_out(1, b).start()
        token_out(2, b).start()
        token_out(0, b).start()
    to_query.begin()
    to_output.begin()
    to_value.join()
    to_key.join()
    for weight in (to_value, to_key, to_query):
        weight.pass_on(0)
    to_up.begin()
    token_in(1, 0)
    token_out(4, 0).start()
    token_in(2, 0)
    token_out(3, 0).start()
    token_out(5, 0).start()
    for weight in (to_value, to_key, to_query):
        weight.pass_on(1)
    to_output.pass_on(0)
    token_in(1, 1)
    token_out(4, 1).start()
    token_in(2, 1)
    token_out(3, 1).start()
    token_out(5, 1).start()
    to_up_too.begin()
    for weight in (to_value, to_key, to_query):
        weight.pass_on(2)
    to_output.pass_on(1)
    to_up.pass_on(0)
    to_up_too.join()
    to_down.begin()

    for b in range(batch):
        for half in range(2):
            row_ids = r.ids[b : b + 1, aligned((seat.ctx if half == 0 else 1 - seat.ctx) * rows, rows)]
            spread = jnp.broadcast_to(row_ids.astype(f32), (128, rows))
            r.ids_down[b, half * rows : (half + 1) * rows, :] = spread.T
    bias_at = aligned(seat.tp * local, local)
    query_offset = r.query_bias[:, bias_at]
    value_offset = r.value_bias[:, bias_at]
    tile_rows = rows // 2
    for weight in weights[:3]:
        weight.land()
    for copy in own_tokens:
        copy.wait()
    for b in range(batch):
        token_in(0, b)
        token_in(4, b)

    def project(half_ref, half):
        def one(index):
            b, piece = index // 2, index % 2
            block = half_ref[b, aligned(piece * tile_rows, tile_rows), :]
            spot = aligned(half * rows + piece * tile_rows, tile_rows)
            if half == 0:
                scaled = (dot(block, r.query_full[...]) + query_offset) * HEAD_DIM ** (-0.5)
                r.queries[b, aligned(piece * tile_rows, tile_rows), :] = scaled.astype(bf16)
            r.keys[b, spot, :] = dot(block, r.key_full[...]).astype(bf16)
            value_rows = dot(block, r.value_full[...]) + value_offset
            r.values[b, spot, :] = value_rows.astype(bf16)
            r.flipped[b, :, spot] = value_rows.T.astype(bf16)

        over(batch * 2, one)

    project(r.tokens, 0)
    to_output.pass_on(2)
    to_up_too.pass_on(0)
    for b in range(batch):
        token_in(3, b)
        token_out(6, b).start()
        token_in(5, b)
        token_in(6, b)
    project(r.other, 1)

    lane_head = lax.broadcasted_iota(jnp.int32, (1, local), 1) // HEAD_DIM
    nothing = jnp.zeros((), bf16)

    def own_ids(b):
        return r.ids[b : b + 1, aligned(seat.ctx * rows, rows)].astype(f32)

    def attend(b, services):
        row_ids = own_ids(b)

        def one(h):
            own = aligned(h * HEAD_DIM, HEAD_DIM)
            chosen = jnp.where(lane_head == h, r.queries[b], nothing)
            same = jnp.tile(r.ids_down[b], (1, rows // 128)) == row_ids
            scores = jnp.where(same, dot_nt(r.keys[b], chosen), LOWEST)
            highest = jnp.max(scores, axis=0, keepdims=True)
            raised = jnp.exp(scores - highest)
            total = jnp.sum(raised, axis=0, keepdims=True)
            shares = (raised * (1.0 / total)).astype(bf16)
            r.mixture[b, own, :] = dot(r.flipped[b, own, :], shares)
            r.logs[b * heads + h] = highest + jnp.log(total)

        over_heads(one, services)
        r.attended[b] = r.mixture[b].T.astype(bf16)

    def passing(step, *which):
        def service():
            for weight in which:
                weight.pass_on(step)

        return service

    to_output.land()

    scatter_parts = (r.pair_out, r.pair_in, r.side_out, r.side_in)
    scatters = [
        TokenScatter(seat, scatter_parts, (r.scatter_send, r.scatter_recv), at, slot)
        for at, slot in list(enumerate(range(3 * batch)))
        + [(3 * batch + at, at) for at in range(2 * batch)]
    ]
    gathers = [
        TokenGather(seat, full, b, part, (r.gather_send, r.gather_recv), k * batch + b)
        for k, full in enumerate((r.normed_rows, r.down_rows, r.output_rows))
        for b in range(batch)
    ]

    def spread_rows(lhs_ref, b, weight, flipped):
        def compute(group):
            lhs = lhs_ref[b, aligned(group * 2 * part, 2 * part), :]

            def tile(index):
                at = aligned(index * wide, wide)
                if flipped:
                    r.total[:, at] = dot_nt(lhs, weight[at, :])
                else:
                    r.total[:, at] = dot(lhs, weight[:, at])

            over(width // wide, tile)

        return compute

    def scatter(k, b, lhs_ref, weight, flipped):
        mine = scatters[k * batch + b].give(spread_rows(lhs_ref, b, weight, flipped), r.total)
        r.total_own[b] = r.total[mine, :]

    def collected(k, b):
        return r.total_own[b] + scatters[k * batch + b].take()

    own_rows = aligned(seat.tp * part, part)
    r.sums[...] = jnp.zeros_like(r.sums)
    up_sum = r.sums.at[pl.ds(ROW_UP + seat.tp, 1), :]

    def add_vector(row, values):
        r.sums[row : row + 1, :] += jnp.sum(values, axis=0, keepdims=True)

    def first_norm(b):
        first_sum = r.tokens[b, own_rows, :].astype(f32) + (collected(0, b) + r.output_bias[...])
        center = first_sum - row_mean(first_sum)
        inverse = lax.rsqrt(row_mean(center * center) + 1e-05)
        normed = center * inverse
        scaled = normed * r.norm_gain[...] + r.norm_shift[...]
        r.keep[0, b] = normed
        r.keep[1, b] = scaled
        r.inverse_keep[b] = inverse
        r.normed_rows[b, own_rows, :] = scaled.astype(bf16)
        gathers[b].give()

    def raise_up(b):
        gathers[b].land()
        lhs = r.normed_rows[b]

        def tile(index):
            at = aligned(index * wide, wide)
            offset = r.up_bias[:, pl.ds(pl.multiple_of(seat.tp * hidden + index * wide, wide), wide)]
            pre = dot(lhs, r.up_full[:, at]) + offset
            half = 0.5 * (1.0 + lax.erf(pre * 0.7071067811865476))
            r.hidden_rows[b, :, at] = (pre * half).astype(bf16)
            slope = half + pre * jnp.exp(-0.5 * pre * pre) * 0.3989422804014327
            r.slope_rows[b, :, at] = slope.astype(bf16)

        over(hidden // wide, tile)

    def second_norm(b):
        second_sum = r.keep[1, b] + (collected(1, b) + r.down_bias[...])
        center = second_sum - row_mean(second_sum)
        inverse = lax.rsqrt(row_mean(center * center) + 1e-05)
        normed = center * inverse
        r.result[b] = (normed * r.final_gain[...] + r.final_shift[...]).astype(bf16)
        gradient = upstream(b)[...].astype(f32)
        add_vector(ROW_FINAL_GAIN, gradient * normed)
        add_vector(ROW_FINAL_SHIFT, gradient)
        scaled = gradient * r.final_gain[...]
        second = inverse * (scaled - row_mean(scaled) - normed * row_mean(scaled * normed))
        r.keep[2, b] = second
        low = second.astype(bf16)
        r.down_rows[b, own_rows, :] = low
        gathers[batch + b].give()
        add_vector(ROW_DOWN, low.astype(f32))

    def lower(b):
        gathers[batch + b].land()
        lhs = r.down_rows[b]

        def tile(index):
            at = aligned(index * wide, wide)
            back = dot_nt(lhs, r.down_full[at, :]) * r.slope_rows[b, :, at].astype(f32)
            back = back.astype(bf16)
            r.back_rows[b, :, at] = back
            up_sum[:, at] += jnp.sum(back.astype(f32), axis=0, keepdims=True)

        over(hidden // wide, tile)

    def first_back(b):
        grad = collected(2, b) + r.keep[2, b]
        normed = r.keep[0, b]
        add_vector(ROW_GAIN, grad * normed)
        add_vector(ROW_SHIFT, grad)
        scaled = grad * r.norm_gain[...]
        first = r.inverse_keep[b] * (
            scaled - row_mean(scaled) - normed * row_mean(scaled * normed)
        )
        r.input_grad[b] = first
        low = first.astype(bf16)
        r.output_rows[b, own_rows, :] = low
        gathers[2 * batch + b].give()
        add_vector(ROW_OUTPUT, low.astype(f32))

    def mix_back(b):
        gathers[2 * batch + b].land()
        r.mixed[b] = dot_nt(r.output_rows[b], r.output_full[...]).astype(bf16)

    def owner_at(step):
        return (seat.dp + 2 * count - 1 - step) % count

    def output_tiles():
        left = r.attended[...].reshape(batch * rows, local)

        def tile(index):
            at = aligned(index * wide, wide)
            right = r.output_rows[:, :, at].reshape(batch * rows, wide)
            r.output_part[:, at] = dot_tn(left, right).astype(bf16)

        over(width // wide, tile)

    def down_tiles(first, last):
        left = r.hidden_rows[...].reshape(batch * rows, hidden)

        def tile(index):
            at = aligned(owner_at(first + index) * 2 * depth, 2 * depth)
            right = r.down_rows[:, :, at].reshape(batch * rows, 2 * depth)
            term = dot_tn(left, right).astype(bf16)
            r.slope_rows[:, :, at] = term.reshape(batch, rows, 2 * depth)

        over(last - first, tile)
        for step in range(first, last):
            from_down.y(step).start()

    def up_tiles():
        left = r.normed_rows[...].reshape(batch * rows, width)

        def tile(index):
            at = aligned(index * wide, wide)
            right = r.back_rows[:, :, at].reshape(batch * rows, wide)
            r.hidden_rows[:, :, at] = dot_tn(left, right).astype(bf16).reshape(batch, rows, wide)

        over(hidden // wide, tile)
        from_up.begin()
        from_up_too.begin()

    reduce_sems = (r.ry_send, r.ry_recv, r.rz_send, r.rz_recv)
    columns = lambda ref, at: ref.at[:, aligned(at * depth, depth)]
    thin = [
        RingReduce(
            seat, r.weight_low.at[k],
            lambda ref, owner: ref.at[:, aligned(owner * 2 * depth, 2 * depth)],
            (lambda step, k=k: r.wide_out.at[k, step]), r.wide_in.at[k],
            r.half_out.at[k], r.half_in.at[k], reduce_sems, k,
        )
        for k in range(2)
    ]
    from_value = PairedReduce(
        seat, r.weight_low.at[2], columns,
        r.value_twin, (lambda step: r.value_out.at[step]), r.value_in, reduce_sems, 2,
    )
    from_output = PairedReduce(
        seat, r.output_part, columns, r.output_twin, (lambda step: r.output_out.at[step]), r.output_in, reduce_sems, 3
    )
    from_down = PairedReduce(
        seat, r.slope_rows, lambda ref, at: ref.at[:, :, aligned(at * depth, depth)],
        r.down_twin, (lambda step: r.down_rows.at[:, :, step * depth : (step + 1) * depth]), r.down_in, reduce_sems, 4,
    )
    held = rows // depth

    split = hidden // 2
    from_up = PairedReduce(
        seat, r.hidden_rows,
        lambda ref, at: ref.at[at // held, aligned((at % held) * depth, depth), :split],
        r.up_twin, (lambda step: r.back_rows.at[0, step * depth : (step + 1) * depth, :split]),
        r.up_in, reduce_sems, 5,
    )
    pairs = held // 2
    from_up_too = RingReduce(
        seat, r.hidden_rows,
        lambda ref, owner: ref.at[
            owner // pairs, aligned((owner % pairs) * 2 * depth, 2 * depth), split:
        ],
        (lambda step: r.back_rows.at[1, step * 2 * depth : (step + 1) * 2 * depth, split:]),
        r.up_pair_in, r.up_half_out, r.up_half_in, reduce_sems, 6,
    )

    attend(0, [(3, passing(0, to_down))])
    scatter(0, 0, r.attended, r.output_full, False)
    to_up.pass_on(1)
    attend(1, [(3, passing(1, to_up_too))])
    scatter(0, 1, r.attended, r.output_full, False)
    first_norm(0)
    to_down.pass_on(1)
    to_up.pass_on(2)
    first_norm(1)
    gathers[0].relay()
    to_up_too.pass_on(2)
    to_up.land()
    to_up_too.land()
    raise_up(0)
    gathers[1].relay()
    to_down.pass_on(2)
    raise_up(1)
    to_down.land()
    scatter(1, 0, r.hidden_rows, r.down_full, False)
    scatter(1, 1, r.hidden_rows, r.down_full, False)
    for copy in own_cotangent:
        copy.wait()
    second_norm(0)
    second_norm(1)
    gathers[batch].relay()
    lower(0)
    gathers[batch + 1].relay()
    scatter(2, 0, r.back_rows, r.up_full, True)
    lower(1)
    scatter(2, 1, r.back_rows, r.up_full, True)
    down_tiles(0, count)
    first_back(0)
    up_tiles()
    first_back(1)
    for piece in gathers[batch : 2 * batch]:
        piece.close()
    gathers[2 * batch].relay()
    mix_back(0)

    key_flip = r.flipped.at[0]

    def heads_back(b, services):
        key_flip[...] = r.keys[b].astype(f32).T.astype(bf16)
        product_rows = r.mixed[b].astype(f32).T * r.mixture[b]
        for h in range(heads):
            r.row_dots[h] = jnp.sum(
                product_rows[h * HEAD_DIM : (h + 1) * HEAD_DIM], axis=0, keepdims=True
            )
        r.key_sum[...] = jnp.zeros_like(r.key_sum)
        r.value_sum[...] = jnp.zeros_like(r.value_sum)
        row_ids = own_ids(b)

        def one(h):
            own = aligned(h * HEAD_DIM, HEAD_DIM)
            query_rows = jnp.where(lane_head == h, r.queries[b], nothing)
            grad_rows = jnp.where(lane_head == h, r.mixed[b], nothing)
            same = jnp.tile(r.ids_down[b], (1, rows // 128)) == row_ids
            scores = jnp.where(same, dot_nt(r.keys[b], query_rows), LOWEST)
            probs = jnp.exp(scores - r.logs[b * heads + h])
            r.value_sum[...] += dot(probs.astype(bf16), grad_rows)
            prob_grad = dot_nt(r.values[b], grad_rows)
            score_grad = (probs * (prob_grad - r.row_dots[h])).astype(bf16)
            r.key_sum[...] += dot(score_grad, query_rows)
            r.query_flip[own, :] = dot(key_flip[own, :], score_grad)

        over_heads(one, services)

    lows = lambda k: slice(k * local, (k + 1) * local)
    low_rows = (r.normed_rows, r.output_rows)

    def sequence_back(b):
        flipped = (r.query_flip[...].astype(bf16).astype(f32) * HEAD_DIM ** (-0.5)).astype(bf16)
        upright = flipped.astype(f32).T
        key_low = r.key_sum[...].astype(bf16)
        value_low = r.value_sum[...].astype(bf16)
        low_rows[b][0, :, lows(0)] = upright.astype(bf16)
        for half in range(2):
            low_rows[b][half, :, lows(1)] = key_low[half * rows : (half + 1) * rows]
            low_rows[b][half, :, lows(2)] = value_low[half * rows : (half + 1) * rows]
        r.sums[ROW_QUERY : ROW_QUERY + 1, bias_at] += jnp.sum(upright, axis=0, keepdims=True)
        r.sums[ROW_VALUE : ROW_VALUE + 1, bias_at] += jnp.sum(
            value_low.astype(f32), axis=0, keepdims=True
        )
        flips = [flipped, key_low.astype(f32).T.astype(bf16), value_low.astype(f32).T.astype(bf16)]

        for k in range(3):
            def tile(index, k=k):
                at = aligned(index * wide, wide)
                term = dot(flips[k][:, :rows], r.tokens[b, :, at])
                if k > 0:
                    term = term + dot(flips[k][:, rows:], r.other[b, :, at])
                if b > 0:
                    term = term + r.keep[k, :, :, at].reshape(local, wide)
                if b == batch - 1:
                    r.weight_low[k, :, at] = term.astype(bf16)
                else:
                    r.keep[k, :, :, at] = term.reshape(2, local // 2, wide)

            over(width // wide, tile)

    def input_back(b, half):
        def compute(group):
            at = aligned(group * 2 * part, 2 * part)

            def tile(index):
                row_at = aligned(index * wide, wide)
                term = dot_nt(low_rows[b][half, at, lows(1)], r.key_full[row_at, :]) + dot_nt(
                    low_rows[b][half, at, lows(2)], r.value_full[row_at, :]
                )
                if half == 0:
                    term = term + dot_nt(
                        low_rows[b][half, at, lows(0)], r.query_full[row_at, :]
                    )
                r.total[:, row_at] = term

            over(width // wide, tile)

        mine = scatters[3 * batch + 2 * b + half].give(compute, r.total)
        r.total_own[2 * b + half] = r.total[mine, :]

    def other_copy(b):
        return remote(
            r.side_out.at[2 * batch + b],
            r.side_in.at[2 * batch + b],
            r.other_send.at[b],
            r.other_recv.at[b],
            seat.twin,
        )

    def other_give(b):
        r.side_out[2 * batch + b] = (
            r.total_own[2 * b + 1] + scatters[3 * batch + 2 * b + 1].take()
        ).astype(bf16)
        other_copy(b).start()

    def input_take(b):
        own = r.total_own[2 * b] + scatters[3 * batch + 2 * b].take()
        other_copy(b).wait_recv()
        r.input_grad[b] = (own + r.side_in[2 * batch + b].astype(f32)) + r.input_grad[b]

    def stepping(step, *which):
        def service():
            for piece in which:
                piece.advance(step)

        return service

    def down_done():
        r.down_grad[...] = from_down.advance(hops).reshape(hidden, depth)

    stepping(0, from_down)()
    heads_back(0, [(0, gathers[2 * batch + 1].relay), (1, stepping(1, from_down)), (3, stepping(1, from_up_too))])
    mix_back(1)
    output_tiles()
    from_output.begin()
    stepping(2, from_down)()
    for piece in scatters[: 3 * batch] + gathers[:batch] + gathers[2 * batch :]:
        piece.close()
    sequence_back(0)
    input_back(0, 1)
    stepping(0, from_up)()
    input_back(0, 0)
    heads_back(1, [(0, down_done), (1, stepping(1, from_up)), (2, stepping(0, from_output)), (3, lambda: other_give(0))])
    stepping(2, from_up_too)()
    stepping(1, from_output)()
    sequence_back(1)
    from_value.begin()
    thin[0].begin()
    thin[1].begin()
    input_back(1, 1)
    stepping(2, from_up)()
    stepping(0, from_value)()
    input_back(1, 0)
    stepping(1, *thin)()

    def sum_copy(stage, to):
        return remote(
            r.sum_all.at[stage], r.sum_in.at[stage], r.sum_send.at[stage], r.sum_recv.at[stage], to
        )

    def sum_stage(stage, to):
        r.sum_all[stage] = r.sums[...]
        sum_copy(stage, to).start()

    def sum_add(stage, to):
        sum_copy(stage, to).wait_recv()
        r.sums[...] = r.sums[...] + r.sum_in[stage]

    def around_copy(away):
        stage = 4 + away
        return remote(
            r.sum_all.at[3], r.sum_in.at[stage], r.sum_send.at[stage], r.sum_recv.at[stage], around[away]
        )

    def halve(piece, at):
        r.total[:, at] = piece.advance(hops)

    mine_at = aligned(seat.ctx * depth, depth)
    other_at = aligned((1 - seat.ctx) * depth, depth)
    sum_stage(0, seat.pair)
    input_take(0)
    sum_add(0, seat.pair)
    sum_stage(1, seat.side)
    other_give(1)
    stepping(1, from_value)()
    stepping(2, from_output)()
    sum_add(1, seat.side)
    sum_stage(2, seat.twin)
    stepping(2, *thin)()
    r.up_grad[:, :split] = from_up.advance(hops)
    halve(from_up_too, slice(split, hidden))
    r.up_half_out[...] = r.total[other_at, split:].astype(bf16)
    from_up_too.y().start()
    sum_add(2, seat.twin)
    r.sum_all[3] = r.sums[...]
    for away in range(hops):
        around_copy(away).start()
    stepping(2, from_value)()
    r.output_grad[...] = from_output.advance(hops)
    input_take(1)
    for k in range(2):
        halve(thin[k], slice(k * 2 * depth, (k + 1) * 2 * depth))
        spot = aligned(k * 2 * depth + (1 - seat.ctx) * depth, depth)
        r.half_out[k] = r.total[:, spot].astype(bf16)
        thin[k].y().start()
    from_up_too.y().wait_recv()
    r.up_grad[:, split:] = r.total[mine_at, split:] + r.up_half_in[...].astype(f32)
    r.value_grad[...] = from_value.advance(hops).T
    r.sum_in[3] = r.sums[...]
    for away in range(hops):
        around_copy(away).wait_recv()
    gathered = jnp.zeros_like(r.sums[...])
    for origin in range(count):
        gathered = gathered + r.sum_in[3 + (seat.dp + count - origin) % count]
    r.sums[...] = gathered
    for k, target in enumerate((r.query_grad, r.key_grad)):
        thin[k].y().wait_recv()
        spot = aligned(k * 2 * depth + seat.ctx * depth, depth)
        target[...] = (r.total[:, spot] + r.half_in[k].astype(f32)).T

    for stage, to in enumerate((seat.pair, seat.side, seat.twin)):
        sum_copy(stage, to).wait_send()
    for away in range(hops):
        around_copy(away).wait_send()
    for b in range(batch):
        other_copy(b).wait_send()
    for relation in range(7):
        for b in range(batch):
            token_out(relation, b).wait_send()
    for piece in weights + scatters[3 * batch :] + thin + [from_value, from_output, from_down, from_up, from_up_too]:
        piece.close()


def layer_call(inputs, segment_ids, cotangent, shards, vectors):
    count = lax.axis_size("dp")
    batch, part, width = inputs.shape
    rows = part * lax.axis_size("tp")
    local = shards[0].shape[1]
    hidden = shards[4].shape[1]
    heads = local // HEAD_DIM
    depth = width // (2 * count)
    bf16, f32 = jnp.bfloat16, jnp.float32
    ins = [
        ("inputs", LEFT),
        ("cotangent", LEFT),
        ("query_weight", LEFT),
        ("key_weight", LEFT),
        ("value_weight", LEFT),
        ("output_weight", LEFT),
        ("up_weight", LEFT),
        ("down_weight", LEFT),
        ("ids", VMEM),
        ("query_bias", VMEM),
        ("value_bias", VMEM),
        ("output_bias", VMEM),
        ("up_bias", VMEM),
        ("down_bias", VMEM),
        ("norm_gain", VMEM),
        ("norm_shift", VMEM),
        ("final_gain", VMEM),
        ("final_shift", VMEM),
    ]
    outs = [
        ("result", (batch, part, width), bf16),
        ("input_grad", (batch, part, width), f32),
        ("query_grad", (depth, local), f32),
        ("key_grad", (depth, local), f32),
        ("value_grad", (depth, local), f32),
        ("output_grad", (local, depth), f32),
        ("up_grad", (depth, hidden), f32),
        ("down_grad", (hidden, depth), f32),
        ("sums", (VECTOR_ROWS, width), f32),
    ]
    scratch = [
        ("tokens", (batch, rows, width), bf16),
        ("other", (batch, rows, width), bf16),
        ("query_full", (width, local), bf16),
        ("key_full", (width, local), bf16),
        ("value_full", (width, local), bf16),
        ("output_full", (local, width), bf16),
        ("up_full", (width, hidden), bf16),
        ("down_full", (hidden, width), bf16),
        ("queries", (batch, rows, local), bf16),
        ("keys", (batch, 2 * rows, local), bf16),
        ("values", (batch, 2 * rows, local), bf16),
        ("flipped", (batch, local, 2 * rows), bf16),
        ("mixture", (batch, local, rows), f32),
        ("logs", (batch * heads, 1, rows), f32),
        ("attended", (batch, rows, local), bf16),
        ("ids_down", (batch, 2 * rows, 128), f32),
        ("normed_rows", (batch, rows, width), bf16),
        ("hidden_rows", (batch, rows, hidden), bf16),
        ("slope_rows", (batch, rows, hidden), bf16),
        ("down_rows", (batch, rows, width), bf16),
        ("back_rows", (batch, rows, hidden), bf16),
        ("output_rows", (batch, rows, width), bf16),
        ("keep", (3, batch, part, width), f32),
        ("inverse_keep", (batch, part, 1), f32),
        ("total_own", (2 * batch, part, width), f32),
        ("total", (2 * part, width), f32),
        ("pair_out", (3 * batch, 2, part, width), bf16),
        ("pair_in", (3 * batch, 2, part, width), bf16),
        ("side_out", (3 * batch, part, width), bf16),
        ("side_in", (3 * batch, part, width), bf16),
        ("mixed", (batch, rows, local), bf16),
        ("output_part", (local, width), bf16),
        ("row_dots", (heads, 1, rows), f32),
        ("query_flip", (local, rows), f32),
        ("key_sum", (2 * rows, local), f32),
        ("value_sum", (2 * rows, local), f32),
        ("weight_low", (3, local, width), bf16),
        ("wide_out", (2, count - 2, local, 2 * depth), bf16),
        ("wide_in", (2, count - 1, local, 2 * depth), bf16),
        ("half_out", (2, local, depth), bf16),
        ("half_in", (2, local, depth), bf16),
        ("value_twin", (count, local, depth), bf16),
        ("value_out", (count - 1, local, depth), bf16),
        ("value_in", (count - 1, local, depth), bf16),
        ("output_twin", (count, local, depth), bf16),
        ("output_out", (count - 1, local, depth), bf16),
        ("output_in", (count - 1, local, depth), bf16),
        ("down_twin", (count, batch, rows, depth), bf16),
        ("down_in", (count - 1, batch, rows, depth), bf16),
        ("up_twin", (count, depth, hidden // 2), bf16),
        ("up_in", (count - 1, depth, hidden // 2), bf16),
        ("up_pair_in", (count - 1, 2 * depth, hidden // 2), bf16),
        ("up_half_out", (depth, hidden // 2), bf16),
        ("up_half_in", (depth, hidden // 2), bf16),
        ("sum_in", (3 + count, VECTOR_ROWS, width), f32),
        ("sum_all", (4, VECTOR_ROWS, width), f32),
    ]
    sems = [
        ("local_sem", (2 * batch,)),
        ("token_send", (14,)),
        ("token_recv", (14,)),
        ("own_sem", (7,)),
        ("gz_send", (7, 2 * (count - 1))),
        ("gz_recv", (7, 2 * (count - 1))),
        ("gy_send", (7, count)),
        ("gy_recv", (7, count)),
        ("scatter_send", (5 * batch, 3)),
        ("scatter_recv", (5 * batch, 3)),
        ("gather_send", (3 * batch, 3)),
        ("gather_recv", (3 * batch, 3)),
        ("other_send", (batch,)),
        ("other_recv", (batch,)),
        ("sum_send", (3 + count,)),
        ("sum_recv", (3 + count,)),
        ("ry_send", (7, count)),
        ("ry_recv", (7, count)),
        ("rz_send", (7, count - 1)),
        ("rz_recv", (7, count - 1)),
    ]
    names = [item[0] for group in (ins, outs, scratch, sems) for item in group]
    return pl.pallas_call(
        functools.partial(layer_kernel, names),
        name="layer",
        out_shape=[jax.ShapeDtypeStruct(shape, kind) for _, shape, kind in outs],
        in_specs=[space for _, space in ins],
        out_specs=[VMEM] * len(outs),
        scratch_shapes=[pltpu.VMEM(shape, kind) for _, shape, kind in scratch]
        + [pltpu.SemaphoreType.DMA(shape) for _, shape in sems],
        compiler_params=pltpu.CompilerParams(
            collective_id=1, has_side_effects=True, vmem_limit_bytes=67043328
        ),
    )(
        inputs,
        cotangent,
        *shards,
        segment_ids,
        *[vector.reshape(1, -1) for vector in vectors],
    )


def settle_kernel(moved, *refs):
    total = moved + 1
    sources, vectors, targets = refs[:moved], refs[moved], refs[total : total + moved]
    rows_out = refs[total + moved : total + moved + 9]
    held = refs[total + moved + 9 : total + 2 * moved + 9]
    in_sem, out_sem = refs[-2:]
    width = vectors.shape[1]
    into = [
        pltpu.make_async_copy(source, place, in_sem.at[k])
        for k, (source, place) in enumerate(zip(sources, held))
    ]
    out = [
        pltpu.make_async_copy(place, target, out_sem.at[k])
        for k, (place, target) in enumerate(zip(held, targets))
    ]
    for copy in into:
        copy.start()
    for row in range(8):
        rows_out[row][...] = vectors[row : row + 1, :]
    for k in range(4):
        rows_out[8][:, k * width : (k + 1) * width] = vectors[ROW_UP + k : ROW_UP + k + 1, :]
    for first, second in zip(into, out):
        first.wait()
        second.start()
    for copy in out:
        copy.wait()


def settle(arrays, sums):
    moved = len(arrays)
    width = sums.shape[1]
    same = [jax.ShapeDtypeStruct(array.shape, array.dtype) for array in arrays]
    rows_out = [jax.ShapeDtypeStruct((1, width), jnp.float32)] * 8
    rows_out.append(jax.ShapeDtypeStruct((1, 4 * width), jnp.float32))
    return pl.pallas_call(
        functools.partial(settle_kernel, moved),
        name="settle",
        out_shape=same + rows_out,
        in_specs=[LEFT] * moved + [VMEM],
        out_specs=[LEFT] * moved + [VMEM] * 9,
        scratch_shapes=[pltpu.VMEM(array.shape, array.dtype) for array in arrays]
        + [pltpu.SemaphoreType.DMA((moved,)), pltpu.SemaphoreType.DMA((moved,))],
        compiler_params=pltpu.CompilerParams(vmem_limit_bytes=56 * 2**20),
    )(*arrays, sums)


def fused_plan(
    inputs,
    segment_ids,
    query_weight,
    key_weight,
    value_weight,
    output_weight,
    up_weight,
    down_weight,
    querybias,
    valuebias,
    outputbias,
    upbias,
    downbias,
    norm_gain,
    norm_shift,
    final_gain,
    final_shift,
    cotangent,
):
    *grads, sums = layer_call(
        inputs,
        segment_ids,
        cotangent,
        (query_weight, key_weight, value_weight, output_weight, up_weight, down_weight),
        (
            querybias,
            valuebias,
            outputbias,
            upbias,
            downbias,
            norm_gain,
            norm_shift,
            final_gain,
            final_shift,
        ),
    )
    *outs, query, value, output, down, gain, shift, last_gain, last_shift, up = settle(grads, sums)
    rows = (query, value, output, up, down, gain, shift, last_gain, last_shift)
    return (*outs, *[row.reshape(-1) for row in rows])


def solution(mesh):
    fits = mesh.shape["ctx"] == 2 and mesh.shape["tp"] == 4 and mesh.shape["dp"] > 2
    placed = (
        P("dp", ("ctx", "tp"), None),
        P("dp", None),
        P(("dp", "ctx"), "tp"),
        P(("dp", "ctx"), "tp"),
        P(("dp", "ctx"), "tp"),
        P("tp", ("dp", "ctx")),
        P(("dp", "ctx"), "tp"),
        P("tp", ("dp", "ctx")),
        P(),
        P(),
        P(),
        P(),
        P(),
        P(),
        P(),
        P(),
        P(),
        P("dp", ("ctx", "tp"), None),
    )
    return jax.shard_map(
        fused_plan if fits else ring_plan,
        mesh=mesh,
        in_specs=placed,
        out_specs=(
            P("dp", ("ctx", "tp"), None),
            P("dp", ("ctx", "tp"), None),
            P(("dp", "ctx"), "tp"),
            P(("dp", "ctx"), "tp"),
            P(("dp", "ctx"), "tp"),
            P("tp", ("dp", "ctx")),
            P(("dp", "ctx"), "tp"),
            P("tp", ("dp", "ctx")),
            P(),
            P(),
            P(),
            P(),
            P(),
            P(),
            P(),
            P(),
            P(),
        ),
        check_vma=False,
    )
```

```python
import functools

import jax
import jax.numpy as jnp
from jax import lax
from jax.experimental import pallas as pl
from jax.experimental.pallas import tpu as pltpu
from jax.sharding import PartitionSpec as P

HEAD_DIM = 64
REACH = 4


def shifted(block, axis, distance):
    devices = range(lax.axis_size(axis))
    route = [(i - distance, i) for i in devices if i - distance in devices]
    return lax.ppermute(block, axis, route)


def for_sending(shard):

    def short(part):
        return part.astype(jnp.bfloat16) if part.dtype == jnp.float32 else part

    return jax.tree.map(short, shard)


def layer_norm(hidden, gain_vec, shift_vec):
    center = hidden - jnp.mean(hidden, axis=-1, keepdims=True)
    inverse = lax.rsqrt(jnp.mean(center * center, axis=-1, keepdims=True) + 1e-05)
    normed = center * inverse
    return (normed * gain_vec + shift_vec, normed, inverse)


def norm_back(upstream, normed, inverse, gain_vec):
    scaled = upstream * gain_vec
    return inverse * (
        scaled
        - jnp.mean(scaled, axis=-1, keepdims=True)
        - normed * jnp.mean(scaled * normed, axis=-1, keepdims=True)
    )


def gelu_curve(pre_act):
    return 0.5 * pre_act * (1.0 + lax.erf(pre_act * 0.7071067811865476))


def gelu_slope(pre_act):
    return (
        0.5 * (1.0 + lax.erf(pre_act * 0.7071067811865476))
        + pre_act * jnp.exp(-0.5 * pre_act * pre_act) * 0.3989422804014327
    )


def product(left_side, right_side):
    return jnp.einsum("btd,de->bte", left_side, right_side, preferred_element_type=jnp.float32)


def transposed(left_side, right_side):
    return jnp.einsum("btn,mn->btm", left_side, right_side, preferred_element_type=jnp.float32)


def weight_term(left_side, right_side):
    return jnp.einsum("btd,bte->de", left_side, right_side, preferred_element_type=jnp.float32)


def block_scores(query_rows, key_rows, block_mask):
    scores = jnp.einsum("bqhd,bkhd->bhqk", query_rows, key_rows, preferred_element_type=jnp.float32)
    return jnp.where(block_mask, scores, -1e30)


def probabilities(query_rows, key_rows, block_mask, log_total):
    scores = block_scores(query_rows, key_rows, block_mask)
    return jnp.where(block_mask, jnp.exp(scores - log_total[..., None]), 0.0)


def placed(local_part, full_len, place_at):
    empty = jnp.zeros((full_len,), jnp.float32)
    return lax.dynamic_update_slice_in_dim(empty, local_part, place_at * local_part.shape[0], 0)


def ring_plan(
    inputs,
    segment_ids,
    query_weight,
    key_weight,
    value_weight,
    output_weight,
    up_weight,
    down_weight,
    querybias,
    valuebias,
    outputbias,
    upbias,
    downbias,
    norm_gain,
    norm_shift,
    final_gain,
    final_shift,
    cotangent,
):
    tp_count = lax.axis_size("tp")
    tp_place = lax.axis_index("tp")
    ctx_count = lax.axis_size("ctx")
    ctx_place = lax.axis_index("ctx")
    batch_rows, part_rows, model_width = inputs.shape
    shard_rows = part_rows * tp_count
    full_query, full_key, full_value, full_output, full_up, full_down = (
        lax.all_gather(query_weight, ("dp", "ctx"), axis=0, tiled=True),
        lax.all_gather(key_weight, ("dp", "ctx"), axis=0, tiled=True),
        lax.all_gather(value_weight, ("dp", "ctx"), axis=0, tiled=True),
        lax.all_gather(output_weight, ("dp", "ctx"), axis=1, tiled=True),
        lax.all_gather(up_weight, ("dp", "ctx"), axis=0, tiled=True),
        lax.all_gather(down_weight, ("dp", "ctx"), axis=1, tiled=True),
    )
    local_width = full_query.shape[1]
    local_heads = local_width // HEAD_DIM
    hidden_width = full_up.shape[1]
    query_offset = lax.dynamic_slice_in_dim(querybias, tp_place * local_width, local_width)
    value_offset = lax.dynamic_slice_in_dim(valuebias, tp_place * local_width, local_width)
    up_offset = lax.dynamic_slice_in_dim(upbias, tp_place * hidden_width, hidden_width)
    score_scale = HEAD_DIM ** (-0.5)

    def split_heads(tensor):
        return tensor.reshape(batch_rows, shard_rows, local_heads, HEAD_DIM)

    def join_heads(tensor):
        return tensor.reshape(batch_rows, shard_rows, local_width)

    tokens = lax.all_gather(inputs, "tp", axis=1, tiled=True)
    queries = split_heads(
        ((product(tokens, full_query) + query_offset) * score_scale).astype(jnp.bfloat16)
    )
    key_rows = split_heads(product(tokens, full_key).astype(jnp.bfloat16))
    value_rows = split_heads((product(tokens, full_value) + value_offset).astype(jnp.bfloat16))
    own_ids = lax.dynamic_slice_in_dim(segment_ids, ctx_place * shard_rows, shard_rows, 1)
    offsets = [0] + [
        offset for offset in range(-REACH, REACH + 1) if offset != 0 and abs(offset) < ctx_count
    ]
    mask_of = {}
    block_of = {}
    for offset in offsets:
        source = ctx_place + offset
        begin_at = jnp.clip(source, 0, ctx_count - 1) * shard_rows
        other_ids = lax.dynamic_slice_in_dim(segment_ids, begin_at, shard_rows, 1)
        inside = jnp.logical_and(source >= 0, source < ctx_count)
        mask_of[offset] = jnp.logical_and(own_ids[:, :, None] == other_ids[:, None, :], inside)[
            :, None
        ]
        if offset == 0:
            block_of[offset] = (key_rows, value_rows)
        else:
            block_of[offset] = shifted((key_rows, value_rows), "ctx", -offset)
    running = jnp.full((batch_rows, local_heads, shard_rows), -1e30, jnp.float32)
    totals = jnp.zeros((batch_rows, local_heads, shard_rows), jnp.float32)
    for offset in offsets:
        scores = block_scores(queries, block_of[offset][0], mask_of[offset])
        highest = jnp.maximum(running, jnp.max(scores, axis=-1))
        weights = jnp.where(mask_of[offset], jnp.exp(scores - highest[..., None]), 0.0)
        totals = totals * jnp.exp(running - highest) + jnp.sum(weights, axis=-1)
        running = highest
    log_total = running + jnp.log(totals)
    mixture = jnp.zeros((batch_rows, shard_rows, local_heads, HEAD_DIM), jnp.float32)
    for offset in offsets:
        attn_probs = probabilities(queries, block_of[offset][0], mask_of[offset], log_total)
        mixture = mixture + jnp.einsum(
            "bhqk,bkhd->bqhd",
            attn_probs.astype(jnp.bfloat16),
            block_of[offset][1],
            preferred_element_type=jnp.float32,
        )
    attended = join_heads(mixture).astype(jnp.bfloat16)
    output_part = lax.psum_scatter(
        product(attended, full_output), "tp", scatter_dimension=1, tiled=True
    )
    first_sum = inputs.astype(jnp.float32) + output_part + outputbias
    normed_first, first_normed, first_inverse = layer_norm(first_sum, norm_gain, norm_shift)
    normed_rows = lax.all_gather(normed_first.astype(jnp.bfloat16), "tp", axis=1, tiled=True)
    hidden_pre = product(normed_rows, full_up) + up_offset
    hidden_low = gelu_curve(hidden_pre).astype(jnp.bfloat16)
    down_part = lax.psum_scatter(
        product(hidden_low, full_down), "tp", scatter_dimension=1, tiled=True
    )
    second_sum = normed_first + down_part + downbias
    result, second_normed, second_inverse = layer_norm(second_sum, final_gain, final_shift)
    upstream = cotangent.astype(jnp.float32)
    finalgain_grad = jnp.sum(upstream * second_normed, axis=(0, 1))
    finalshift_grad = jnp.sum(upstream, axis=(0, 1))
    second_grad = norm_back(upstream, second_normed, second_inverse, final_gain)
    down_low = second_grad.astype(jnp.bfloat16)
    downbias_grad = jnp.sum(down_low, axis=(0, 1), dtype=jnp.float32)
    down_rows = lax.all_gather(down_low, "tp", axis=1, tiled=True)
    down_grad = weight_term(hidden_low, down_rows)
    hidden_grad = (transposed(down_rows, full_down) * gelu_slope(hidden_pre)).astype(jnp.bfloat16)
    upbias_part = jnp.sum(hidden_grad, axis=(0, 1), dtype=jnp.float32)
    up_grad = weight_term(normed_rows, hidden_grad)
    normed_grad = (
        lax.psum_scatter(transposed(hidden_grad, full_up), "tp", scatter_dimension=1, tiled=True)
        + second_grad
    )
    normgain_grad = jnp.sum(normed_grad * first_normed, axis=(0, 1))
    normshift_grad = jnp.sum(normed_grad, axis=(0, 1))
    first_grad = norm_back(normed_grad, first_normed, first_inverse, norm_gain)
    output_low = first_grad.astype(jnp.bfloat16)
    outputbias_grad = jnp.sum(output_low, axis=(0, 1), dtype=jnp.float32)
    output_rows = lax.all_gather(output_low, "tp", axis=1, tiled=True)
    output_grad = weight_term(attended, output_rows)
    mixed_grad = split_heads(transposed(output_rows, full_output).astype(jnp.bfloat16))
    row_dot = jnp.zeros((batch_rows, local_heads, shard_rows), jnp.float32)
    for offset in offsets:
        attn_probs = probabilities(queries, block_of[offset][0], mask_of[offset], log_total)
        prob_grad = jnp.einsum(
            "bqhd,bkhd->bhqk", mixed_grad, block_of[offset][1], preferred_element_type=jnp.float32
        )
        row_dot = row_dot + jnp.sum(attn_probs * prob_grad, axis=-1)
    query_acc = jnp.zeros((batch_rows, shard_rows, local_heads, HEAD_DIM), jnp.float32)
    key_parts = {}
    for offset in offsets:
        attn_probs = probabilities(queries, block_of[offset][0], mask_of[offset], log_total)
        prob_grad = jnp.einsum(
            "bqhd,bkhd->bhqk", mixed_grad, block_of[offset][1], preferred_element_type=jnp.float32
        )
        score_grad = (attn_probs * (prob_grad - row_dot[..., None])).astype(jnp.bfloat16)
        query_acc = query_acc + jnp.einsum(
            "bhqk,bkhd->bqhd", score_grad, block_of[offset][0], preferred_element_type=jnp.float32
        )
        key_term = jnp.einsum(
            "bhqk,bqhd->bkhd", score_grad, queries, preferred_element_type=jnp.float32
        )
        value_term = jnp.einsum(
            "bhqk,bqhd->bkhd",
            attn_probs.astype(jnp.bfloat16),
            mixed_grad,
            preferred_element_type=jnp.float32,
        )
        key_parts[offset] = (key_term, value_term)
    own_key, own_value = key_parts[0]
    for offset in offsets[1:]:
        back_key, back_value = shifted(for_sending(key_parts[offset]), "ctx", offset)
        own_key = own_key + back_key
        own_value = own_value + back_value
    query_pre = (
        join_heads(query_acc.astype(jnp.bfloat16)).astype(jnp.float32) * score_scale
    ).astype(jnp.bfloat16)
    key_low = join_heads(own_key.astype(jnp.bfloat16))
    value_low = join_heads(own_value.astype(jnp.bfloat16))
    querybias_part = jnp.sum(query_pre, axis=(0, 1), dtype=jnp.float32)
    valuebias_part = jnp.sum(value_low, axis=(0, 1), dtype=jnp.float32)
    query_grad = weight_term(tokens, query_pre)
    key_grad = weight_term(tokens, key_low)
    value_grad = weight_term(tokens, value_low)
    input_part = (
        transposed(query_pre, full_query)
        + transposed(key_low, full_key)
        + transposed(value_low, full_value)
    )
    input_grad = (
        lax.psum_scatter(
            input_part.astype(jnp.bfloat16), "tp", scatter_dimension=1, tiled=True
        ).astype(jnp.float32)
        + first_grad
    )
    query_grad, key_grad, value_grad, output_grad, up_grad, down_grad = (
        lax.psum_scatter(query_grad, ("dp", "ctx"), scatter_dimension=0, tiled=True),
        lax.psum_scatter(key_grad, ("dp", "ctx"), scatter_dimension=0, tiled=True),
        lax.psum_scatter(value_grad, ("dp", "ctx"), scatter_dimension=0, tiled=True),
        lax.psum_scatter(output_grad, ("dp", "ctx"), scatter_dimension=1, tiled=True),
        lax.psum_scatter(up_grad, ("dp", "ctx"), scatter_dimension=0, tiled=True),
        lax.psum_scatter(down_grad, ("dp", "ctx"), scatter_dimension=1, tiled=True),
    )
    summed = lax.psum(
        (
            placed(querybias_part, model_width, tp_place),
            placed(valuebias_part, model_width, tp_place),
            outputbias_grad,
            placed(upbias_part, hidden_width * tp_count, tp_place),
            downbias_grad,
            normgain_grad,
            normshift_grad,
            finalgain_grad,
            finalshift_grad,
        ),
        ("dp", "ctx", "tp"),
    )
    return (
        result.astype(jnp.bfloat16),
        input_grad,
        query_grad,
        key_grad,
        value_grad,
        output_grad,
        up_grad,
        down_grad,
        summed[0],
        summed[1],
        summed[2],
        summed[3],
        summed[4],
        summed[5],
        summed[6],
        summed[7],
        summed[8],
    )


MESH = pl.DeviceIdType.MESH
LOWEST = -1e30
VMEM = pl.BlockSpec(memory_space=pltpu.VMEM)
LEFT = pl.BlockSpec(memory_space=pl.ANY)


class Seat:
    def __init__(self):
        self.dp_count = lax.axis_size("dp")
        self.dp = lax.axis_index("dp")
        self.ctx = lax.axis_index("ctx")
        self.tp = lax.axis_index("tp")
        self.tp_pair = self.tp + 1 - 2 * (self.tp % 2)
        self.tp_side = (self.tp + 2) % 4
        self.tp_far = (self.tp_pair + 2) % 4
        self.pair = (self.dp, self.ctx, self.tp_pair)
        self.side = (self.dp, self.ctx, self.tp_side)
        self.twin = (self.dp, 1 - self.ctx, self.tp)
        self.above = ((self.dp + 1) % self.dp_count, self.ctx, self.tp)
        self.below = ((self.dp + self.dp_count - 1) % self.dp_count, self.ctx, self.tp)

    def meet(self, names):
        barrier = pltpu.get_barrier_semaphore()
        for name in names:
            pl.semaphore_signal(
                barrier, inc=1, device_id=getattr(self, name), device_id_type=MESH
            )
        pl.semaphore_wait(barrier, len(names))


def remote(source, target, send_sem, recv_sem, to):
    return pltpu.make_async_remote_copy(
        src_ref=source,
        dst_ref=target,
        send_sem=send_sem,
        recv_sem=recv_sem,
        device_id=to,
        device_id_type=MESH,
    )


class RingGather:
    def __init__(self, seat, shard, block, sems, at, twice=False):
        self.seat, self.shard, self.block, self.at = seat, shard, block, at
        self.own_sem, self.z_send, self.z_recv, self.y_send, self.y_recv = sems
        self.count = seat.dp_count
        self.twice = twice

    def held(self, step, other=0):
        origin = (self.seat.dp + self.count - step) % self.count
        place = self.seat.ctx if other == 0 else 1 - self.seat.ctx
        return self.block(origin * 2 + place)

    def own(self):
        return pltpu.make_async_copy(self.shard, self.held(0), self.own_sem.at[self.at])

    def z(self, step, other=0):
        source = self.shard if step == 0 and other == 0 else self.held(step, other)
        return remote(
            source,
            self.held(step, other),
            self.z_send.at[self.at, 2 * step + other],
            self.z_recv.at[self.at, 2 * step + other],
            self.seat.above,
        )

    def z_in(self, step, other=0):
        view = self.held(step + 1, other)
        return remote(
            view,
            view,
            self.z_send.at[self.at, 2 * step + other],
            self.z_recv.at[self.at, 2 * step + other],
            self.seat.above,
        )

    def y(self, step):
        source = self.shard if step == 0 else self.held(step)
        return remote(
            source,
            self.held(step),
            self.y_send.at[self.at, step],
            self.y_recv.at[self.at, step],
            self.seat.twin,
        )

    def y_in(self, step):
        view = self.held(step, 1)
        return remote(
            view,
            view,
            self.y_send.at[self.at, step],
            self.y_recv.at[self.at, step],
            self.seat.twin,
        )

    def begin(self):
        self.own().start()
        self.y(0).start()
        self.z(0).start()

    def join(self):
        self.y_in(0).wait_recv()
        self.z(0, 1).start()

    def pass_on(self, step):
        for other in range(2 if self.twice else 1):
            self.z_in(step, other).wait_recv()
            if step + 1 < self.count - 1:
                self.z(step + 1, other).start()
        if not self.twice:
            self.y(step + 1).start()

    def land(self):
        self.own().wait()
        if not self.twice:
            for step in range(self.count):
                self.y_in(step).wait_recv()

    def close(self):
        for step in range(self.count - 1):
            for other in range(2 if self.twice else 1):
                self.z(step, other).wait_send()
        for step in range(1 if self.twice else self.count):
            self.y(step).wait_send()


def dot(left_side, right_side):
    return jnp.dot(left_side, right_side, preferred_element_type=jnp.float32)


def dot_nt(left_side, right_side):
    return lax.dot_general(
        left_side, right_side, (((1,), (1,)), ((), ())), preferred_element_type=jnp.float32
    )


def dot_tn(left_side, right_side):
    return lax.dot_general(
        left_side, right_side, (((0,), (0,)), ((), ())), preferred_element_type=jnp.float32
    )


def aligned(start, size):
    return pl.ds(pl.multiple_of(start, size), size)


VECTOR_ROWS = 16
ROW_QUERY, ROW_VALUE, ROW_OUTPUT, ROW_DOWN = 0, 1, 2, 3
ROW_GAIN, ROW_SHIFT, ROW_FINAL_GAIN, ROW_FINAL_SHIFT, ROW_UP = 4, 5, 6, 7, 8


class TokenScatter:
    def __init__(self, seat, buffers, sems, at, slot):
        self.seat, self.at, self.slot = seat, at, slot
        self.pair_out, self.pair_in, self.side_out, self.side_in = buffers
        self.send, self.recv = sems

    def copy(self, k):
        at, seat, slot = self.at, self.seat, self.slot
        if k < 2:
            source, target, to = self.pair_out.at[slot, k], self.pair_in.at[slot, k], seat.pair
        else:
            source, target, to = self.side_out.at[slot], self.side_in.at[slot], seat.side
        return remote(source, target, self.send.at[at, k], self.recv.at[at, k], to)

    def give(self, compute, total):
        seat, at = self.seat, self.slot
        part = self.side_out.shape[1]
        group = seat.tp // 2
        mine = aligned((seat.tp % 2) * part, part)
        others = aligned((1 - seat.tp % 2) * part, part)
        compute(1 - group)
        self.pair_out[at, 0] = total[others, :].astype(jnp.bfloat16)
        self.copy(0).start()
        self.side_out[at] = total[mine, :].astype(jnp.bfloat16)
        compute(group)
        self.pair_out[at, 1] = total[others, :].astype(jnp.bfloat16)
        self.copy(1).start()
        self.copy(0).wait_recv()
        self.side_out[at] = (
            self.side_out[at].astype(jnp.float32) + self.pair_in[at, 0].astype(jnp.float32)
        ).astype(jnp.bfloat16)
        self.copy(2).start()
        return mine

    def take(self):
        self.copy(1).wait_recv()
        self.copy(2).wait_recv()
        return self.pair_in[self.slot, 1].astype(jnp.float32) + self.side_in[self.slot].astype(
            jnp.float32
        )

    def close(self):
        for k in range(3):
            self.copy(k).wait_send()


class TokenGather:
    def __init__(self, seat, full, b, part, sems, at):
        self.seat = seat
        self.send, self.recv = sems
        self.at = at
        self.view = lambda place: full.at[b, aligned(place * part, part), :]

    def copy(self, k, place, to):
        view = self.view(place)
        return remote(view, view, self.send.at[self.at, k], self.recv.at[self.at, k], to)

    def give(self):
        seat = self.seat
        self.copy(0, seat.tp, seat.side).start()
        self.copy(1, seat.tp, seat.pair).start()

    def relay(self):
        seat = self.seat
        self.copy(0, seat.tp_side, seat.side).wait_recv()
        self.copy(2, seat.tp_side, seat.pair).start()

    def land(self):
        seat = self.seat
        self.copy(1, seat.tp_pair, seat.pair).wait_recv()
        self.copy(2, seat.tp_far, seat.pair).wait_recv()

    def close(self):
        seat = self.seat
        for k, place in ((0, seat.tp), (1, seat.tp), (2, seat.tp_side)):
            self.copy(k, place, seat.pair).wait_send()


def row_mean(rows):
    return jnp.mean(rows, axis=-1, keepdims=True)


class PairedReduce:
    def __init__(self, seat, partial, block, twin_in, ring_out, ring_in, sems, at):
        self.seat, self.partial, self.block, self.at = seat, partial, block, at
        self.twin_in, self.ring_out, self.ring_in = twin_in, ring_out, ring_in
        self.y_send, self.y_recv, self.z_send, self.z_recv = sems
        self.count = seat.dp_count

    def mine(self, step, ctx):
        owner = (self.seat.dp + 2 * self.count - 1 - step) % self.count
        return self.block(self.partial, owner * 2 + ctx)

    def y(self, step):
        return remote(
            self.mine(step, 1 - self.seat.ctx),
            self.twin_in.at[step],
            self.y_send.at[self.at, step],
            self.y_recv.at[self.at, step],
            self.seat.twin,
        )

    def z(self, step):
        return remote(
            self.ring_out(step),
            self.ring_in.at[step],
            self.z_send.at[self.at, step],
            self.z_recv.at[self.at, step],
            self.seat.above,
        )

    def begin(self):
        for step in range(self.count):
            self.y(step).start()

    def advance(self, step):
        self.y(step).wait_recv()
        total = self.mine(step, self.seat.ctx)[...].astype(jnp.float32) + self.twin_in[
            step
        ].astype(jnp.float32)
        if step > 0:
            self.z(step - 1).wait_recv()
            total = total + self.ring_in[step - 1].astype(jnp.float32)
        if step == self.count - 1:
            return total
        self.ring_out(step)[...] = total.astype(jnp.bfloat16)
        self.z(step).start()

    def close(self):
        for step in range(self.count):
            self.y(step).wait_send()
        for step in range(self.count - 1):
            self.z(step).wait_send()


class RingReduce:
    def __init__(self, seat, partial, pair, ring_out, ring_in, half_out, half_in, sems, at):
        self.seat, self.partial, self.pair, self.at = seat, partial, pair, at
        self.ring_out, self.ring_in, self.half_out, self.half_in = ring_out, ring_in, half_out, half_in
        self.y_send, self.y_recv, self.z_send, self.z_recv = sems
        self.count = seat.dp_count

    def mine(self, step):
        owner = (self.seat.dp + 2 * self.count - 1 - step) % self.count
        return self.pair(self.partial, owner)

    def z(self, step):
        return remote(
            self.mine(0) if step == 0 else self.ring_out(step - 1),
            self.ring_in.at[step],
            self.z_send.at[self.at, step],
            self.z_recv.at[self.at, step],
            self.seat.above,
        )

    def y(self):
        return remote(
            self.half_out,
            self.half_in,
            self.y_send.at[self.at, 0],
            self.y_recv.at[self.at, 0],
            self.seat.twin,
        )

    def begin(self):
        self.z(0).start()

    def advance(self, step):
        self.z(step - 1).wait_recv()
        total = self.mine(step)[...].astype(jnp.float32) + self.ring_in[step - 1].astype(
            jnp.float32
        )
        if step == self.count - 1:
            return total
        self.ring_out(step - 1)[...] = total.astype(jnp.bfloat16)
        self.z(step).start()

    def close(self):
        self.y().wait_send()
        for step in range(self.count - 1):
            self.z(step).wait_send()


class Parts:
    def __init__(self, names, refs):
        self.__dict__.update(zip(names, refs))


def layer_kernel(names, *refs):
    r = Parts(names, refs)
    seat = Seat()
    count = seat.dp_count
    hops = count - 1
    batch, part, width = r.result.shape
    rows = r.tokens.shape[1]
    local = r.query_full.shape[1]
    hidden = r.up_full.shape[1]
    heads = local // HEAD_DIM
    depth = width // (2 * count)
    wide = 512
    f32, bf16 = jnp.float32, jnp.bfloat16

    barrier = pltpu.get_barrier_semaphore()
    around = [((seat.dp + away) % count, seat.ctx, seat.tp) for away in range(1, count)]
    for to in [seat.pair, seat.side, seat.twin] + around:
        pl.semaphore_signal(barrier, inc=1, device_id=to, device_id_type=MESH)
    pl.semaphore_wait(barrier, 2 + count)

    def over(tiles, body):
        def one(index, carry):
            body(index)
            return carry

        lax.fori_loop(0, tiles, one, 0)

    def over_heads(body, services):
        def one(h):
            for when, service in services:
                pl.when(h == when)(service)
            body(h)

        over(heads, one)

    def cut(half, place):
        return lambda b: half.at[b, aligned(place * part, part), :]

    def token_copy(relation, b, source, target, to):
        at = 2 * relation + b
        return remote(source(b), target(b), r.token_send.at[at], r.token_recv.at[at], to)

    here, there = cut(r.tokens, seat.tp), cut(r.other, seat.tp)
    here_side, there_side = cut(r.tokens, seat.tp_side), cut(r.other, seat.tp_side)
    given = lambda b: r.inputs.at[b]
    landed = [
        cut(r.tokens, seat.tp_pair),
        here_side,
        there,
        there_side,
        cut(r.tokens, seat.tp_far),
        cut(r.other, seat.tp_pair),
        cut(r.other, seat.tp_far),
    ]

    def token_out(relation, b):
        return token_copy(
            relation,
            b,
            *(
                (given, here, seat.pair),
                (given, here, seat.side),
                (given, there, seat.twin),
                (there, there, seat.side),
                (here_side, here_side, seat.pair),
                (there, there, seat.pair),
                (there_side, there_side, seat.pair),
            )[relation],
        )

    def token_in(relation, b):
        token_copy(relation, b, landed[relation], landed[relation], seat.pair).wait_recv()

    own_tokens = [
        pltpu.make_async_copy(r.inputs.at[b], here(b), r.local_sem.at[b]) for b in range(batch)
    ]
    upstream = lambda b: r.weight_low.at[0, b * part : (b + 1) * part, :]
    own_cotangent = [
        pltpu.make_async_copy(r.cotangent.at[b], upstream(b), r.local_sem.at[batch + b])
        for b in range(batch)
    ]
    for copy in own_tokens + own_cotangent:
        copy.start()

    def by_rows(full):
        return lambda at: full.at[aligned(at * depth, depth), :]

    def by_columns(full):
        return lambda at: full.at[:, aligned(at * depth, depth)]

    def by_half_rows(half):
        def view(full):
            return lambda at: full.at[aligned(at * depth + half * (depth // 2), depth // 2), :]

        return view

    gather_sems = (r.own_sem, r.gz_send, r.gz_recv, r.gy_send, r.gy_recv)
    weights = [
        RingGather(seat, shard, view(full), gather_sems, at, twice)
        for at, (shard, full, view, twice) in enumerate(
            (
                (r.query_weight, r.query_full, by_rows, False),
                (r.key_weight, r.key_full, by_rows, True),
                (r.value_weight, r.value_full, by_rows, True),
                (r.output_weight, r.output_full, by_columns, False),
                (r.up_weight.at[: depth // 2, :], r.up_full, by_half_rows(0), False),
                (r.up_weight.at[depth // 2 :, :], r.up_full, by_half_rows(1), True),
                (r.down_weight, r.down_full, by_columns, False),
            )
        )
    ]
    to_output, to_up, to_up_too, to_down = weights[3:]
    to_query, to_key, to_value = weights[:3]
    to_value.begin()
    to_key.begin()
    for b in range(batch):
        token_out(1, b).start()
        token_out(2, b).start()
        token_out(0, b).start()
    to_query.begin()
    to_output.begin()
    to_value.join()
    to_key.join()
    for weight in (to_value, to_key, to_query):
        weight.pass_on(0)
    to_up.begin()
    token_in(1, 0)
    token_out(4, 0).start()
    token_in(2, 0)
    token_out(3, 0).start()
    token_out(5, 0).start()
    for weight in (to_value, to_key, to_query):
        weight.pass_on(1)
    to_output.pass_on(0)
    token_in(1, 1)
    token_out(4, 1).start()
    token_in(2, 1)
    token_out(3, 1).start()
    token_out(5, 1).start()
    to_up_too.begin()
    for weight in (to_value, to_key, to_query):
        weight.pass_on(2)
    to_output.pass_on(1)
    to_up.pass_on(0)
    to_up_too.join()
    to_down.begin()

    for b in range(batch):
        for half in range(2):
            row_ids = r.ids[b : b + 1, aligned((seat.ctx if half == 0 else 1 - seat.ctx) * rows, rows)]
            spread = jnp.broadcast_to(row_ids.astype(f32), (128, rows))
            r.ids_down[b, half * rows : (half + 1) * rows, :] = spread.T
    bias_at = aligned(seat.tp * local, local)
    query_offset = r.query_bias[:, bias_at]
    value_offset = r.value_bias[:, bias_at]
    tile_rows = rows // 2
    for weight in weights[:3]:
        weight.land()
    for copy in own_tokens:
        copy.wait()
    for b in range(batch):
        token_in(0, b)
        token_in(4, b)

    def project(half_ref, half):
        def one(index):
            b, piece = index // 2, index % 2
            block = half_ref[b, aligned(piece * tile_rows, tile_rows), :]
            spot = aligned(half * rows + piece * tile_rows, tile_rows)
            if half == 0:
                scaled = (dot(block, r.query_full[...]) + query_offset) * HEAD_DIM ** (-0.5)
                r.queries[b, aligned(piece * tile_rows, tile_rows), :] = scaled.astype(bf16)
            r.keys[b, spot, :] = dot(block, r.key_full[...]).astype(bf16)
            value_rows = dot(block, r.value_full[...]) + value_offset
            r.values[b, spot, :] = value_rows.astype(bf16)
            r.flipped[b, :, spot] = value_rows.T.astype(bf16)

        over(batch * 2, one)

    project(r.tokens, 0)
    to_output.pass_on(2)
    to_up_too.pass_on(0)
    for b in range(batch):
        token_in(3, b)
        token_out(6, b).start()
        token_in(5, b)
        token_in(6, b)
    project(r.other, 1)

    lane_head = lax.broadcasted_iota(jnp.int32, (1, local), 1) // HEAD_DIM
    nothing = jnp.zeros((), bf16)

    def own_ids(b):
        return r.ids[b : b + 1, aligned(seat.ctx * rows, rows)].astype(f32)

    def attend(b, services):
        row_ids = own_ids(b)

        def one(h):
            own = aligned(h * HEAD_DIM, HEAD_DIM)
            chosen = jnp.where(lane_head == h, r.queries[b], nothing)
            same = jnp.tile(r.ids_down[b], (1, rows // 128)) == row_ids
            scores = jnp.where(same, dot_nt(r.keys[b], chosen), LOWEST)
            highest = jnp.max(scores, axis=0, keepdims=True)
            raised = jnp.exp(scores - highest)
            total = jnp.sum(raised, axis=0, keepdims=True)
            shares = (raised * (1.0 / total)).astype(bf16)
            r.mixture[b, own, :] = dot(r.flipped[b, own, :], shares)
            r.logs[b * heads + h] = highest + jnp.log(total)

        over_heads(one, services)
        r.attended[b] = r.mixture[b].T.astype(bf16)

    def passing(step, *which):
        def service():
            for weight in which:
                weight.pass_on(step)

        return service

    to_output.land()

    scatter_parts = (r.pair_out, r.pair_in, r.side_out, r.side_in)
    scatters = [
        TokenScatter(seat, scatter_parts, (r.scatter_send, r.scatter_recv), at, slot)
        for at, slot in list(enumerate(range(3 * batch)))
        + [(3 * batch + at, at) for at in range(2 * batch)]
    ]
    gathers = [
        TokenGather(seat, full, b, part, (r.gather_send, r.gather_recv), k * batch + b)
        for k, full in enumerate((r.normed_rows, r.down_rows, r.output_rows))
        for b in range(batch)
    ]

    def spread_rows(lhs_ref, b, weight, flipped):
        def compute(group):
            lhs = lhs_ref[b, aligned(group * 2 * part, 2 * part), :]

            def tile(index):
                at = aligned(index * wide, wide)
                if flipped:
                    r.total[:, at] = dot_nt(lhs, weight[at, :])
                else:
                    r.total[:, at] = dot(lhs, weight[:, at])

            over(width // wide, tile)

        return compute

    def scatter(k, b, lhs_ref, weight, flipped):
        mine = scatters[k * batch + b].give(spread_rows(lhs_ref, b, weight, flipped), r.total)
        r.total_own[b] = r.total[mine, :]

    def collected(k, b):
        return r.total_own[b] + scatters[k * batch + b].take()

    own_rows = aligned(seat.tp * part, part)
    r.sums[...] = jnp.zeros_like(r.sums)
    up_sum = r.sums.at[pl.ds(ROW_UP + seat.tp, 1), :]

    def add_vector(row, values):
        r.sums[row : row + 1, :] += jnp.sum(values, axis=0, keepdims=True)

    def first_norm(b):
        first_sum = r.tokens[b, own_rows, :].astype(f32) + (collected(0, b) + r.output_bias[...])
        center = first_sum - row_mean(first_sum)
        inverse = lax.rsqrt(row_mean(center * center) + 1e-05)
        normed = center * inverse
        scaled = normed * r.norm_gain[...] + r.norm_shift[...]
        r.keep[0, b] = normed
        r.keep[1, b] = scaled
        r.inverse_keep[b] = inverse
        r.normed_rows[b, own_rows, :] = scaled.astype(bf16)
        gathers[b].give()

    def raise_up(b):
        gathers[b].land()
        lhs = r.normed_rows[b]

        def tile(index):
            at = aligned(index * wide, wide)
            offset = r.up_bias[:, pl.ds(pl.multiple_of(seat.tp * hidden + index * wide, wide), wide)]
            pre = dot(lhs, r.up_full[:, at]) + offset
            half = 0.5 * (1.0 + lax.erf(pre * 0.7071067811865476))
            r.hidden_rows[b, :, at] = (pre * half).astype(bf16)
            slope = half + pre * jnp.exp(-0.5 * pre * pre) * 0.3989422804014327
            r.slope_rows[b, :, at] = slope.astype(bf16)

        over(hidden // wide, tile)

    def second_norm(b):
        second_sum = r.keep[1, b] + (collected(1, b) + r.down_bias[...])
        center = second_sum - row_mean(second_sum)
        inverse = lax.rsqrt(row_mean(center * center) + 1e-05)
        normed = center * inverse
        r.result[b] = (normed * r.final_gain[...] + r.final_shift[...]).astype(bf16)
        gradient = upstream(b)[...].astype(f32)
        add_vector(ROW_FINAL_GAIN, gradient * normed)
        add_vector(ROW_FINAL_SHIFT, gradient)
        scaled = gradient * r.final_gain[...]
        second = inverse * (scaled - row_mean(scaled) - normed * row_mean(scaled * normed))
        r.keep[2, b] = second
        low = second.astype(bf16)
        r.down_rows[b, own_rows, :] = low
        gathers[batch + b].give()
        add_vector(ROW_DOWN, low.astype(f32))

    def lower(b):
        gathers[batch + b].land()
        lhs = r.down_rows[b]

        def tile(index):
            at = aligned(index * wide, wide)
            back = dot_nt(lhs, r.down_full[at, :]) * r.slope_rows[b, :, at].astype(f32)
            back = back.astype(bf16)
            r.back_rows[b, :, at] = back
            up_sum[:, at] += jnp.sum(back.astype(f32), axis=0, keepdims=True)

        over(hidden // wide, tile)

    def first_back(b):
        grad = collected(2, b) + r.keep[2, b]
        normed = r.keep[0, b]
        add_vector(ROW_GAIN, grad * normed)
        add_vector(ROW_SHIFT, grad)
        scaled = grad * r.norm_gain[...]
        first = r.inverse_keep[b] * (
            scaled - row_mean(scaled) - normed * row_mean(scaled * normed)
        )
        r.input_grad[b] = first
        low = first.astype(bf16)
        r.output_rows[b, own_rows, :] = low
        gathers[2 * batch + b].give()
        add_vector(ROW_OUTPUT, low.astype(f32))

    def mix_back(b):
        gathers[2 * batch + b].land()
        r.mixed[b] = dot_nt(r.output_rows[b], r.output_full[...]).astype(bf16)

    def owner_at(step):
        return (seat.dp + 2 * count - 1 - step) % count

    def output_tiles():
        left = r.attended[...].reshape(batch * rows, local)

        def tile(index):
            at = aligned(index * wide, wide)
            right = r.output_rows[:, :, at].reshape(batch * rows, wide)
            r.output_part[:, at] = dot_tn(left, right).astype(bf16)

        over(width // wide, tile)

    def down_tiles(first, last):
        left = r.hidden_rows[...].reshape(batch * rows, hidden)

        def tile(index):
            at = aligned(owner_at(first + index) * 2 * depth, 2 * depth)
            right = r.down_rows[:, :, at].reshape(batch * rows, 2 * depth)
            term = dot_tn(left, right).astype(bf16)
            r.slope_rows[:, :, at] = term.reshape(batch, rows, 2 * depth)

        over(last - first, tile)
        for step in range(first, last):
            from_down.y(step).start()

    def up_tiles():
        left = r.normed_rows[...].reshape(batch * rows, width)

        def tile(index):
            at = aligned(index * wide, wide)
            right = r.back_rows[:, :, at].reshape(batch * rows, wide)
            r.hidden_rows[:, :, at] = dot_tn(left, right).astype(bf16).reshape(batch, rows, wide)

        over(hidden // wide, tile)
        from_up.begin()
        from_up_too.begin()

    reduce_sems = (r.ry_send, r.ry_recv, r.rz_send, r.rz_recv)
    columns = lambda ref, at: ref.at[:, aligned(at * depth, depth)]
    thin = [
        RingReduce(
            seat, r.weight_low.at[k],
            lambda ref, owner: ref.at[:, aligned(owner * 2 * depth, 2 * depth)],
            (lambda step, k=k: r.wide_out.at[k, step]), r.wide_in.at[k],
            r.half_out.at[k], r.half_in.at[k], reduce_sems, k,
        )
        for k in range(2)
    ]
    from_value = PairedReduce(
        seat, r.weight_low.at[2], columns,
        r.value_twin, (lambda step: r.value_out.at[step]), r.value_in, reduce_sems, 2,
    )
    from_output = PairedReduce(
        seat, r.output_part, columns, r.output_twin, (lambda step: r.output_out.at[step]), r.output_in, reduce_sems, 3
    )
    from_down = PairedReduce(
        seat, r.slope_rows, lambda ref, at: ref.at[:, :, aligned(at * depth, depth)],
        r.down_twin, (lambda step: r.down_rows.at[:, :, step * depth : (step + 1) * depth]), r.down_in, reduce_sems, 4,
    )
    held = rows // depth

    split = hidden // 2
    from_up = PairedReduce(
        seat, r.hidden_rows,
        lambda ref, at: ref.at[at // held, aligned((at % held) * depth, depth), :split],
        r.up_twin, (lambda step: r.back_rows.at[0, step * depth : (step + 1) * depth, :split]),
        r.up_in, reduce_sems, 5,
    )
    pairs = held // 2
    from_up_too = RingReduce(
        seat, r.hidden_rows,
        lambda ref, owner: ref.at[
            owner // pairs, aligned((owner % pairs) * 2 * depth, 2 * depth), split:
        ],
        (lambda step: r.back_rows.at[1, step * 2 * depth : (step + 1) * 2 * depth, split:]),
        r.up_pair_in, r.up_half_out, r.up_half_in, reduce_sems, 6,
    )

    attend(0, [(3, passing(0, to_down))])
    scatter(0, 0, r.attended, r.output_full, False)
    to_up.pass_on(1)
    attend(1, [(3, passing(1, to_up_too))])
    scatter(0, 1, r.attended, r.output_full, False)
    first_norm(0)
    to_down.pass_on(1)
    to_up.pass_on(2)
    first_norm(1)
    gathers[0].relay()
    to_up_too.pass_on(2)
    to_up.land()
    to_up_too.land()
    raise_up(0)
    gathers[1].relay()
    to_down.pass_on(2)
    raise_up(1)
    to_down.land()
    scatter(1, 0, r.hidden_rows, r.down_full, False)
    scatter(1, 1, r.hidden_rows, r.down_full, False)
    for copy in own_cotangent:
        copy.wait()
    second_norm(0)
    second_norm(1)
    gathers[batch].relay()
    lower(0)
    gathers[batch + 1].relay()
    scatter(2, 0, r.back_rows, r.up_full, True)
    lower(1)
    scatter(2, 1, r.back_rows, r.up_full, True)
    down_tiles(0, count)
    first_back(0)
    up_tiles()
    first_back(1)
    for piece in gathers[batch : 2 * batch]:
        piece.close()
    gathers[2 * batch].relay()
    mix_back(0)

    key_flip = r.flipped.at[0]

    def heads_back(b, services):
        key_flip[...] = r.keys[b].astype(f32).T.astype(bf16)
        product_rows = r.mixed[b].astype(f32).T * r.mixture[b]
        for h in range(heads):
            r.row_dots[h] = jnp.sum(
                product_rows[h * HEAD_DIM : (h + 1) * HEAD_DIM], axis=0, keepdims=True
            )
        r.key_sum[...] = jnp.zeros_like(r.key_sum)
        r.value_sum[...] = jnp.zeros_like(r.value_sum)
        row_ids = own_ids(b)

        def one(h):
            own = aligned(h * HEAD_DIM, HEAD_DIM)
            query_rows = jnp.where(lane_head == h, r.queries[b], nothing)
            grad_rows = jnp.where(lane_head == h, r.mixed[b], nothing)
            same = jnp.tile(r.ids_down[b], (1, rows // 128)) == row_ids
            scores = jnp.where(same, dot_nt(r.keys[b], query_rows), LOWEST)
            probs = jnp.exp(scores - r.logs[b * heads + h])
            r.value_sum[...] += dot(probs.astype(bf16), grad_rows)
            prob_grad = dot_nt(r.values[b], grad_rows)
            score_grad = (probs * (prob_grad - r.row_dots[h])).astype(bf16)
            r.key_sum[...] += dot(score_grad, query_rows)
            r.query_flip[own, :] = dot(key_flip[own, :], score_grad)

        over_heads(one, services)

    lows = lambda k: slice(k * local, (k + 1) * local)
    low_rows = (r.normed_rows, r.output_rows)

    def sequence_back(b):
        flipped = (r.query_flip[...].astype(bf16).astype(f32) * HEAD_DIM ** (-0.5)).astype(bf16)
        upright = flipped.astype(f32).T
        key_low = r.key_sum[...].astype(bf16)
        value_low = r.value_sum[...].astype(bf16)
        low_rows[b][0, :, lows(0)] = upright.astype(bf16)
        for half in range(2):
            low_rows[b][half, :, lows(1)] = key_low[half * rows : (half + 1) * rows]
            low_rows[b][half, :, lows(2)] = value_low[half * rows : (half + 1) * rows]
        r.sums[ROW_QUERY : ROW_QUERY + 1, bias_at] += jnp.sum(upright, axis=0, keepdims=True)
        r.sums[ROW_VALUE : ROW_VALUE + 1, bias_at] += jnp.sum(
            value_low.astype(f32), axis=0, keepdims=True
        )
        flips = [flipped, key_low.astype(f32).T.astype(bf16), value_low.astype(f32).T.astype(bf16)]

        for k in range(3):
            def tile(index, k=k):
                at = aligned(index * wide, wide)
                term = dot(flips[k][:, :rows], r.tokens[b, :, at])
                if k > 0:
                    term = term + dot(flips[k][:, rows:], r.other[b, :, at])
                if b > 0:
                    term = term + r.keep[k, :, :, at].reshape(local, wide)
                if b == batch - 1:
                    r.weight_low[k, :, at] = term.astype(bf16)
                else:
                    r.keep[k, :, :, at] = term.reshape(2, local // 2, wide)

            over(width // wide, tile)

    def input_back(b, half):
        def compute(group):
            at = aligned(group * 2 * part, 2 * part)

            def tile(index):
                row_at = aligned(index * wide, wide)
                term = dot_nt(low_rows[b][half, at, lows(1)], r.key_full[row_at, :]) + dot_nt(
                    low_rows[b][half, at, lows(2)], r.value_full[row_at, :]
                )
                if half == 0:
                    term = term + dot_nt(
                        low_rows[b][half, at, lows(0)], r.query_full[row_at, :]
                    )
                r.total[:, row_at] = term

            over(width // wide, tile)

        mine = scatters[3 * batch + 2 * b + half].give(compute, r.total)
        r.total_own[2 * b + half] = r.total[mine, :]

    def other_copy(b):
        return remote(
            r.side_out.at[2 * batch + b],
            r.side_in.at[2 * batch + b],
            r.other_send.at[b],
            r.other_recv.at[b],
            seat.twin,
        )

    def other_give(b):
        r.side_out[2 * batch + b] = (
            r.total_own[2 * b + 1] + scatters[3 * batch + 2 * b + 1].take()
        ).astype(bf16)
        other_copy(b).start()

    def input_take(b):
        own = r.total_own[2 * b] + scatters[3 * batch + 2 * b].take()
        other_copy(b).wait_recv()
        r.input_grad[b] = (own + r.side_in[2 * batch + b].astype(f32)) + r.input_grad[b]

    def stepping(step, *which):
        def service():
            for piece in which:
                piece.advance(step)

        return service

    def down_done():
        r.down_grad[...] = from_down.advance(hops).reshape(hidden, depth)

    stepping(0, from_down)()
    heads_back(0, [(0, gathers[2 * batch + 1].relay), (1, stepping(1, from_down)), (3, stepping(1, from_up_too))])
    mix_back(1)
    output_tiles()
    from_output.begin()
    stepping(2, from_down)()
    for piece in scatters[: 3 * batch] + gathers[:batch] + gathers[2 * batch :]:
        piece.close()
    sequence_back(0)
    input_back(0, 1)
    stepping(0, from_up)()
    input_back(0, 0)
    heads_back(1, [(0, down_done), (1, stepping(1, from_up)), (2, stepping(0, from_output)), (3, lambda: other_give(0))])
    stepping(2, from_up_too)()
    stepping(1, from_output)()
    sequence_back(1)
    from_value.begin()
    thin[0].begin()
    thin[1].begin()
    input_back(1, 1)
    stepping(2, from_up)()
    stepping(0, from_value)()
    input_back(1, 0)
    stepping(1, *thin)()

    def sum_copy(stage, to):
        return remote(
            r.sum_all.at[stage], r.sum_in.at[stage], r.sum_send.at[stage], r.sum_recv.at[stage], to
        )

    def sum_stage(stage, to):
        r.sum_all[stage] = r.sums[...]
        sum_copy(stage, to).start()

    def sum_add(stage, to):
        sum_copy(stage, to).wait_recv()
        r.sums[...] = r.sums[...] + r.sum_in[stage]

    def around_copy(away):
        stage = 4 + away
        return remote(
            r.sum_all.at[3], r.sum_in.at[stage], r.sum_send.at[stage], r.sum_recv.at[stage], around[away]
        )

    def halve(piece, at):
        r.total[:, at] = piece.advance(hops)

    mine_at = aligned(seat.ctx * depth, depth)
    other_at = aligned((1 - seat.ctx) * depth, depth)
    sum_stage(0, seat.pair)
    input_take(0)
    sum_add(0, seat.pair)
    sum_stage(1, seat.side)
    other_give(1)
    stepping(1, from_value)()
    stepping(2, from_output)()
    sum_add(1, seat.side)
    sum_stage(2, seat.twin)
    stepping(2, *thin)()
    r.up_grad[:, :split] = from_up.advance(hops)
    halve(from_up_too, slice(split, hidden))
    r.up_half_out[...] = r.total[other_at, split:].astype(bf16)
    from_up_too.y().start()
    sum_add(2, seat.twin)
    r.sum_all[3] = r.sums[...]
    for away in range(hops):
        around_copy(away).start()
    stepping(2, from_value)()
    r.output_grad[...] = from_output.advance(hops)
    input_take(1)
    for k in range(2):
        halve(thin[k], slice(k * 2 * depth, (k + 1) * 2 * depth))
        spot = aligned(k * 2 * depth + (1 - seat.ctx) * depth, depth)
        r.half_out[k] = r.total[:, spot].astype(bf16)
        thin[k].y().start()
    from_up_too.y().wait_recv()
    r.up_grad[:, split:] = r.total[mine_at, split:] + r.up_half_in[...].astype(f32)
    r.value_grad[...] = from_value.advance(hops).T
    r.sum_in[3] = r.sums[...]
    for away in range(hops):
        around_copy(away).wait_recv()
    gathered = jnp.zeros_like(r.sums[...])
    for origin in range(count):
        gathered = gathered + r.sum_in[3 + (seat.dp + count - origin) % count]
    r.sums[...] = gathered
    for k, target in enumerate((r.query_grad, r.key_grad)):
        thin[k].y().wait_recv()
        spot = aligned(k * 2 * depth + seat.ctx * depth, depth)
        target[...] = (r.total[:, spot] + r.half_in[k].astype(f32)).T

    for stage, to in enumerate((seat.pair, seat.side, seat.twin)):
        sum_copy(stage, to).wait_send()
    for away in range(hops):
        around_copy(away).wait_send()
    for b in range(batch):
        other_copy(b).wait_send()
    for relation in range(7):
        for b in range(batch):
            token_out(relation, b).wait_send()
    for piece in weights + scatters[3 * batch :] + thin + [from_value, from_output, from_down, from_up, from_up_too]:
        piece.close()


def layer_call(inputs, segment_ids, cotangent, shards, vectors):
    count = lax.axis_size("dp")
    batch, part, width = inputs.shape
    rows = part * lax.axis_size("tp")
    local = shards[0].shape[1]
    hidden = shards[4].shape[1]
    heads = local // HEAD_DIM
    depth = width // (2 * count)
    bf16, f32 = jnp.bfloat16, jnp.float32
    ins = [
        ("inputs", LEFT),
        ("cotangent", LEFT),
        ("query_weight", LEFT),
        ("key_weight", LEFT),
        ("value_weight", LEFT),
        ("output_weight", LEFT),
        ("up_weight", LEFT),
        ("down_weight", LEFT),
        ("ids", VMEM),
        ("query_bias", VMEM),
        ("value_bias", VMEM),
        ("output_bias", VMEM),
        ("up_bias", VMEM),
        ("down_bias", VMEM),
        ("norm_gain", VMEM),
        ("norm_shift", VMEM),
        ("final_gain", VMEM),
        ("final_shift", VMEM),
    ]
    outs = [
        ("result", (batch, part, width), bf16),
        ("input_grad", (batch, part, width), f32),
        ("query_grad", (depth, local), f32),
        ("key_grad", (depth, local), f32),
        ("value_grad", (depth, local), f32),
        ("output_grad", (local, depth), f32),
        ("up_grad", (depth, hidden), f32),
        ("down_grad", (hidden, depth), f32),
        ("sums", (VECTOR_ROWS, width), f32),
    ]
    scratch = [
        ("tokens", (batch, rows, width), bf16),
        ("other", (batch, rows, width), bf16),
        ("query_full", (width, local), bf16),
        ("key_full", (width, local), bf16),
        ("value_full", (width, local), bf16),
        ("output_full", (local, width), bf16),
        ("up_full", (width, hidden), bf16),
        ("down_full", (hidden, width), bf16),
        ("queries", (batch, rows, local), bf16),
        ("keys", (batch, 2 * rows, local), bf16),
        ("values", (batch, 2 * rows, local), bf16),
        ("flipped", (batch, local, 2 * rows), bf16),
        ("mixture", (batch, local, rows), f32),
        ("logs", (batch * heads, 1, rows), f32),
        ("attended", (batch, rows, local), bf16),
        ("ids_down", (batch, 2 * rows, 128), f32),
        ("normed_rows", (batch, rows, width), bf16),
        ("hidden_rows", (batch, rows, hidden), bf16),
        ("slope_rows", (batch, rows, hidden), bf16),
        ("down_rows", (batch, rows, width), bf16),
        ("back_rows", (batch, rows, hidden), bf16),
        ("output_rows", (batch, rows, width), bf16),
        ("keep", (3, batch, part, width), f32),
        ("inverse_keep", (batch, part, 1), f32),
        ("total_own", (2 * batch, part, width), f32),
        ("total", (2 * part, width), f32),
        ("pair_out", (3 * batch, 2, part, width), bf16),
        ("pair_in", (3 * batch, 2, part, width), bf16),
        ("side_out", (3 * batch, part, width), bf16),
        ("side_in", (3 * batch, part, width), bf16),
        ("mixed", (batch, rows, local), bf16),
        ("output_part", (local, width), bf16),
        ("row_dots", (heads, 1, rows), f32),
        ("query_flip", (local, rows), f32),
        ("key_sum", (2 * rows, local), f32),
        ("value_sum", (2 * rows, local), f32),
        ("weight_low", (3, local, width), bf16),
        ("wide_out", (2, count - 2, local, 2 * depth), bf16),
        ("wide_in", (2, count - 1, local, 2 * depth), bf16),
        ("half_out", (2, local, depth), bf16),
        ("half_in", (2, local, depth), bf16),
        ("value_twin", (count, local, depth), bf16),
        ("value_out", (count - 1, local, depth), bf16),
        ("value_in", (count - 1, local, depth), bf16),
        ("output_twin", (count, local, depth), bf16),
        ("output_out", (count - 1, local, depth), bf16),
        ("output_in", (count - 1, local, depth), bf16),
        ("down_twin", (count, batch, rows, depth), bf16),
        ("down_in", (count - 1, batch, rows, depth), bf16),
        ("up_twin", (count, depth, hidden // 2), bf16),
        ("up_in", (count - 1, depth, hidden // 2), bf16),
        ("up_pair_in", (count - 1, 2 * depth, hidden // 2), bf16),
        ("up_half_out", (depth, hidden // 2), bf16),
        ("up_half_in", (depth, hidden // 2), bf16),
        ("sum_in", (3 + count, VECTOR_ROWS, width), f32),
        ("sum_all", (4, VECTOR_ROWS, width), f32),
    ]
    sems = [
        ("local_sem", (2 * batch,)),
        ("token_send", (14,)),
        ("token_recv", (14,)),
        ("own_sem", (7,)),
        ("gz_send", (7, 2 * (count - 1))),
        ("gz_recv", (7, 2 * (count - 1))),
        ("gy_send", (7, count)),
        ("gy_recv", (7, count)),
        ("scatter_send", (5 * batch, 3)),
        ("scatter_recv", (5 * batch, 3)),
        ("gather_send", (3 * batch, 3)),
        ("gather_recv", (3 * batch, 3)),
        ("other_send", (batch,)),
        ("other_recv", (batch,)),
        ("sum_send", (3 + count,)),
        ("sum_recv", (3 + count,)),
        ("ry_send", (7, count)),
        ("ry_recv", (7, count)),
        ("rz_send", (7, count - 1)),
        ("rz_recv", (7, count - 1)),
    ]
    names = [item[0] for group in (ins, outs, scratch, sems) for item in group]
    return pl.pallas_call(
        functools.partial(layer_kernel, names),
        name="layer",
        out_shape=[jax.ShapeDtypeStruct(shape, kind) for _, shape, kind in outs],
        in_specs=[space for _, space in ins],
        out_specs=[VMEM] * len(outs),
        scratch_shapes=[pltpu.VMEM(shape, kind) for _, shape, kind in scratch]
        + [pltpu.SemaphoreType.DMA(shape) for _, shape in sems],
        compiler_params=pltpu.CompilerParams(
            collective_id=1, has_side_effects=True, vmem_limit_bytes=67043328
        ),
    )(
        inputs,
        cotangent,
        *shards,
        segment_ids,
        *[vector.reshape(1, -1) for vector in vectors],
    )


def settle_kernel(moved, *refs):
    total = moved + 1
    sources, vectors, targets = refs[:moved], refs[moved], refs[total : total + moved]
    rows_out = refs[total + moved : total + moved + 9]
    held = refs[total + moved + 9 : total + 2 * moved + 9]
    in_sem, out_sem = refs[-2:]
    width = vectors.shape[1]
    into = [
        pltpu.make_async_copy(source, place, in_sem.at[k])
        for k, (source, place) in enumerate(zip(sources, held))
    ]
    out = [
        pltpu.make_async_copy(place, target, out_sem.at[k])
        for k, (place, target) in enumerate(zip(held, targets))
    ]
    for copy in into:
        copy.start()
    for row in range(8):
        rows_out[row][...] = vectors[row : row + 1, :]
    for k in range(4):
        rows_out[8][:, k * width : (k + 1) * width] = vectors[ROW_UP + k : ROW_UP + k + 1, :]
    for first, second in zip(into, out):
        first.wait()
        second.start()
    for copy in out:
        copy.wait()


def settle(arrays, sums):
    moved = len(arrays)
    width = sums.shape[1]
    same = [jax.ShapeDtypeStruct(array.shape, array.dtype) for array in arrays]
    rows_out = [jax.ShapeDtypeStruct((1, width), jnp.float32)] * 8
    rows_out.append(jax.ShapeDtypeStruct((1, 4 * width), jnp.float32))
    return pl.pallas_call(
        functools.partial(settle_kernel, moved),
        name="settle",
        out_shape=same + rows_out,
        in_specs=[LEFT] * moved + [VMEM],
        out_specs=[LEFT] * moved + [VMEM] * 9,
        scratch_shapes=[pltpu.VMEM(array.shape, array.dtype) for array in arrays]
        + [pltpu.SemaphoreType.DMA((moved,)), pltpu.SemaphoreType.DMA((moved,))],
        compiler_params=pltpu.CompilerParams(vmem_limit_bytes=56 * 2**20),
    )(*arrays, sums)


def fused_plan(
    inputs,
    segment_ids,
    query_weight,
    key_weight,
    value_weight,
    output_weight,
    up_weight,
    down_weight,
    querybias,
    valuebias,
    outputbias,
    upbias,
    downbias,
    norm_gain,
    norm_shift,
    final_gain,
    final_shift,
    cotangent,
):
    *grads, sums = layer_call(
        inputs,
        segment_ids,
        cotangent,
        (query_weight, key_weight, value_weight, output_weight, up_weight, down_weight),
        (
            querybias,
            valuebias,
            outputbias,
            upbias,
            downbias,
            norm_gain,
            norm_shift,
            final_gain,
            final_shift,
        ),
    )
    *outs, query, value, output, down, gain, shift, last_gain, last_shift, up = settle(grads, sums)
    rows = (query, value, output, up, down, gain, shift, last_gain, last_shift)
    return (*outs, *[row.reshape(-1) for row in rows])


def solution(mesh):
    fits = mesh.shape["ctx"] == 2 and mesh.shape["tp"] == 4 and mesh.shape["dp"] > 2
    placed = (
        P("dp", ("ctx", "tp"), None),
        P("dp", None),
        P(("dp", "ctx"), "tp"),
        P(("dp", "ctx"), "tp"),
        P(("dp", "ctx"), "tp"),
        P("tp", ("dp", "ctx")),
        P(("dp", "ctx"), "tp"),
        P("tp", ("dp", "ctx")),
        P(),
        P(),
        P(),
        P(),
        P(),
        P(),
        P(),
        P(),
        P(),
        P("dp", ("ctx", "tp"), None),
    )
    return jax.shard_map(
        fused_plan if fits else ring_plan,
        mesh=mesh,
        in_specs=placed,
        out_specs=(
            P("dp", ("ctx", "tp"), None),
            P("dp", ("ctx", "tp"), None),
            P(("dp", "ctx"), "tp"),
            P(("dp", "ctx"), "tp"),
            P(("dp", "ctx"), "tp"),
            P("tp", ("dp", "ctx")),
            P(("dp", "ctx"), "tp"),
            P("tp", ("dp", "ctx")),
            P(),
            P(),
            P(),
            P(),
            P(),
            P(),
            P(),
            P(),
            P(),
        ),
        check_vma=False,
    )
```

```python
import functools

import jax
import jax.numpy as jnp
from jax import lax
from jax.experimental import pallas as pl
from jax.experimental.pallas import tpu as pltpu
from jax.sharding import PartitionSpec as P

HEAD_DIM = 64
REACH = 4


def shifted(block, axis, distance):
    devices = range(lax.axis_size(axis))
    route = [(i - distance, i) for i in devices if i - distance in devices]
    return lax.ppermute(block, axis, route)


def for_sending(shard):

    def short(part):
        return part.astype(jnp.bfloat16) if part.dtype == jnp.float32 else part

    return jax.tree.map(short, shard)


def layer_norm(hidden, gain_vec, shift_vec):
    center = hidden - jnp.mean(hidden, axis=-1, keepdims=True)
    inverse = lax.rsqrt(jnp.mean(center * center, axis=-1, keepdims=True) + 1e-05)
    normed = center * inverse
    return (normed * gain_vec + shift_vec, normed, inverse)


def norm_back(upstream, normed, inverse, gain_vec):
    scaled = upstream * gain_vec
    return inverse * (
        scaled
        - jnp.mean(scaled, axis=-1, keepdims=True)
        - normed * jnp.mean(scaled * normed, axis=-1, keepdims=True)
    )


def gelu_curve(pre_act):
    return 0.5 * pre_act * (1.0 + lax.erf(pre_act * 0.7071067811865476))


def gelu_slope(pre_act):
    return (
        0.5 * (1.0 + lax.erf(pre_act * 0.7071067811865476))
        + pre_act * jnp.exp(-0.5 * pre_act * pre_act) * 0.3989422804014327
    )


def product(left_side, right_side):
    return jnp.einsum("btd,de->bte", left_side, right_side, preferred_element_type=jnp.float32)


def transposed(left_side, right_side):
    return jnp.einsum("btn,mn->btm", left_side, right_side, preferred_element_type=jnp.float32)


def weight_term(left_side, right_side):
    return jnp.einsum("btd,bte->de", left_side, right_side, preferred_element_type=jnp.float32)


def block_scores(query_rows, key_rows, block_mask):
    scores = jnp.einsum("bqhd,bkhd->bhqk", query_rows, key_rows, preferred_element_type=jnp.float32)
    return jnp.where(block_mask, scores, -1e30)


def probabilities(query_rows, key_rows, block_mask, log_total):
    scores = block_scores(query_rows, key_rows, block_mask)
    return jnp.where(block_mask, jnp.exp(scores - log_total[..., None]), 0.0)


def placed(local_part, full_len, place_at):
    empty = jnp.zeros((full_len,), jnp.float32)
    return lax.dynamic_update_slice_in_dim(empty, local_part, place_at * local_part.shape[0], 0)


def ring_plan(
    inputs,
    segment_ids,
    query_weight,
    key_weight,
    value_weight,
    output_weight,
    up_weight,
    down_weight,
    querybias,
    valuebias,
    outputbias,
    upbias,
    downbias,
    norm_gain,
    norm_shift,
    final_gain,
    final_shift,
    cotangent,
):
    tp_count = lax.axis_size("tp")
    tp_place = lax.axis_index("tp")
    ctx_count = lax.axis_size("ctx")
    ctx_place = lax.axis_index("ctx")
    batch_rows, part_rows, model_width = inputs.shape
    shard_rows = part_rows * tp_count
    full_query, full_key, full_value, full_output, full_up, full_down = (
        lax.all_gather(query_weight, ("dp", "ctx"), axis=0, tiled=True),
        lax.all_gather(key_weight, ("dp", "ctx"), axis=0, tiled=True),
        lax.all_gather(value_weight, ("dp", "ctx"), axis=0, tiled=True),
        lax.all_gather(output_weight, ("dp", "ctx"), axis=1, tiled=True),
        lax.all_gather(up_weight, ("dp", "ctx"), axis=0, tiled=True),
        lax.all_gather(down_weight, ("dp", "ctx"), axis=1, tiled=True),
    )
    local_width = full_query.shape[1]
    local_heads = local_width // HEAD_DIM
    hidden_width = full_up.shape[1]
    query_offset = lax.dynamic_slice_in_dim(querybias, tp_place * local_width, local_width)
    value_offset = lax.dynamic_slice_in_dim(valuebias, tp_place * local_width, local_width)
    up_offset = lax.dynamic_slice_in_dim(upbias, tp_place * hidden_width, hidden_width)
    score_scale = HEAD_DIM ** (-0.5)

    def split_heads(tensor):
        return tensor.reshape(batch_rows, shard_rows, local_heads, HEAD_DIM)

    def join_heads(tensor):
        return tensor.reshape(batch_rows, shard_rows, local_width)

    tokens = lax.all_gather(inputs, "tp", axis=1, tiled=True)
    queries = split_heads(
        ((product(tokens, full_query) + query_offset) * score_scale).astype(jnp.bfloat16)
    )
    key_rows = split_heads(product(tokens, full_key).astype(jnp.bfloat16))
    value_rows = split_heads((product(tokens, full_value) + value_offset).astype(jnp.bfloat16))
    own_ids = lax.dynamic_slice_in_dim(segment_ids, ctx_place * shard_rows, shard_rows, 1)
    offsets = [0] + [
        offset for offset in range(-REACH, REACH + 1) if offset != 0 and abs(offset) < ctx_count
    ]
    mask_of = {}
    block_of = {}
    for offset in offsets:
        source = ctx_place + offset
        begin_at = jnp.clip(source, 0, ctx_count - 1) * shard_rows
        other_ids = lax.dynamic_slice_in_dim(segment_ids, begin_at, shard_rows, 1)
        inside = jnp.logical_and(source >= 0, source < ctx_count)
        mask_of[offset] = jnp.logical_and(own_ids[:, :, None] == other_ids[:, None, :], inside)[
            :, None
        ]
        if offset == 0:
            block_of[offset] = (key_rows, value_rows)
        else:
            block_of[offset] = shifted((key_rows, value_rows), "ctx", -offset)
    running = jnp.full((batch_rows, local_heads, shard_rows), -1e30, jnp.float32)
    totals = jnp.zeros((batch_rows, local_heads, shard_rows), jnp.float32)
    for offset in offsets:
        scores = block_scores(queries, block_of[offset][0], mask_of[offset])
        highest = jnp.maximum(running, jnp.max(scores, axis=-1))
        weights = jnp.where(mask_of[offset], jnp.exp(scores - highest[..., None]), 0.0)
        totals = totals * jnp.exp(running - highest) + jnp.sum(weights, axis=-1)
        running = highest
    log_total = running + jnp.log(totals)
    mixture = jnp.zeros((batch_rows, shard_rows, local_heads, HEAD_DIM), jnp.float32)
    for offset in offsets:
        attn_probs = probabilities(queries, block_of[offset][0], mask_of[offset], log_total)
        mixture = mixture + jnp.einsum(
            "bhqk,bkhd->bqhd",
            attn_probs.astype(jnp.bfloat16),
            block_of[offset][1],
            preferred_element_type=jnp.float32,
        )
    attended = join_heads(mixture).astype(jnp.bfloat16)
    output_part = lax.psum_scatter(
        product(attended, full_output), "tp", scatter_dimension=1, tiled=True
    )
    first_sum = inputs.astype(jnp.float32) + output_part + outputbias
    normed_first, first_normed, first_inverse = layer_norm(first_sum, norm_gain, norm_shift)
    normed_rows = lax.all_gather(normed_first.astype(jnp.bfloat16), "tp", axis=1, tiled=True)
    hidden_pre = product(normed_rows, full_up) + up_offset
    hidden_low = gelu_curve(hidden_pre).astype(jnp.bfloat16)
    down_part = lax.psum_scatter(
        product(hidden_low, full_down), "tp", scatter_dimension=1, tiled=True
    )
    second_sum = normed_first + down_part + downbias
    result, second_normed, second_inverse = layer_norm(second_sum, final_gain, final_shift)
    upstream = cotangent.astype(jnp.float32)
    finalgain_grad = jnp.sum(upstream * second_normed, axis=(0, 1))
    finalshift_grad = jnp.sum(upstream, axis=(0, 1))
    second_grad = norm_back(upstream, second_normed, second_inverse, final_gain)
    down_low = second_grad.astype(jnp.bfloat16)
    downbias_grad = jnp.sum(down_low, axis=(0, 1), dtype=jnp.float32)
    down_rows = lax.all_gather(down_low, "tp", axis=1, tiled=True)
    down_grad = weight_term(hidden_low, down_rows)
    hidden_grad = (transposed(down_rows, full_down) * gelu_slope(hidden_pre)).astype(jnp.bfloat16)
    upbias_part = jnp.sum(hidden_grad, axis=(0, 1), dtype=jnp.float32)
    up_grad = weight_term(normed_rows, hidden_grad)
    normed_grad = (
        lax.psum_scatter(transposed(hidden_grad, full_up), "tp", scatter_dimension=1, tiled=True)
        + second_grad
    )
    normgain_grad = jnp.sum(normed_grad * first_normed, axis=(0, 1))
    normshift_grad = jnp.sum(normed_grad, axis=(0, 1))
    first_grad = norm_back(normed_grad, first_normed, first_inverse, norm_gain)
    output_low = first_grad.astype(jnp.bfloat16)
    outputbias_grad = jnp.sum(output_low, axis=(0, 1), dtype=jnp.float32)
    output_rows = lax.all_gather(output_low, "tp", axis=1, tiled=True)
    output_grad = weight_term(attended, output_rows)
    mixed_grad = split_heads(transposed(output_rows, full_output).astype(jnp.bfloat16))
    row_dot = jnp.zeros((batch_rows, local_heads, shard_rows), jnp.float32)
    for offset in offsets:
        attn_probs = probabilities(queries, block_of[offset][0], mask_of[offset], log_total)
        prob_grad = jnp.einsum(
            "bqhd,bkhd->bhqk", mixed_grad, block_of[offset][1], preferred_element_type=jnp.float32
        )
        row_dot = row_dot + jnp.sum(attn_probs * prob_grad, axis=-1)
    query_acc = jnp.zeros((batch_rows, shard_rows, local_heads, HEAD_DIM), jnp.float32)
    key_parts = {}
    for offset in offsets:
        attn_probs = probabilities(queries, block_of[offset][0], mask_of[offset], log_total)
        prob_grad = jnp.einsum(
            "bqhd,bkhd->bhqk", mixed_grad, block_of[offset][1], preferred_element_type=jnp.float32
        )
        score_grad = (attn_probs * (prob_grad - row_dot[..., None])).astype(jnp.bfloat16)
        query_acc = query_acc + jnp.einsum(
            "bhqk,bkhd->bqhd", score_grad, block_of[offset][0], preferred_element_type=jnp.float32
        )
        key_term = jnp.einsum(
            "bhqk,bqhd->bkhd", score_grad, queries, preferred_element_type=jnp.float32
        )
        value_term = jnp.einsum(
            "bhqk,bqhd->bkhd",
            attn_probs.astype(jnp.bfloat16),
            mixed_grad,
            preferred_element_type=jnp.float32,
        )
        key_parts[offset] = (key_term, value_term)
    own_key, own_value = key_parts[0]
    for offset in offsets[1:]:
        back_key, back_value = shifted(for_sending(key_parts[offset]), "ctx", offset)
        own_key = own_key + back_key
        own_value = own_value + back_value
    query_pre = (
        join_heads(query_acc.astype(jnp.bfloat16)).astype(jnp.float32) * score_scale
    ).astype(jnp.bfloat16)
    key_low = join_heads(own_key.astype(jnp.bfloat16))
    value_low = join_heads(own_value.astype(jnp.bfloat16))
    querybias_part = jnp.sum(query_pre, axis=(0, 1), dtype=jnp.float32)
    valuebias_part = jnp.sum(value_low, axis=(0, 1), dtype=jnp.float32)
    query_grad = weight_term(tokens, query_pre)
    key_grad = weight_term(tokens, key_low)
    value_grad = weight_term(tokens, value_low)
    input_part = (
        transposed(query_pre, full_query)
        + transposed(key_low, full_key)
        + transposed(value_low, full_value)
    )
    input_grad = (
        lax.psum_scatter(
            input_part.astype(jnp.bfloat16), "tp", scatter_dimension=1, tiled=True
        ).astype(jnp.float32)
        + first_grad
    )
    query_grad, key_grad, value_grad, output_grad, up_grad, down_grad = (
        lax.psum_scatter(query_grad, ("dp", "ctx"), scatter_dimension=0, tiled=True),
        lax.psum_scatter(key_grad, ("dp", "ctx"), scatter_dimension=0, tiled=True),
        lax.psum_scatter(value_grad, ("dp", "ctx"), scatter_dimension=0, tiled=True),
        lax.psum_scatter(output_grad, ("dp", "ctx"), scatter_dimension=1, tiled=True),
        lax.psum_scatter(up_grad, ("dp", "ctx"), scatter_dimension=0, tiled=True),
        lax.psum_scatter(down_grad, ("dp", "ctx"), scatter_dimension=1, tiled=True),
    )
    summed = lax.psum(
        (
            placed(querybias_part, model_width, tp_place),
            placed(valuebias_part, model_width, tp_place),
            outputbias_grad,
            placed(upbias_part, hidden_width * tp_count, tp_place),
            downbias_grad,
            normgain_grad,
            normshift_grad,
            finalgain_grad,
            finalshift_grad,
        ),
        ("dp", "ctx", "tp"),
    )
    return (
        result.astype(jnp.bfloat16),
        input_grad,
        query_grad,
        key_grad,
        value_grad,
        output_grad,
        up_grad,
        down_grad,
        summed[0],
        summed[1],
        summed[2],
        summed[3],
        summed[4],
        summed[5],
        summed[6],
        summed[7],
        summed[8],
    )


MESH = pl.DeviceIdType.MESH
LOWEST = -1e30
VMEM = pl.BlockSpec(memory_space=pltpu.VMEM)
LEFT = pl.BlockSpec(memory_space=pl.ANY)


class Seat:
    def __init__(self):
        self.dp_count = lax.axis_size("dp")
        self.dp = lax.axis_index("dp")
        self.ctx = lax.axis_index("ctx")
        self.tp = lax.axis_index("tp")
        self.tp_pair = self.tp + 1 - 2 * (self.tp % 2)
        self.tp_side = (self.tp + 2) % 4
        self.tp_far = (self.tp_pair + 2) % 4
        self.pair = (self.dp, self.ctx, self.tp_pair)
        self.side = (self.dp, self.ctx, self.tp_side)
        self.twin = (self.dp, 1 - self.ctx, self.tp)
        self.above = ((self.dp + 1) % self.dp_count, self.ctx, self.tp)
        self.below = ((self.dp + self.dp_count - 1) % self.dp_count, self.ctx, self.tp)

    def meet(self, names):
        barrier = pltpu.get_barrier_semaphore()
        for name in names:
            pl.semaphore_signal(
                barrier, inc=1, device_id=getattr(self, name), device_id_type=MESH
            )
        pl.semaphore_wait(barrier, len(names))


def remote(source, target, send_sem, recv_sem, to):
    return pltpu.make_async_remote_copy(
        src_ref=source,
        dst_ref=target,
        send_sem=send_sem,
        recv_sem=recv_sem,
        device_id=to,
        device_id_type=MESH,
    )


class RingGather:
    def __init__(self, seat, shard, block, sems, at, twice=False):
        self.seat, self.shard, self.block, self.at = seat, shard, block, at
        self.own_sem, self.z_send, self.z_recv, self.y_send, self.y_recv = sems
        self.count = seat.dp_count
        self.twice = twice

    def held(self, step, other=0):
        origin = (self.seat.dp + self.count - step) % self.count
        place = self.seat.ctx if other == 0 else 1 - self.seat.ctx
        return self.block(origin * 2 + place)

    def own(self):
        return pltpu.make_async_copy(self.shard, self.held(0), self.own_sem.at[self.at])

    def z(self, step, other=0):
        source = self.shard if step == 0 and other == 0 else self.held(step, other)
        return remote(
            source,
            self.held(step, other),
            self.z_send.at[self.at, 2 * step + other],
            self.z_recv.at[self.at, 2 * step + other],
            self.seat.above,
        )

    def z_in(self, step, other=0):
        view = self.held(step + 1, other)
        return remote(
            view,
            view,
            self.z_send.at[self.at, 2 * step + other],
            self.z_recv.at[self.at, 2 * step + other],
            self.seat.above,
        )

    def y(self, step):
        source = self.shard if step == 0 else self.held(step)
        return remote(
            source,
            self.held(step),
            self.y_send.at[self.at, step],
            self.y_recv.at[self.at, step],
            self.seat.twin,
        )

    def y_in(self, step):
        view = self.held(step, 1)
        return remote(
            view,
            view,
            self.y_send.at[self.at, step],
            self.y_recv.at[self.at, step],
            self.seat.twin,
        )

    def begin(self):
        self.own().start()
        self.y(0).start()
        self.z(0).start()

    def join(self):
        self.y_in(0).wait_recv()
        self.z(0, 1).start()

    def pass_on(self, step):
        for other in range(2 if self.twice else 1):
            self.z_in(step, other).wait_recv()
            if step + 1 < self.count - 1:
                self.z(step + 1, other).start()
        if not self.twice:
            self.y(step + 1).start()

    def land(self):
        self.own().wait()
        if not self.twice:
            for step in range(self.count):
                self.y_in(step).wait_recv()

    def close(self):
        for step in range(self.count - 1):
            for other in range(2 if self.twice else 1):
                self.z(step, other).wait_send()
        for step in range(1 if self.twice else self.count):
            self.y(step).wait_send()


def dot(left_side, right_side):
    return jnp.dot(left_side, right_side, preferred_element_type=jnp.float32)


def dot_nt(left_side, right_side):
    return lax.dot_general(
        left_side, right_side, (((1,), (1,)), ((), ())), preferred_element_type=jnp.float32
    )


def dot_tn(left_side, right_side):
    return lax.dot_general(
        left_side, right_side, (((0,), (0,)), ((), ())), preferred_element_type=jnp.float32
    )


def aligned(start, size):
    return pl.ds(pl.multiple_of(start, size), size)


VECTOR_ROWS = 16
ROW_QUERY, ROW_VALUE, ROW_OUTPUT, ROW_DOWN = 0, 1, 2, 3
ROW_GAIN, ROW_SHIFT, ROW_FINAL_GAIN, ROW_FINAL_SHIFT, ROW_UP = 4, 5, 6, 7, 8


class TokenScatter:
    def __init__(self, seat, buffers, sems, at, slot):
        self.seat, self.at, self.slot = seat, at, slot
        self.pair_out, self.pair_in, self.side_out, self.side_in = buffers
        self.send, self.recv = sems

    def copy(self, k):
        at, seat, slot = self.at, self.seat, self.slot
        if k < 2:
            source, target, to = self.pair_out.at[slot, k], self.pair_in.at[slot, k], seat.pair
        else:
            source, target, to = self.side_out.at[slot], self.side_in.at[slot], seat.side
        return remote(source, target, self.send.at[at, k], self.recv.at[at, k], to)

    def give(self, compute, total):
        seat, at = self.seat, self.slot
        part = self.side_out.shape[1]
        group = seat.tp // 2
        mine = aligned((seat.tp % 2) * part, part)
        others = aligned((1 - seat.tp % 2) * part, part)
        compute(1 - group)
        self.pair_out[at, 0] = total[others, :].astype(jnp.bfloat16)
        self.copy(0).start()
        self.side_out[at] = total[mine, :].astype(jnp.bfloat16)
        compute(group)
        self.pair_out[at, 1] = total[others, :].astype(jnp.bfloat16)
        self.copy(1).start()
        self.copy(0).wait_recv()
        self.side_out[at] = (
            self.side_out[at].astype(jnp.float32) + self.pair_in[at, 0].astype(jnp.float32)
        ).astype(jnp.bfloat16)
        self.copy(2).start()
        return mine

    def take(self):
        self.copy(1).wait_recv()
        self.copy(2).wait_recv()
        return self.pair_in[self.slot, 1].astype(jnp.float32) + self.side_in[self.slot].astype(
            jnp.float32
        )

    def close(self):
        for k in range(3):
            self.copy(k).wait_send()


class TokenGather:
    def __init__(self, seat, full, b, part, sems, at):
        self.seat = seat
        self.send, self.recv = sems
        self.at = at
        self.view = lambda place: full.at[b, aligned(place * part, part), :]

    def copy(self, k, place, to):
        view = self.view(place)
        return remote(view, view, self.send.at[self.at, k], self.recv.at[self.at, k], to)

    def give(self):
        seat = self.seat
        self.copy(0, seat.tp, seat.side).start()
        self.copy(1, seat.tp, seat.pair).start()

    def relay(self):
        seat = self.seat
        self.copy(0, seat.tp_side, seat.side).wait_recv()
        self.copy(2, seat.tp_side, seat.pair).start()

    def land(self):
        seat = self.seat
        self.copy(1, seat.tp_pair, seat.pair).wait_recv()
        self.copy(2, seat.tp_far, seat.pair).wait_recv()

    def close(self):
        seat = self.seat
        for k, place in ((0, seat.tp), (1, seat.tp), (2, seat.tp_side)):
            self.copy(k, place, seat.pair).wait_send()


def row_mean(rows):
    return jnp.mean(rows, axis=-1, keepdims=True)


class PairedReduce:
    def __init__(self, seat, partial, block, twin_in, ring_out, ring_in, sems, at):
        self.seat, self.partial, self.block, self.at = seat, partial, block, at
        self.twin_in, self.ring_out, self.ring_in = twin_in, ring_out, ring_in
        self.y_send, self.y_recv, self.z_send, self.z_recv = sems
        self.count = seat.dp_count

    def mine(self, step, ctx):
        owner = (self.seat.dp + 2 * self.count - 1 - step) % self.count
        return self.block(self.partial, owner * 2 + ctx)

    def y(self, step):
        return remote(
            self.mine(step, 1 - self.seat.ctx),
            self.twin_in.at[step],
            self.y_send.at[self.at, step],
            self.y_recv.at[self.at, step],
            self.seat.twin,
        )

    def z(self, step):
        return remote(
            self.ring_out(step),
            self.ring_in.at[step],
            self.z_send.at[self.at, step],
            self.z_recv.at[self.at, step],
            self.seat.above,
        )

    def begin(self):
        for step in range(self.count):
            self.y(step).start()

    def advance(self, step):
        self.y(step).wait_recv()
        total = self.mine(step, self.seat.ctx)[...].astype(jnp.float32) + self.twin_in[
            step
        ].astype(jnp.float32)
        if step > 0:
            self.z(step - 1).wait_recv()
            total = total + self.ring_in[step - 1].astype(jnp.float32)
        if step == self.count - 1:
            return total
        self.ring_out(step)[...] = total.astype(jnp.bfloat16)
        self.z(step).start()

    def close(self):
        for step in range(self.count):
            self.y(step).wait_send()
        for step in range(self.count - 1):
            self.z(step).wait_send()


class RingReduce:
    def __init__(self, seat, partial, pair, ring_out, ring_in, half_out, half_in, sems, at):
        self.seat, self.partial, self.pair, self.at = seat, partial, pair, at
        self.ring_out, self.ring_in, self.half_out, self.half_in = ring_out, ring_in, half_out, half_in
        self.y_send, self.y_recv, self.z_send, self.z_recv = sems
        self.count = seat.dp_count

    def mine(self, step):
        owner = (self.seat.dp + 2 * self.count - 1 - step) % self.count
        return self.pair(self.partial, owner)

    def z(self, step):
        return remote(
            self.mine(0) if step == 0 else self.ring_out(step - 1),
            self.ring_in.at[step],
            self.z_send.at[self.at, step],
            self.z_recv.at[self.at, step],
            self.seat.above,
        )

    def y(self):
        return remote(
            self.half_out,
            self.half_in,
            self.y_send.at[self.at, 0],
            self.y_recv.at[self.at, 0],
            self.seat.twin,
        )

    def begin(self):
        self.z(0).start()

    def advance(self, step):
        self.z(step - 1).wait_recv()
        total = self.mine(step)[...].astype(jnp.float32) + self.ring_in[step - 1].astype(
            jnp.float32
        )
        if step == self.count - 1:
            return total
        self.ring_out(step - 1)[...] = total.astype(jnp.bfloat16)
        self.z(step).start()

    def close(self):
        self.y().wait_send()
        for step in range(self.count - 1):
            self.z(step).wait_send()


class Parts:
    def __init__(self, names, refs):
        self.__dict__.update(zip(names, refs))


def layer_kernel(names, *refs):
    r = Parts(names, refs)
    seat = Seat()
    count = seat.dp_count
    hops = count - 1
    batch, part, width = r.result.shape
    rows = r.tokens.shape[1]
    local = r.query_full.shape[1]
    hidden = r.up_full.shape[1]
    heads = local // HEAD_DIM
    depth = width // (2 * count)
    wide = 512
    f32, bf16 = jnp.float32, jnp.bfloat16

    barrier = pltpu.get_barrier_semaphore()
    around = [((seat.dp + away) % count, seat.ctx, seat.tp) for away in range(1, count)]
    for to in [seat.pair, seat.side, seat.twin] + around:
        pl.semaphore_signal(barrier, inc=1, device_id=to, device_id_type=MESH)
    pl.semaphore_wait(barrier, 2 + count)

    def over(tiles, body):
        def one(index, carry):
            body(index)
            return carry

        lax.fori_loop(0, tiles, one, 0)

    def over_heads(body, services):
        def one(h):
            for when, service in services:
                pl.when(h == when)(service)
            body(h)

        over(heads, one)

    def cut(half, place):
        return lambda b: half.at[b, aligned(place * part, part), :]

    def token_copy(relation, b, source, target, to):
        at = 2 * relation + b
        return remote(source(b), target(b), r.token_send.at[at], r.token_recv.at[at], to)

    here, there = cut(r.tokens, seat.tp), cut(r.other, seat.tp)
    here_side, there_side = cut(r.tokens, seat.tp_side), cut(r.other, seat.tp_side)
    given = lambda b: r.inputs.at[b]
    landed = [
        cut(r.tokens, seat.tp_pair),
        here_side,
        there,
        there_side,
        cut(r.tokens, seat.tp_far),
        cut(r.other, seat.tp_pair),
        cut(r.other, seat.tp_far),
    ]

    def token_out(relation, b):
        return token_copy(
            relation,
            b,
            *(
                (given, here, seat.pair),
                (given, here, seat.side),
                (given, there, seat.twin),
                (there, there, seat.side),
                (here_side, here_side, seat.pair),
                (there, there, seat.pair),
                (there_side, there_side, seat.pair),
            )[relation],
        )

    def token_in(relation, b):
        token_copy(relation, b, landed[relation], landed[relation], seat.pair).wait_recv()

    own_tokens = [
        pltpu.make_async_copy(r.inputs.at[b], here(b), r.local_sem.at[b]) for b in range(batch)
    ]
    upstream = lambda b: r.weight_low.at[0, b * part : (b + 1) * part, :]
    own_cotangent = [
        pltpu.make_async_copy(r.cotangent.at[b], upstream(b), r.local_sem.at[batch + b])
        for b in range(batch)
    ]
    for copy in own_tokens + own_cotangent:
        copy.start()

    def by_rows(full):
        return lambda at: full.at[aligned(at * depth, depth), :]

    def by_columns(full):
        return lambda at: full.at[:, aligned(at * depth, depth)]

    def by_half_rows(half):
        def view(full):
            return lambda at: full.at[aligned(at * depth + half * (depth // 2), depth // 2), :]

        return view

    gather_sems = (r.own_sem, r.gz_send, r.gz_recv, r.gy_send, r.gy_recv)
    weights = [
        RingGather(seat, shard, view(full), gather_sems, at, twice)
        for at, (shard, full, view, twice) in enumerate(
            (
                (r.query_weight, r.query_full, by_rows, False),
                (r.key_weight, r.key_full, by_rows, True),
                (r.value_weight, r.value_full, by_rows, True),
                (r.output_weight, r.output_full, by_columns, False),
                (r.up_weight.at[: depth // 2, :], r.up_full, by_half_rows(0), False),
                (r.up_weight.at[depth // 2 :, :], r.up_full, by_half_rows(1), True),
                (r.down_weight, r.down_full, by_columns, False),
            )
        )
    ]
    to_output, to_up, to_up_too, to_down = weights[3:]
    to_query, to_key, to_value = weights[:3]
    to_value.begin()
    to_key.begin()
    for b in range(batch):
        token_out(1, b).start()
        token_out(2, b).start()
        token_out(0, b).start()
    to_query.begin()
    to_output.begin()
    to_value.join()
    to_key.join()
    for weight in (to_value, to_key, to_query):
        weight.pass_on(0)
    to_up.begin()
    token_in(1, 0)
    token_out(4, 0).start()
    token_in(2, 0)
    token_out(3, 0).start()
    token_out(5, 0).start()
    for weight in (to_value, to_key, to_query):
        weight.pass_on(1)
    to_output.pass_on(0)
    token_in(1, 1)
    token_out(4, 1).start()
    token_in(2, 1)
    token_out(3, 1).start()
    token_out(5, 1).start()
    to_up_too.begin()
    for weight in (to_value, to_key, to_query):
        weight.pass_on(2)
    to_output.pass_on(1)
    to_up.pass_on(0)
    to_up_too.join()
    to_down.begin()

    for b in range(batch):
        for half in range(2):
            row_ids = r.ids[b : b + 1, aligned((seat.ctx if half == 0 else 1 - seat.ctx) * rows, rows)]
            spread = jnp.broadcast_to(row_ids.astype(f32), (128, rows))
            r.ids_down[b, half * rows : (half + 1) * rows, :] = spread.T
    bias_at = aligned(seat.tp * local, local)
    query_offset = r.query_bias[:, bias_at]
    value_offset = r.value_bias[:, bias_at]
    tile_rows = rows // 2
    for weight in weights[:3]:
        weight.land()
    for copy in own_tokens:
        copy.wait()
    for b in range(batch):
        token_in(0, b)
        token_in(4, b)

    def project(half_ref, half):
        def one(index):
            b, piece = index // 2, index % 2
            block = half_ref[b, aligned(piece * tile_rows, tile_rows), :]
            spot = aligned(half * rows + piece * tile_rows, tile_rows)
            if half == 0:
                scaled = (dot(block, r.query_full[...]) + query_offset) * HEAD_DIM ** (-0.5)
                r.queries[b, aligned(piece * tile_rows, tile_rows), :] = scaled.astype(bf16)
            r.keys[b, spot, :] = dot(block, r.key_full[...]).astype(bf16)
            value_rows = dot(block, r.value_full[...]) + value_offset
            r.values[b, spot, :] = value_rows.astype(bf16)
            r.flipped[b, :, spot] = value_rows.T.astype(bf16)

        over(batch * 2, one)

    project(r.tokens, 0)
    to_output.pass_on(2)
    to_up_too.pass_on(0)
    for b in range(batch):
        token_in(3, b)
        token_out(6, b).start()
        token_in(5, b)
        token_in(6, b)
    project(r.other, 1)

    lane_head = lax.broadcasted_iota(jnp.int32, (1, local), 1) // HEAD_DIM
    nothing = jnp.zeros((), bf16)

    def own_ids(b):
        return r.ids[b : b + 1, aligned(seat.ctx * rows, rows)].astype(f32)

    def attend(b, services):
        row_ids = own_ids(b)

        def one(h):
            own = aligned(h * HEAD_DIM, HEAD_DIM)
            chosen = jnp.where(lane_head == h, r.queries[b], nothing)
            same = jnp.tile(r.ids_down[b], (1, rows // 128)) == row_ids
            scores = jnp.where(same, dot_nt(r.keys[b], chosen), LOWEST)
            highest = jnp.max(scores, axis=0, keepdims=True)
            raised = jnp.exp(scores - highest)
            total = jnp.sum(raised, axis=0, keepdims=True)
            shares = (raised * (1.0 / total)).astype(bf16)
            r.mixture[b, own, :] = dot(r.flipped[b, own, :], shares)
            r.logs[b * heads + h] = highest + jnp.log(total)

        over_heads(one, services)
        r.attended[b] = r.mixture[b].T.astype(bf16)

    def passing(step, *which):
        def service():
            for weight in which:
                weight.pass_on(step)

        return service

    to_output.land()

    scatter_parts = (r.pair_out, r.pair_in, r.side_out, r.side_in)
    scatters = [
        TokenScatter(seat, scatter_parts, (r.scatter_send, r.scatter_recv), at, slot)
        for at, slot in list(enumerate(range(3 * batch)))
        + [(3 * batch + at, at) for at in range(2 * batch)]
    ]
    gathers = [
        TokenGather(seat, full, b, part, (r.gather_send, r.gather_recv), k * batch + b)
        for k, full in enumerate((r.normed_rows, r.down_rows, r.output_rows))
        for b in range(batch)
    ]

    def spread_rows(lhs_ref, b, weight, flipped):
        def compute(group):
            lhs = lhs_ref[b, aligned(group * 2 * part, 2 * part), :]

            def tile(index):
                at = aligned(index * width, width)
                if flipped:
                    r.total[:, at] = dot_nt(lhs, weight[at, :])
                else:
                    r.total[:, at] = dot(lhs, weight[:, at])

            over(1, tile)

        return compute

    def scatter(k, b, lhs_ref, weight, flipped):
        mine = scatters[k * batch + b].give(spread_rows(lhs_ref, b, weight, flipped), r.total)
        r.total_own[b] = r.total[mine, :]

    def collected(k, b):
        return r.total_own[b] + scatters[k * batch + b].take()

    own_rows = aligned(seat.tp * part, part)
    r.sums[...] = jnp.zeros_like(r.sums)
    up_sum = r.sums.at[pl.ds(ROW_UP + seat.tp, 1), :]

    def add_vector(row, values):
        r.sums[row : row + 1, :] += jnp.sum(values, axis=0, keepdims=True)

    def first_norm(b):
        first_sum = r.tokens[b, own_rows, :].astype(f32) + (collected(0, b) + r.output_bias[...])
        center = first_sum - row_mean(first_sum)
        inverse = lax.rsqrt(row_mean(center * center) + 1e-05)
        normed = center * inverse
        scaled = normed * r.norm_gain[...] + r.norm_shift[...]
        r.keep[0, b] = normed
        r.keep[1, b] = scaled
        r.inverse_keep[b] = inverse
        r.normed_rows[b, own_rows, :] = scaled.astype(bf16)
        gathers[b].give()

    def raise_up(b):
        gathers[b].land()
        lhs = r.normed_rows[b]

        def tile(index):
            at = aligned(index * wide, wide)
            offset = r.up_bias[:, pl.ds(pl.multiple_of(seat.tp * hidden + index * wide, wide), wide)]
            pre = dot(lhs, r.up_full[:, at]) + offset
            half = 0.5 * (1.0 + lax.erf(pre * 0.7071067811865476))
            r.hidden_rows[b, :, at] = (pre * half).astype(bf16)
            slope = half + pre * jnp.exp(-0.5 * pre * pre) * 0.3989422804014327
            r.slope_rows[b, :, at] = slope.astype(bf16)

        over(hidden // wide, tile)

    def second_norm(b):
        second_sum = r.keep[1, b] + (collected(1, b) + r.down_bias[...])
        center = second_sum - row_mean(second_sum)
        inverse = lax.rsqrt(row_mean(center * center) + 1e-05)
        normed = center * inverse
        r.result[b] = (normed * r.final_gain[...] + r.final_shift[...]).astype(bf16)
        gradient = upstream(b)[...].astype(f32)
        add_vector(ROW_FINAL_GAIN, gradient * normed)
        add_vector(ROW_FINAL_SHIFT, gradient)
        scaled = gradient * r.final_gain[...]
        second = inverse * (scaled - row_mean(scaled) - normed * row_mean(scaled * normed))
        r.keep[2, b] = second
        low = second.astype(bf16)
        r.down_rows[b, own_rows, :] = low
        gathers[batch + b].give()
        add_vector(ROW_DOWN, low.astype(f32))

    def lower(b):
        gathers[batch + b].land()
        lhs = r.down_rows[b]

        def tile(index):
            at = aligned(index * wide, wide)
            back = dot_nt(lhs, r.down_full[at, :]) * r.slope_rows[b, :, at].astype(f32)
            back = back.astype(bf16)
            r.back_rows[b, :, at] = back
            up_sum[:, at] += jnp.sum(back.astype(f32), axis=0, keepdims=True)

        over(hidden // wide, tile)

    def first_back(b):
        grad = collected(2, b) + r.keep[2, b]
        normed = r.keep[0, b]
        add_vector(ROW_GAIN, grad * normed)
        add_vector(ROW_SHIFT, grad)
        scaled = grad * r.norm_gain[...]
        first = r.inverse_keep[b] * (
            scaled - row_mean(scaled) - normed * row_mean(scaled * normed)
        )
        r.input_grad[b] = first
        low = first.astype(bf16)
        r.output_rows[b, own_rows, :] = low
        gathers[2 * batch + b].give()
        add_vector(ROW_OUTPUT, low.astype(f32))

    def mix_back(b):
        gathers[2 * batch + b].land()
        r.mixed[b] = dot_nt(r.output_rows[b], r.output_full[...]).astype(bf16)

    def owner_at(step):
        return (seat.dp + 2 * count - 1 - step) % count

    def output_tiles():
        left = r.attended[...].reshape(batch * rows, local)

        def tile(index):
            at = aligned(index * wide, wide)
            right = r.output_rows[:, :, at].reshape(batch * rows, wide)
            r.output_part[:, at] = dot_tn(left, right).astype(bf16)

        over(width // wide, tile)

    def down_tiles(first, last):
        left = r.hidden_rows[...].reshape(batch * rows, hidden)

        def tile(index):
            at = aligned(owner_at(first + index) * 2 * depth, 2 * depth)
            right = r.down_rows[:, :, at].reshape(batch * rows, 2 * depth)
            term = dot_tn(left, right).astype(bf16)
            r.slope_rows[:, :, at] = term.reshape(batch, rows, 2 * depth)

        over(last - first, tile)
        for step in range(first, last):
            from_down.y(step).start()

    def up_tiles():
        left = r.normed_rows[...].reshape(batch * rows, width)

        def tile(index):
            at = aligned(index * wide, wide)
            right = r.back_rows[:, :, at].reshape(batch * rows, wide)
            r.hidden_rows[:, :, at] = dot_tn(left, right).astype(bf16).reshape(batch, rows, wide)

        over(hidden // wide, tile)
        from_up.begin()
        from_up_too.begin()

    reduce_sems = (r.ry_send, r.ry_recv, r.rz_send, r.rz_recv)
    columns = lambda ref, at: ref.at[:, aligned(at * depth, depth)]
    thin = [
        RingReduce(
            seat, r.weight_low.at[k],
            lambda ref, owner: ref.at[:, aligned(owner * 2 * depth, 2 * depth)],
            (lambda step, k=k: r.wide_out.at[k, step]), r.wide_in.at[k],
            r.half_out.at[k], r.half_in.at[k], reduce_sems, k,
        )
        for k in range(2)
    ]
    from_value = PairedReduce(
        seat, r.weight_low.at[2], columns,
        r.value_twin, (lambda step: r.value_out.at[step]), r.value_in, reduce_sems, 2,
    )
    from_output = PairedReduce(
        seat, r.output_part, columns, r.output_twin, (lambda step: r.output_out.at[step]), r.output_in, reduce_sems, 3
    )
    from_down = PairedReduce(
        seat, r.slope_rows, lambda ref, at: ref.at[:, :, aligned(at * depth, depth)],
        r.down_twin, (lambda step: r.down_rows.at[:, :, step * depth : (step + 1) * depth]), r.down_in, reduce_sems, 4,
    )
    held = rows // depth

    split = hidden * 3 // 4
    from_up = PairedReduce(
        seat, r.hidden_rows,
        lambda ref, at: ref.at[at // held, aligned((at % held) * depth, depth), :split],
        r.up_twin, (lambda step: r.back_rows.at[0, step * depth : (step + 1) * depth, :split]),
        r.up_in, reduce_sems, 5,
    )
    pairs = held // 2
    from_up_too = RingReduce(
        seat, r.hidden_rows,
        lambda ref, owner: ref.at[
            owner // pairs, aligned((owner % pairs) * 2 * depth, 2 * depth), split:
        ],
        (lambda step: r.back_rows.at[1, step * 2 * depth : (step + 1) * 2 * depth, split:]),
        r.up_pair_in, r.up_half_out, r.up_half_in, reduce_sems, 6,
    )

    attend(0, [(3, passing(0, to_down))])
    scatter(0, 0, r.attended, r.output_full, False)
    to_up.pass_on(1)
    attend(1, [(3, passing(1, to_up_too))])
    scatter(0, 1, r.attended, r.output_full, False)
    first_norm(0)
    to_down.pass_on(1)
    to_up.pass_on(2)
    first_norm(1)
    gathers[0].relay()
    to_up_too.pass_on(2)
    to_up.land()
    to_up_too.land()
    raise_up(0)
    gathers[1].relay()
    to_down.pass_on(2)
    raise_up(1)
    to_down.land()
    scatter(1, 0, r.hidden_rows, r.down_full, False)
    scatter(1, 1, r.hidden_rows, r.down_full, False)
    for copy in own_cotangent:
        copy.wait()
    second_norm(0)
    second_norm(1)
    gathers[batch].relay()
    lower(0)
    gathers[batch + 1].relay()
    scatter(2, 0, r.back_rows, r.up_full, True)
    lower(1)
    scatter(2, 1, r.back_rows, r.up_full, True)
    down_tiles(0, count)
    first_back(0)
    up_tiles()
    first_back(1)
    for piece in gathers[batch : 2 * batch]:
        piece.close()
    gathers[2 * batch].relay()
    mix_back(0)

    key_flip = r.flipped.at[0]

    def heads_back(b, services):
        key_flip[...] = r.keys[b].astype(f32).T.astype(bf16)
        product_rows = r.mixed[b].astype(f32).T * r.mixture[b]
        for h in range(heads):
            r.row_dots[h] = jnp.sum(
                product_rows[h * HEAD_DIM : (h + 1) * HEAD_DIM], axis=0, keepdims=True
            )
        r.key_sum[...] = jnp.zeros_like(r.key_sum)
        r.value_sum[...] = jnp.zeros_like(r.value_sum)
        row_ids = own_ids(b)

        def one(h):
            own = aligned(h * HEAD_DIM, HEAD_DIM)
            query_rows = jnp.where(lane_head == h, r.queries[b], nothing)
            grad_rows = jnp.where(lane_head == h, r.mixed[b], nothing)
            same = jnp.tile(r.ids_down[b], (1, rows // 128)) == row_ids
            scores = jnp.where(same, dot_nt(r.keys[b], query_rows), LOWEST)
            probs = jnp.exp(scores - r.logs[b * heads + h])
            r.value_sum[...] += dot(probs.astype(bf16), grad_rows)
            prob_grad = dot_nt(r.values[b], grad_rows)
            score_grad = (probs * (prob_grad - r.row_dots[h])).astype(bf16)
            r.key_sum[...] += dot(score_grad, query_rows)
            r.query_flip[own, :] = dot(key_flip[own, :], score_grad)

        over_heads(one, services)

    lows = lambda k: slice(k * local, (k + 1) * local)
    low_rows = (r.normed_rows, r.output_rows)

    def sequence_back(b):
        flipped = (r.query_flip[...].astype(bf16).astype(f32) * HEAD_DIM ** (-0.5)).astype(bf16)
        upright = flipped.astype(f32).T
        key_low = r.key_sum[...].astype(bf16)
        value_low = r.value_sum[...].astype(bf16)
        low_rows[b][0, :, lows(0)] = upright.astype(bf16)
        for half in range(2):
            low_rows[b][half, :, lows(1)] = key_low[half * rows : (half + 1) * rows]
            low_rows[b][half, :, lows(2)] = value_low[half * rows : (half + 1) * rows]
        r.sums[ROW_QUERY : ROW_QUERY + 1, bias_at] += jnp.sum(upright, axis=0, keepdims=True)
        r.sums[ROW_VALUE : ROW_VALUE + 1, bias_at] += jnp.sum(
            value_low.astype(f32), axis=0, keepdims=True
        )
        flips = [flipped, key_low.astype(f32).T.astype(bf16), value_low.astype(f32).T.astype(bf16)]

        for k in range(3):
            def tile(index, k=k):
                at = aligned(index * wide, wide)
                term = dot(flips[k][:, :rows], r.tokens[b, :, at])
                if k > 0:
                    term = term + dot(flips[k][:, rows:], r.other[b, :, at])
                if b > 0:
                    term = term + r.keep[k, :, :, at].reshape(local, wide)
                if b == batch - 1:
                    r.weight_low[k, :, at] = term.astype(bf16)
                else:
                    r.keep[k, :, :, at] = term.reshape(2, local // 2, wide)

            over(width // wide, tile)

    def input_back(b, half):
        def compute(group):
            at = aligned(group * 2 * part, 2 * part)

            def tile(index):
                row_at = aligned(index * wide, wide)
                term = dot_nt(low_rows[b][half, at, lows(1)], r.key_full[row_at, :]) + dot_nt(
                    low_rows[b][half, at, lows(2)], r.value_full[row_at, :]
                )
                if half == 0:
                    term = term + dot_nt(
                        low_rows[b][half, at, lows(0)], r.query_full[row_at, :]
                    )
                r.total[:, row_at] = term

            over(width // wide, tile)

        mine = scatters[3 * batch + 2 * b + half].give(compute, r.total)
        r.total_own[2 * b + half] = r.total[mine, :]

    def other_copy(b):
        return remote(
            r.side_out.at[2 * batch + b],
            r.side_in.at[2 * batch + b],
            r.other_send.at[b],
            r.other_recv.at[b],
            seat.twin,
        )

    def other_give(b):
        r.side_out[2 * batch + b] = (
            r.total_own[2 * b + 1] + scatters[3 * batch + 2 * b + 1].take()
        ).astype(bf16)
        other_copy(b).start()

    def input_take(b):
        own = r.total_own[2 * b] + scatters[3 * batch + 2 * b].take()
        other_copy(b).wait_recv()
        r.input_grad[b] = (own + r.side_in[2 * batch + b].astype(f32)) + r.input_grad[b]

    def stepping(step, *which):
        def service():
            for piece in which:
                piece.advance(step)

        return service

    def down_done():
        r.down_grad[...] = from_down.advance(hops).reshape(hidden, depth)

    stepping(0, from_down)()
    heads_back(0, [(0, gathers[2 * batch + 1].relay), (1, stepping(1, from_down)), (3, stepping(1, from_up_too))])
    mix_back(1)
    output_tiles()
    from_output.begin()
    stepping(2, from_down)()
    for piece in scatters[: 3 * batch] + gathers[:batch] + gathers[2 * batch :]:
        piece.close()
    sequence_back(0)
    input_back(0, 1)
    stepping(0, from_up)()
    input_back(0, 0)
    heads_back(1, [(0, down_done), (1, stepping(1, from_up)), (2, stepping(0, from_output)), (3, lambda: other_give(0))])
    stepping(2, from_up_too)()
    stepping(1, from_output)()
    sequence_back(1)
    from_value.begin()
    thin[0].begin()
    thin[1].begin()
    input_back(1, 1)
    stepping(2, from_up)()
    stepping(0, from_value)()
    input_back(1, 0)
    stepping(1, *thin)()

    def sum_copy(stage, to):
        return remote(
            r.sum_all.at[stage], r.sum_in.at[stage], r.sum_send.at[stage], r.sum_recv.at[stage], to
        )

    def sum_stage(stage, to):
        r.sum_all[stage] = r.sums[...]
        sum_copy(stage, to).start()

    def sum_add(stage, to):
        sum_copy(stage, to).wait_recv()
        r.sums[...] = r.sums[...] + r.sum_in[stage]

    def around_copy(away):
        stage = 4 + away
        return remote(
            r.sum_all.at[3], r.sum_in.at[stage], r.sum_send.at[stage], r.sum_recv.at[stage], around[away]
        )

    def halve(piece, at):
        r.total[:, at] = piece.advance(hops)

    mine_at = aligned(seat.ctx * depth, depth)
    other_at = aligned((1 - seat.ctx) * depth, depth)
    sum_stage(0, seat.pair)
    input_take(0)
    sum_add(0, seat.pair)
    sum_stage(1, seat.side)
    other_give(1)
    stepping(1, from_value)()
    stepping(2, from_output)()
    sum_add(1, seat.side)
    sum_stage(2, seat.twin)
    stepping(2, *thin)()
    r.up_grad[:, :split] = from_up.advance(hops)
    halve(from_up_too, slice(split, hidden))
    r.up_half_out[...] = r.total[other_at, split:].astype(bf16)
    from_up_too.y().start()
    sum_add(2, seat.twin)
    r.sum_all[3] = r.sums[...]
    for away in range(hops):
        around_copy(away).start()
    stepping(2, from_value)()
    r.output_grad[...] = from_output.advance(hops)
    input_take(1)
    for k in range(2):
        halve(thin[k], slice(k * 2 * depth, (k + 1) * 2 * depth))
        spot = aligned(k * 2 * depth + (1 - seat.ctx) * depth, depth)
        r.half_out[k] = r.total[:, spot].astype(bf16)
        thin[k].y().start()
    from_up_too.y().wait_recv()
    r.up_grad[:, split:] = r.total[mine_at, split:] + r.up_half_in[...].astype(f32)
    r.value_grad[...] = from_value.advance(hops).T
    r.sum_in[3] = r.sums[...]
    for away in range(hops):
        around_copy(away).wait_recv()
    gathered = jnp.zeros_like(r.sums[...])
    for origin in range(count):
        gathered = gathered + r.sum_in[3 + (seat.dp + count - origin) % count]
    r.sums[...] = gathered
    for k, target in enumerate((r.query_grad, r.key_grad)):
        thin[k].y().wait_recv()
        spot = aligned(k * 2 * depth + seat.ctx * depth, depth)
        target[...] = (r.total[:, spot] + r.half_in[k].astype(f32)).T

    for stage, to in enumerate((seat.pair, seat.side, seat.twin)):
        sum_copy(stage, to).wait_send()
    for away in range(hops):
        around_copy(away).wait_send()
    for b in range(batch):
        other_copy(b).wait_send()
    for relation in range(7):
        for b in range(batch):
            token_out(relation, b).wait_send()
    for piece in weights + scatters[3 * batch :] + thin + [from_value, from_output, from_down, from_up, from_up_too]:
        piece.close()


def layer_call(inputs, segment_ids, cotangent, shards, vectors):
    count = lax.axis_size("dp")
    batch, part, width = inputs.shape
    rows = part * lax.axis_size("tp")
    local = shards[0].shape[1]
    hidden = shards[4].shape[1]
    heads = local // HEAD_DIM
    depth = width // (2 * count)
    bf16, f32 = jnp.bfloat16, jnp.float32
    ins = [
        ("inputs", LEFT),
        ("cotangent", LEFT),
        ("query_weight", LEFT),
        ("key_weight", LEFT),
        ("value_weight", LEFT),
        ("output_weight", LEFT),
        ("up_weight", LEFT),
        ("down_weight", LEFT),
        ("ids", VMEM),
        ("query_bias", VMEM),
        ("value_bias", VMEM),
        ("output_bias", VMEM),
        ("up_bias", VMEM),
        ("down_bias", VMEM),
        ("norm_gain", VMEM),
        ("norm_shift", VMEM),
        ("final_gain", VMEM),
        ("final_shift", VMEM),
    ]
    outs = [
        ("result", (batch, part, width), bf16),
        ("input_grad", (batch, part, width), f32),
        ("query_grad", (depth, local), f32),
        ("key_grad", (depth, local), f32),
        ("value_grad", (depth, local), f32),
        ("output_grad", (local, depth), f32),
        ("up_grad", (depth, hidden), f32),
        ("down_grad", (hidden, depth), f32),
        ("sums", (VECTOR_ROWS, width), f32),
    ]
    scratch = [
        ("tokens", (batch, rows, width), bf16),
        ("other", (batch, rows, width), bf16),
        ("query_full", (width, local), bf16),
        ("key_full", (width, local), bf16),
        ("value_full", (width, local), bf16),
        ("output_full", (local, width), bf16),
        ("up_full", (width, hidden), bf16),
        ("down_full", (hidden, width), bf16),
        ("queries", (batch, rows, local), bf16),
        ("keys", (batch, 2 * rows, local), bf16),
        ("values", (batch, 2 * rows, local), bf16),
        ("flipped", (batch, local, 2 * rows), bf16),
        ("mixture", (batch, local, rows), f32),
        ("logs", (batch * heads, 1, rows), f32),
        ("attended", (batch, rows, local), bf16),
        ("ids_down", (batch, 2 * rows, 128), f32),
        ("normed_rows", (batch, rows, width), bf16),
        ("hidden_rows", (batch, rows, hidden), bf16),
        ("slope_rows", (batch, rows, hidden), bf16),
        ("down_rows", (batch, rows, width), bf16),
        ("back_rows", (batch, rows, hidden), bf16),
        ("output_rows", (batch, rows, width), bf16),
        ("keep", (3, batch, part, width), f32),
        ("inverse_keep", (batch, part, 1), f32),
        ("total_own", (2 * batch, part, width), f32),
        ("total", (2 * part, width), f32),
        ("pair_out", (3 * batch, 2, part, width), bf16),
        ("pair_in", (3 * batch, 2, part, width), bf16),
        ("side_out", (3 * batch, part, width), bf16),
        ("side_in", (3 * batch, part, width), bf16),
        ("mixed", (batch, rows, local), bf16),
        ("output_part", (local, width), bf16),
        ("row_dots", (heads, 1, rows), f32),
        ("query_flip", (local, rows), f32),
        ("key_sum", (2 * rows, local), f32),
        ("value_sum", (2 * rows, local), f32),
        ("weight_low", (3, local, width), bf16),
        ("wide_out", (2, count - 2, local, 2 * depth), bf16),
        ("wide_in", (2, count - 1, local, 2 * depth), bf16),
        ("half_out", (2, local, depth), bf16),
        ("half_in", (2, local, depth), bf16),
        ("value_twin", (count, local, depth), bf16),
        ("value_out", (count - 1, local, depth), bf16),
        ("value_in", (count - 1, local, depth), bf16),
        ("output_twin", (count, local, depth), bf16),
        ("output_out", (count - 1, local, depth), bf16),
        ("output_in", (count - 1, local, depth), bf16),
        ("down_twin", (count, batch, rows, depth), bf16),
        ("down_in", (count - 1, batch, rows, depth), bf16),
        ("up_twin", (count, depth, hidden * 3 // 4), bf16),
        ("up_in", (count - 1, depth, hidden * 3 // 4), bf16),
        ("up_pair_in", (count - 1, 2 * depth, hidden // 4), bf16),
        ("up_half_out", (depth, hidden // 4), bf16),
        ("up_half_in", (depth, hidden // 4), bf16),
        ("sum_in", (3 + count, VECTOR_ROWS, width), f32),
        ("sum_all", (4, VECTOR_ROWS, width), f32),
    ]
    sems = [
        ("local_sem", (2 * batch,)),
        ("token_send", (14,)),
        ("token_recv", (14,)),
        ("own_sem", (7,)),
        ("gz_send", (7, 2 * (count - 1))),
        ("gz_recv", (7, 2 * (count - 1))),
        ("gy_send", (7, count)),
        ("gy_recv", (7, count)),
        ("scatter_send", (5 * batch, 3)),
        ("scatter_recv", (5 * batch, 3)),
        ("gather_send", (3 * batch, 3)),
        ("gather_recv", (3 * batch, 3)),
        ("other_send", (batch,)),
        ("other_recv", (batch,)),
        ("sum_send", (3 + count,)),
        ("sum_recv", (3 + count,)),
        ("ry_send", (7, count)),
        ("ry_recv", (7, count)),
        ("rz_send", (7, count - 1)),
        ("rz_recv", (7, count - 1)),
    ]
    names = [item[0] for group in (ins, outs, scratch, sems) for item in group]
    return pl.pallas_call(
        functools.partial(layer_kernel, names),
        name="layer",
        out_shape=[jax.ShapeDtypeStruct(shape, kind) for _, shape, kind in outs],
        in_specs=[space for _, space in ins],
        out_specs=[VMEM] * len(outs),
        scratch_shapes=[pltpu.VMEM(shape, kind) for _, shape, kind in scratch]
        + [pltpu.SemaphoreType.DMA(shape) for _, shape in sems],
        compiler_params=pltpu.CompilerParams(
            collective_id=1, has_side_effects=True, vmem_limit_bytes=67043328
        ),
    )(
        inputs,
        cotangent,
        *shards,
        segment_ids,
        *[vector.reshape(1, -1) for vector in vectors],
    )


def settle_kernel(moved, *refs):
    total = moved + 1
    sources, vectors, targets = refs[:moved], refs[moved], refs[total : total + moved]
    rows_out = refs[total + moved : total + moved + 9]
    held = refs[total + moved + 9 : total + 2 * moved + 9]
    in_sem, out_sem = refs[-2:]
    width = vectors.shape[1]
    into = [
        pltpu.make_async_copy(source, place, in_sem.at[k])
        for k, (source, place) in enumerate(zip(sources, held))
    ]
    out = [
        pltpu.make_async_copy(place, target, out_sem.at[k])
        for k, (place, target) in enumerate(zip(held, targets))
    ]
    for copy in into:
        copy.start()
    for row in range(8):
        rows_out[row][...] = vectors[row : row + 1, :]
    for k in range(4):
        rows_out[8][:, k * width : (k + 1) * width] = vectors[ROW_UP + k : ROW_UP + k + 1, :]
    for first, second in zip(into, out):
        first.wait()
        second.start()
    for copy in out:
        copy.wait()


def settle(arrays, sums):
    moved = len(arrays)
    width = sums.shape[1]
    same = [jax.ShapeDtypeStruct(array.shape, array.dtype) for array in arrays]
    rows_out = [jax.ShapeDtypeStruct((1, width), jnp.float32)] * 8
    rows_out.append(jax.ShapeDtypeStruct((1, 4 * width), jnp.float32))
    return pl.pallas_call(
        functools.partial(settle_kernel, moved),
        name="settle",
        out_shape=same + rows_out,
        in_specs=[LEFT] * moved + [VMEM],
        out_specs=[LEFT] * moved + [VMEM] * 9,
        scratch_shapes=[pltpu.VMEM(array.shape, array.dtype) for array in arrays]
        + [pltpu.SemaphoreType.DMA((moved,)), pltpu.SemaphoreType.DMA((moved,))],
        compiler_params=pltpu.CompilerParams(vmem_limit_bytes=56 * 2**20),
    )(*arrays, sums)


def fused_plan(
    inputs,
    segment_ids,
    query_weight,
    key_weight,
    value_weight,
    output_weight,
    up_weight,
    down_weight,
    querybias,
    valuebias,
    outputbias,
    upbias,
    downbias,
    norm_gain,
    norm_shift,
    final_gain,
    final_shift,
    cotangent,
):
    *grads, sums = layer_call(
        inputs,
        segment_ids,
        cotangent,
        (query_weight, key_weight, value_weight, output_weight, up_weight, down_weight),
        (
            querybias,
            valuebias,
            outputbias,
            upbias,
            downbias,
            norm_gain,
            norm_shift,
            final_gain,
            final_shift,
        ),
    )
    *outs, query, value, output, down, gain, shift, last_gain, last_shift, up = settle(grads, sums)
    rows = (query, value, output, up, down, gain, shift, last_gain, last_shift)
    return (*outs, *[row.reshape(-1) for row in rows])


def solution(mesh):
    fits = mesh.shape["ctx"] == 2 and mesh.shape["tp"] == 4 and mesh.shape["dp"] > 2
    placed = (
        P("dp", ("ctx", "tp"), None),
        P("dp", None),
        P(("dp", "ctx"), "tp"),
        P(("dp", "ctx"), "tp"),
        P(("dp", "ctx"), "tp"),
        P("tp", ("dp", "ctx")),
        P(("dp", "ctx"), "tp"),
        P("tp", ("dp", "ctx")),
        P(),
        P(),
        P(),
        P(),
        P(),
        P(),
        P(),
        P(),
        P(),
        P("dp", ("ctx", "tp"), None),
    )
    return jax.shard_map(
        fused_plan if fits else ring_plan,
        mesh=mesh,
        in_specs=placed,
        out_specs=(
            P("dp", ("ctx", "tp"), None),
            P("dp", ("ctx", "tp"), None),
            P(("dp", "ctx"), "tp"),
            P(("dp", "ctx"), "tp"),
            P(("dp", "ctx"), "tp"),
            P("tp", ("dp", "ctx")),
            P(("dp", "ctx"), "tp"),
            P("tp", ("dp", "ctx")),
            P(),
            P(),
            P(),
            P(),
            P(),
            P(),
            P(),
            P(),
            P(),
        ),
        check_vma=False,
    )
```
